32 devices in a mesh: img: 8 (over z, x), seq: 4 (over y, core).
Axes of the slice: x: 2, y: 2, z: 4, core: 2. Of those that a mesh axis runs over, the one named last changes fastest.
Arguments:
- patches: bfloat16 [16, 1024, 1024], P('img', 'seq'), may hold values from -6 to 6
- cotangent: bfloat16 [16, 1024, 1024], P('img', 'seq'), may hold values from -6 to 6
- res_ids: int32 [16, 20], P('img'), may hold values from 0 to 384, as said below
- pos_table: float32 [49, 1024], replicated, may hold values from -3 to 3
- attn_in: float32 [1024, 3072], P(('img', 'seq')), may hold values from -0.1875 to 0.1875
- attn_out: float32 [1024, 1024], P(('img', 'seq')), may hold values from -0.5 to 0.5
- mlp_in: float32 [1024, 4096], P(('img', 'seq')), may hold values from -0.1875 to 0.1875
- mlp_out: float32 [4096, 1024], P(('img', 'seq')), may hold values from -0.09375 to 0.09375
- vectors: float32 [1024, 12], P(('img', 'seq')), may hold values from -1 to 1.75
- first_attn_in: float32 [1024, 3072], P(('img', 'seq')), may hold values from -0.0018 to 0.0018
- first_attn_out: float32 [1024, 1024], P(('img', 'seq')), may hold values from -0.0018 to 0.0018
- first_mlp_in: float32 [1024, 4096], P(('img', 'seq')), may hold values from -0.0018 to 0.0018
- first_mlp_out: float32 [4096, 1024], P(('img', 'seq')), may hold values from -0.0018 to 0.0018
- first_vectors: float32 [1024, 12], P(('img', 'seq')), may hold values from -0.0018 to 0.0018
- second_attn_in: float32 [1024, 3072], P(('img', 'seq')), may hold values from 3e-09 to 3e-07
- second_attn_out: float32 [1024, 1024], P(('img', 'seq')), may hold values from 3e-09 to 3e-07
- second_mlp_in: float32 [1024, 4096], P(('img', 'seq')), may hold values from 3e-09 to 3e-07
- second_mlp_out: float32 [4096, 1024], P(('img', 'seq')), may hold values from 3e-09 to 3e-07
- second_vectors: float32 [1024, 12], P(('img', 'seq')), may hold values from 3e-09 to 3e-07
Outputs:
- output: bfloat16 [16, 1024, 1024], P('img', 'seq')
- input_grad: bfloat16 [16, 1024, 1024], P('img', 'seq')
- table_grad: float32 [49, 1024], replicated
- grad_attn_in: float32 [1024, 3072], P(('img', 'seq'))
- grad_attn_out: float32 [1024, 1024], P(('img', 'seq'))
- grad_mlp_in: float32 [1024, 4096], P(('img', 'seq'))
- grad_mlp_out: float32 [4096, 1024], P(('img', 'seq'))
- grad_vectors: float32 [1024, 12], P(('img', 'seq'))
- update_attn_in: float32 [1024, 3072], P(('img', 'seq'))
- update_attn_out: float32 [1024, 1024], P(('img', 'seq'))
- update_mlp_in: float32 [1024, 4096], P(('img', 'seq'))
- update_mlp_out: float32 [4096, 1024], P(('img', 'seq'))
- update_vectors: float32 [1024, 12], P(('img', 'seq'))
- new_first_attn_in: float32 [1024, 3072], P(('img', 'seq'))
- new_first_attn_out: float32 [1024, 1024], P(('img', 'seq'))
- new_first_mlp_in: float32 [1024, 4096], P(('img', 'seq'))
- new_first_mlp_out: float32 [4096, 1024], P(('img', 'seq'))
- new_first_vectors: float32 [1024, 12], P(('img', 'seq'))
- new_second_attn_in: float32 [1024, 3072], P(('img', 'seq'))
- new_second_attn_out: float32 [1024, 1024], P(('img', 'seq'))
- new_second_mlp_in: float32 [1024, 4096], P(('img', 'seq'))
- new_second_mlp_out: float32 [4096, 1024], P(('img', 'seq'))
- new_second_vectors: float32 [1024, 12], P(('img', 'seq'))
The draws below stay inside these ranges and needn't reach their ends.
Inputs may be any that keep to these rules, and one draw needn't show every extreme that they name: `res_ids`: each entry is 224, 384 or 0; a 0 is followed only by 0s in its row; a row's images fit within its 1024 tokens.
All inputs are finite; a program needn't handle non-finite values.
Results may differ from the reference program's by a relative error of at most 0.018.
Values may be sent and summed in bfloat16 or wider, within the bound.
No kernel may reach another device: no remote copies, remote signals or barrier semaphores. Data moves between devices by JAX's collectives and lax.ppermute only.
A program may use at most 256 MiB of HBM per device.

```python
import math
import jax
import jax.numpy as jnp
from jax import lax

D = 1024
HEADS = 16
HD = 64
FF = 4096
GRID = 7
GRID_HI = 12
ROW_LEN = 1024
ROWS = 16
MAXIMG = 20
POS = 49
VCOLS = 12


def draw_res_ids(key, part):
    picked = jax.random.randint(key, (ROWS, MAXIMG), 0, 2)
    resolution = jnp.where(picked == 1, 384, 224).astype(jnp.int32)
    lengths = jnp.where(picked == 1, GRID_HI * GRID_HI, GRID * GRID).astype(jnp.int32)
    endings = jnp.cumsum(lengths, axis=1)
    return jnp.where(endings <= ROW_LEN, resolution, 0).astype(jnp.int32)


def draw_vectors(key, part):
    noise = jnp.clip(jax.random.normal(key, (D, VCOLS), jnp.float32), -5.0, 5.0)
    column = jnp.arange(VCOLS, dtype=jnp.int32)
    is_gain = (column == 0) | (column == 5)
    return jnp.where(is_gain[None, :], 1.0 + 0.15 * noise, 0.2 * noise).astype(jnp.float32)


def block_scale(stream_key, dims, pieces, least, largest):
    loudness = 1.0
    for dim, parts in pieces:
        heights = jax.random.uniform(jax.random.fold_in(jax.random.fold_in(stream_key, 6), dim), (parts,), jnp.float32, least / len(pieces), largest / len(pieces))
        loudness = loudness * jnp.repeat(jnp.exp(heights), dims[dim] // parts).reshape((-1,) + (1,) * (len(dims) - 1 - dim))
    return loudness


def gaussian(own_key, shape, scale, reach, cuts=(), kind=jnp.bfloat16):
    entries = scale * jax.random.normal(own_key, shape, jnp.float32)
    if cuts:
        entries = entries * block_scale(own_key, shape, cuts, -0.22, 0.18)
    return jnp.clip(entries, -reach, reach).astype(kind)


def setup_inputs(seed: int = 0) -> dict:
    arg_keys = jax.random.split(jax.random.key(seed), 20)
    patches = gaussian(arg_keys[0], (ROWS, ROW_LEN, D), 1.0, 6.0, ((0, 8), (1, 4)))
    cotangent = gaussian(arg_keys[1], (ROWS, ROW_LEN, D), 1.0, 6.0, ((0, 8), (1, 4)))
    res_ids = draw_res_ids(jax.random.fold_in(arg_keys[19], 71), 0)
    pos_table = gaussian(arg_keys[3], (POS, D), 0.5, 3.0, (), jnp.float32)
    attn_in = gaussian(arg_keys[4], (D, 3 * D), D ** -0.5, 0.1875, ((0, 32),), jnp.float32)
    attn_out = gaussian(arg_keys[5], (D, D), (D // 8) ** -0.5, 0.5, ((0, 32),), jnp.float32)
    mlp_in = gaussian(arg_keys[6], (D, FF), D ** -0.5, 0.1875, ((0, 32),), jnp.float32)
    mlp_out = gaussian(arg_keys[7], (FF, D), FF ** -0.5, 0.09375, ((0, 32),), jnp.float32)
    vectors = draw_vectors(jax.random.fold_in(arg_keys[19], 71), 0)
    first_attn_in = gaussian(arg_keys[9], (D, 3 * D), 0.0003, 0.0018, ((0, 32),), jnp.float32)
    first_attn_out = gaussian(arg_keys[10], (D, D), 0.0003, 0.0018, ((0, 32),), jnp.float32)
    first_mlp_in = gaussian(arg_keys[11], (D, FF), 0.0003, 0.0018, ((0, 32),), jnp.float32)
    first_mlp_out = gaussian(arg_keys[12], (FF, D), 0.0003, 0.0018, ((0, 32),), jnp.float32)
    first_vectors = gaussian(arg_keys[13], (D, VCOLS), 0.0003, 0.0018, ((0, 32),), jnp.float32)
    second_attn_in = jnp.clip(jnp.exp(math.log(3.000000106112566e-07) - 4.6051702 * jax.random.uniform(arg_keys[14], (D, 3 * D), jnp.float32) ** block_scale(arg_keys[14], (D, 3 * D), ((0, 32),), -0.2, 0.2)), 3.000000026176508e-09, 3.000000106112566e-07)
    second_attn_out = jnp.clip(jnp.exp(math.log(3.000000106112566e-07) - 4.6051702 * jax.random.uniform(arg_keys[15], (D, D), jnp.float32) ** block_scale(arg_keys[15], (D, D), ((0, 32),), -0.2, 0.2)), 3.000000026176508e-09, 3.000000106112566e-07)
    second_mlp_in = jnp.clip(jnp.exp(math.log(3.000000106112566e-07) - 4.6051702 * jax.random.uniform(arg_keys[16], (D, FF), jnp.float32) ** block_scale(arg_keys[16], (D, FF), ((0, 32),), -0.2, 0.2)), 3.000000026176508e-09, 3.000000106112566e-07)
    second_mlp_out = jnp.clip(jnp.exp(math.log(3.000000106112566e-07) - 4.6051702 * jax.random.uniform(arg_keys[17], (FF, D), jnp.float32) ** block_scale(arg_keys[17], (FF, D), ((0, 32),), -0.2, 0.2)), 3.000000026176508e-09, 3.000000106112566e-07)
    second_vectors = jnp.clip(jnp.exp(math.log(3.000000106112566e-07) - 4.6051702 * jax.random.uniform(arg_keys[18], (D, VCOLS), jnp.float32) ** block_scale(arg_keys[18], (D, VCOLS), ((0, 32),), -0.2, 0.2)), 3.000000026176508e-09, 3.000000106112566e-07)
    return {"patches": patches, "cotangent": cotangent, "res_ids": res_ids, "pos_table": pos_table, "attn_in": attn_in, "attn_out": attn_out, "mlp_in": mlp_in, "mlp_out": mlp_out, "vectors": vectors, "first_attn_in": first_attn_in, "first_attn_out": first_attn_out, "first_mlp_in": first_mlp_in, "first_mlp_out": first_mlp_out, "first_vectors": first_vectors, "second_attn_in": second_attn_in, "second_attn_out": second_attn_out, "second_mlp_in": second_mlp_in, "second_mlp_out": second_mlp_out, "second_vectors": second_vectors}


PRECISE = lax.Precision.HIGHEST
FIRST_CORRECTION = 0.9999734386011124
SECOND_CORRECTION = 0.0952078528862911

@jax.custom_vjp
def low(v):
    return lax.optimization_barrier(v.astype(jnp.bfloat16)).astype(jnp.float32)

@jax.custom_vjp
def low_back(v):
    return v

def low_keep(v):
    return (low(v), None)

def low_pass(kept, grad):
    return (grad,)

def back_keep(v):
    return (v, None)

def back_low(kept, grad):
    return (low(grad),)
low.defvjp(low_keep, low_pass)
low_back.defvjp(back_keep, back_low)

def layout(res_ids, positions):
    grid_side = jnp.where(res_ids == 384, GRID_HI, jnp.where(res_ids == 224, GRID, 0)).astype(jnp.int32)
    lengths = grid_side * grid_side
    starts = jnp.cumsum(lengths, axis=1).astype(jnp.int32) - lengths
    places = positions[None, :, None]
    inside = ((places >= starts[:, None, :]) & (places < (starts + lengths)[:, None, :])).astype(jnp.int32)
    image_number = jnp.arange(res_ids.shape[1], dtype=jnp.int32)
    usable = lax.optimization_barrier(jnp.sum(inside, axis=2)).astype(jnp.int32)
    segment = lax.optimization_barrier(jnp.sum(inside * image_number, axis=2)).astype(jnp.int32) + (1 - usable) * res_ids.shape[1]
    start_of = lax.optimization_barrier(jnp.sum(inside * starts[:, None, :], axis=2)).astype(jnp.int32)
    side_of = lax.optimization_barrier(jnp.sum(inside * grid_side[:, None, :], axis=2)).astype(jnp.int32)
    patch_index = (positions[None, :] - start_of) * usable
    return (segment, side_of, patch_index, usable)

def axis_weights(coord, side_of):
    scaled = jnp.maximum((2 * coord + 1) * GRID - GRID_HI, 0)
    lower_fine = scaled // (2 * GRID_HI)
    fraction_fine = (scaled - lower_fine * 2 * GRID_HI).astype(jnp.float32) / (2.0 * GRID_HI)
    resized = side_of == GRID_HI
    lower_cell = jnp.where(resized, lower_fine, coord)
    fraction = jnp.where(resized, fraction_fine, jnp.zeros_like(fraction_fine))
    upper_cell = jnp.minimum(lower_cell + 1, GRID - 1)
    cell_index = jnp.arange(GRID, dtype=jnp.int32)
    below = (cell_index == lower_cell[..., None]).astype(jnp.float32)
    above = (cell_index == upper_cell[..., None]).astype(jnp.float32)
    return (1.0 - fraction)[..., None] * below + fraction[..., None] * above

def table_weights(side_of, patch_index, usable):
    safe_side = jnp.maximum(side_of, 1)
    row_coord = patch_index // safe_side
    column_coord = patch_index % safe_side
    outer = axis_weights(row_coord, side_of)[..., :, None] * axis_weights(column_coord, side_of)[..., None, :]
    outer = outer * usable.astype(jnp.float32)[..., None, None]
    return outer.reshape(side_of.shape + (GRID * GRID,))

def layer_norm(stream, gain, shift):
    center = lax.optimization_barrier(jnp.mean(stream, axis=-1, keepdims=True))
    centered = stream - center
    spread = lax.optimization_barrier(jnp.mean(centered * centered, axis=-1, keepdims=True))
    return centered * lax.rsqrt(spread + 1e-06) * gain + shift

def attend(inputs):
    query_heads, key_heads, value_heads, segment = inputs
    scores = jnp.einsum('qhe,khe->hqk', query_heads, key_heads, precision=PRECISE) * HD ** (-0.5)
    scores = low_back(scores)
    allowed = segment[:, None] == segment[None, :]
    scores = jnp.where(allowed[None], scores, -1e+30)
    probs = low(jax.nn.softmax(scores, axis=-1))
    return jnp.einsum('hqk,khe->qhe', probs, value_heads, precision=PRECISE)

def forward(patch_rows, table, attn_in, attn_out, mlp_in, mlp_out, vectors, segment, place, usable):
    vector_cols = low(vectors)
    stream = patch_rows + jnp.einsum('rtp,pd->rtd', place, table, precision=PRECISE)
    normed_one = low(layer_norm(stream, vector_cols[:, 0], vector_cols[:, 1]))
    projected = jnp.einsum('rtd,de->rte', normed_one, low(attn_in), precision=PRECISE)
    query = low(low_back(projected[..., :D] + vector_cols[:, 2]))
    key_rows = low(low_back(projected[..., D:2 * D]))
    value_rows = low(low_back(projected[..., 2 * D:] + vector_cols[:, 3]))
    head_shape = query.shape[:2] + (HEADS, HD)
    attended = lax.map(jax.checkpoint(attend), (query.reshape(head_shape), key_rows.reshape(head_shape), value_rows.reshape(head_shape), segment))
    attended = low(low_back(attended.reshape(query.shape)))
    branch = low_back(jnp.einsum('rtd,de->rte', attended, low(attn_out), precision=PRECISE) + vector_cols[:, 4])
    stream_two = stream + branch
    normed_two = low(layer_norm(stream_two, vector_cols[:, 5], vector_cols[:, 6]))
    hidden_pre = low_back(jnp.einsum('rtd,df->rtf', normed_two, low(mlp_in), precision=PRECISE) + vector_cols[:, 8:].reshape(FF))
    hidden = low(jax.nn.gelu(hidden_pre, approximate=False))
    last = low_back(jnp.einsum('rtf,fd->rtd', hidden, low(mlp_out), precision=PRECISE) + vector_cols[:, 7])
    return (stream_two + last) * usable[..., None]

def adam_update(weight, gradient, first_moment, second_moment, factor, decay):
    scaled = gradient * factor
    first_new = 0.9 * first_moment + 0.1 * scaled
    second_new = 0.999 * second_moment + 0.001 * scaled * scaled
    first_hat = first_new / FIRST_CORRECTION
    second_hat = second_new / SECOND_CORRECTION
    direction = first_hat / (jnp.sqrt(second_hat) + 1e-08) + decay * weight
    return (direction, first_new, second_new)

def reference(patches, cotangent, res_ids, pos_table, attn_in, attn_out, mlp_in, mlp_out, vectors, first_attn_in, first_attn_out, first_mlp_in, first_mlp_out, first_vectors, second_attn_in, second_attn_out, second_mlp_in, second_mlp_out, second_vectors):
    grouped = math.gcd(ROWS, max(1, 4096 // ROW_LEN))
    group_count = ROWS // grouped
    positions = jnp.arange(ROW_LEN, dtype=jnp.int32)
    segment, side_of, patch_index, usable = layout(res_ids, positions)
    place = table_weights(side_of, patch_index, usable)
    usable_float = usable.astype(jnp.float32)
    params = (pos_table, attn_in, attn_out, mlp_in, mlp_out, vectors)

    def regroup(array):
        return array.reshape((group_count, grouped) + array.shape[1:])
    inputs = (regroup(patches.astype(jnp.float32)), regroup(cotangent.astype(jnp.float32)), regroup(segment), regroup(place), regroup(usable_float))

    def step(totals, item):
        patch_group, cot_group, segment_group, place_group, usable_group = item

        def run(patch_rows, *weights):
            return forward(patch_rows, *weights, segment_group, place_group, usable_group)
        result, pull = jax.vjp(run, patch_group, *params)
        gradients = pull(cot_group)
        totals = tuple((acc + part for acc, part in zip(totals, gradients[1:])))
        return (totals, (result.astype(jnp.bfloat16), gradients[0].astype(jnp.bfloat16)))
    initial = tuple((jnp.zeros_like(param) for param in params))
    totals, (results, patch_grads) = lax.scan(step, initial, inputs)
    output = results.reshape(ROWS, ROW_LEN, D)
    input_grad = patch_grads.reshape(ROWS, ROW_LEN, D)
    table_grad = totals[0]
    weight_grads = totals[1:]
    factor = jnp.float32(1.0 / (ROWS * ROW_LEN))
    weights = (attn_in, attn_out, mlp_in, mlp_out, vectors)
    firsts = (first_attn_in, first_attn_out, first_mlp_in, first_mlp_out, first_vectors)
    seconds = (second_attn_in, second_attn_out, second_mlp_in, second_mlp_out, second_vectors)
    decays = (0.05, 0.05, 0.05, 0.05, 0.0)
    updated = [adam_update(weights[index], weight_grads[index], firsts[index], seconds[index], factor, decays[index]) for index in range(5)]
    return (output, input_grad, table_grad, weight_grads[0], weight_grads[1], weight_grads[2], weight_grads[3], weight_grads[4], updated[0][0], updated[1][0], updated[2][0], updated[3][0], updated[4][0], updated[0][1], updated[1][1], updated[2][1], updated[3][1], updated[4][1], updated[0][2], updated[1][2], updated[2][2], updated[3][2], updated[4][2])
```

```python
import functools
import math

import jax
import jax.numpy as jnp
from jax import lax
from jax.experimental import pallas as pl
from jax.experimental.pallas import tpu as pltpu
from jax.sharding import Mesh
from jax.sharding import PartitionSpec as P

HEADS = 16
GRID = 7
GRID_HI = 12
TILE = 128

PRECISE = lax.Precision.HIGHEST
FIRST_CORRECTION = 0.9999734386011124
SECOND_CORRECTION = 0.0952078528862911
EPS = 1e-06

F32 = jnp.float32
BF16 = jnp.bfloat16


def image_spans(res_row):
    side = jnp.where(res_row == 384, GRID_HI, jnp.where(res_row == 224, GRID, 0)).astype(jnp.int32)
    lengths = side * side
    slots = res_row.shape[0]
    order = jnp.arange(slots, dtype=jnp.int32)
    earlier = order[None, :] < order[:, None]
    starts = jnp.sum(jnp.where(earlier, lengths[None, :], 0), axis=1)
    return side, lengths, starts


def layout(res_row, positions):
    side, lengths, starts = image_spans(res_row)
    slots = res_row.shape[0]
    places = positions[:, None]
    inside = ((places >= starts[None, :]) & (places < (starts + lengths)[None, :])).astype(jnp.int32)
    usable = jnp.sum(inside, axis=1)
    image_number = jnp.arange(slots, dtype=jnp.int32)
    segment = jnp.sum(inside * image_number, axis=1) + (1 - usable) * slots
    start_of = jnp.sum(inside * starts[None, :], axis=1)
    side_of = jnp.sum(inside * side[None, :], axis=1)
    patch_index = (positions - start_of) * usable
    return segment, side_of, patch_index, usable


def key_bounds(res_row, row_len):
    _, lengths, starts = image_spans(res_row)
    total = jnp.sum(lengths)
    firsts = jnp.arange(row_len // TILE, dtype=jnp.int32) * TILE

    def span(positions):
        places = positions[:, None]
        inside = (places >= starts[None, :]) & (places < (starts + lengths)[None, :])
        found = positions < total
        begin = jnp.sum(jnp.where(inside, starts[None, :], 0), axis=1)
        end = jnp.sum(jnp.where(inside, (starts + lengths)[None, :], 0), axis=1)
        return jnp.where(found, begin, total), jnp.where(found, end, row_len)

    begin, _ = span(firsts)
    _, end = span(firsts + (TILE - 1))
    return begin // TILE, (end + TILE - 1) // TILE


def axis_weights(coord, side_of):
    scaled = jnp.maximum((2 * coord + 1) * GRID - GRID_HI, 0)
    lower_fine = scaled // (2 * GRID_HI)
    fraction_fine = (scaled - lower_fine * 2 * GRID_HI).astype(F32) / (2.0 * GRID_HI)
    resized = side_of == GRID_HI
    lower_cell = jnp.where(resized, lower_fine, coord)
    fraction = jnp.where(resized, fraction_fine, jnp.zeros_like(fraction_fine))
    upper_cell = jnp.minimum(lower_cell + 1, GRID - 1)
    cell_index = jnp.arange(GRID, dtype=jnp.int32)
    below = (cell_index == lower_cell[..., None]).astype(F32)
    above = (cell_index == upper_cell[..., None]).astype(F32)
    return (1.0 - fraction)[..., None] * below + fraction[..., None] * above


def table_weights(side_of, patch_index, usable):
    safe_side = jnp.maximum(side_of, 1)
    row_coord = patch_index // safe_side
    column_coord = patch_index % safe_side
    outer = axis_weights(row_coord, side_of)[:, :, None] * axis_weights(column_coord, side_of)[:, None, :]
    outer = outer * usable.astype(F32)[:, None, None]
    return outer.reshape(side_of.shape[0], GRID * GRID)


def place_of(block, own_y, own_c, per):
    quarter = block // per
    core = (quarter % 2 + own_c) % 2
    half = (quarter // 2 + own_y) % 2
    return (core * 2 + half) * per + block % per


def split_heads(pair):
    lane = lax.broadcasted_iota(jnp.int32, pair.shape, 1)
    zero = jnp.zeros_like(pair)
    low = lane < pair.shape[1] // 2
    return jnp.concatenate([jnp.where(low, pair, zero), jnp.where(low, zero, pair)], axis=0)


def join_heads(stacked):
    half = stacked.shape[0] // 2
    lane = lax.broadcasted_iota(jnp.int32, (half, stacked.shape[1]), 1)
    return jnp.where(lane < stacked.shape[1] // 2, stacked[:half], stacked[half:])


def down_lanes(row):
    return jnp.transpose(jnp.broadcast_to(row, (TILE, TILE)))


def nt(left, right):
    return lax.dot_general(left, right, (((1,), (1,)), ((), ())), preferred_element_type=F32)


def tn(left, right):
    return lax.dot_general(left, right, (((0,), (0,)), ((), ())), preferred_element_type=F32)


def nn(left, right):
    return jnp.dot(left, right, preferred_element_type=F32)


def attend_kernel(pairs, width, per, scale, info, qkv, seg, out, log_sum, scores, high, total, mixed):
    tile = pl.program_id(0)
    own_y, own_c = info[0], info[1]
    first, last = info[2 + tile], info[2 + pl.num_programs(0) + tile]
    q_at = pl.multiple_of(place_of(tile, own_y, own_c, per) * TILE, TILE)
    seg_q = down_lanes(seg[0:1, pl.ds(pl.multiple_of(tile * TILE, TILE), TILE)])
    high[...] = jnp.full_like(high, -1e30)
    total[...] = jnp.zeros_like(total)
    mixed[...] = jnp.zeros_like(mixed)
    queries = []
    for j in range(pairs):
        queries.append(split_heads(qkv[pl.ds(q_at, TILE), j * TILE : (j + 1) * TILE] * jnp.asarray(scale, BF16)))

    def score(block, carry):
        k_at = pl.multiple_of(place_of(block, own_y, own_c, per) * TILE, TILE)
        seg_k = seg[0:1, pl.ds(pl.multiple_of(block * TILE, TILE), TILE)]
        same = seg_q == seg_k
        same = jnp.concatenate([same, same], axis=0)
        for j in range(pairs):
            keys = qkv[pl.ds(k_at, TILE), width + j * TILE : width + (j + 1) * TILE]
            s = jnp.where(same, nt(queries[j], keys), -1e30)
            scores[j, block] = s
            high[j] = jnp.maximum(high[j], s)
        return carry

    lax.fori_loop(first, last, score, 0)
    tops = [jnp.max(high[j], axis=1, keepdims=True) for j in range(pairs)]

    def mix(block, carry):
        k_at = pl.multiple_of(place_of(block, own_y, own_c, per) * TILE, TILE)
        for j in range(pairs):
            values = qkv[pl.ds(k_at, TILE), 2 * width + j * TILE : 2 * width + (j + 1) * TILE]
            p = jnp.exp(scores[j, block] - tops[j])
            total[j] += p
            mixed[j] += nn(p.astype(BF16), values)
        return carry

    lax.fori_loop(first, last, mix, 0)
    lane = lax.broadcasted_iota(jnp.int32, (TILE, TILE), 1)
    logs = jnp.zeros((TILE, TILE), F32)
    for j in range(pairs):
        sums = jnp.sum(total[j], axis=1, keepdims=True)
        out[:, j * TILE : (j + 1) * TILE] = join_heads(mixed[j] / sums).astype(BF16)
        log_total = tops[j] + jnp.log(sums)
        logs = jnp.where(lane == 2 * j, log_total[:TILE], logs)
        logs = jnp.where(lane == 2 * j + 1, log_total[TILE:], logs)
    log_sum[...] = jnp.transpose(logs)[: 2 * pairs]


def attend_back_kernel(
    pairs, width, per, scale, info, qkv, mixed, grad, seg, log_sum, out, grad_keys, grad_values, grad_query
):
    tile = pl.program_id(0)
    own_y, own_c = info[0], info[1]
    first, last = info[2 + tile], info[2 + pl.num_programs(0) + tile]
    q_at = pl.multiple_of(place_of(tile, own_y, own_c, per) * TILE, TILE)
    q_from = pl.multiple_of(tile * TILE, TILE)
    seg_q = seg[0:1, pl.ds(q_from, TILE)]

    @pl.when(tile == 0)
    def _():
        grad_keys[...] = jnp.zeros_like(grad_keys)
        grad_values[...] = jnp.zeros_like(grad_values)

    grad_query[...] = jnp.zeros_like(grad_query)
    queries, grads, logs, inner = [], [], [], []
    for j in range(pairs):
        columns = slice(j * TILE, (j + 1) * TILE)
        queries.append(split_heads(qkv[pl.ds(q_at, TILE), columns] * jnp.asarray(scale, BF16)))
        g = grad[pl.ds(q_at, TILE), columns]
        grads.append(split_heads(g))
        both = jnp.transpose(g.astype(F32) * mixed[pl.ds(q_at, TILE), columns].astype(F32))
        low = jnp.sum(both[: TILE // 2], axis=0, keepdims=True)
        high = jnp.sum(both[TILE // 2 :], axis=0, keepdims=True)
        inner.append(jnp.concatenate([low, high], axis=1))
        here = log_sum[2 * j : 2 * j + 2, pl.ds(q_from, TILE)]
        logs.append(jnp.concatenate([here[0:1], here[1:2]], axis=1))

    def step(block, carry):
        at = place_of(block, own_y, own_c, per) * TILE
        k_at = pl.multiple_of(at, TILE)
        seg_k = down_lanes(seg[0:1, pl.ds(pl.multiple_of(block * TILE, TILE), TILE)])
        same = seg_k == seg_q
        same = jnp.concatenate([same, same], axis=1)
        for j in range(pairs):
            columns = slice(j * TILE, (j + 1) * TILE)
            keys = qkv[pl.ds(k_at, TILE), width + j * TILE : width + (j + 1) * TILE]
            values = qkv[pl.ds(k_at, TILE), 2 * width + j * TILE : 2 * width + (j + 1) * TILE]
            s = jnp.where(same, nt(keys, queries[j]), -1e30)
            p = jnp.exp(s - logs[j])
            grad_values[pl.ds(k_at, TILE), columns] += nn(p.astype(BF16), grads[j])
            ds = (p * (nt(values, grads[j]) - inner[j])).astype(BF16)
            grad_keys[pl.ds(k_at, TILE), columns] += nn(ds, queries[j])
            grad_query[j] += tn(ds, keys)
        return carry

    lax.fori_loop(first, last, step, 0)
    for j in range(pairs):
        out[pl.ds(q_at, TILE), j * TILE : (j + 1) * TILE] = (join_heads(grad_query[j]) * scale).astype(BF16)

    @pl.when(tile == pl.num_programs(0) - 1)
    def _():
        out[:, width : 2 * width] = grad_keys[...].astype(BF16)
        out[:, 2 * width :] = grad_values[...].astype(BF16)


def attention(qkv, seg, info, per, head_size):
    length, width = qkv.shape[0], qkv.shape[1] // 3
    pairs, tiles = width // TILE, length // TILE
    scale = head_size ** (-0.5)

    def place(i, info):
        return place_of(i, info[0], info[1], per)

    return pl.pallas_call(
        functools.partial(attend_kernel, pairs, width, per, scale),
        name="attend",
        out_shape=(
            jax.ShapeDtypeStruct((length, width), BF16),
            jax.ShapeDtypeStruct((2 * pairs, length), F32),
        ),
        grid_spec=pltpu.PrefetchScalarGridSpec(
            num_scalar_prefetch=1,
            grid=(tiles,),
            in_specs=[
                pl.BlockSpec(qkv.shape, lambda i, info: (0, 0), pipeline_mode=pl.Buffered(1)),
                pl.BlockSpec(seg.shape, lambda i, info: (0, 0), pipeline_mode=pl.Buffered(1)),
            ],
            out_specs=[
                pl.BlockSpec((TILE, width), lambda i, info: (place(i, info), 0)),
                pl.BlockSpec((2 * pairs, TILE), lambda i, info: (0, i)),
            ],
            scratch_shapes=[
                pltpu.VMEM((pairs, tiles, 2 * TILE, TILE), F32),
                pltpu.VMEM((pairs, 2 * TILE, TILE), F32),
                pltpu.VMEM((pairs, 2 * TILE, TILE), F32),
                pltpu.VMEM((pairs, 2 * TILE, TILE), F32),
            ],
        ),
        compiler_params=pltpu.CompilerParams(
            dimension_semantics=("arbitrary",), vmem_limit_bytes=40 << 20
        ),
        cost_estimate=pl.CostEstimate(
            flops=length * length * width * 2, bytes_accessed=4 * length * width * 2, transcendentals=0
        ),
    )(info, qkv, seg)


def attention_back(qkv, mixed, grad, seg, log_sum, info, per, head_size):
    length, width = qkv.shape[0], qkv.shape[1] // 3
    pairs, tiles = width // TILE, length // TILE
    scale = head_size ** (-0.5)

    def whole(array):
        return pl.BlockSpec(array.shape, lambda i, info: (0, 0), pipeline_mode=pl.Buffered(1))

    return pl.pallas_call(
        functools.partial(attend_back_kernel, pairs, width, per, scale),
        name="attend_back",
        out_shape=jax.ShapeDtypeStruct(qkv.shape, BF16),
        grid_spec=pltpu.PrefetchScalarGridSpec(
            num_scalar_prefetch=1,
            grid=(tiles,),
            in_specs=[whole(qkv), whole(mixed), whole(grad), whole(seg), whole(log_sum)],
            out_specs=pl.BlockSpec(qkv.shape, lambda i, info: (0, 0)),
            scratch_shapes=[
                pltpu.VMEM((length, width), F32),
                pltpu.VMEM((length, width), F32),
                pltpu.VMEM((pairs, 2 * TILE, TILE), F32),
            ],
        ),
        compiler_params=pltpu.CompilerParams(
            dimension_semantics=("arbitrary",), vmem_limit_bytes=48 << 20
        ),
        cost_estimate=pl.CostEstimate(
            flops=length * length * width * 5, bytes_accessed=8 * length * width * 2, transcendentals=0
        ),
    )(info, qkv, mixed, grad, seg, log_sum)


SWAP = [(0, 1), (1, 0)]


def swap_core(array):
    return lax.ppermute(array, "sc", SWAP)


def swap_chip(array):
    return lax.ppermute(array, "sy", SWAP)


def swap_bit(array, bit):
    if bit == 0:
        return swap_chip(array)
    count = lax.axis_size("img")
    return lax.ppermute(array, "img", [(i, i ^ (1 << (bit - 1))) for i in range(count)])


def own_bit(bit):
    if bit == 0:
        return lax.axis_index("sy")
    return (lax.axis_index("img") >> (bit - 1)) & 1


def bit_orders():
    bits = int(math.log2(lax.axis_size("img"))) + 1
    rest = list(range(2, bits))
    return rest + [1, 0], rest + [0, 1]


def axis_of(bit, done):
    return sum(1 for other in done if other > bit)


def pick(index, low, high):
    return jnp.where(index == 0, low, high)


def gather_chips(block, order):
    held, done = block, []
    for bit in order:
        came = swap_bit(held, bit)
        mine = own_bit(bit)
        held = jnp.stack([pick(mine, held, came), pick(mine, came, held)], axis=axis_of(bit, done))
        done.append(bit)
    return held.reshape(-1, block.shape[1])


def scatter_chips(total, order):
    rows, columns = total.shape
    bits = sorted(order, reverse=True)
    held = total.astype(BF16).reshape((2,) * len(bits) + (rows >> len(bits), columns))
    for bit in reversed(order):
        axis = bits.index(bit)
        mine = own_bit(bit)
        away = lax.dynamic_index_in_dim(held, 1 - mine, axis, keepdims=False)
        keep = lax.dynamic_index_in_dim(held, mine, axis, keepdims=False)
        held = keep.astype(F32) + swap_bit(away, bit).astype(F32)
        bits.remove(bit)
        if bits:
            held = held.astype(BF16)
    return held


def gather_halves(block):
    first, second = bit_orders()
    half = block.shape[1] // 2
    return gather_chips(block[:, :half], first), gather_chips(block[:, half:], second)


def gather_all(block):
    return jnp.concatenate(gather_halves(block), axis=1)


def scatter_all(total):
    first, second = bit_orders()
    half = total.shape[1] // 2
    return jnp.concatenate(
        [scatter_chips(total[:, :half], first), scatter_chips(total[:, half:], second)], axis=1
    )


def normalize(stream):
    center = jnp.mean(stream, axis=-1, keepdims=True)
    centered = stream - center
    spread = jnp.mean(centered * centered, axis=-1, keepdims=True)
    inverse = lax.rsqrt(spread + EPS)
    return centered * inverse, inverse


def normalize_back(normed, inverse, gain, grad):
    scaled = grad * gain
    middle = jnp.mean(scaled, axis=-1, keepdims=True)
    along = jnp.mean(scaled * normed, axis=-1, keepdims=True)
    return (
        inverse * (scaled - middle - normed * along),
        jnp.sum(grad * normed, axis=0),
        jnp.sum(grad, axis=0),
    )


def gelu_and_slope(values):
    cdf = 0.5 * (1.0 + lax.erf(values * (0.5**0.5)))
    density = jnp.exp(-0.5 * values * values) * (1.0 / math.sqrt(2.0 * math.pi))
    return values * cdf, cdf + values * density


def adam_update(weight, gradient, first_moment, second_moment, factor, decay):
    scaled = gradient * factor
    first_new = 0.9 * first_moment + 0.1 * scaled
    second_new = 0.999 * second_moment + 0.001 * scaled * scaled
    first_hat = first_new / FIRST_CORRECTION
    second_hat = second_new / SECOND_CORRECTION
    direction = first_hat / (jnp.sqrt(second_hat) + 1e-08) + decay * weight
    return (direction, first_new, second_new)


def per_device(
    patches,
    cotangent,
    res_ids,
    pos_table,
    attn_in,
    attn_out,
    mlp_in,
    mlp_out,
    vectors,
    first_attn_in,
    first_attn_out,
    first_mlp_in,
    first_mlp_out,
    first_vectors,
    second_attn_in,
    second_attn_out,
    second_mlp_in,
    second_mlp_out,
    second_vectors,
):
    row_count, local_len, width = patches.shape
    img_count, halves = lax.axis_size("img"), lax.axis_size("sy")
    chips = img_count * halves
    row_len = local_len * halves * 2
    slot_total = row_count * img_count * row_len
    head_size = width // HEADS
    own_y, own_c = lax.axis_index("sy"), lax.axis_index("sc")
    rows = attn_in.shape[0]
    half = width // 2
    ff_rows = mlp_out.shape[0]
    ff_half = chips * ff_rows
    table_size = GRID * GRID
    vector_count = vectors.shape[1]

    def to_row(array):
        mine = lax.dynamic_index_in_dim(array, own_y, 0, keepdims=False)
        other = lax.dynamic_index_in_dim(array, 1 - own_y, 0, keepdims=False)
        return jnp.concatenate([mine, swap_chip(other)], axis=0)

    def from_row(array):
        mine, other = array[:local_len], swap_chip(array[local_len:])
        return jnp.stack([pick(own_y, mine, other), pick(own_y, other, mine)], axis=0)

    res_row = lax.dynamic_index_in_dim(res_ids, own_y, 0, keepdims=False)
    all_positions = jnp.arange(row_len, dtype=jnp.int32)
    segment_all, _, _, _ = layout(res_row, all_positions)
    seg = jnp.broadcast_to(segment_all.astype(F32)[None, :], (8, row_len))
    begin, end = key_bounds(res_row, row_len)
    info = jnp.concatenate([jnp.stack([own_y, own_c]).astype(jnp.int32), begin, end])
    near = jnp.arange(local_len, dtype=jnp.int32)
    positions = jnp.concatenate(
        [(2 * own_y + own_c) * local_len + near, (2 * (1 - own_y) + own_c) * local_len + near]
    )
    _, side_of, patch_index, usable = layout(res_row, positions)
    place = table_weights(side_of, patch_index, usable)
    usable = usable.astype(F32)[:, None]

    def by_core(array, blocks):
        split = array.reshape(rows, blocks, 2, -1)
        low, high = split[:, :, 0].reshape(rows, -1), split[:, :, 1].reshape(rows, -1)
        return pick(own_c, low, high), pick(own_c, high, low)

    vector_pad = jnp.pad(vectors, ((0, 0), (0, TILE - vector_count))).astype(BF16)
    mine_in, away_in = by_core(attn_in.astype(BF16), 3)
    mine_out, away_out = by_core(attn_out.astype(BF16), 1)
    mine_up, away_up = by_core(mlp_in.astype(BF16), chips)
    came = swap_core(jnp.concatenate([away_in, vector_pad, away_out, away_up], axis=1))
    mine = jnp.concatenate([mine_in, vector_pad, mine_out, mine_up], axis=1)
    shard = jnp.concatenate([pick(own_c, mine, came), pick(own_c, came, mine)], axis=0)
    in_width = 3 * half
    head_end = in_width + TILE
    attn_part = gather_all(shard[:, : head_end + half])
    in_matrix = attn_part[:, :in_width]
    vector_cols = attn_part[:, in_width : in_width + vector_count].astype(F32)
    out_columns = attn_part[:, head_end:]
    up_matrix = gather_all(shard[:, head_end + half :])
    down_matrix = gather_all(mlp_out.astype(BF16))
    keep_out = lax.dynamic_slice_in_dim(out_columns, own_c * half, half, 0)
    came_out = swap_core(lax.dynamic_slice_in_dim(out_columns, (1 - own_c) * half, half, 0))
    out_matrix = jnp.concatenate([pick(own_c, keep_out, came_out), pick(own_c, came_out, keep_out)], axis=1)

    gain_one, shift_one = vector_cols[:, 0], vector_cols[:, 1]
    bias_query = lax.dynamic_slice_in_dim(vector_cols[:, 2], own_c * half, half, 0)
    bias_value = lax.dynamic_slice_in_dim(vector_cols[:, 3], own_c * half, half, 0)
    bias_out, gain_two, shift_two, bias_down = (vector_cols[:, i] for i in (4, 5, 6, 7))
    bias_up = lax.dynamic_index_in_dim(
        vector_cols[:, 8:].reshape(chips, 2, ff_rows), own_c, 1, keepdims=False
    ).reshape(-1)

    own = local_len * row_count

    def with_core(array):
        return jnp.concatenate([array, swap_core(array)], axis=0)

    def sum_core(left, weights, product):
        away = product(left[own:], weights).astype(BF16)
        came = swap_core(away)
        return product(left[:own], weights) + came.astype(F32)

    stream = to_row(patches).astype(F32) + jnp.dot(
        place, pos_table, precision=PRECISE, preferred_element_type=F32
    )
    hat_one, inverse_one = normalize(stream)
    normed_one = with_core((hat_one * gain_one + shift_one).astype(BF16))
    bias_qkv = jnp.concatenate([bias_query, jnp.zeros_like(bias_query), bias_value])
    qkv = (nn(normed_one, in_matrix) + bias_qkv).astype(BF16)
    per = local_len // TILE
    mixed, log_sum = attention(qkv, seg, info, per, head_size)
    stream_two = stream + sum_core(mixed, out_matrix, nn) + bias_out
    hat_two, inverse_two = normalize(stream_two)
    normed_two = with_core((hat_two * gain_two + shift_two).astype(BF16))
    hidden_pre = nn(normed_two, up_matrix) + bias_up
    hidden, slope = gelu_and_slope(hidden_pre)
    hidden = hidden.astype(BF16)
    last = sum_core(hidden, down_matrix, nn) + bias_down
    output = from_row(((stream_two + last) * usable).astype(BF16))

    grad_own = to_row(cotangent).astype(F32) * usable
    grad_last = with_core(grad_own.astype(BF16))
    grad_bias_down = jnp.sum(grad_own, axis=0)
    grad_down = tn(hidden, grad_last)
    shard_down = scatter_all(grad_down)
    grad_pre = (nt(grad_last, down_matrix) * slope).astype(BF16)
    grad_bias_up = jnp.sum(grad_pre.astype(F32), axis=0)
    grad_up = tn(normed_two, grad_pre)
    shard_up = scatter_all(grad_up)
    grad_normed_two = sum_core(grad_pre, up_matrix, nt)
    back_two, grad_gain_two, grad_shift_two = normalize_back(hat_two, inverse_two, gain_two, grad_normed_two)
    grad_two = grad_own + back_two
    grad_branch = grad_two.astype(BF16)
    grad_bias_out = jnp.sum(grad_branch.astype(F32), axis=0)
    grad_branch = with_core(grad_branch)
    grad_out_rows = tn(mixed, grad_branch).astype(BF16)
    keep_rows = lax.dynamic_slice_in_dim(grad_out_rows, own_c * half, half, 1)
    came_rows = swap_core(lax.dynamic_slice_in_dim(grad_out_rows, (1 - own_c) * half, half, 1))
    shard_out = scatter_all(
        jnp.concatenate([pick(own_c, keep_rows, came_rows), pick(own_c, came_rows, keep_rows)], axis=0)
    )
    grad_mixed = nt(grad_branch, out_matrix).astype(BF16)
    grad_qkv = attention_back(qkv, mixed, grad_mixed, seg, log_sum, info, per, head_size)
    grad_bias_qkv = jnp.sum(grad_qkv.astype(F32), axis=0)
    grad_in = tn(normed_one, grad_qkv)
    grad_normed_one = sum_core(grad_qkv, in_matrix, nt)
    back_one, grad_gain_one, grad_shift_one = normalize_back(hat_one, inverse_one, gain_one, grad_normed_one)
    grad_stream = grad_two + back_one
    input_grad = from_row(grad_stream.astype(BF16))
    table_part = lax.dot_general(
        grad_stream, place, (((0,), (0,)), ((), ())), precision=PRECISE, preferred_element_type=F32
    )

    def widen(array, blocks):
        array = array.reshape(blocks, -1)
        zero = jnp.zeros_like(array)
        return jnp.stack([pick(own_c, array, zero), pick(own_c, zero, array)], axis=1).reshape(-1)

    narrow = jnp.stack(
        [
            grad_gain_one,
            grad_shift_one,
            widen(grad_bias_qkv[:half], 1),
            widen(grad_bias_qkv[2 * half :], 1),
            grad_bias_out,
            grad_gain_two,
            grad_shift_two,
            grad_bias_down,
        ],
        axis=1,
    )
    narrow = jnp.concatenate(
        [
            narrow,
            widen(grad_bias_up, chips).reshape(width, -1),
            table_part,
            jnp.zeros((width, TILE - vector_count - table_size), F32),
        ],
        axis=1,
    )
    shard_in = scatter_all(jnp.concatenate([grad_in, narrow], axis=1))

    def rows_of(array, core):
        return lax.dynamic_slice_in_dim(array, core * rows, rows, 0)

    def trade(array, blocks):
        away, keep = rows_of(array, 1 - own_c), rows_of(array, own_c)
        came = swap_core(away).reshape(rows, blocks, -1)
        keep = keep.reshape(rows, blocks, -1)
        both = jnp.stack([pick(own_c, keep, came), pick(own_c, came, keep)], axis=2)
        return both.reshape(rows, -1)

    grad_up_shard = trade(shard_up, chips)
    grad_out_shard = trade(shard_out, 1)
    grad_in_shard = trade(shard_in[:, :in_width], 3)
    narrow_shard = shard_in[:, in_width:]
    narrow_shard = rows_of(narrow_shard, own_c) + swap_core(rows_of(narrow_shard, 1 - own_c))
    grad_vectors_shard = narrow_shard[:, :vector_count]
    both = jnp.stack(
        [
            pick(own_c, narrow_shard, swap_core(narrow_shard)),
            pick(own_c, swap_core(narrow_shard), narrow_shard),
        ],
        axis=0,
    ).reshape(2 * rows, TILE)
    table_grad = gather_chips(both, bit_orders()[0])[:, vector_count : vector_count + table_size].T

    factor = jnp.float32(1.0 / slot_total)
    shards = (grad_in_shard, grad_out_shard, grad_up_shard, shard_down, grad_vectors_shard)
    weights = (attn_in, attn_out, mlp_in, mlp_out, vectors)
    firsts = (first_attn_in, first_attn_out, first_mlp_in, first_mlp_out, first_vectors)
    seconds = (second_attn_in, second_attn_out, second_mlp_in, second_mlp_out, second_vectors)
    decays = (0.05, 0.05, 0.05, 0.05, 0.0)
    updated = [
        adam_update(weights[i], shards[i], firsts[i], seconds[i], factor, decays[i]) for i in range(5)
    ]
    return (
        output,
        input_grad,
        table_grad,
        *shards,
        *(updated[i][0] for i in range(5)),
        *(updated[i][1] for i in range(5)),
        *(updated[i][2] for i in range(5)),
    )


def solution(mesh):
    img, seq = mesh.shape["img"], mesh.shape["seq"]
    inner = Mesh(mesh.devices.reshape(img, seq // 2, 2), ("img", "sy", "sc"))
    tokens = P("img", ("sy", "sc"), None)
    shard = P(("img", "sy", "sc"), None)
    return jax.shard_map(
        per_device,
        mesh=inner,
        in_specs=(tokens, tokens, P("img", None), P()) + (shard,) * 15,
        out_specs=(tokens, tokens, P()) + (shard,) * 20,
        check_vma=False,
    )
```

```python
import functools
import math

import jax
import jax.numpy as jnp
from jax import lax
from jax.experimental import pallas as pl
from jax.experimental.pallas import tpu as pltpu
from jax.sharding import Mesh
from jax.sharding import PartitionSpec as P

HEADS = 16
GRID = 7
GRID_HI = 12
TILE = 128

PRECISE = lax.Precision.HIGHEST
FIRST_CORRECTION = 0.9999734386011124
SECOND_CORRECTION = 0.0952078528862911
EPS = 1e-06

F32 = jnp.float32
BF16 = jnp.bfloat16


def image_spans(res_row):
    side = jnp.where(res_row == 384, GRID_HI, jnp.where(res_row == 224, GRID, 0)).astype(jnp.int32)
    lengths = side * side
    slots = res_row.shape[0]
    order = jnp.arange(slots, dtype=jnp.int32)
    earlier = order[None, :] < order[:, None]
    starts = jnp.sum(jnp.where(earlier, lengths[None, :], 0), axis=1)
    return side, lengths, starts


def layout(res_row, positions):
    side, lengths, starts = image_spans(res_row)
    slots = res_row.shape[0]
    places = positions[:, None]
    inside = ((places >= starts[None, :]) & (places < (starts + lengths)[None, :])).astype(jnp.int32)
    usable = jnp.sum(inside, axis=1)
    image_number = jnp.arange(slots, dtype=jnp.int32)
    segment = jnp.sum(inside * image_number, axis=1) + (1 - usable) * slots
    start_of = jnp.sum(inside * starts[None, :], axis=1)
    side_of = jnp.sum(inside * side[None, :], axis=1)
    patch_index = (positions - start_of) * usable
    return segment, side_of, patch_index, usable


def key_bounds(res_row, row_len):
    _, lengths, starts = image_spans(res_row)
    total = jnp.sum(lengths)
    firsts = jnp.arange(row_len // TILE, dtype=jnp.int32) * TILE

    def span(positions):
        places = positions[:, None]
        inside = (places >= starts[None, :]) & (places < (starts + lengths)[None, :])
        found = positions < total
        begin = jnp.sum(jnp.where(inside, starts[None, :], 0), axis=1)
        end = jnp.sum(jnp.where(inside, (starts + lengths)[None, :], 0), axis=1)
        return jnp.where(found, begin, total), jnp.where(found, end, row_len)

    begin, _ = span(firsts)
    _, end = span(firsts + (TILE - 1))
    return begin // TILE, (end + TILE - 1) // TILE


def axis_weights(coord, side_of):
    scaled = jnp.maximum((2 * coord + 1) * GRID - GRID_HI, 0)
    lower_fine = scaled // (2 * GRID_HI)
    fraction_fine = (scaled - lower_fine * 2 * GRID_HI).astype(F32) / (2.0 * GRID_HI)
    resized = side_of == GRID_HI
    lower_cell = jnp.where(resized, lower_fine, coord)
    fraction = jnp.where(resized, fraction_fine, jnp.zeros_like(fraction_fine))
    upper_cell = jnp.minimum(lower_cell + 1, GRID - 1)
    cell_index = jnp.arange(GRID, dtype=jnp.int32)
    below = (cell_index == lower_cell[..., None]).astype(F32)
    above = (cell_index == upper_cell[..., None]).astype(F32)
    return (1.0 - fraction)[..., None] * below + fraction[..., None] * above


def table_weights(side_of, patch_index, usable):
    safe_side = jnp.maximum(side_of, 1)
    row_coord = patch_index // safe_side
    column_coord = patch_index % safe_side
    outer = axis_weights(row_coord, side_of)[:, :, None] * axis_weights(column_coord, side_of)[:, None, :]
    outer = outer * usable.astype(F32)[:, None, None]
    return outer.reshape(side_of.shape[0], GRID * GRID)


def place_of(block, own_y, own_c, per):
    quarter = block // per
    core = (quarter % 2 + own_c) % 2
    half = (quarter // 2 + own_y) % 2
    return (core * 2 + half) * per + block % per


def split_heads(pair):
    lane = lax.broadcasted_iota(jnp.int32, pair.shape, 1)
    zero = jnp.zeros_like(pair)
    low = lane < pair.shape[1] // 2
    return jnp.concatenate([jnp.where(low, pair, zero), jnp.where(low, zero, pair)], axis=0)


def join_heads(stacked):
    half = stacked.shape[0] // 2
    lane = lax.broadcasted_iota(jnp.int32, (half, stacked.shape[1]), 1)
    return jnp.where(lane < stacked.shape[1] // 2, stacked[:half], stacked[half:])


def down_lanes(row):
    return jnp.transpose(jnp.broadcast_to(row, (TILE, TILE)))


def nt(left, right):
    return lax.dot_general(left, right, (((1,), (1,)), ((), ())), preferred_element_type=F32)


def tn(left, right):
    return lax.dot_general(left, right, (((0,), (0,)), ((), ())), preferred_element_type=F32)


def nn(left, right):
    return jnp.dot(left, right, preferred_element_type=F32)


def fold(array, over):
    parts = array.reshape(array.shape[0] // 8, 8, array.shape[1])
    return jnp.max(parts, axis=0) if over == "max" else jnp.sum(parts, axis=0)


def same_segment(seg_down, chunk, seg_q):
    same = seg_down[chunk] == seg_q
    return jnp.concatenate([same, same], axis=1)


def fill_segments(seg, seg_down):
    chunks, span, _ = seg_down.shape
    for chunk in range(chunks):
        row = seg[0:1, chunk * span : (chunk + 1) * span]
        seg_down[chunk] = jnp.transpose(jnp.broadcast_to(row, (TILE, span)))


def join_turned(turned):
    half = turned.shape[1] // 2
    row = lax.broadcasted_iota(jnp.int32, (turned.shape[0], half), 0)
    return jnp.transpose(jnp.where(row < turned.shape[0] // 2, turned[:, :half], turned[:, half:]))


def columns_of(base, j):
    return slice(base + j * TILE, base + (j + 1) * TILE)


def attend_kernel(pairs, width, per, scale, info, qkv, seg, out, log_sum, scores, turned, seg_down):
    tile = pl.program_id(0)
    chunks, span, _ = seg_down.shape
    own_y, own_c = info[0], info[1]
    ratio = span // TILE
    first = info[2 + tile] // ratio
    last = (info[2 + pl.num_programs(0) + tile] + ratio - 1) // ratio

    def at(chunk):
        return pl.multiple_of(place_of(chunk * ratio, own_y, own_c, per) * TILE, TILE)

    @pl.when(tile == 0)
    def _():
        fill_segments(seg, seg_down)
        for chunk in range(chunks):
            for j in range(pairs):
                turned[chunk, j] = jnp.transpose(qkv[pl.ds(at(chunk), span), columns_of(2 * width, j)])

    q_at = pl.multiple_of(place_of(tile, own_y, own_c, per) * TILE, TILE)
    seg_q = seg[0:1, pl.ds(pl.multiple_of(tile * TILE, TILE), TILE)]
    queries = [
        split_heads(qkv[pl.ds(q_at, TILE), columns_of(0, j)] * jnp.asarray(scale, BF16)) for j in range(pairs)
    ]

    def score(chunk, high):
        same = same_segment(seg_down, chunk, seg_q)
        products = [nt(qkv[pl.ds(at(chunk), span), columns_of(width, j)], queries[j]) for j in range(pairs)]
        made = []
        for j in range(pairs):
            s = jnp.where(same, products[j], -1e30)
            scores[j, chunk] = s
            made.append(jnp.maximum(high[j], fold(s, "max")))
        return tuple(made)

    high = lax.fori_loop(first, last, score, (jnp.full((8, 2 * TILE), -1e30, F32),) * pairs)
    tops = [jnp.max(high[j], axis=0, keepdims=True) for j in range(pairs)]

    def mix(chunk, carry):
        total, mixed = carry
        powers = [jnp.exp(scores[j, chunk] - tops[j]) for j in range(pairs)]
        return (
            tuple(total[j] + fold(powers[j], "sum") for j in range(pairs)),
            tuple(mixed[j] + nn(turned[chunk, j], powers[j].astype(BF16)) for j in range(pairs)),
        )

    total, mixed = lax.fori_loop(
        first,
        last,
        mix,
        ((jnp.zeros((8, 2 * TILE), F32),) * pairs, (jnp.zeros((TILE, 2 * TILE), F32),) * pairs),
    )
    for j in range(pairs):
        sums = jnp.sum(total[j], axis=0, keepdims=True)
        out[:, columns_of(0, j)] = join_turned(mixed[j] / sums).astype(BF16)
        log_total = tops[j] + jnp.log(sums)
        log_sum[2 * j : 2 * j + 1] = log_total[:, :TILE]
        log_sum[2 * j + 1 : 2 * j + 2] = log_total[:, TILE:]


def attend_back_kernel(
    start, pairs, width, per, scale, info, qkv, mixed, grad, seg, log_sum, out, grad_keys, grad_values, turned, seg_down
):
    tile = pl.program_id(0)
    chunks, span, _ = seg_down.shape
    own_y, own_c = info[0], info[1]
    ratio = span // TILE
    first = info[2 + tile] // ratio
    last = (info[2 + pl.num_programs(0) + tile] + ratio - 1) // ratio
    heads = range(start, start + pairs)

    def at(chunk):
        return pl.multiple_of(place_of(chunk * ratio, own_y, own_c, per) * TILE, TILE)

    @pl.when(tile == 0)
    def _():
        fill_segments(seg, seg_down)
        grad_keys[...] = jnp.zeros_like(grad_keys)
        grad_values[...] = jnp.zeros_like(grad_values)
        for chunk in range(chunks):
            for i, j in enumerate(heads):
                turned[chunk, i] = jnp.transpose(qkv[pl.ds(at(chunk), span), columns_of(width, j)])

    q_at = pl.multiple_of(place_of(tile, own_y, own_c, per) * TILE, TILE)
    q_from = pl.multiple_of(tile * TILE, TILE)
    seg_q = seg[0:1, pl.ds(q_from, TILE)]
    queries, grads, logs, inner = [], [], [], []
    for j in heads:
        queries.append(split_heads(qkv[pl.ds(q_at, TILE), columns_of(0, j)] * jnp.asarray(scale, BF16)))
        g = grad[pl.ds(q_at, TILE), columns_of(0, j)]
        grads.append(split_heads(g))
        both = jnp.transpose(g.astype(F32) * mixed[pl.ds(q_at, TILE), columns_of(0, j)].astype(F32))
        low = jnp.sum(both[: TILE // 2], axis=0, keepdims=True)
        high = jnp.sum(both[TILE // 2 :], axis=0, keepdims=True)
        inner.append(jnp.concatenate([low, high], axis=1))
        here = log_sum[2 * j : 2 * j + 2, pl.ds(q_from, TILE)]
        logs.append(jnp.concatenate([here[0:1], here[1:2]], axis=1))

    def step(chunk, carry):
        k_at = at(chunk)
        same = same_segment(seg_down, chunk, seg_q)
        scores = [nt(qkv[pl.ds(k_at, span), columns_of(width, j)], queries[i]) for i, j in enumerate(heads)]
        slopes = [nt(qkv[pl.ds(k_at, span), columns_of(2 * width, j)], grads[i]) for i, j in enumerate(heads)]
        powers = [jnp.exp(jnp.where(same, scores[i], -1e30) - logs[i]) for i in range(pairs)]
        changes = [(powers[i] * (slopes[i] - inner[i])).astype(BF16) for i in range(pairs)]
        to_values = [nn(powers[i].astype(BF16), grads[i]) for i in range(pairs)]
        to_keys = [nn(changes[i], queries[i]) for i in range(pairs)]
        to_query = tuple(carry[i] + nn(turned[chunk, i], changes[i]) for i in range(pairs))
        for i in range(pairs):
            grad_values[chunk, :, columns_of(0, i)] += to_values[i]
            grad_keys[chunk, :, columns_of(0, i)] += to_keys[i]
        return to_query

    grad_query = lax.fori_loop(first, last, step, (jnp.zeros((TILE, 2 * TILE), F32),) * pairs)
    for i in range(pairs):
        out[pl.ds(q_at, TILE), columns_of(0, i)] = (join_turned(grad_query[i]) * scale).astype(BF16)

    @pl.when(tile == pl.num_programs(0) - 1)
    def _():
        all_heads = pairs * TILE
        for chunk in range(chunks):
            out[pl.ds(at(chunk), span), all_heads : 2 * all_heads] = grad_keys[chunk].astype(BF16)
            out[pl.ds(at(chunk), span), 2 * all_heads :] = grad_values[chunk].astype(BF16)


def attention(qkv, seg, info, per, head_size):
    length, width = qkv.shape[0], qkv.shape[1] // 3
    pairs, tiles = width // TILE, length // TILE
    span = per * TILE
    chunks = length // span
    scale = head_size ** (-0.5)

    def place(i, info):
        return place_of(i, info[0], info[1], per)

    return pl.pallas_call(
        functools.partial(attend_kernel, pairs, width, per, scale),
        name="attend",
        out_shape=(
            jax.ShapeDtypeStruct((length, width), BF16),
            jax.ShapeDtypeStruct((2 * pairs, length), F32),
        ),
        grid_spec=pltpu.PrefetchScalarGridSpec(
            num_scalar_prefetch=1,
            grid=(tiles,),
            in_specs=[
                pl.BlockSpec(qkv.shape, lambda i, info: (0, 0), pipeline_mode=pl.Buffered(1)),
                pl.BlockSpec(seg.shape, lambda i, info: (0, 0), pipeline_mode=pl.Buffered(1)),
            ],
            out_specs=[
                pl.BlockSpec((TILE, width), lambda i, info: (place(i, info), 0)),
                pl.BlockSpec((2 * pairs, TILE), lambda i, info: (0, i)),
            ],
            scratch_shapes=[
                pltpu.VMEM((pairs, chunks, span, 2 * TILE), F32),
                pltpu.VMEM((chunks, pairs, TILE, span), BF16),
                pltpu.VMEM((chunks, span, TILE), F32),
            ],
        ),
        compiler_params=pltpu.CompilerParams(
            dimension_semantics=("arbitrary",), vmem_limit_bytes=40 << 20
        ),
        cost_estimate=pl.CostEstimate(
            flops=length * length * width * 2, bytes_accessed=4 * length * width * 2, transcendentals=0
        ),
    )(info, qkv, seg)


def attention_back(part, parts, qkv, mixed, grad, seg, log_sum, info, per, head_size):
    length, width = qkv.shape[0], qkv.shape[1] // 3
    pairs, tiles = width // TILE // parts, length // TILE
    span = per * TILE
    chunks = length // span
    out = jax.ShapeDtypeStruct((length, 3 * pairs * TILE), BF16)
    scale = head_size ** (-0.5)

    def whole(array):
        return pl.BlockSpec(array.shape, lambda i, info: (0, 0), pipeline_mode=pl.Buffered(1))

    return pl.pallas_call(
        functools.partial(attend_back_kernel, part * pairs, pairs, width, per, scale),
        name="attend_back",
        out_shape=out,
        grid_spec=pltpu.PrefetchScalarGridSpec(
            num_scalar_prefetch=1,
            grid=(tiles,),
            in_specs=[whole(qkv), whole(mixed), whole(grad), whole(seg), whole(log_sum)],
            out_specs=pl.BlockSpec(out.shape, lambda i, info: (0, 0)),
            scratch_shapes=[
                pltpu.VMEM((chunks, span, pairs * TILE), F32),
                pltpu.VMEM((chunks, span, pairs * TILE), F32),
                pltpu.VMEM((chunks, pairs, TILE, span), BF16),
                pltpu.VMEM((chunks, span, TILE), F32),
            ],
        ),
        compiler_params=pltpu.CompilerParams(
            dimension_semantics=("arbitrary",), vmem_limit_bytes=48 << 20
        ),
        cost_estimate=pl.CostEstimate(
            flops=length * length * width * 5 // parts,
            bytes_accessed=8 * length * width * 2 // parts,
            transcendentals=0,
        ),
    )(info, qkv, mixed, grad, seg, log_sum)


SWAP = [(0, 1), (1, 0)]


def swap_core(array):
    return lax.ppermute(array, "sc", SWAP)


def swap_chip(array):
    return lax.ppermute(array, "sy", SWAP)


def swap_bit(array, bit):
    if bit == 0:
        return swap_chip(array)
    count = lax.axis_size("img")
    return lax.ppermute(array, "img", [(i, i ^ (1 << (bit - 1))) for i in range(count)])


def own_bit(bit):
    if bit == 0:
        return lax.axis_index("sy")
    return (lax.axis_index("img") >> (bit - 1)) & 1


def fence(*values):
    return lax.optimization_barrier(values)


def axis_of(bit, done):
    return sum(1 for other in done if other > bit)


def pick(index, low, high):
    return jnp.where(index == 0, low, high)


def far_bits():
    return list(range(2, int(math.log2(lax.axis_size("img"))) + 1))


def join(first, second, axis):
    shape = list(first.shape)
    shape[axis] += second.shape[axis]
    held = lax.dynamic_update_slice_in_dim(jnp.zeros(shape, first.dtype), first, 0, axis)
    return lax.dynamic_update_slice_in_dim(held, second, first.shape[axis], axis)


class Gather:
    def __init__(self, block, cut):
        self.rows, self.width, self.cut = block.shape[0], block.shape[1], cut
        self.steps = [*[(bit,) for bit in reversed(far_bits())], (1, 0), (0, 1)]
        self.held, self.done = [block], [[]]

    def send(self):
        bits = self.steps[0]
        if len(bits) > len(self.held):
            whole = self.held[0]
            self.held = [whole[..., : self.cut], whole[..., self.cut :]]
            self.done = [list(self.done[0]), list(self.done[0])]
        return [swap_bit(array, bit) for array, bit in zip(self.held, bits)]

    def take(self, came):
        bits = self.steps.pop(0)
        for i, bit in enumerate(bits):
            mine = own_bit(bit)
            low, high = pick(mine, self.held[i], came[i]), pick(mine, came[i], self.held[i])
            self.held[i] = jnp.stack([low, high], axis=axis_of(bit, self.done[i]))
            self.done[i].append(bit)

    def result(self):
        flat = [array.reshape(-1, array.shape[-1]) for array in self.held]
        return flat[0] if len(flat) == 1 else join(*flat, axis=1)


class Scatter:
    def __init__(self, left, right):
        far = far_bits()
        self.bits = [sorted([0, 1, *far], reverse=True) for _ in range(2)]
        count = len(self.bits[0])
        self.held = [
            array.astype(BF16).reshape((2,) * count + (array.shape[0] >> count, array.shape[1]))
            for array in (left, right)
        ]
        self.steps = [(0, 1), (1, 0), *[(bit,) for bit in far]]

    def send(self):
        bits = self.steps[0]
        if len(bits) < len(self.held):
            self.held = [join(*self.held, axis=self.held[0].ndim - 1)]
        return [
            swap_bit(lax.dynamic_index_in_dim(array, 1 - own_bit(bit), self.bits[i].index(bit), keepdims=False), bit)
            for i, (array, bit) in enumerate(zip(self.held, bits))
        ]

    def take(self, came):
        bits = self.steps.pop(0)
        for i, bit in enumerate(bits):
            keep = lax.dynamic_index_in_dim(self.held[i], own_bit(bit), self.bits[i].index(bit), keepdims=False)
            total = keep.astype(F32) + came[i].astype(F32)
            self.held[i] = total.astype(BF16) if self.steps else total
            self.bits[i].remove(bit)

    def result(self):
        return self.held[0]


def add_over(array, *bits):
    for bit in bits:
        own = array.astype(BF16)
        array = own.astype(F32) + (swap_core(own) if bit == "core" else swap_bit(own, bit)).astype(F32)
    return array


def phase(moves, work, *values):
    moves = [move if isinstance(move, tuple) else (move, 1) for move in moves]
    moves = [(move, min(count, len(move.steps))) for move, count in moves if move.steps]
    held, values = fence([move.held for move, _ in moves], values)
    came = []
    for (move, count), arrays in zip(moves, held):
        move.held = list(arrays)
        for _ in range(count - 1):
            move.take(move.send())
        came.append(move.send())
    made = work(*values) if work else ()
    came, made = fence(came, made)
    for (move, _), arrays in zip(moves, came):
        move.take(arrays)
    return made


def normalize(stream):
    center = jnp.mean(stream, axis=-1, keepdims=True)
    centered = stream - center
    spread = jnp.mean(centered * centered, axis=-1, keepdims=True)
    inverse = lax.rsqrt(spread + EPS)
    return centered * inverse, inverse


def normalize_back(normed, inverse, gain, grad):
    scaled = grad * gain
    middle = jnp.mean(scaled, axis=-1, keepdims=True)
    along = jnp.mean(scaled * normed, axis=-1, keepdims=True)
    return (
        inverse * (scaled - middle - normed * along),
        jnp.sum(grad * normed, axis=0, keepdims=True),
        jnp.sum(grad, axis=0, keepdims=True),
    )


def rows_from(columns, count):
    one_hot = (jnp.arange(16)[:, None] == jnp.arange(TILE)[None, :]).astype(BF16)
    rows = nt(one_hot, columns)
    return [rows[i : i + 1] for i in range(count)]


def column_choice(rows, columns):
    row, lane = jnp.arange(rows)[:, None], jnp.arange(TILE)[None, :]
    return (row == 8 + lane % columns).astype(F32)


def own_place(width, columns):
    per_run = TILE // columns
    row, lane = jnp.arange(width)[:, None], jnp.arange(TILE)[None, :]
    return row % per_run == lane // columns


def unroll_bias(columns, own_c, ff_rows):
    width, extra = columns.shape[0], 4
    spread = nn(columns, column_choice(TILE, extra).astype(BF16))
    runs = jnp.where(own_place(width, extra), spread, 0.0).reshape(-1, TILE // extra, TILE).sum(axis=1)
    runs = runs.reshape(-1, 2, ff_rows)
    return pick(own_c, runs[:, 0], runs[:, 1]).reshape(1, -1)


def roll_bias(sums, own_c, width, rows, ff_rows):
    extra = 4
    runs = sums.reshape(-1, ff_rows)
    zero = jnp.zeros_like(runs)
    runs = jnp.stack([pick(own_c, runs, zero), pick(own_c, zero, runs)], axis=1).reshape(-1, 1, TILE)
    spread = jnp.broadcast_to(runs, (runs.shape[0], TILE // extra, TILE)).reshape(width, TILE)
    spread = jnp.where(own_place(width, extra), spread, 0.0)
    return lax.dot_general(
        column_choice(rows, extra), spread, (((1,), (1,)), ((), ())), precision=PRECISE, preferred_element_type=F32
    )


def token_sums(array):
    return nn(jnp.ones((8, array.shape[0]), BF16), array)[:1]


def gelu_and_slope(values):
    cdf = 0.5 * (1.0 + lax.erf(values * (0.5**0.5)))
    density = jnp.exp(-0.5 * values * values) * (1.0 / math.sqrt(2.0 * math.pi))
    return values * cdf, cdf + values * density


def adam_update(weight, gradient, first_moment, second_moment, factor, decay):
    scaled = gradient * factor
    first_new = 0.9 * first_moment + 0.1 * scaled
    second_new = 0.999 * second_moment + 0.001 * scaled * scaled
    first_hat = first_new / FIRST_CORRECTION
    second_hat = second_new / SECOND_CORRECTION
    direction = first_hat / (jnp.sqrt(second_hat) + 1e-08) + decay * weight
    return (direction, first_new, second_new)


def per_device(
    patches,
    cotangent,
    res_ids,
    pos_table,
    attn_in,
    attn_out,
    mlp_in,
    mlp_out,
    vectors,
    first_attn_in,
    first_attn_out,
    first_mlp_in,
    first_mlp_out,
    first_vectors,
    second_attn_in,
    second_attn_out,
    second_mlp_in,
    second_mlp_out,
    second_vectors,
):
    row_count, local_len, width = patches.shape
    img_count, halves = lax.axis_size("img"), lax.axis_size("sy")
    chips = img_count * halves
    row_len = local_len * halves * 2
    slot_total = row_count * img_count * row_len
    head_size = width // HEADS
    own_y, own_c = lax.axis_index("sy"), lax.axis_index("sc")
    rows = attn_in.shape[0]
    half = width // 2
    ff_rows = mlp_out.shape[0]
    ff_half = chips * ff_rows
    table_size = GRID * GRID
    vector_count = vectors.shape[1]

    def to_rows(*arrays):
        mine = [lax.dynamic_index_in_dim(array, own_y, 0, keepdims=False) for array in arrays]
        other = [lax.dynamic_index_in_dim(array, 1 - own_y, 0, keepdims=False) for array in arrays]
        came = swap_chip(jnp.stack(other))
        return [join(mine[i], came[i], 0) for i in range(len(arrays))]

    def from_row(array):
        mine, other = array[:local_len], swap_chip(array[local_len:])
        return jnp.stack([pick(own_y, mine, other), pick(own_y, other, mine)], axis=0)

    res_row = lax.dynamic_index_in_dim(res_ids, own_y, 0, keepdims=False)
    all_positions = jnp.arange(row_len, dtype=jnp.int32)
    segment_all, _, _, _ = layout(res_row, all_positions)
    seg = jnp.broadcast_to(segment_all.astype(F32)[None, :], (8, row_len))
    begin, end = key_bounds(res_row, row_len)
    info = jnp.concatenate([jnp.stack([own_y, own_c]).astype(jnp.int32), begin, end])
    near = jnp.arange(local_len, dtype=jnp.int32)
    positions = jnp.concatenate(
        [(2 * own_y + own_c) * local_len + near, (2 * (1 - own_y) + own_c) * local_len + near]
    )
    _, side_of, patch_index, usable = layout(res_row, positions)
    place = table_weights(side_of, patch_index, usable)
    usable = usable.astype(F32)[:, None]

    def by_core(array, blocks):
        split = array.reshape(rows, blocks, 2, -1)
        low, high = split[:, :, 0].reshape(rows, -1), split[:, :, 1].reshape(rows, -1)
        return pick(own_c, low, high), pick(own_c, high, low)

    vector_pad = jnp.pad(vectors, ((0, 0), (0, TILE - vector_count))).astype(BF16)
    mine_in, away_in = by_core(attn_in.astype(BF16), 3)
    mine_out, away_out = by_core(attn_out.astype(BF16), 1)
    mine_up, away_up = by_core(mlp_in.astype(BF16), chips)
    came = swap_core(jnp.concatenate([away_in, vector_pad, away_out, away_up], axis=1))
    mine = jnp.concatenate([mine_in, vector_pad, mine_out, mine_up], axis=1)
    shard = jnp.concatenate([pick(own_c, mine, came), pick(own_c, came, mine)], axis=0)
    in_width = 3 * half
    head_end = in_width + TILE
    own = local_len * row_count
    per = local_len // TILE

    def cut_of(columns):
        return columns // (2 * TILE) * TILE

    def with_core(array):
        return join(array, swap_core(array), 0)

    def sum_core(left, weights, product):
        away = product(left[own:], weights).astype(BF16)
        came = swap_core(away)
        return product(left[:own], weights) + came.astype(F32)

    gather_in = Gather(shard[:, :head_end], cut_of(head_end))
    gather_up = Gather(shard[:, head_end:], cut_of(half + ff_half))
    gather_down = Gather(mlp_out.astype(BF16), cut_of(width))

    def first(patches, cotangent):
        patches, cotangent = to_rows(patches, cotangent)
        stream = patches.astype(F32) + jnp.dot(
            place, pos_table, precision=PRECISE, preferred_element_type=F32
        )
        hat_one, inverse_one = normalize(stream)
        grad_own = cotangent.astype(F32) * usable
        return stream, hat_one, inverse_one, grad_own, with_core(grad_own.astype(BF16))

    stream, hat_one, inverse_one, grad_own, grad_last = phase(
        [(gather_in, len(far_bits()))], first, patches, cotangent
    )
    phase([gather_in, gather_up], None)
    phase([gather_in, gather_up], None)
    attn_part = gather_in.result()
    in_matrix = attn_part[:, :in_width]
    vector_part = attn_part[:, in_width:]
    gain_one, shift_one, bias_query, bias_value, bias_out, gain_two, shift_two, bias_down = (
        rows_from(vector_part, 8)
    )
    bias_query = pick(own_c, bias_query[:, :half], bias_query[:, half:])
    bias_value = pick(own_c, bias_value[:, :half], bias_value[:, half:])
    bias_up = unroll_bias(vector_part, own_c, ff_rows)
    bias_qkv = jnp.concatenate([bias_query, jnp.zeros_like(bias_query), bias_value], axis=1)

    def project(hat_one, in_matrix):
        normed_one = with_core((hat_one * gain_one + shift_one).astype(BF16))
        return normed_one, (nn(normed_one, in_matrix) + bias_qkv).astype(BF16)

    normed_one, qkv = phase([gather_up, gather_down], project, hat_one, in_matrix)
    mixed, log_sum = phase(
        [gather_up, gather_down],
        lambda qkv: attention(qkv, seg, info, per, head_size),
        qkv,
    )
    while gather_up.steps:
        phase([gather_up, gather_down], None)
    up_part = gather_up.result()
    out_columns, up_matrix = up_part[:, :half], up_part[:, half:]

    def project_out(stream, mixed, out_columns):
        low, high = out_columns[:half], out_columns[half:]
        keep_out, came_out = pick(own_c, low, high), swap_core(pick(own_c, high, low))
        out_matrix = jnp.concatenate(
            [pick(own_c, keep_out, came_out), pick(own_c, came_out, keep_out)], axis=1
        )
        stream_two = stream + sum_core(mixed, out_matrix, nn) + bias_out
        hat_two, inverse_two = normalize(stream_two)
        normed_two = with_core((hat_two * gain_two + shift_two).astype(BF16))
        return out_matrix, stream_two, hat_two, inverse_two, normed_two

    out_matrix, stream_two, hat_two, inverse_two, normed_two = phase(
        [gather_down], project_out, stream, mixed, out_columns
    )

    def expand(normed_two, up_matrix, grad_last):
        hidden_pre = nn(normed_two, up_matrix) + bias_up
        hidden, slope = gelu_and_slope(hidden_pre)
        hidden = hidden.astype(BF16)
        cut = cut_of(width)
        return hidden, slope, tn(hidden, grad_last[:, :cut]).astype(BF16), tn(hidden, grad_last[:, cut:]).astype(BF16)

    hidden, slope, *grad_down = phase([gather_down], expand, normed_two, up_matrix, grad_last)
    while gather_down.steps:
        phase([gather_down], None)
    down_matrix = gather_down.result()

    scatter_down = Scatter(*grad_down)

    def hidden_back(grad_last, down_matrix, slope, normed_two):
        grad_pre = (nt(grad_last, down_matrix) * slope).astype(BF16)
        cut = cut_of(ff_half + half)
        return (
            grad_pre,
            tn(normed_two, grad_pre[:, :cut]).astype(BF16),
            tn(normed_two, grad_pre[:, cut:]).astype(BF16),
        )

    grad_pre, *grad_up = phase([scatter_down], hidden_back, grad_last, down_matrix, slope, normed_two)
    def norm_two_back(grad_pre, up_matrix, hat_two, inverse_two, grad_own):
        grad_normed_two = sum_core(grad_pre, up_matrix, nt)
        back_two, grad_gain_two, grad_shift_two = normalize_back(
            hat_two, inverse_two, gain_two, grad_normed_two
        )
        grad_two = grad_own + back_two
        grad_branch = grad_two.astype(BF16)
        return grad_two, with_core(grad_branch), grad_gain_two, grad_shift_two

    def finish_output(hidden, stream_two, down_matrix):
        last = sum_core(hidden, down_matrix, nn) + bias_down
        return ((stream_two + last) * usable).astype(BF16)

    (grad_two, grad_branch, grad_gain_two, grad_shift_two), output = phase(
        [scatter_down],
        lambda values, others: (norm_two_back(*values), finish_output(*others)),
        (grad_pre, up_matrix, hat_two, inverse_two, grad_own),
        (hidden, stream_two, down_matrix),
    )

    grad_rows = tn(mixed, grad_branch).astype(BF16)
    low, high = grad_rows[:, :half], grad_rows[:, half:]
    keep_rows, came_rows = pick(own_c, low, high), swap_core(pick(own_c, high, low))
    grad_out = join(pick(own_c, keep_rows, came_rows), pick(own_c, came_rows, keep_rows), 0)
    scatter_up = Scatter(grad_up[0], join(grad_up[1], grad_out, 1))

    def attention_grads(grad_branch, out_matrix, qkv, mixed, log_sum, normed_one):
        grad_mixed = nt(grad_branch, out_matrix).astype(BF16)
        grad_qkv = attention_back(0, 1, qkv, mixed, grad_mixed, seg, log_sum, info, per, head_size)
        cut = cut_of(in_width)
        return (
            grad_qkv,
            tn(normed_one, grad_qkv[:, :cut]).astype(BF16),
            tn(normed_one, grad_qkv[:, cut:]).astype(BF16),
        )

    grad_qkv, *grad_in = phase(
        [scatter_up, (scatter_down, 9)], attention_grads, grad_branch, out_matrix, qkv, mixed, log_sum, normed_one
    )
    scatter_in = Scatter(*grad_in)

    def widen(row):
        zero = jnp.zeros_like(row)
        return jnp.concatenate([pick(own_c, row, zero), pick(own_c, zero, row)], axis=1)

    narrow_rows = vector_count + table_size
    narrow_rows += -narrow_rows % 16

    def norm_one_back(grad_qkv, in_matrix, hat_one, inverse_one, grad_two, grad_pre, grad_branch, grad_last):
        grad_normed_one = sum_core(grad_qkv, in_matrix, nt)
        back_one, grad_gain_one, grad_shift_one = normalize_back(
            hat_one, inverse_one, gain_one, grad_normed_one
        )
        grad_stream = grad_two + back_one
        wide_place = jnp.pad(place, ((0, 0), (vector_count, narrow_rows - vector_count - table_size)))
        narrow = lax.dot_general(
            wide_place, grad_stream, (((0,), (0,)), ((), ())), precision=PRECISE, preferred_element_type=F32
        ) + roll_bias(token_sums(grad_pre), own_c, width, narrow_rows, ff_rows)
        sums = token_sums(grad_qkv)
        rows_of_sums = [
            grad_gain_one,
            grad_shift_one,
            widen(sums[:, :half]),
            widen(sums[:, 2 * half :]),
            token_sums(grad_branch[:own]),
            grad_gain_two,
            grad_shift_two,
            token_sums(grad_last[:own]),
        ]
        row = jnp.arange(narrow_rows)[:, None]
        for i, values in enumerate(rows_of_sums):
            narrow = jnp.where(row == i, values, narrow)
        return grad_stream, narrow

    scatters = [scatter_in, scatter_up]
    grad_stream, narrow = phase(
        scatters, norm_one_back, grad_qkv, in_matrix, hat_one, inverse_one, grad_two, grad_pre, grad_branch, grad_last
    )
    far = far_bits()
    (narrow,) = phase(scatters, lambda narrow: (add_over(narrow, "core", *far[1:]),), narrow)

    def send_back(narrow, output, grad_stream):
        return add_over(narrow, 0, 1), from_row(output), from_row(grad_stream.astype(BF16))

    narrow, output, input_grad = phase(scatters, send_back, narrow, output, grad_stream)
    (narrow,) = phase(scatters, lambda narrow: (add_over(narrow, *far[:1]),), narrow)
    while any(move.steps for move in scatters):
        phase(scatters, None)
    shard_down, shard_in = scatter_down.result(), scatter_in.result()
    shard_up, shard_out = scatter_up.result()[:, :ff_half], scatter_up.result()[:, ff_half:]

    def rows_of(array, core):
        return lax.dynamic_slice_in_dim(array, core * rows, rows, 0)

    def trade(array, blocks):
        away, keep = rows_of(array, 1 - own_c), rows_of(array, own_c)
        came = swap_core(away).reshape(rows, blocks, -1)
        keep = keep.reshape(rows, blocks, -1)
        both = jnp.stack([pick(own_c, keep, came), pick(own_c, came, keep)], axis=2)
        return both.reshape(rows, -1)

    grad_up_shard = trade(shard_up, chips)
    grad_out_shard = trade(shard_out, 1)
    grad_in_shard = trade(shard_in, 3)
    device = (lax.axis_index("img") * halves + own_y) * 2 + own_c
    grad_vectors_shard = lax.dynamic_slice_in_dim(narrow[:vector_count], device * rows, rows, 1).T
    table_grad = narrow[vector_count : vector_count + table_size]

    factor = jnp.float32(1.0 / slot_total)
    shards = (grad_in_shard, grad_out_shard, grad_up_shard, shard_down, grad_vectors_shard)
    weights = (attn_in, attn_out, mlp_in, mlp_out, vectors)
    firsts = (first_attn_in, first_attn_out, first_mlp_in, first_mlp_out, first_vectors)
    seconds = (second_attn_in, second_attn_out, second_mlp_in, second_mlp_out, second_vectors)
    decays = (0.05, 0.05, 0.05, 0.05, 0.0)
    updated = [
        adam_update(weights[i], shards[i], firsts[i], seconds[i], factor, decays[i]) for i in range(5)
    ]
    return (
        output,
        input_grad,
        table_grad,
        *shards,
        *(updated[i][0] for i in range(5)),
        *(updated[i][1] for i in range(5)),
        *(updated[i][2] for i in range(5)),
    )


def solution(mesh):
    img, seq = mesh.shape["img"], mesh.shape["seq"]
    inner = Mesh(mesh.devices.reshape(img, seq // 2, 2), ("img", "sy", "sc"))
    tokens = P("img", ("sy", "sc"), None)
    shard = P(("img", "sy", "sc"), None)
    return jax.shard_map(
        per_device,
        mesh=inner,
        in_specs=(tokens, tokens, P("img", None), P()) + (shard,) * 15,
        out_specs=(tokens, tokens, P()) + (shard,) * 20,
        check_vma=False,
    )
```

```python
import functools
import math

import jax
import jax.numpy as jnp
from jax import lax
from jax.experimental import pallas as pl
from jax.experimental.pallas import tpu as pltpu
from jax.sharding import Mesh
from jax.sharding import PartitionSpec as P

HEADS = 16
GRID = 7
GRID_HI = 12
TILE = 128

PRECISE = lax.Precision.HIGHEST
FIRST_CORRECTION = 0.9999734386011124
SECOND_CORRECTION = 0.0952078528862911
EPS = 1e-06

F32 = jnp.float32
BF16 = jnp.bfloat16


def image_spans(res_row):
    side = jnp.where(res_row == 384, GRID_HI, jnp.where(res_row == 224, GRID, 0)).astype(jnp.int32)
    lengths = side * side
    slots = res_row.shape[0]
    order = jnp.arange(slots, dtype=jnp.int32)
    earlier = order[None, :] < order[:, None]
    starts = jnp.sum(jnp.where(earlier, lengths[None, :], 0), axis=1)
    return side, lengths, starts


def layout(res_row, positions):
    side, lengths, starts = image_spans(res_row)
    slots = res_row.shape[0]
    places = positions[:, None]
    inside = ((places >= starts[None, :]) & (places < (starts + lengths)[None, :])).astype(jnp.int32)
    usable = jnp.sum(inside, axis=1)
    image_number = jnp.arange(slots, dtype=jnp.int32)
    segment = jnp.sum(inside * image_number, axis=1) + (1 - usable) * slots
    start_of = jnp.sum(inside * starts[None, :], axis=1)
    side_of = jnp.sum(inside * side[None, :], axis=1)
    patch_index = (positions - start_of) * usable
    return segment, side_of, patch_index, usable


def key_bounds(res_row, row_len):
    _, lengths, starts = image_spans(res_row)
    total = jnp.sum(lengths)
    firsts = jnp.arange(row_len // TILE, dtype=jnp.int32) * TILE

    def span(positions):
        places = positions[:, None]
        inside = (places >= starts[None, :]) & (places < (starts + lengths)[None, :])
        found = positions < total
        begin = jnp.sum(jnp.where(inside, starts[None, :], 0), axis=1)
        end = jnp.sum(jnp.where(inside, (starts + lengths)[None, :], 0), axis=1)
        return jnp.where(found, begin, total), jnp.where(found, end, row_len)

    begin, _ = span(firsts)
    _, end = span(firsts + (TILE - 1))
    return begin // TILE, (end + TILE - 1) // TILE


def axis_weights(coord, side_of):
    scaled = jnp.maximum((2 * coord + 1) * GRID - GRID_HI, 0)
    lower_fine = scaled // (2 * GRID_HI)
    fraction_fine = (scaled - lower_fine * 2 * GRID_HI).astype(F32) / (2.0 * GRID_HI)
    resized = side_of == GRID_HI
    lower_cell = jnp.where(resized, lower_fine, coord)
    fraction = jnp.where(resized, fraction_fine, jnp.zeros_like(fraction_fine))
    upper_cell = jnp.minimum(lower_cell + 1, GRID - 1)
    cell_index = jnp.arange(GRID, dtype=jnp.int32)
    below = (cell_index == lower_cell[..., None]).astype(F32)
    above = (cell_index == upper_cell[..., None]).astype(F32)
    return (1.0 - fraction)[..., None] * below + fraction[..., None] * above


def table_weights(side_of, patch_index, usable):
    safe_side = jnp.maximum(side_of, 1)
    row_coord = patch_index // safe_side
    column_coord = patch_index % safe_side
    outer = axis_weights(row_coord, side_of)[:, :, None] * axis_weights(column_coord, side_of)[:, None, :]
    outer = outer * usable.astype(F32)[:, None, None]
    return outer.reshape(side_of.shape[0], GRID * GRID)


def place_of(block, own_y, own_c, per):
    quarter = block // per
    core = (quarter % 2 + own_c) % 2
    half = (quarter // 2 + own_y) % 2
    return (core * 2 + half) * per + block % per


def split_heads(pair):
    lane = lax.broadcasted_iota(jnp.int32, pair.shape, 1)
    zero = jnp.zeros_like(pair)
    low = lane < pair.shape[1] // 2
    return jnp.concatenate([jnp.where(low, pair, zero), jnp.where(low, zero, pair)], axis=0)


def join_heads(stacked):
    half = stacked.shape[0] // 2
    lane = lax.broadcasted_iota(jnp.int32, (half, stacked.shape[1]), 1)
    return jnp.where(lane < stacked.shape[1] // 2, stacked[:half], stacked[half:])


def down_lanes(row):
    return jnp.transpose(jnp.broadcast_to(row, (TILE, TILE)))


def nt(left, right):
    return lax.dot_general(left, right, (((1,), (1,)), ((), ())), preferred_element_type=F32)


def tn(left, right):
    return lax.dot_general(left, right, (((0,), (0,)), ((), ())), preferred_element_type=F32)


def nn(left, right):
    return jnp.dot(left, right, preferred_element_type=F32)


def fold(array, over):
    parts = array.reshape(array.shape[0] // 8, 8, array.shape[1])
    return jnp.max(parts, axis=0) if over == "max" else jnp.sum(parts, axis=0)


def same_segment(seg_down, chunk, seg_q):
    same = seg_down[chunk] == seg_q
    return jnp.concatenate([same, same], axis=1)


def fill_segments(seg, seg_down):
    chunks, span, _ = seg_down.shape
    for chunk in range(chunks):
        row = seg[0:1, chunk * span : (chunk + 1) * span]
        seg_down[chunk] = jnp.transpose(jnp.broadcast_to(row, (TILE, span)))


def join_turned(turned):
    half = turned.shape[1] // 2
    row = lax.broadcasted_iota(jnp.int32, (turned.shape[0], half), 0)
    return jnp.transpose(jnp.where(row < turned.shape[0] // 2, turned[:, :half], turned[:, half:]))


def columns_of(base, j):
    return slice(base + j * TILE, base + (j + 1) * TILE)


def attend_kernel(pairs, width, per, scale, info, qkv, seg, out, log_sum, scores, turned, seg_down):
    tile = pl.program_id(0)
    chunks, span, _ = seg_down.shape
    own_y, own_c = info[0], info[1]
    ratio = span // TILE
    first = info[2 + tile] // ratio
    last = (info[2 + pl.num_programs(0) + tile] + ratio - 1) // ratio

    def at(chunk):
        return pl.multiple_of(place_of(chunk * ratio, own_y, own_c, per) * TILE, TILE)

    @pl.when(tile == 0)
    def _():
        fill_segments(seg, seg_down)
        for chunk in range(chunks):
            for j in range(pairs):
                turned[chunk, j] = jnp.transpose(qkv[pl.ds(at(chunk), span), columns_of(2 * width, j)])

    q_at = pl.multiple_of(place_of(tile, own_y, own_c, per) * TILE, TILE)
    seg_q = seg[0:1, pl.ds(pl.multiple_of(tile * TILE, TILE), TILE)]
    queries = [
        split_heads(qkv[pl.ds(q_at, TILE), columns_of(0, j)] * jnp.asarray(scale, BF16)) for j in range(pairs)
    ]

    def score(chunk, high):
        same = same_segment(seg_down, chunk, seg_q)
        products = [nt(qkv[pl.ds(at(chunk), span), columns_of(width, j)], queries[j]) for j in range(pairs)]
        made = []
        for j in range(pairs):
            s = jnp.where(same, products[j], -1e30)
            scores[j, chunk] = s
            made.append(jnp.maximum(high[j], fold(s, "max")))
        return tuple(made)

    high = lax.fori_loop(first, last, score, (jnp.full((8, 2 * TILE), -1e30, F32),) * pairs)
    tops = [jnp.max(high[j], axis=0, keepdims=True) for j in range(pairs)]

    def mix(chunk, carry):
        total, mixed = carry
        powers = [jnp.exp(scores[j, chunk] - tops[j]) for j in range(pairs)]
        return (
            tuple(total[j] + fold(powers[j], "sum") for j in range(pairs)),
            tuple(mixed[j] + nn(turned[chunk, j], powers[j].astype(BF16)) for j in range(pairs)),
        )

    total, mixed = lax.fori_loop(
        first,
        last,
        mix,
        ((jnp.zeros((8, 2 * TILE), F32),) * pairs, (jnp.zeros((TILE, 2 * TILE), F32),) * pairs),
    )
    for j in range(pairs):
        sums = jnp.sum(total[j], axis=0, keepdims=True)
        out[:, columns_of(0, j)] = join_turned(mixed[j] / sums).astype(BF16)
        log_total = tops[j] + jnp.log(sums)
        log_sum[2 * j : 2 * j + 1] = log_total[:, :TILE]
        log_sum[2 * j + 1 : 2 * j + 2] = log_total[:, TILE:]


def attend_back_kernel(
    start, pairs, width, per, scale, info, qkv, mixed, grad, seg, log_sum, out, grad_keys, grad_values, turned, seg_down
):
    tile = pl.program_id(0)
    chunks, span, _ = seg_down.shape
    own_y, own_c = info[0], info[1]
    ratio = span // TILE
    first = info[2 + tile] // ratio
    last = (info[2 + pl.num_programs(0) + tile] + ratio - 1) // ratio
    heads = range(start, start + pairs)

    def at(chunk):
        return pl.multiple_of(place_of(chunk * ratio, own_y, own_c, per) * TILE, TILE)

    @pl.when(tile == 0)
    def _():
        fill_segments(seg, seg_down)
        grad_keys[...] = jnp.zeros_like(grad_keys)
        grad_values[...] = jnp.zeros_like(grad_values)
        for chunk in range(chunks):
            for i, j in enumerate(heads):
                turned[chunk, i] = jnp.transpose(qkv[pl.ds(at(chunk), span), columns_of(width, j)])

    q_at = pl.multiple_of(place_of(tile, own_y, own_c, per) * TILE, TILE)
    q_from = pl.multiple_of(tile * TILE, TILE)
    seg_q = seg[0:1, pl.ds(q_from, TILE)]
    queries, grads, logs, inner = [], [], [], []
    for j in heads:
        queries.append(split_heads(qkv[pl.ds(q_at, TILE), columns_of(0, j)] * jnp.asarray(scale, BF16)))
        g = grad[pl.ds(q_at, TILE), columns_of(0, j)]
        grads.append(split_heads(g))
        both = jnp.transpose(g.astype(F32) * mixed[pl.ds(q_at, TILE), columns_of(0, j)].astype(F32))
        low = jnp.sum(both[: TILE // 2], axis=0, keepdims=True)
        high = jnp.sum(both[TILE // 2 :], axis=0, keepdims=True)
        inner.append(jnp.concatenate([low, high], axis=1))
        here = log_sum[2 * j : 2 * j + 2, pl.ds(q_from, TILE)]
        logs.append(jnp.concatenate([here[0:1], here[1:2]], axis=1))

    def step(chunk, carry):
        k_at = at(chunk)
        same = same_segment(seg_down, chunk, seg_q)
        scores = [nt(qkv[pl.ds(k_at, span), columns_of(width, j)], queries[i]) for i, j in enumerate(heads)]
        slopes = [nt(qkv[pl.ds(k_at, span), columns_of(2 * width, j)], grads[i]) for i, j in enumerate(heads)]
        powers = [jnp.exp(jnp.where(same, scores[i], -1e30) - logs[i]) for i in range(pairs)]
        changes = [(powers[i] * (slopes[i] - inner[i])).astype(BF16) for i in range(pairs)]
        to_values = [nn(powers[i].astype(BF16), grads[i]) for i in range(pairs)]
        to_keys = [nn(changes[i], queries[i]) for i in range(pairs)]
        to_query = tuple(carry[i] + nn(turned[chunk, i], changes[i]) for i in range(pairs))
        for i in range(pairs):
            grad_values[chunk, :, columns_of(0, i)] += to_values[i]
            grad_keys[chunk, :, columns_of(0, i)] += to_keys[i]
        return to_query

    grad_query = lax.fori_loop(first, last, step, (jnp.zeros((TILE, 2 * TILE), F32),) * pairs)
    for i in range(pairs):
        out[pl.ds(q_at, TILE), columns_of(0, i)] = (join_turned(grad_query[i]) * scale).astype(BF16)

    @pl.when(tile == pl.num_programs(0) - 1)
    def _():
        all_heads = pairs * TILE
        for chunk in range(chunks):
            out[pl.ds(at(chunk), span), all_heads : 2 * all_heads] = grad_keys[chunk].astype(BF16)
            out[pl.ds(at(chunk), span), 2 * all_heads :] = grad_values[chunk].astype(BF16)


def attention(qkv, seg, info, per, head_size):
    length, width = qkv.shape[0], qkv.shape[1] // 3
    pairs, tiles = width // TILE, length // TILE
    span = per * TILE
    chunks = length // span
    scale = head_size ** (-0.5)

    def place(i, info):
        return place_of(i, info[0], info[1], per)

    return pl.pallas_call(
        functools.partial(attend_kernel, pairs, width, per, scale),
        name="attend",
        out_shape=(
            jax.ShapeDtypeStruct((length, width), BF16),
            jax.ShapeDtypeStruct((2 * pairs, length), F32),
        ),
        grid_spec=pltpu.PrefetchScalarGridSpec(
            num_scalar_prefetch=1,
            grid=(tiles,),
            in_specs=[
                pl.BlockSpec(qkv.shape, lambda i, info: (0, 0), pipeline_mode=pl.Buffered(1)),
                pl.BlockSpec(seg.shape, lambda i, info: (0, 0), pipeline_mode=pl.Buffered(1)),
            ],
            out_specs=[
                pl.BlockSpec((TILE, width), lambda i, info: (place(i, info), 0)),
                pl.BlockSpec((2 * pairs, TILE), lambda i, info: (0, i)),
            ],
            scratch_shapes=[
                pltpu.VMEM((pairs, chunks, span, 2 * TILE), F32),
                pltpu.VMEM((chunks, pairs, TILE, span), BF16),
                pltpu.VMEM((chunks, span, TILE), F32),
            ],
        ),
        compiler_params=pltpu.CompilerParams(
            dimension_semantics=("arbitrary",), vmem_limit_bytes=20 << 20
        ),
        cost_estimate=pl.CostEstimate(flops=0, bytes_accessed=0, transcendentals=0),
    )(info, qkv, seg)


def attention_back(part, parts, qkv, mixed, grad, seg, log_sum, info, per, head_size):
    length, width = qkv.shape[0], qkv.shape[1] // 3
    pairs, tiles = width // TILE // parts, length // TILE
    span = per * TILE
    chunks = length // span
    out = jax.ShapeDtypeStruct((length, 3 * pairs * TILE), BF16)
    scale = head_size ** (-0.5)

    def whole(array):
        return pl.BlockSpec(array.shape, lambda i, info: (0, 0), pipeline_mode=pl.Buffered(1))

    return pl.pallas_call(
        functools.partial(attend_back_kernel, part * pairs, pairs, width, per, scale),
        name="attend_back",
        out_shape=out,
        grid_spec=pltpu.PrefetchScalarGridSpec(
            num_scalar_prefetch=1,
            grid=(tiles,),
            in_specs=[whole(qkv), whole(mixed), whole(grad), whole(seg), whole(log_sum)],
            out_specs=pl.BlockSpec(out.shape, lambda i, info: (0, 0)),
            scratch_shapes=[
                pltpu.VMEM((chunks, span, pairs * TILE), F32),
                pltpu.VMEM((chunks, span, pairs * TILE), F32),
                pltpu.VMEM((chunks, pairs, TILE, span), BF16),
                pltpu.VMEM((chunks, span, TILE), F32),
            ],
        ),
        compiler_params=pltpu.CompilerParams(
            dimension_semantics=("arbitrary",), vmem_limit_bytes=28 << 20
        ),
        cost_estimate=pl.CostEstimate(
            flops=32 * length * length * width, bytes_accessed=8 * length * width * 2, transcendentals=0
        ),
    )(info, qkv, mixed, grad, seg, log_sum)


SWAP = [(0, 1), (1, 0)]


def swap_core(array):
    return lax.ppermute(array, "sc", SWAP)


def swap_chip(array):
    return lax.ppermute(array, "sy", SWAP)


def swap_bit(array, bit):
    if bit == 0:
        return swap_chip(array)
    count = lax.axis_size("img")
    return lax.ppermute(array, "img", [(i, i ^ (1 << (bit - 1))) for i in range(count)])


def own_bit(bit):
    if bit == 0:
        return lax.axis_index("sy")
    return (lax.axis_index("img") >> (bit - 1)) & 1


def fence(*values):
    return lax.optimization_barrier(values)


def axis_of(bit, done):
    return sum(1 for other in done if other > bit)


def pick(index, low, high):
    return jnp.where(index == 0, low, high)


def far_bits():
    return list(range(2, int(math.log2(lax.axis_size("img"))) + 1))


def join(first, second, axis):
    shape = list(first.shape)
    shape[axis] += second.shape[axis]
    held = lax.dynamic_update_slice_in_dim(jnp.zeros(shape, first.dtype), first, 0, axis)
    return lax.dynamic_update_slice_in_dim(held, second, first.shape[axis], axis)


class Turn:
    def __init__(self):
        self.arrays, self.shapes, self.jobs = [], [], []

    def read(self, array):
        for i, other in enumerate(self.arrays):
            if other is array:
                return i
        self.arrays.append(array)
        return len(self.arrays) - 1

    def write(self, shape, dtype):
        self.shapes.append(jax.ShapeDtypeStruct(shape, dtype))
        return len(self.shapes) - 1

    def run(self, bits):
        count = len(self.arrays)

        def kernel(own, *refs):
            mine = [own[i] for i in range(bits.shape[0])]
            for job in self.jobs:
                job(mine, refs[:count], refs[count:])

        spent = sum(a.size * jnp.dtype(a.dtype).itemsize for a in [*self.arrays, *self.shapes])
        return pl.pallas_call(
            kernel,
            name="turn",
            out_shape=tuple(self.shapes),
            in_specs=[pl.BlockSpec(memory_space=pltpu.SMEM)] + [pl.BlockSpec(memory_space=pltpu.VMEM)] * count,
            out_specs=tuple(pl.BlockSpec(memory_space=pltpu.VMEM) for _ in self.shapes),
            compiler_params=pltpu.CompilerParams(vmem_limit_bytes=spent + (2 << 20)),
            cost_estimate=pl.CostEstimate(flops=0, bytes_accessed=0, transcendentals=0),
        )(bits, *self.arrays)


def combinations(bits):
    made = [{}]
    for bit in bits:
        made = [{**choice, bit: value} for choice in made for value in (0, 1)]
    return made


def flat_index(choice, bits):
    at = 0
    for bit in sorted(bits, reverse=True):
        at = at * 2 + choice[bit]
    return at


def block_of(at, rows, base=0):
    start = at * rows + base
    if isinstance(start, int):
        return pl.ds(start, rows)
    return pl.ds(pl.multiple_of(start, math.gcd(rows, base) if base else rows), rows)


class Piece:
    def __init__(self, array, rows, bits, order, stride=None, base=0):
        self.held, self.rows, self.bits = (array, base), rows, list(bits)
        self.fixed, self.order, self.came = [], list(order), None
        self.stride, self.source = stride or rows, bool(bits)


class Gather:
    def __init__(self, first, second):
        far = list(reversed(far_bits()))
        self.pieces = [
            Piece(array, array.shape[0], [], [*far, *last])
            for array, last in ((first, (1, 0)), (second, (0, 1)))
        ]

    def wants(self):
        return [(p.order[0], p.rows << (len(p.bits) + (p.came is not None))) for p in self.pieces]

    def turn(self, turn, places):
        for p, (out, base) in zip(self.pieces, places):
            if p.came is None:
                turn.jobs.append(copy_rows(turn.read(p.held[0]), p.held[1], out, base, p.rows << len(p.bits)))
            else:
                bit = p.sent
                absorb_gather(turn, p, bit, lambda choice, p=p, out=out, base=base: [(out, choice, base)])
            p.sent = p.order.pop(0)
            p.next_held = (out, base)

    def settle(self, outs, came):
        for p, where in zip(self.pieces, came):
            if p.came is not None:
                p.bits.append(p.last)
            p.held, p.came, p.last = (outs[p.next_held[0]], p.next_held[1]), where, p.sent

    def arrays(self):
        return [a for p in self.pieces for a in ([p.held[0]] + ([p.came[0]] if p.came else []))]

    def relabel(self, swap):
        for p in self.pieces:
            p.held = (swap(p.held[0]), p.held[1])
            if p.came:
                p.came = (swap(p.came[0]), p.came[1])

    def left(self):
        return len(self.pieces[0].order)

    def result(self, bits, outs):
        turn = Turn()
        made = [turn.write(shape, BF16) for shape, _ in outs]
        for i, p in enumerate(self.pieces):
            held, came = turn.read(p.held[0]), turn.read(p.came[0])
            moves = [(out, move) for out, (_, moves) in zip(made, outs) for move in moves[i]]

            def job(mine, ins, refs, p=p, held=held, came=came, moves=moves):
                everyone = [*p.bits, p.last]
                for choice in combinations(p.bits):
                    at = flat_index(choice, p.bits)
                    for source, base, value in (
                        (ins[held], p.held[1], mine[p.last]),
                        (ins[came], p.came[1], 1 - mine[p.last]),
                    ):
                        chip = flat_index({**choice, p.last: value}, everyone)
                        for out, ((low, high), (left, right), stride, row, column) in moves:
                            start = pl.multiple_of(chip * stride + row, math.gcd(stride, row) if row else stride)
                            refs[out][pl.ds(start, high - low), column : column + right - left] = source[
                                pl.ds(base + at * p.rows + low, high - low), left:right
                            ]

            turn.jobs.append(job)
        return turn.run(bits)


class Spread:
    def __init__(self, array):
        self.pieces = [Piece(array, array.shape[0], [], [*reversed(far_bits()), 0, 1])]

    def wants(self):
        return [(self.pieces[0].order[0], self.pieces[0].rows)]

    def turn(self, turn, places):
        [p], [(out, base)] = self.pieces, places
        p.order.pop(0)
        p.next_held = (out, base)
        if p.came is None:
            turn.jobs.append(copy_rows(turn.read(p.held[0]), p.held[1], out, base, p.rows))
            return
        held, came, held_base, came_base, rows = turn.read(p.held[0]), turn.read(p.came[0]), p.held[1], p.came[1], p.rows

        def job(mine, ins, refs):
            refs[out][base : base + rows] = (
                ins[held][held_base : held_base + rows] + ins[came][came_base : came_base + rows]
            )

        turn.jobs.append(job)

    def settle(self, outs, came):
        [p] = self.pieces
        p.held, p.came = (outs[p.next_held[0]], p.next_held[1]), came[0]

    arrays, relabel, left = Gather.arrays, Gather.relabel, Gather.left

    def result(self):
        [p] = self.pieces
        return sum(array[base : base + p.rows] for array, base in (p.held, p.came))


class Rider:
    def __init__(self, array, bit):
        self.pieces = [Piece(array, array.shape[0], [], [bit])]

    wants, turn, settle = Spread.wants, Spread.turn, Spread.settle
    arrays, relabel, left = Gather.arrays, Gather.relabel, Gather.left

    def result(self):
        [p] = self.pieces
        return p.came[0][p.came[1] : p.came[1] + p.rows]


def copy_rows(source, source_base, out, base, rows):
    def job(mine, ins, refs):
        refs[out][base : base + rows] = ins[source][source_base : source_base + rows]

    return job


def absorb_gather(turn, p, bit, targets):
    held, came = turn.read(p.held[0]), turn.read(p.came[0])
    last = p.last
    known = list(p.bits)
    held_base, came_base, rows = p.held[1], p.came[1], p.rows
    [(out, _, base)] = targets(None)

    def job(mine, ins, refs):
        for choice in combinations(known):
            at = flat_index(choice, known)
            for source, start, value in ((held, held_base, mine[last]), (came, came_base, 1 - mine[last])):
                to = flat_index({**choice, last: value}, [*known, last])
                refs[out][block_of(to, rows, base)] = ins[source][block_of(at, rows, start)]

    turn.jobs.append(job)


class Scatter:
    def __init__(self, first, second=None):
        far = far_bits()
        bits = sorted([0, 1, *far], reverse=True)
        rows = first.shape[0] >> len(bits)
        if second is None:
            half = rows // 2
            self.pieces = [
                Piece(first, half, bits, [*near, *far], rows, base) for near, base in (((0, 1), 0), ((1, 0), half))
            ]
        else:
            self.pieces = [
                Piece(array, rows, bits, [*near, *far]) for array, near in ((first, (0, 1)), (second, (1, 0)))
            ]

    def wants(self):
        return [(p.order[0], p.rows << (len(p.bits) - len(p.fixed) - 1)) for p in self.pieces]

    def turn(self, turn, places):
        for p, (out, base) in zip(self.pieces, places):
            bit = p.order.pop(0)
            free = [b for b in p.bits if b not in p.fixed and b != bit]
            rows, bits, fixed = p.rows, list(p.bits), list(p.fixed)
            held = turn.read(p.held[0])
            stride, first = p.stride, p.held[1]

            def block(choice, bits=bits, stride=stride, first=first, rows=rows):
                start = flat_index(choice, bits) * stride + first
                return pl.ds(pl.multiple_of(start, math.gcd(stride, first) if first else stride), rows)

            if p.came is None:
                p.next = None

                def job(mine, ins, refs, held=held, rows=rows, free=free, bit=bit, out=out, base=base, block=block):
                    for choice in combinations(free):
                        refs[out][block_of(flat_index(choice, free), rows, base)] = ins[held][
                            block({**choice, bit: 1 - mine[bit]})
                        ]

            else:
                came, came_base = turn.read(p.came[0]), p.came[1]
                keep = turn.write((rows << len(free), p.held[0].shape[1]), BF16)
                p.next = keep

                def job(
                    mine, ins, refs, held=held, rows=rows, fixed=fixed, free=free, bit=bit, out=out, base=base,
                    came=came, came_base=came_base, keep=keep, block=block,
                ):
                    settled = {b: mine[b] for b in fixed}
                    for choice in combinations(free):
                        for value, target, start in ((1 - mine[bit], out, base), (mine[bit], keep, 0)):
                            now = {**choice, bit: value}
                            total = ins[held][block({**now, **settled})].astype(F32) + ins[came][
                                block_of(flat_index(now, [*free, bit]), rows, came_base)
                            ].astype(F32)
                            refs[target][block_of(flat_index(choice, free), rows, start)] = total.astype(BF16)

            turn.jobs.append(job)
            p.sent, p.free = bit, free

    def settle(self, outs, came):
        for p, where in zip(self.pieces, came):
            if p.next is None:
                p.fixed = [p.sent]
            else:
                p.held, p.bits, p.fixed = (outs[p.next], 0), list(p.free), []
                p.stride, p.source = p.rows, False
            p.came = where

    arrays, relabel, left = Gather.arrays, Gather.relabel, Gather.left

    def result(self, bits):
        turn = Turn()
        for p in self.pieces:
            held, came, base, rows = turn.read(p.held[0]), turn.read(p.came[0]), p.came[1], p.rows
            out = turn.write((rows, p.held[0].shape[1]), F32)

            def job(mine, ins, refs, held=held, came=came, base=base, rows=rows, out=out):
                refs[out][...] = ins[held][...].astype(F32) + ins[came][base : base + rows].astype(F32)

            turn.jobs.append(job)
        return turn.run(bits)


def swap_rows(moves, bits):
    wants = [move.wants() for move in moves]
    sizes, places = {}, []
    for bit, rows in (want for group in wants for want in group):
        places.append((bit, sizes.get(bit, 0)))
        sizes[bit] = sizes.get(bit, 0) + rows
    turn = Turn()
    width = moves[0].pieces[0].held[0].shape[1]
    outs = {bit: turn.write((rows, width), BF16) for bit, rows in sizes.items()}
    located = [(outs[bit], base) for bit, base in places]
    starts = [0]
    for move in moves:
        starts.append(starts[-1] + len(move.pieces))
    for i, move in enumerate(moves):
        move.turn(turn, located[starts[i] : starts[i + 1]])
    made = turn.run(bits)
    got = {bit: swap_bit(made[out], bit) for bit, out in outs.items()}
    came = [(got[bit], base) for bit, base in places]
    for i, move in enumerate(moves):
        move.settle(made, came[starts[i] : starts[i + 1]])


def add_came(own, came):
    return own.astype(BF16).astype(F32) + came.astype(F32)


def add_hop(array, bit):
    return add_came(array, swap_bit(array.astype(BF16), bit))


def phase(bits, moves, work, *values):
    chains = [move if isinstance(move, tuple) else (move, 1) for move in moves]
    chains = [
        ([move for move in chain[:-1] if move.left()], min(chain[-1], chain[0].left())) for chain in chains
    ]
    moves = [move for chain, _ in chains for move in chain]

    def tie(extra):
        arrays = [a for move in moves for a in move.arrays()]
        held, extra = fence(arrays, extra)
        table = list(zip(arrays, held))
        for move in moves:
            move.relabel(lambda array: next(new for old, new in table if old is array))
        return extra

    values = tie(values)
    if moves:
        swap_rows(moves, bits)
    for chain, count in chains:
        for _ in range(count - 1):
            swap_rows(chain, bits)
    made = work(*values) if work else ()
    return tie(made)


def by_rows(body, rows, whole, outs, sums=0, tile=TILE, name="rows"):
    rows = [array if isinstance(array, tuple) else (array, 0, array.shape[0]) for array in rows]
    length = rows[0][2]
    width = outs[0][0]

    def kernel(*refs):
        ins, results = refs[: len(rows) + len(whole)], refs[len(rows) + len(whole) :]
        made = body(*(ref[...] for ref in ins))
        for ref, value in zip(results, made):
            if ref.shape[0] == 1:

                @pl.when(pl.program_id(0) == 0)
                def _(ref=ref):
                    ref[...] = jnp.zeros_like(ref)

                ref[...] += value
            else:
                ref[...] = value.astype(ref.dtype)

    spent = sum(array.size * array.dtype.itemsize for array in whole)
    for columns, kind in [*outs, *((array.shape[1], array.dtype) for array, _, _ in rows)]:
        spent += 2 * tile * columns * jnp.dtype(kind).itemsize

    def steps(columns, first=0):
        return pl.BlockSpec((tile, columns), lambda i: (i + first // tile, 0))

    def fixed(shape, **how):
        return pl.BlockSpec(shape, lambda i: (0,) * len(shape), **how)

    return pl.pallas_call(
        kernel,
        name=name,
        grid=(length // tile,),
        out_shape=[jax.ShapeDtypeStruct((length, columns), dtype) for columns, dtype in outs]
        + [jax.ShapeDtypeStruct((1, width), F32)] * sums,
        in_specs=[steps(array.shape[1], first) for array, first, _ in rows]
        + [fixed(array.shape, pipeline_mode=pl.Buffered(1)) for array in whole],
        out_specs=[steps(columns) for columns, _ in outs] + [fixed((1, width))] * sums,
        compiler_params=pltpu.CompilerParams(
            dimension_semantics=("arbitrary",), vmem_limit_bytes=spent + (12 << 20)
        ),
        cost_estimate=pl.CostEstimate(flops=0, bytes_accessed=0, transcendentals=0),
    )(*(array for array, _, _ in rows), *whole)


def normalize(stream):
    center = jnp.mean(stream, axis=-1, keepdims=True)
    centered = stream - center
    spread = jnp.mean(centered * centered, axis=-1, keepdims=True)
    inverse = lax.rsqrt(spread + EPS)
    return centered * inverse, inverse


def normalize_back(normed, inverse, gain, grad):
    scaled = grad * gain
    middle = jnp.mean(scaled, axis=-1, keepdims=True)
    along = jnp.mean(scaled * normed, axis=-1, keepdims=True)
    return (
        inverse[:, :1] * (scaled - middle - normed * along),
        jnp.sum(grad * normed, axis=0, keepdims=True),
        jnp.sum(grad, axis=0, keepdims=True),
    )


def rows_from(columns, count):
    one_hot = (jnp.arange(16)[:, None] == jnp.arange(TILE)[None, :]).astype(BF16)
    rows = nt(one_hot, columns)
    return [rows[i : i + 1] for i in range(count)]


def column_choice(rows, columns):
    row, lane = jnp.arange(rows)[:, None], jnp.arange(TILE)[None, :]
    return (row == 8 + lane % columns).astype(F32)


def own_place(width, columns):
    per_run = TILE // columns
    row, lane = jnp.arange(width)[:, None], jnp.arange(TILE)[None, :]
    return row % per_run == lane // columns


def unroll_bias(columns, own_c, ff_rows):
    width, extra = columns.shape[0], 4
    spread = nn(columns, column_choice(TILE, extra).astype(BF16))
    runs = jnp.where(own_place(width, extra), spread, 0.0).reshape(-1, TILE // extra, TILE).sum(axis=1)
    runs = runs.reshape(-1, 2, ff_rows)
    return pick(own_c, runs[:, 0], runs[:, 1]).reshape(1, -1)


def roll_bias(sums, own_c, width, rows, ff_rows):
    extra = 4
    runs = sums.reshape(-1, ff_rows)
    zero = jnp.zeros_like(runs)
    runs = jnp.stack([pick(own_c, runs, zero), pick(own_c, zero, runs)], axis=1).reshape(-1, 1, TILE)
    spread = jnp.broadcast_to(runs, (runs.shape[0], TILE // extra, TILE)).reshape(width, TILE)
    spread = jnp.where(own_place(width, extra), spread, 0.0)
    return lax.dot_general(
        column_choice(rows, extra), spread, (((1,), (1,)), ((), ())), precision=PRECISE, preferred_element_type=F32
    )


def token_sums(array):
    return nn(jnp.ones((8, array.shape[0]), BF16), array)[:1]


def gelu_and_slope(values):
    cdf = 0.5 * (1.0 + lax.erf(values * (0.5**0.5)))
    density = jnp.exp(-0.5 * values * values) * (1.0 / math.sqrt(2.0 * math.pi))
    return values * cdf, cdf + values * density


def adam_update(weight, gradient, first_moment, second_moment, factor, decay):
    scaled = gradient * factor
    first_new = 0.9 * first_moment + 0.1 * scaled
    second_new = 0.999 * second_moment + 0.001 * scaled * scaled
    first_hat = first_new / FIRST_CORRECTION
    second_hat = second_new / SECOND_CORRECTION
    direction = first_hat / (jnp.sqrt(second_hat) + 1e-08) + decay * weight
    return (direction, first_new, second_new)


def per_device(
    patches,
    cotangent,
    res_ids,
    pos_table,
    attn_in,
    attn_out,
    mlp_in,
    mlp_out,
    vectors,
    first_attn_in,
    first_attn_out,
    first_mlp_in,
    first_mlp_out,
    first_vectors,
    second_attn_in,
    second_attn_out,
    second_mlp_in,
    second_mlp_out,
    second_vectors,
):
    row_count, local_len, width = patches.shape
    img_count, halves = lax.axis_size("img"), lax.axis_size("sy")
    chips = img_count * halves
    row_len = local_len * halves * 2
    slot_total = row_count * img_count * row_len
    head_size = width // HEADS
    own_y, own_c = lax.axis_index("sy"), lax.axis_index("sc")
    rows = attn_in.shape[0]
    half = width // 2
    ff_rows = mlp_out.shape[0]
    ff_half = chips * ff_rows
    table_size = GRID * GRID
    vector_count = vectors.shape[1]

    bits = jnp.stack([own_bit(bit) for bit in [0, 1, *far_bits()]]).astype(jnp.int32)

    def to_rows(array):
        mine = lax.dynamic_index_in_dim(array, own_y, 0, keepdims=False)
        other = lax.dynamic_index_in_dim(array, 1 - own_y, 0, keepdims=False)
        return join(mine, swap_chip(other), 0)

    res_row = pick(own_y, res_ids[0], res_ids[1])
    all_positions = jnp.arange(row_len, dtype=jnp.int32)
    segment_all, _, _, _ = layout(res_row, all_positions)
    seg = jnp.broadcast_to(segment_all.astype(F32)[None, :], (8, row_len))
    begin, end = key_bounds(res_row, row_len)
    info = jnp.concatenate([jnp.stack([own_y, own_c]).astype(jnp.int32), begin, end])
    near = jnp.arange(local_len, dtype=jnp.int32)
    positions = jnp.concatenate(
        [(2 * own_y + own_c) * local_len + near, (2 * (1 - own_y) + own_c) * local_len + near]
    )
    _, side_of, patch_index, usable = layout(res_row, positions)
    place = table_weights(side_of, patch_index, usable)
    usable = usable.astype(F32)[:, None]

    def by_core(array, blocks):
        split = array.reshape(rows, blocks, 2, -1)
        low, high = split[:, :, 0].reshape(rows, -1), split[:, :, 1].reshape(rows, -1)
        return pick(own_c, low, high), pick(own_c, high, low)

    vector_pad = jnp.pad(vectors, ((0, 0), (0, TILE - vector_count))).astype(BF16)
    mine_in, away_in = by_core(attn_in.astype(BF16), 3)
    mine_out, away_out = by_core(attn_out.astype(BF16), 1)
    mine_up, away_up = by_core(mlp_in.astype(BF16), chips)
    mine = jnp.concatenate([mine_in, mine_out, mine_up], axis=1)
    away = jnp.concatenate([away_in, away_out, away_up], axis=1)
    came, came_vector = swap_core(away), swap_core(vector_pad)
    shard = jnp.concatenate([pick(own_c, mine, came), pick(own_c, came, mine)], axis=0)
    vector_shard = jnp.concatenate(
        [pick(own_c, vector_pad, came_vector), pick(own_c, came_vector, vector_pad)], axis=0
    )[:, :16].reshape(1, -1)
    vector_row = jnp.pad(vector_shard, ((0, 0), (0, width - vector_shard.shape[1])))
    chip = lax.axis_index("img") * halves + own_y
    vector_rows = jnp.where(jnp.arange(chips)[:, None] == chip, vector_row, jnp.zeros_like(vector_row))
    in_width = 3 * half
    own = local_len * row_count
    per = local_len // TILE

    def with_core(array):
        return join(array, swap_core(array), 0)

    def sum_core(left, weights, product):
        away = product(left[own:], weights).astype(BF16)
        came = swap_core(away)
        return product(left[:own], weights) + came.astype(F32)

    low_down, high_down = jnp.split(mlp_out.astype(BF16), 2)
    gather_in = Gather(shard[:, :width], shard[:, width : 2 * width])
    gather_vectors = Spread(vector_rows)
    gather_up = Gather(shard[:, 2 * width : 2 * width + half * 2], shard[:, 2 * width + half * 2 :])
    gather_down = Gather(low_down, high_down)

    patches, cotangent = phase(
        bits,
        [(gather_in, gather_vectors, len(far_bits()))],
        lambda *arrays: [to_rows(array) for array in arrays],
        patches,
        cotangent,
    )

    wide_place = jnp.pad(place, ((0, 0), (0, TILE - table_size)))
    wide_table = jnp.pad(pos_table, ((0, TILE - table_size), (0, 0)))
    wide_usable = jnp.broadcast_to(usable, (own, TILE))
    small = TILE

    def first(patches, cotangent):
        def body(patches, place, cotangent, usable, table):
            stream = patches.astype(F32) + jnp.dot(place, table, precision=PRECISE, preferred_element_type=F32)
            normed, inverse = normalize(stream)
            grad = cotangent.astype(F32) * usable[:, :1]
            return stream, normed, jnp.broadcast_to(inverse, (stream.shape[0], TILE)), grad

        stream, hat_one, inverse_one, grad_own = by_rows(
            body,
            [patches, wide_place, cotangent, wide_usable],
            [wide_table],
            [(width, F32), (width, F32), (TILE, F32), (width, BF16)],
            name="first",
        )
        return stream, hat_one, inverse_one, grad_own

    far = far_bits()
    stream, hat_one, inverse_one, grad_own = phase(
        bits, [gather_in, gather_vectors, gather_up], first, patches, cotangent
    )
    phase(bits, [gather_in, gather_vectors, (gather_up, len(far) - 1), gather_down], None)
    block = 2 * rows
    spare = in_width - width
    in_matrix, out_columns = gather_in.result(
        bits,
        [
            (
                (width, in_width),
                ([((0, block), (0, width), block, 0, 0)], [((0, block), (0, spare), block, 0, width)]),
            ),
            ((width, width - spare), ([], [((0, block), (spare, width), block, 0, 0)])),
        ],
    )
    vector_part = jnp.pad(
        gather_vectors.result()[:, : block * 16].reshape(-1, 16), ((0, 0), (0, TILE - 16))
    )
    gain_one, shift_one, bias_query, bias_value, bias_out, gain_two, shift_two, bias_down = (
        rows_from(vector_part, 8)
    )
    bias_query = pick(own_c, bias_query[:, :half], bias_query[:, half:])
    bias_value = pick(own_c, bias_value[:, :half], bias_value[:, half:])
    bias_up = unroll_bias(vector_part, own_c, ff_rows)
    bias_qkv = jnp.concatenate([bias_query, jnp.zeros_like(bias_query), bias_value], axis=1)

    def project(hat_one, in_matrix, out_columns):
        normed_one = with_core((hat_one * gain_one + shift_one).astype(BF16))
        low, high = out_columns[:half], out_columns[half:]
        keep_out, came_out = pick(own_c, low, high), swap_core(pick(own_c, high, low))
        out_matrix = join(pick(own_c, keep_out, came_out), pick(own_c, came_out, keep_out), 1)
        return normed_one, out_matrix, (nn(normed_one, in_matrix) + bias_qkv).astype(BF16)

    normed_one, out_matrix, qkv = phase(
        bits,
        [gather_up, (gather_down, len(far) - 1)], project, hat_one, in_matrix, out_columns
    )

    def matmul_rows(left, right, product, name):
        return product(left[own:], right).astype(BF16)

    def attend(qkv, out_matrix, grad_own):
        mixed, log_sum = attention(qkv, seg, info, per, head_size)
        return mixed, log_sum, matmul_rows(mixed, out_matrix, nn, "out_away"), with_core(grad_own)

    mixed, log_sum, out_away, grad_last = phase(bits, [gather_up], attend, qkv, out_matrix, grad_own)

    def project_out(stream, mixed, out_away, out_matrix):
        def body(stream, mixed, came, matrix, bias, gain, shift):
            stream_two = stream + nn(mixed, matrix) + came.astype(F32) + bias
            normed, inverse = normalize(stream_two)
            return stream_two, normed, jnp.broadcast_to(inverse, (stream.shape[0], TILE)), normed * gain + shift

        return by_rows(
            body,
            [(stream, 0, own), mixed, swap_core(out_away)],
            [out_matrix, bias_out, gain_two, shift_two],
            [(width, F32), (width, F32), (TILE, F32), (width, BF16)],
            name="out_norm",
            tile=own // 2,
        )

    stream_two, hat_two, inverse_two, normed_two = phase(
        bits, [gather_down], project_out, stream, mixed, out_away, out_matrix
    )
    (up_matrix,) = gather_up.result(
        bits,
        [
            (
                (width, ff_half),
                ([((0, block), (0, width), block, 0, 0)], [((0, block), (0, width), block, 0, width)]),
            )
        ],
    )

    def expand(normed_two, up_matrix, grad_last):
        normed_two = with_core(normed_two)
        hidden_pre = nn(normed_two, up_matrix) + bias_up
        hidden, slope = gelu_and_slope(hidden_pre)
        hidden = hidden.astype(BF16)
        return normed_two, hidden, slope, tn(hidden, grad_last).astype(BF16)

    normed_two, hidden, slope, grad_down = phase(bits, [gather_down], expand, normed_two, up_matrix, grad_last)
    part_rows = ff_rows // 2
    (down_matrix,) = gather_down.result(
        bits,
        [
            (
                (ff_half, width),
                (
                    [((0, part_rows), (0, width), ff_rows, 0, 0)],
                    [((0, part_rows), (0, width), ff_rows, part_rows, 0)],
                ),
            )
        ],
    )

    scatter_down = Scatter(grad_down)

    def hidden_back(grad_last, down_matrix, slope, normed_two, up_matrix):
        grad_pre = (nt(grad_last, down_matrix) * slope).astype(BF16)
        return (
            grad_pre,
            matmul_rows(grad_pre, up_matrix, nt, "norm_two_away"),
            tn(normed_two, grad_pre[:, :width]).astype(BF16),
            tn(normed_two, grad_pre[:, width:]).astype(BF16),
        )

    grad_pre, two_away, *grad_up = phase(
        bits, [scatter_down], hidden_back, grad_last, down_matrix, slope, normed_two, up_matrix
    )
    scatter_up = Scatter(*grad_up)

    def norm_back(grad, away, matrix, hat, inverse, added, gain, name):
        def body(grad, came, hat, inverse, added, matrix, gain):
            back, gain_sum, shift_sum = normalize_back(hat, inverse, gain, nt(grad, matrix) + came.astype(F32))
            total = added.astype(F32) + back
            return total, total, gain_sum, shift_sum

        return by_rows(
            body,
            [(grad, 0, own), swap_core(away), hat, inverse, added],
            [matrix, gain],
            [(width, F32), (width, BF16)],
            sums=2,
            name=name,
            tile=own // 2,
        )

    def middle(values, hidden, down_matrix):
        return norm_back(*values, "norm_two_back"), matmul_rows(hidden, down_matrix, nn, "output_away")

    (grad_two, grad_branch, grad_gain_two, grad_shift_two), output_away = phase(
        bits,
        [scatter_down],
        middle,
        (grad_pre, two_away, up_matrix, hat_two, inverse_two, grad_own, gain_two),
        hidden,
        down_matrix,
    )

    def attention_grads(grad_branch, out_matrix, qkv, mixed, log_sum, output_away):
        grad_branch = with_core(grad_branch)
        grad_mixed = nt(grad_branch, out_matrix).astype(BF16)
        grad_qkv = attention_back(0, 1, qkv, mixed, grad_mixed, seg, log_sum, info, per, head_size)
        return grad_branch, swap_core(output_away), grad_qkv

    grad_branch, came_output, grad_qkv = phase(
        bits,
        [scatter_up, scatter_down],
        attention_grads,
        grad_branch,
        out_matrix,
        qkv,
        mixed,
        log_sum,
        output_away,
    )

    def in_grads(mixed, grad_branch, normed_one, grad_qkv, in_matrix):
        grad_rows = tn(mixed, grad_branch).astype(BF16)
        low, high = grad_rows[:, :half], grad_rows[:, half:]
        keep_rows, came_rows = pick(own_c, low, high), swap_core(pick(own_c, high, low))
        grad_out = join(pick(own_c, keep_rows, came_rows), pick(own_c, came_rows, keep_rows), 0)
        return (
            matmul_rows(grad_qkv, in_matrix, nt, "norm_one_away"),
            tn(normed_one, grad_qkv[:, :width]).astype(BF16),
            tn(normed_one, grad_qkv[:, width:]).astype(BF16),
            grad_out,
        )

    one_away, left, right, grad_out = phase(
        bits, [scatter_up, scatter_down], in_grads, mixed, grad_branch, normed_one, grad_qkv, in_matrix
    )
    scatter_in = Scatter(left, join(right, grad_out, 1))

    def widen(row):
        zero = jnp.zeros_like(row)
        return jnp.concatenate([pick(own_c, row, zero), pick(own_c, zero, row)], axis=1)

    narrow_rows = vector_count + table_size
    narrow_rows += -narrow_rows % 16

    def norm_one_back(grad_qkv, one_away, in_matrix, hat_one, inverse_one, grad_two, grad_pre, grad_branch, grad_last):
        grad_stream, grad_low, grad_gain_one, grad_shift_one = norm_back(
            grad_qkv, one_away, in_matrix, hat_one, inverse_one, grad_two, gain_one, "norm_one_back"
        )
        wide_place = jnp.pad(place, ((0, 0), (vector_count, narrow_rows - vector_count - table_size)))
        narrow = lax.dot_general(
            wide_place, grad_stream, (((0,), (0,)), ((), ())), precision=PRECISE, preferred_element_type=F32
        ) + roll_bias(token_sums(grad_pre), own_c, width, narrow_rows, ff_rows)
        sums = token_sums(grad_qkv)
        rows_of_sums = [
            grad_gain_one,
            grad_shift_one,
            widen(sums[:, :half]),
            widen(sums[:, 2 * half :]),
            token_sums(grad_branch[:own]),
            grad_gain_two,
            grad_shift_two,
            token_sums(grad_last[:own]),
        ]
        row = jnp.arange(narrow_rows)[:, None]
        for i, values in enumerate(rows_of_sums):
            narrow = jnp.where(row == i, values, narrow)
        return grad_low, add_came(narrow, swap_core(narrow.astype(BF16)))

    def finish_output(hidden, came, stream_two, down_matrix):
        def body(hidden, came, stream_two, usable, matrix, bias):
            return ((stream_two + nn(hidden, matrix) + came.astype(F32) + bias) * usable[:, :1],)

        return by_rows(
            body,
            [(hidden, 0, own), came, stream_two, wide_usable],
            [down_matrix, bias_down],
            [(width, BF16)],
            name="output",
            tile=own // 2,
        )

    (grad_low, narrow), (output,) = phase(
        bits,
        [scatter_in, scatter_up, (scatter_down, len(far) - 1)],
        lambda values, others: (norm_one_back(*values), finish_output(*others)),
        (grad_qkv, one_away, in_matrix, hat_one, inverse_one, grad_two, grad_pre, grad_branch, grad_last),
        (hidden, came_output, stream_two, down_matrix),
    )

    def ride(narrow, bit):
        return Rider(narrow.astype(BF16), bit)

    scatters = [scatter_in, scatter_up]
    rider = ride(narrow, 0)
    phase(bits, [*scatters, rider], None)
    narrow = add_came(narrow, rider.result())
    sent = [Rider(output[local_len:], 0), Rider(grad_low[local_len:], 0)]
    for step, bit in enumerate(far):
        rider = ride(narrow, bit)
        phase(bits, [*scatters, rider, *sent[step : step + 1]], None)
        narrow = add_came(narrow, rider.result())
    while any(move.left() for move in [*scatters, *sent]):
        phase(bits, [*scatters, *sent], None)
    narrow = add_hop(narrow, 1)
    came_output, came_grad = (rider.result() for rider in sent)

    def back_to_rows(array, other):
        mine = array[:local_len]
        return jnp.stack([pick(own_y, mine, other), pick(own_y, other, mine)], axis=0)

    output, input_grad = back_to_rows(output, came_output), back_to_rows(grad_low, came_grad)
    shard_down = jnp.concatenate(scatter_down.result(bits), axis=0)
    shard_up = jnp.concatenate(scatter_up.result(bits), axis=1)
    shard_in = jnp.concatenate(scatter_in.result(bits), axis=1)
    shard_in, shard_out = shard_in[:, :in_width], shard_in[:, in_width:]

    def rows_of(array, core):
        return lax.dynamic_slice_in_dim(array, core * rows, rows, 0)

    def trade(array, blocks):
        away, keep = rows_of(array, 1 - own_c), rows_of(array, own_c)
        came = swap_core(away).reshape(rows, blocks, -1)
        keep = keep.reshape(rows, blocks, -1)
        both = jnp.stack([pick(own_c, keep, came), pick(own_c, came, keep)], axis=2)
        return both.reshape(rows, -1)

    grad_up_shard = trade(shard_up, chips)
    grad_out_shard = trade(shard_out, 1)
    grad_in_shard = trade(shard_in, 3)
    device = (lax.axis_index("img") * halves + own_y) * 2 + own_c
    grad_vectors_shard = lax.dynamic_slice_in_dim(narrow[:vector_count], device * rows, rows, 1).T
    table_grad = narrow[vector_count : vector_count + table_size]

    factor = 1.0 / slot_total
    shards = (grad_in_shard, grad_out_shard, grad_up_shard, shard_down, grad_vectors_shard)
    weights = (attn_in, attn_out, mlp_in, mlp_out, vectors)
    firsts = (first_attn_in, first_attn_out, first_mlp_in, first_mlp_out, first_vectors)
    seconds = (second_attn_in, second_attn_out, second_mlp_in, second_mlp_out, second_vectors)
    decays = (0.05, 0.05, 0.05, 0.05, 0.0)
    updated = [
        by_rows(
            lambda w, g, m, v, decay=decays[i]: adam_update(w, g, m, v, factor, decay),
            [weights[i], shards[i], firsts[i], seconds[i]],
            [],
            [(weights[i].shape[1], F32)] * 3,
            name="adam",
            tile=weights[i].shape[0],
        )
        for i in range(4)
    ]
    updated.append(adam_update(vectors, grad_vectors_shard, first_vectors, second_vectors, factor, 0.0))
    return (
        output,
        input_grad,
        table_grad,
        *shards,
        *(updated[i][0] for i in range(5)),
        *(updated[i][1] for i in range(5)),
        *(updated[i][2] for i in range(5)),
    )


def solution(mesh):
    img, seq = mesh.shape["img"], mesh.shape["seq"]
    inner = Mesh(mesh.devices.reshape(img, seq // 2, 2), ("img", "sy", "sc"))
    tokens = P("img", ("sy", "sc"), None)
    shard = P(("img", "sy", "sc"), None)
    return jax.shard_map(
        per_device,
        mesh=inner,
        in_specs=(tokens, tokens, P("img", None), P()) + (shard,) * 15,
        out_specs=(tokens, tokens, P()) + (shard,) * 20,
        check_vma=False,
    )
```

```python
import functools
import math

import jax
import jax.numpy as jnp
from jax import lax
from jax.experimental import pallas as pl
from jax.experimental.pallas import tpu as pltpu
from jax.sharding import Mesh
from jax.sharding import PartitionSpec as P

HEADS = 16
GRID = 7
GRID_HI = 12
TILE = 128

PRECISE = lax.Precision.HIGHEST
FIRST_CORRECTION = 0.9999734386011124
SECOND_CORRECTION = 0.0952078528862911
EPS = 1e-06

F32 = jnp.float32
BF16 = jnp.bfloat16


def image_spans(res_row):
    side = jnp.where(res_row == 384, GRID_HI, jnp.where(res_row == 224, GRID, 0)).astype(jnp.int32)
    lengths = side * side
    slots = res_row.shape[0]
    order = jnp.arange(slots, dtype=jnp.int32)
    earlier = order[None, :] < order[:, None]
    starts = jnp.sum(jnp.where(earlier, lengths[None, :], 0), axis=1)
    return side, lengths, starts


def layout(res_row, positions):
    side, lengths, starts = image_spans(res_row)
    slots = res_row.shape[0]
    places = positions[:, None]
    inside = ((places >= starts[None, :]) & (places < (starts + lengths)[None, :])).astype(jnp.int32)
    usable = jnp.sum(inside, axis=1)
    image_number = jnp.arange(slots, dtype=jnp.int32)
    segment = jnp.sum(inside * image_number, axis=1) + (1 - usable) * slots
    start_of = jnp.sum(inside * starts[None, :], axis=1)
    side_of = jnp.sum(inside * side[None, :], axis=1)
    patch_index = (positions - start_of) * usable
    return segment, side_of, patch_index, usable


def key_bounds(res_row, row_len):
    _, lengths, starts = image_spans(res_row)
    total = jnp.sum(lengths)
    firsts = jnp.arange(row_len // TILE, dtype=jnp.int32) * TILE

    def span(positions):
        places = positions[:, None]
        inside = (places >= starts[None, :]) & (places < (starts + lengths)[None, :])
        found = positions < total
        begin = jnp.sum(jnp.where(inside, starts[None, :], 0), axis=1)
        end = jnp.sum(jnp.where(inside, (starts + lengths)[None, :], 0), axis=1)
        return jnp.where(found, begin, total), jnp.where(found, end, row_len)

    begin, _ = span(firsts)
    _, end = span(firsts + (TILE - 1))
    return begin // TILE, (end + TILE - 1) // TILE


def axis_weights(coord, side_of):
    scaled = jnp.maximum((2 * coord + 1) * GRID - GRID_HI, 0)
    lower_fine = scaled // (2 * GRID_HI)
    fraction_fine = (scaled - lower_fine * 2 * GRID_HI).astype(F32) / (2.0 * GRID_HI)
    resized = side_of == GRID_HI
    lower_cell = jnp.where(resized, lower_fine, coord)
    fraction = jnp.where(resized, fraction_fine, jnp.zeros_like(fraction_fine))
    upper_cell = jnp.minimum(lower_cell + 1, GRID - 1)
    cell_index = jnp.arange(GRID, dtype=jnp.int32)
    below = (cell_index == lower_cell[..., None]).astype(F32)
    above = (cell_index == upper_cell[..., None]).astype(F32)
    return (1.0 - fraction)[..., None] * below + fraction[..., None] * above


def table_weights(side_of, patch_index, usable):
    safe_side = jnp.maximum(side_of, 1)
    row_coord = patch_index // safe_side
    column_coord = patch_index % safe_side
    outer = axis_weights(row_coord, side_of)[:, :, None] * axis_weights(column_coord, side_of)[:, None, :]
    outer = outer * usable.astype(F32)[:, None, None]
    return outer.reshape(side_of.shape[0], GRID * GRID)


def place_of(block, own_y, own_c, per):
    quarter = block // per
    core = (quarter % 2 + own_c) % 2
    half = (quarter // 2 + own_y) % 2
    return (core * 2 + half) * per + block % per


def split_heads(pair):
    lane = lax.broadcasted_iota(jnp.int32, pair.shape, 1)
    zero = jnp.zeros_like(pair)
    low = lane < pair.shape[1] // 2
    return jnp.concatenate([jnp.where(low, pair, zero), jnp.where(low, zero, pair)], axis=0)


def join_heads(stacked):
    half = stacked.shape[0] // 2
    lane = lax.broadcasted_iota(jnp.int32, (half, stacked.shape[1]), 1)
    return jnp.where(lane < stacked.shape[1] // 2, stacked[:half], stacked[half:])


def down_lanes(row):
    return jnp.transpose(jnp.broadcast_to(row, (TILE, TILE)))


def nt(left, right):
    return lax.dot_general(left, right, (((1,), (1,)), ((), ())), preferred_element_type=F32)


def tn(left, right):
    return lax.dot_general(left, right, (((0,), (0,)), ((), ())), preferred_element_type=F32)


def nn(left, right):
    return jnp.dot(left, right, preferred_element_type=F32)


def fold(array, over):
    parts = array.reshape(array.shape[0] // 8, 8, array.shape[1])
    return jnp.max(parts, axis=0) if over == "max" else jnp.sum(parts, axis=0)


def same_segment(seg_down, chunk, seg_q):
    same = seg_down[chunk] == seg_q
    return jnp.concatenate([same, same], axis=1)


def fill_segments(seg, seg_down):
    chunks, span, _ = seg_down.shape
    for chunk in range(chunks):
        row = seg[0:1, chunk * span : (chunk + 1) * span]
        seg_down[chunk] = jnp.transpose(jnp.broadcast_to(row, (TILE, span)))


def join_turned(turned):
    half = turned.shape[1] // 2
    row = lax.broadcasted_iota(jnp.int32, (turned.shape[0], half), 0)
    return jnp.transpose(jnp.where(row < turned.shape[0] // 2, turned[:, :half], turned[:, half:]))


def columns_of(base, j):
    return slice(base + j * TILE, base + (j + 1) * TILE)


def attend_kernel(pairs, width, per, scale, info, qkv, seg, out, log_sum, scores, turned, seg_down):
    tile = pl.program_id(0)
    chunks, span, _ = seg_down.shape
    own_y, own_c = info[0], info[1]
    ratio = span // TILE
    first = info[2 + tile] // ratio
    last = (info[2 + pl.num_programs(0) + tile] + ratio - 1) // ratio

    def at(chunk):
        return pl.multiple_of(place_of(chunk * ratio, own_y, own_c, per) * TILE, TILE)

    @pl.when(tile == 0)
    def _():
        fill_segments(seg, seg_down)
        for chunk in range(chunks):
            for j in range(pairs):
                turned[chunk, j] = jnp.transpose(qkv[pl.ds(at(chunk), span), columns_of(2 * width, j)])

    q_at = pl.multiple_of(place_of(tile, own_y, own_c, per) * TILE, TILE)
    seg_q = seg[0:1, pl.ds(pl.multiple_of(tile * TILE, TILE), TILE)]
    queries = [
        split_heads(qkv[pl.ds(q_at, TILE), columns_of(0, j)] * jnp.asarray(scale, BF16)) for j in range(pairs)
    ]

    def score(chunk, high):
        same = same_segment(seg_down, chunk, seg_q)
        products = [nt(qkv[pl.ds(at(chunk), span), columns_of(width, j)], queries[j]) for j in range(pairs)]
        made = []
        for j in range(pairs):
            s = jnp.where(same, products[j], -1e30)
            scores[j, chunk] = s
            made.append(jnp.maximum(high[j], fold(s, "max")))
        return tuple(made)

    high = lax.fori_loop(first, last, score, (jnp.full((8, 2 * TILE), -1e30, F32),) * pairs)
    tops = [jnp.max(high[j], axis=0, keepdims=True) for j in range(pairs)]

    def mix(chunk, carry):
        total, mixed = carry
        powers = [jnp.exp(scores[j, chunk] - tops[j]) for j in range(pairs)]
        return (
            tuple(total[j] + fold(powers[j], "sum") for j in range(pairs)),
            tuple(mixed[j] + nn(turned[chunk, j], powers[j].astype(BF16)) for j in range(pairs)),
        )

    total, mixed = lax.fori_loop(
        first,
        last,
        mix,
        ((jnp.zeros((8, 2 * TILE), F32),) * pairs, (jnp.zeros((TILE, 2 * TILE), F32),) * pairs),
    )
    for j in range(pairs):
        sums = jnp.sum(total[j], axis=0, keepdims=True)
        out[:, columns_of(0, j)] = join_turned(mixed[j] / sums).astype(BF16)
        log_total = tops[j] + jnp.log(sums)
        log_sum[2 * j : 2 * j + 1] = log_total[:, :TILE]
        log_sum[2 * j + 1 : 2 * j + 2] = log_total[:, TILE:]


def attend_back_kernel(
    start, pairs, width, per, scale, info, qkv, mixed, grad, seg, log_sum, out, grad_keys, grad_values, turned, seg_down
):
    tile = pl.program_id(0)
    chunks, span, _ = seg_down.shape
    own_y, own_c = info[0], info[1]
    ratio = span // TILE
    first = info[2 + tile] // ratio
    last = (info[2 + pl.num_programs(0) + tile] + ratio - 1) // ratio
    heads = range(start, start + pairs)

    def at(chunk):
        return pl.multiple_of(place_of(chunk * ratio, own_y, own_c, per) * TILE, TILE)

    @pl.when(tile == 0)
    def _():
        fill_segments(seg, seg_down)
        grad_keys[...] = jnp.zeros_like(grad_keys)
        grad_values[...] = jnp.zeros_like(grad_values)
        for chunk in range(chunks):
            for i, j in enumerate(heads):
                turned[chunk, i] = jnp.transpose(qkv[pl.ds(at(chunk), span), columns_of(width, j)])

    q_at = pl.multiple_of(place_of(tile, own_y, own_c, per) * TILE, TILE)
    q_from = pl.multiple_of(tile * TILE, TILE)
    seg_q = seg[0:1, pl.ds(q_from, TILE)]
    queries, grads, logs, inner = [], [], [], []
    for j in heads:
        queries.append(split_heads(qkv[pl.ds(q_at, TILE), columns_of(0, j)] * jnp.asarray(scale, BF16)))
        g = grad[pl.ds(q_at, TILE), columns_of(0, j)]
        grads.append(split_heads(g))
        both = jnp.transpose(g.astype(F32) * mixed[pl.ds(q_at, TILE), columns_of(0, j)].astype(F32))
        low = jnp.sum(both[: TILE // 2], axis=0, keepdims=True)
        high = jnp.sum(both[TILE // 2 :], axis=0, keepdims=True)
        inner.append(jnp.concatenate([low, high], axis=1))
        here = log_sum[2 * j : 2 * j + 2, pl.ds(q_from, TILE)]
        logs.append(jnp.concatenate([here[0:1], here[1:2]], axis=1))

    def step(chunk, carry):
        k_at = at(chunk)
        same = same_segment(seg_down, chunk, seg_q)
        scores = [nt(qkv[pl.ds(k_at, span), columns_of(width, j)], queries[i]) for i, j in enumerate(heads)]
        slopes = [nt(qkv[pl.ds(k_at, span), columns_of(2 * width, j)], grads[i]) for i, j in enumerate(heads)]
        powers = [jnp.exp(jnp.where(same, scores[i], -1e30) - logs[i]) for i in range(pairs)]
        changes = [(powers[i] * (slopes[i] - inner[i])).astype(BF16) for i in range(pairs)]
        to_values = [nn(powers[i].astype(BF16), grads[i]) for i in range(pairs)]
        to_keys = [nn(changes[i], queries[i]) for i in range(pairs)]
        to_query = tuple(carry[i] + nn(turned[chunk, i], changes[i]) for i in range(pairs))
        for i in range(pairs):
            grad_values[chunk, :, columns_of(0, i)] += to_values[i]
            grad_keys[chunk, :, columns_of(0, i)] += to_keys[i]
        return to_query

    grad_query = lax.fori_loop(first, last, step, (jnp.zeros((TILE, 2 * TILE), F32),) * pairs)
    for i in range(pairs):
        out[pl.ds(q_at, TILE), columns_of(0, i)] = (join_turned(grad_query[i]) * scale).astype(BF16)

    @pl.when(tile == pl.num_programs(0) - 1)
    def _():
        all_heads = pairs * TILE
        for chunk in range(chunks):
            out[pl.ds(at(chunk), span), all_heads : 2 * all_heads] = grad_keys[chunk].astype(BF16)
            out[pl.ds(at(chunk), span), 2 * all_heads :] = grad_values[chunk].astype(BF16)


def attention(qkv, seg, info, per, head_size):
    length, width = qkv.shape[0], qkv.shape[1] // 3
    pairs, tiles = width // TILE, length // TILE
    span = per * TILE
    chunks = length // span
    scale = head_size ** (-0.5)

    def place(i, info):
        return place_of(i, info[0], info[1], per)

    return pl.pallas_call(
        functools.partial(attend_kernel, pairs, width, per, scale),
        name="attend",
        out_shape=(
            jax.ShapeDtypeStruct((length, width), BF16),
            jax.ShapeDtypeStruct((2 * pairs, length), F32),
        ),
        grid_spec=pltpu.PrefetchScalarGridSpec(
            num_scalar_prefetch=1,
            grid=(tiles,),
            in_specs=[
                pl.BlockSpec(qkv.shape, lambda i, info: (0, 0), pipeline_mode=pl.Buffered(1)),
                pl.BlockSpec(seg.shape, lambda i, info: (0, 0), pipeline_mode=pl.Buffered(1)),
            ],
            out_specs=[
                pl.BlockSpec((TILE, width), lambda i, info: (place(i, info), 0)),
                pl.BlockSpec((2 * pairs, TILE), lambda i, info: (0, i)),
            ],
            scratch_shapes=[
                pltpu.VMEM((pairs, chunks, span, 2 * TILE), F32),
                pltpu.VMEM((chunks, pairs, TILE, span), BF16),
                pltpu.VMEM((chunks, span, TILE), F32),
            ],
        ),
        compiler_params=pltpu.CompilerParams(
            dimension_semantics=("arbitrary",), vmem_limit_bytes=20 << 20
        ),
        cost_estimate=pl.CostEstimate(flops=0, bytes_accessed=0, transcendentals=0),
    )(info, qkv, seg)


def attention_back(part, parts, qkv, mixed, grad, seg, log_sum, info, per, head_size):
    length, width = qkv.shape[0], qkv.shape[1] // 3
    pairs, tiles = width // TILE // parts, length // TILE
    span = per * TILE
    chunks = length // span
    out = jax.ShapeDtypeStruct((length, 3 * pairs * TILE), BF16)
    scale = head_size ** (-0.5)

    def whole(array):
        return pl.BlockSpec(array.shape, lambda i, info: (0, 0), pipeline_mode=pl.Buffered(1))

    return pl.pallas_call(
        functools.partial(attend_back_kernel, part * pairs, pairs, width, per, scale),
        name="attend_back",
        out_shape=out,
        grid_spec=pltpu.PrefetchScalarGridSpec(
            num_scalar_prefetch=1,
            grid=(tiles,),
            in_specs=[whole(qkv), whole(mixed), whole(grad), whole(seg), whole(log_sum)],
            out_specs=pl.BlockSpec(out.shape, lambda i, info: (0, 0)),
            scratch_shapes=[
                pltpu.VMEM((chunks, span, pairs * TILE), F32),
                pltpu.VMEM((chunks, span, pairs * TILE), F32),
                pltpu.VMEM((chunks, pairs, TILE, span), BF16),
                pltpu.VMEM((chunks, span, TILE), F32),
            ],
        ),
        compiler_params=pltpu.CompilerParams(
            dimension_semantics=("arbitrary",), vmem_limit_bytes=28 << 20
        ),
        cost_estimate=pl.CostEstimate(
            flops=32 * length * length * width, bytes_accessed=8 * length * width * 2, transcendentals=0
        ),
    )(info, qkv, mixed, grad, seg, log_sum)


SWAP = [(0, 1), (1, 0)]


def swap_core(array):
    return lax.ppermute(array, "sc", SWAP)


def swap_chip(array):
    return lax.ppermute(array, "sy", SWAP)


def swap_bit(array, bit):
    if bit == 0:
        return swap_chip(array)
    count = lax.axis_size("img")
    return lax.ppermute(array, "img", [(i, i ^ (1 << (bit - 1))) for i in range(count)])


def own_bit(bit):
    if bit == 0:
        return lax.axis_index("sy")
    return (lax.axis_index("img") >> (bit - 1)) & 1


def fence(*values):
    return lax.optimization_barrier(values)


def axis_of(bit, done):
    return sum(1 for other in done if other > bit)


def pick(index, low, high):
    return jnp.where(index == 0, low, high)


def far_bits():
    return list(range(2, int(math.log2(lax.axis_size("img"))) + 1))


def join(first, second, axis):
    shape = list(first.shape)
    shape[axis] += second.shape[axis]
    held = lax.dynamic_update_slice_in_dim(jnp.zeros(shape, first.dtype), first, 0, axis)
    return lax.dynamic_update_slice_in_dim(held, second, first.shape[axis], axis)


class Turn:
    def __init__(self):
        self.arrays, self.shapes, self.jobs = [], [], []
        self.kept = None

    def keep(self, rows, columns):
        if self.kept is None:
            self.kept = self.write((0, columns), BF16)
        before = self.shapes[self.kept].shape[0]
        self.shapes[self.kept] = jax.ShapeDtypeStruct((before + rows, columns), BF16)
        return self.kept, before

    def read(self, array):
        for i, other in enumerate(self.arrays):
            if other is array:
                return i
        self.arrays.append(array)
        return len(self.arrays) - 1

    def write(self, shape, dtype):
        self.shapes.append(jax.ShapeDtypeStruct(shape, dtype))
        return len(self.shapes) - 1

    def run(self, bits):
        count = len(self.arrays)

        def kernel(own, *refs):
            mine = [own[i] for i in range(bits.shape[0])]
            for job in self.jobs:
                job(mine, refs[:count], refs[count:])

        spent = sum(a.size * jnp.dtype(a.dtype).itemsize for a in [*self.arrays, *self.shapes])
        return pl.pallas_call(
            kernel,
            name="turn",
            out_shape=tuple(self.shapes),
            in_specs=[pl.BlockSpec(memory_space=pltpu.SMEM)] + [pl.BlockSpec(memory_space=pltpu.VMEM)] * count,
            out_specs=tuple(pl.BlockSpec(memory_space=pltpu.VMEM) for _ in self.shapes),
            compiler_params=pltpu.CompilerParams(vmem_limit_bytes=spent + (2 << 20)),
            cost_estimate=pl.CostEstimate(flops=0, bytes_accessed=0, transcendentals=0),
        )(bits, *self.arrays)


def combinations(bits):
    made = [{}]
    for bit in bits:
        made = [{**choice, bit: value} for choice in made for value in (0, 1)]
    return made


def flat_index(choice, bits):
    at = 0
    for bit in sorted(bits, reverse=True):
        at = at * 2 + choice[bit]
    return at


def block_of(at, rows, base=0):
    start = at * rows + base
    if isinstance(start, int):
        return pl.ds(start, rows)
    return pl.ds(pl.multiple_of(start, math.gcd(rows, base) if base else rows), rows)


class Piece:
    def __init__(self, array, rows, bits, order, stride=None, base=0):
        self.held, self.rows, self.bits = (array, base), rows, list(bits)
        self.fixed, self.order, self.came = [], list(order), None
        self.stride, self.source = stride or rows, bool(bits)


class Gather:
    def __init__(self, *parts):
        self.pieces = []
        for array, first, rows, order in parts:
            piece = Piece(array, rows, [], order)
            piece.held = (array, first)
            self.pieces.append(piece)

    def wants(self):
        return [(p.order[0], p.rows << (len(p.bits) + (p.came is not None))) for p in self.pieces]

    def turn(self, turn, places):
        for p, (out, base) in zip(self.pieces, places):
            if p.came is None:
                turn.jobs.append(copy_rows(turn.read(p.held[0]), p.held[1], out, base, p.rows << len(p.bits)))
            else:
                bit = p.sent
                absorb_gather(turn, p, bit, lambda choice, p=p, out=out, base=base: [(out, choice, base)])
            p.sent = p.order.pop(0)
            p.next_held = (out, base)

    def settle(self, outs, came):
        for p, where in zip(self.pieces, came):
            if p.came is not None:
                p.bits.append(p.last)
            p.held, p.came, p.last = (outs[p.next_held[0]], p.next_held[1]), where, p.sent

    def arrays(self):
        return [a for p in self.pieces for a in ([p.held[0]] + ([p.came[0]] if p.came else []))]

    def relabel(self, swap):
        for p in self.pieces:
            p.held = (swap(p.held[0]), p.held[1])
            if p.came:
                p.came = (swap(p.came[0]), p.came[1])

    def left(self):
        return len(self.pieces[0].order)


def gathered(pieces, bits, outs):
    turn = Turn()
    made = [turn.write(shape, BF16) for shape, _ in outs]
    for i, p in enumerate(pieces):
        held, came = turn.read(p.held[0]), turn.read(p.came[0])
        moves = [(out, move) for out, (_, moves) in zip(made, outs) for move in moves[i]]

        def job(mine, ins, refs, p=p, held=held, came=came, moves=moves):
            everyone = [*p.bits, p.last]
            for choice in combinations(p.bits):
                at = flat_index(choice, p.bits)
                for source, base, value in (
                    (ins[held], p.held[1], mine[p.last]),
                    (ins[came], p.came[1], 1 - mine[p.last]),
                ):
                    chip = flat_index({**choice, p.last: value}, everyone)
                    for out, ((low, high), (left, right), stride, row, column) in moves:
                        start = pl.multiple_of(chip * stride + row, math.gcd(stride, row) if row else stride)
                        refs[out][pl.ds(start, high - low), column : column + right - left] = source[
                            pl.ds(base + at * p.rows + low, high - low), left:right
                        ]

        turn.jobs.append(job)
    return turn.run(bits)


class Spread:
    def __init__(self, array):
        self.pieces = [Piece(array, array.shape[0], [], [*reversed(far_bits()), 0, 1])]

    def wants(self):
        return [(self.pieces[0].order[0], self.pieces[0].rows)]

    def turn(self, turn, places):
        [p], [(out, base)] = self.pieces, places
        p.order.pop(0)
        p.next_held = (out, base)
        if p.came is None:
            turn.jobs.append(copy_rows(turn.read(p.held[0]), p.held[1], out, base, p.rows))
            return
        held, came, held_base, came_base, rows = turn.read(p.held[0]), turn.read(p.came[0]), p.held[1], p.came[1], p.rows

        def job(mine, ins, refs):
            refs[out][base : base + rows] = (
                ins[held][held_base : held_base + rows] + ins[came][came_base : came_base + rows]
            )

        turn.jobs.append(job)

    def settle(self, outs, came):
        [p] = self.pieces
        p.held, p.came = (outs[p.next_held[0]], p.next_held[1]), came[0]

    arrays, relabel, left = Gather.arrays, Gather.relabel, Gather.left

    def result(self):
        [p] = self.pieces
        return sum(array[base : base + p.rows] for array, base in (p.held, p.came))


class Rider:
    def __init__(self, array, bit, first, rows):
        self.pieces = [Piece(array, rows, [], [bit])]
        self.pieces[0].held = (array, first)

    wants, turn, settle = Spread.wants, Spread.turn, Spread.settle
    arrays, relabel, left = Gather.arrays, Gather.relabel, Gather.left

    def result(self):
        [p] = self.pieces
        return p.came[0][p.came[1] : p.came[1] + p.rows]


class Total:
    def __init__(self, array, order):
        self.pieces = [Piece(array, array.shape[0], [], order)]

    wants, arrays, relabel, left = Spread.wants, Gather.arrays, Gather.relabel, Gather.left

    def turn(self, turn, places):
        [p], [(out, base)] = self.pieces, places
        p.order.pop(0)
        held, rows = turn.read(p.held[0]), p.rows
        came, came_base = (None, 0) if p.came is None else (turn.read(p.came[0]), p.came[1])
        p.next = None if came is None else turn.write(p.held[0].shape, F32)

        def job(mine, ins, refs, keep=p.next):
            own = ins[held][...].astype(BF16)
            if came is not None:
                total = own.astype(F32) + ins[came][came_base : came_base + rows].astype(F32)
                refs[keep][...] = total
                own = total.astype(BF16)
            refs[out][base : base + rows] = own

        turn.jobs.append(job)

    def settle(self, outs, came):
        [p] = self.pieces
        if p.next is not None:
            p.held = (outs[p.next], 0)
        p.came = came[0]

    def result(self):
        [p] = self.pieces
        return add_came(p.held[0], p.came[0][p.came[1] : p.came[1] + p.rows])


def copy_rows(source, source_base, out, base, rows):
    def job(mine, ins, refs):
        refs[out][base : base + rows] = ins[source][source_base : source_base + rows]

    return job


def absorb_gather(turn, p, bit, targets):
    held, came = turn.read(p.held[0]), turn.read(p.came[0])
    last = p.last
    known = list(p.bits)
    held_base, came_base, rows = p.held[1], p.came[1], p.rows
    [(out, _, base)] = targets(None)

    def job(mine, ins, refs):
        for choice in combinations(known):
            at = flat_index(choice, known)
            for source, start, value in ((held, held_base, mine[last]), (came, came_base, 1 - mine[last])):
                to = flat_index({**choice, last: value}, [*known, last])
                refs[out][block_of(to, rows, base)] = ins[source][block_of(at, rows, start)]

    turn.jobs.append(job)


class Scatter:
    def __init__(self, *parts):
        far = far_bits()
        bits = sorted([0, 1, *far], reverse=True)
        self.pieces = [
            Piece(array, rows, bits, [*((1, 0) if turned else (0, 1)), *far], stride, first)
            for array, rows, stride, first, turned in parts
        ]

    def wants(self):
        return [(p.order[0], p.rows << (len(p.bits) - len(p.fixed) - 1)) for p in self.pieces]

    def turn(self, turn, places):
        for p, (out, base) in zip(self.pieces, places):
            bit = p.order.pop(0)
            free = [b for b in p.bits if b not in p.fixed and b != bit]
            rows, bits, fixed = p.rows, list(p.bits), list(p.fixed)
            held = turn.read(p.held[0])
            stride, first = p.stride, p.held[1]

            def block(choice, bits=bits, stride=stride, first=first, rows=rows):
                start = flat_index(choice, bits) * stride + first
                return pl.ds(pl.multiple_of(start, math.gcd(stride, first) if first else stride), rows)

            if p.came is None:
                p.next = None

                def job(mine, ins, refs, held=held, rows=rows, free=free, bit=bit, out=out, base=base, block=block):
                    for choice in combinations(free):
                        refs[out][block_of(flat_index(choice, free), rows, base)] = ins[held][
                            block({**choice, bit: 1 - mine[bit]})
                        ]

            else:
                came, came_base = turn.read(p.came[0]), p.came[1]
                keep, keep_base = turn.keep(rows << len(free), p.held[0].shape[1])
                p.next = (keep, keep_base)

                def job(
                    mine, ins, refs, held=held, rows=rows, fixed=fixed, free=free, bit=bit, out=out, base=base,
                    came=came, came_base=came_base, keep=keep, keep_base=keep_base, block=block,
                ):
                    settled = {b: mine[b] for b in fixed}
                    for choice in combinations(free):
                        for value, target, start in ((1 - mine[bit], out, base), (mine[bit], keep, keep_base)):
                            now = {**choice, bit: value}
                            total = ins[held][block({**now, **settled})].astype(F32) + ins[came][
                                block_of(flat_index(now, [*free, bit]), rows, came_base)
                            ].astype(F32)
                            refs[target][block_of(flat_index(choice, free), rows, start)] = total.astype(BF16)

            turn.jobs.append(job)
            p.sent, p.free = bit, free

    def settle(self, outs, came):
        for p, where in zip(self.pieces, came):
            if p.next is None:
                p.fixed = [p.sent]
            else:
                p.held, p.bits, p.fixed = (outs[p.next[0]], p.next[1]), list(p.free), []
                p.stride, p.source = p.rows, False
            p.came = where

    arrays, relabel, left = Gather.arrays, Gather.relabel, Gather.left

    def result(self, bits):
        turn = Turn()
        for p in self.pieces:
            held, came, base, rows, first = turn.read(p.held[0]), turn.read(p.came[0]), p.came[1], p.rows, p.held[1]
            out = turn.write((rows, p.held[0].shape[1]), F32)

            def job(mine, ins, refs, held=held, came=came, base=base, rows=rows, out=out, first=first):
                refs[out][...] = ins[held][first : first + rows].astype(F32) + ins[came][base : base + rows].astype(F32)

            turn.jobs.append(job)
        return turn.run(bits)


def swap_rows(moves, bits):
    wants = [move.wants() for move in moves]
    sizes, places = {}, []
    for bit, rows in (want for group in wants for want in group):
        places.append((bit, sizes.get(bit, 0)))
        sizes[bit] = sizes.get(bit, 0) + rows
    turn = Turn()
    width = moves[0].pieces[0].held[0].shape[1]
    outs = {bit: turn.write((rows, width), BF16) for bit, rows in sizes.items()}
    located = [(outs[bit], base) for bit, base in places]
    starts = [0]
    for move in moves:
        starts.append(starts[-1] + len(move.pieces))
    for i, move in enumerate(moves):
        move.turn(turn, located[starts[i] : starts[i + 1]])
    made = turn.run(bits)
    got = {bit: swap_bit(made[out], bit) for bit, out in outs.items()}
    came = [(got[bit], base) for bit, base in places]
    for i, move in enumerate(moves):
        move.settle(made, came[starts[i] : starts[i + 1]])


def add_came(own, came):
    return own.astype(BF16).astype(F32) + came.astype(F32)


def add_hop(array, bit):
    return add_came(array, swap_bit(array.astype(BF16), bit))


def phase(bits, moves, work, *values, also=()):
    chains = [move if isinstance(move, tuple) else (move, 1) for move in moves]
    chains = [
        ([move for move in chain[:-1] if move.left()], min(chain[-1], chain[0].left())) for chain in chains
    ]
    moves = [move for chain, _ in chains for move in chain]

    def tie(extra):
        arrays = []
        for array in (a for move in [*moves, *also] for a in move.arrays()):
            if not any(array is other for other in arrays):
                arrays.append(array)
        held, extra = fence(arrays, extra)
        table = list(zip(arrays, held))
        for move in [*moves, *also]:
            move.relabel(lambda array: next(new for old, new in table if old is array))
        return extra

    values = tie(values)
    if moves:
        swap_rows(moves, bits)
    for chain, count in chains:
        for _ in range(count - 1):
            swap_rows(chain, bits)
    made = work(*values) if work else ()
    return tie(made)


def by_rows(body, rows, whole, outs, sums=0, tile=TILE, name="rows"):
    rows = [array if isinstance(array, tuple) else (array, 0, array.shape[0]) for array in rows]
    length = rows[0][2]
    width = outs[0][0]

    def kernel(*refs):
        ins, results = refs[: len(rows) + len(whole)], refs[len(rows) + len(whole) :]
        made = body(*(ref[...] for ref in ins))
        for ref, value in zip(results, made):
            if ref.shape[0] == 1:

                @pl.when(pl.program_id(0) == 0)
                def _(ref=ref):
                    ref[...] = jnp.zeros_like(ref)

                ref[...] += value
            else:
                ref[...] = value.astype(ref.dtype)

    spent = sum(array.size * array.dtype.itemsize for array in whole)
    for columns, kind in [*outs, *((array.shape[1], array.dtype) for array, _, _ in rows)]:
        spent += 2 * tile * columns * jnp.dtype(kind).itemsize

    def steps(columns, first=0):
        return pl.BlockSpec((tile, columns), lambda i: (i + first // tile, 0))

    def fixed(shape, **how):
        return pl.BlockSpec(shape, lambda i: (0,) * len(shape), **how)

    return pl.pallas_call(
        kernel,
        name=name,
        grid=(length // tile,),
        out_shape=[jax.ShapeDtypeStruct((length, columns), dtype) for columns, dtype in outs]
        + [jax.ShapeDtypeStruct((1, width), F32)] * sums,
        in_specs=[steps(array.shape[1], first) for array, first, _ in rows]
        + [fixed(array.shape, pipeline_mode=pl.Buffered(1)) for array in whole],
        out_specs=[steps(columns) for columns, _ in outs] + [fixed((1, width))] * sums,
        compiler_params=pltpu.CompilerParams(
            dimension_semantics=("arbitrary",), vmem_limit_bytes=spent + (12 << 20)
        ),
        cost_estimate=pl.CostEstimate(flops=0, bytes_accessed=0, transcendentals=0),
    )(*(array for array, _, _ in rows), *whole)


def normalize(stream):
    center = jnp.mean(stream, axis=-1, keepdims=True)
    centered = stream - center
    spread = jnp.mean(centered * centered, axis=-1, keepdims=True)
    inverse = lax.rsqrt(spread + EPS)
    return centered * inverse, inverse


def normalize_back(normed, inverse, gain, grad):
    scaled = grad * gain
    middle = jnp.mean(scaled, axis=-1, keepdims=True)
    along = jnp.mean(scaled * normed, axis=-1, keepdims=True)
    return (
        inverse[:, :1] * (scaled - middle - normed * along),
        jnp.sum(grad * normed, axis=0, keepdims=True),
        jnp.sum(grad, axis=0, keepdims=True),
    )


def rows_from(columns, count):
    one_hot = (jnp.arange(16)[:, None] == jnp.arange(TILE)[None, :]).astype(BF16)
    rows = nt(one_hot, columns)
    return [rows[i : i + 1] for i in range(count)]


def column_choice(rows, columns):
    row, lane = jnp.arange(rows)[:, None], jnp.arange(TILE)[None, :]
    return (row == 8 + lane % columns).astype(F32)


def own_place(width, columns):
    per_run = TILE // columns
    row, lane = jnp.arange(width)[:, None], jnp.arange(TILE)[None, :]
    return row % per_run == lane // columns


def unroll_bias(columns, own_c, ff_rows):
    width, extra = columns.shape[0], 4
    spread = nn(columns, column_choice(TILE, extra).astype(BF16))
    runs = jnp.where(own_place(width, extra), spread, 0.0).reshape(-1, TILE // extra, TILE).sum(axis=1)
    runs = runs.reshape(-1, 2, ff_rows)
    return pick(own_c, runs[:, 0], runs[:, 1]).reshape(1, -1)


def roll_bias(sums, own_c, width, rows, ff_rows):
    extra = 4
    runs = sums.reshape(-1, ff_rows)
    zero = jnp.zeros_like(runs)
    runs = jnp.stack([pick(own_c, runs, zero), pick(own_c, zero, runs)], axis=1).reshape(-1, 1, TILE)
    spread = jnp.broadcast_to(runs, (runs.shape[0], TILE // extra, TILE)).reshape(width, TILE)
    spread = jnp.where(own_place(width, extra), spread, 0.0)
    return lax.dot_general(
        column_choice(rows, extra), spread, (((1,), (1,)), ((), ())), precision=PRECISE, preferred_element_type=F32
    )


def token_sums(array):
    return nn(jnp.ones((8, array.shape[0]), BF16), array)[:1]


def gelu_and_slope(values):
    cdf = 0.5 * (1.0 + lax.erf(values * (0.5**0.5)))
    density = jnp.exp(-0.5 * values * values) * (1.0 / math.sqrt(2.0 * math.pi))
    return values * cdf, cdf + values * density


def adam_update(weight, gradient, first_moment, second_moment, factor, decay):
    scaled = gradient * factor
    first_new = 0.9 * first_moment + 0.1 * scaled
    second_new = 0.999 * second_moment + 0.001 * scaled * scaled
    first_hat = first_new / FIRST_CORRECTION
    second_hat = second_new / SECOND_CORRECTION
    direction = first_hat / (jnp.sqrt(second_hat) + 1e-08) + decay * weight
    return (direction, first_new, second_new)


def per_device(
    patches,
    cotangent,
    res_ids,
    pos_table,
    attn_in,
    attn_out,
    mlp_in,
    mlp_out,
    vectors,
    first_attn_in,
    first_attn_out,
    first_mlp_in,
    first_mlp_out,
    first_vectors,
    second_attn_in,
    second_attn_out,
    second_mlp_in,
    second_mlp_out,
    second_vectors,
):
    row_count, local_len, width = patches.shape
    img_count, halves = lax.axis_size("img"), lax.axis_size("sy")
    chips = img_count * halves
    row_len = local_len * halves * 2
    slot_total = row_count * img_count * row_len
    head_size = width // HEADS
    own_y, own_c = lax.axis_index("sy"), lax.axis_index("sc")
    rows = attn_in.shape[0]
    half = width // 2
    ff_rows = mlp_out.shape[0]
    ff_half = chips * ff_rows
    table_size = GRID * GRID
    vector_count = vectors.shape[1]

    bits = jnp.stack([own_bit(bit) for bit in [0, 1, *far_bits()]]).astype(jnp.int32)

    def to_rows(array):
        mine = lax.dynamic_index_in_dim(array, own_y, 0, keepdims=False)
        other = lax.dynamic_index_in_dim(array, 1 - own_y, 0, keepdims=False)
        return join(mine, swap_chip(other), 0)

    res_row = pick(own_y, res_ids[0], res_ids[1])
    all_positions = jnp.arange(row_len, dtype=jnp.int32)
    segment_all, _, _, _ = layout(res_row, all_positions)
    seg = jnp.broadcast_to(segment_all.astype(F32)[None, :], (8, row_len))
    begin, end = key_bounds(res_row, row_len)
    info = jnp.concatenate([jnp.stack([own_y, own_c]).astype(jnp.int32), begin, end])
    near = jnp.arange(local_len, dtype=jnp.int32)
    positions = jnp.concatenate(
        [(2 * own_y + own_c) * local_len + near, (2 * (1 - own_y) + own_c) * local_len + near]
    )
    _, side_of, patch_index, usable = layout(res_row, positions)
    place = table_weights(side_of, patch_index, usable)
    usable = usable.astype(F32)[:, None]

    def by_core(array, blocks):
        split = array.reshape(rows, blocks, 2, -1)
        low, high = split[:, :, 0].reshape(rows, -1), split[:, :, 1].reshape(rows, -1)
        return pick(own_c, low, high), pick(own_c, high, low)

    vector_pad = jnp.pad(vectors, ((0, 0), (0, TILE - vector_count))).astype(BF16)
    mine_in, away_in = by_core(attn_in.astype(BF16), 3)
    mine_out, away_out = by_core(attn_out.astype(BF16), 1)
    mine_up, away_up = by_core(mlp_in.astype(BF16), chips)
    mine = jnp.concatenate([mine_in, mine_out, mine_up], axis=1)
    away = jnp.concatenate([away_in, away_out, away_up], axis=1)
    came, came_vector = swap_core(away), swap_core(vector_pad)
    shard = jnp.concatenate([pick(own_c, mine, came), pick(own_c, came, mine)], axis=0)
    vector_shard = jnp.concatenate(
        [pick(own_c, vector_pad, came_vector), pick(own_c, came_vector, vector_pad)], axis=0
    )[:, :16].reshape(1, -1)
    vector_row = jnp.pad(vector_shard, ((0, 0), (0, width - vector_shard.shape[1])))
    chip = lax.axis_index("img") * halves + own_y
    vector_rows = jnp.where(jnp.arange(chips)[:, None] == chip, vector_row, jnp.zeros_like(vector_row))
    in_width = 3 * half
    own = local_len * row_count
    per = local_len // TILE

    def with_core(array):
        return join(array, swap_core(array), 0)

    def sum_core(left, weights, product):
        away = product(left[own:], weights).astype(BF16)
        came = swap_core(away)
        return product(left[:own], weights) + came.astype(F32)

    low_down, high_down = jnp.split(mlp_out.astype(BF16), 2)
    ahead = list(reversed(far_bits()))
    one_way, other_way = [*ahead, 1, 0], [*ahead, 0, 1]
    block = 2 * rows
    gather_in = Gather(
        (shard[:, :width], 0, block, one_way), (shard[:, width : 2 * width], 0, block, other_way)
    )
    gather_vectors = Spread(vector_rows)
    gather_up = Gather(
        (shard[:, 2 * width : 2 * width + half * 2], 0, block, one_way),
        (shard[:, 2 * width + half * 2 :], 0, block, other_way),
    )
    low_down = mlp_out.astype(BF16)
    side = 3 * ff_rows // 8 if ff_rows % 128 == 0 else ff_rows // 2
    rest_rows = ff_rows - 2 * side
    gather_down = Gather((low_down, 0, side, one_way), (low_down, side, side, other_way))
    gather_rest = [Gather((low_down, 2 * side, rest_rows, [1, 0, *ahead]))] if rest_rows else []

    patches, cotangent = phase(
        bits,
        [(gather_in, gather_vectors, len(far_bits()))],
        lambda *arrays: [to_rows(array) for array in arrays],
        patches,
        cotangent,
    )

    wide_place = jnp.pad(place, ((0, 0), (0, TILE - table_size)))
    wide_table = jnp.pad(pos_table, ((0, TILE - table_size), (0, 0)))
    wide_usable = jnp.broadcast_to(usable, (own, TILE))
    small = TILE

    def first(patches, cotangent):
        def body(patches, place, cotangent, usable, table):
            stream = patches.astype(F32) + jnp.dot(place, table, precision=PRECISE, preferred_element_type=F32)
            normed, inverse = normalize(stream)
            grad = cotangent.astype(F32) * usable[:, :1]
            return stream, normed, jnp.broadcast_to(inverse, (stream.shape[0], TILE)), grad

        stream, hat_one, inverse_one, grad_own = by_rows(
            body,
            [patches, wide_place, cotangent, wide_usable],
            [wide_table],
            [(width, F32), (width, F32), (TILE, F32), (width, BF16)],
            name="first",
        )
        return stream, hat_one, inverse_one, grad_own

    far = far_bits()
    stream, hat_one, inverse_one, grad_own = phase(
        bits, [gather_in, gather_vectors, gather_up, *gather_rest], first, patches, cotangent
    )
    phase(bits, [gather_in, gather_vectors, (gather_up, len(far) - 1), gather_down], None)
    spare = in_width - width
    in_matrix, out_columns = gathered(
        gather_in.pieces,
        bits,
        [
            (
                (width, in_width),
                ([((0, block), (0, width), block, 0, 0)], [((0, block), (0, spare), block, 0, width)]),
            ),
            ((width, width - spare), ([], [((0, block), (spare, width), block, 0, 0)])),
        ],
    )
    vector_part = jnp.pad(
        gather_vectors.result()[:, : block * 16].reshape(-1, 16), ((0, 0), (0, TILE - 16))
    )
    gain_one, shift_one, bias_query, bias_value, bias_out, gain_two, shift_two, bias_down = (
        rows_from(vector_part, 8)
    )
    bias_query = pick(own_c, bias_query[:, :half], bias_query[:, half:])
    bias_value = pick(own_c, bias_value[:, :half], bias_value[:, half:])
    bias_up = unroll_bias(vector_part, own_c, ff_rows)
    bias_qkv = jnp.concatenate([bias_query, jnp.zeros_like(bias_query), bias_value], axis=1)

    def project(hat_one, out_columns):
        low, high = out_columns[:half], out_columns[half:]
        keep_out, came_out = pick(own_c, low, high), swap_core(pick(own_c, high, low))
        out_matrix = join(pick(own_c, keep_out, came_out), pick(own_c, came_out, keep_out), 1)
        return out_matrix, (hat_one * gain_one + shift_one).astype(BF16)

    out_matrix, normed_one = phase(
        bits, [gather_up, (gather_down, len(far) - 1), *gather_rest], project, hat_one, out_columns
    )

    def matmul_rows(left, right, product, name):
        return product(left[own:], right).astype(BF16)

    def attend(normed_one, in_matrix, out_matrix, grad_own):
        normed_one = with_core(normed_one)
        qkv = (nn(normed_one, in_matrix) + bias_qkv).astype(BF16)
        mixed, log_sum = attention(qkv, seg, info, per, head_size)
        away = matmul_rows(mixed, out_matrix, nn, "out_away")
        return normed_one, qkv, mixed, log_sum, away, with_core(grad_own)

    normed_one, qkv, mixed, log_sum, out_away, grad_last = phase(
        bits, [gather_up, *gather_rest], attend, normed_one, in_matrix, out_matrix, grad_own
    )

    def project_out(stream, mixed, out_away, out_matrix):
        def body(stream, mixed, came, matrix, bias, gain, shift):
            stream_two = stream + nn(mixed, matrix) + came.astype(F32) + bias
            normed, inverse = normalize(stream_two)
            return stream_two, normed, jnp.broadcast_to(inverse, (stream.shape[0], TILE)), normed * gain + shift

        return by_rows(
            body,
            [(stream, 0, own), mixed, swap_core(out_away)],
            [out_matrix, bias_out, gain_two, shift_two],
            [(width, F32), (width, F32), (TILE, F32), (width, BF16)],
            name="out_norm",
            tile=own // 2,
        )

    stream_two, hat_two, inverse_two, normed_two = phase(
        bits, [gather_down], project_out, stream, mixed, out_away, out_matrix
    )
    (up_matrix,) = gathered(
        gather_up.pieces,
        bits,
        [
            (
                (width, ff_half),
                ([((0, block), (0, width), block, 0, 0)], [((0, block), (0, width), block, 0, width)]),
            )
        ],
    )

    def expand(normed_two, up_matrix, grad_last):
        normed_two = with_core(normed_two)
        hidden_pre = nn(normed_two, up_matrix) + bias_up
        hidden, slope = gelu_and_slope(hidden_pre)
        hidden = hidden.astype(BF16)
        return normed_two, hidden, slope, tn(hidden, grad_last).astype(BF16)

    normed_two, hidden, slope, grad_down = phase(
        bits, [gather_down, *((move, 9) for move in gather_rest)], expand, normed_two, up_matrix, grad_last
    )
    part_rows = ff_rows // 2
    down_pieces = [piece for move in [gather_down, *gather_rest] for piece in move.pieces]
    (down_matrix,) = gathered(
        down_pieces,
        bits,
        [
            (
                (ff_half, width),
                [[((0, piece.rows), (0, width), ff_rows, i * side, 0)] for i, piece in enumerate(down_pieces)],
            )
        ],
    )

    scatter_down = Scatter(
        (grad_down, part_rows, ff_rows, 0, False), (grad_down, part_rows, ff_rows, part_rows, True)
    )

    def hidden_back(grad_last, down_matrix, slope, normed_two, up_matrix):
        grad_pre = (nt(grad_last, down_matrix) * slope).astype(BF16)
        return (
            grad_pre,
            matmul_rows(grad_pre, up_matrix, nt, "norm_two_away"),
            tn(normed_two, grad_pre[:, :width]).astype(BF16),
            tn(normed_two, grad_pre[:, width:]).astype(BF16),
        )

    grad_pre, two_away, *grad_up = phase(
        bits, [scatter_down], hidden_back, grad_last, down_matrix, slope, normed_two, up_matrix
    )
    scatter_up = Scatter((grad_up[0], block, block, 0, False), (grad_up[1], block, block, 0, True))

    def norm_back(grad, away, matrix, hat, inverse, added, gain, name):
        def body(grad, came, hat, inverse, added, matrix, gain):
            back, gain_sum, shift_sum = normalize_back(hat, inverse, gain, nt(grad, matrix) + came.astype(F32))
            total = added.astype(F32) + back
            return total, total, gain_sum, shift_sum

        return by_rows(
            body,
            [(grad, 0, own), swap_core(away), hat, inverse, added],
            [matrix, gain],
            [(width, F32), (width, BF16)],
            sums=2,
            name=name,
            tile=own // 2,
        )

    def middle(values, hidden, down_matrix):
        return norm_back(*values, "norm_two_back"), matmul_rows(hidden, down_matrix, nn, "output_away")

    (grad_two, grad_branch, grad_gain_two, grad_shift_two), output_away = phase(
        bits,
        [scatter_down],
        middle,
        (grad_pre, two_away, up_matrix, hat_two, inverse_two, grad_own, gain_two),
        hidden,
        down_matrix,
    )

    paired = block % 64 == 0

    def pair(array):
        blocks = array.reshape(chips, 2, -1, array.shape[1])
        return jnp.concatenate([blocks[:, 0], blocks[:, 1]], axis=2).reshape(-1, 2 * array.shape[1])

    def part(array):
        columns = array.shape[1] // 2
        return jnp.concatenate([array[:, :columns], array[:, columns:]], axis=0)

    def attention_grads(grad_branch, out_matrix, qkv, mixed, log_sum, output_away):
        grad_branch = with_core(grad_branch)
        grad_mixed = nt(grad_branch, out_matrix).astype(BF16)
        grad_qkv = attention_back(0, 1, qkv, mixed, grad_mixed, seg, log_sum, info, per, head_size)
        grad_rows = tn(mixed, grad_branch).astype(BF16)
        low, high = grad_rows[:, :half], grad_rows[:, half:]
        keep_rows, came_rows = pick(own_c, low, high), swap_core(pick(own_c, high, low))
        grad_out = join(pick(own_c, keep_rows, came_rows), pick(own_c, came_rows, keep_rows), 0)
        return grad_branch, swap_core(output_away), grad_qkv, pair(grad_out) if paired else grad_out

    grad_branch, came_output, grad_qkv, grad_out = phase(
        bits,
        [scatter_up, scatter_down],
        attention_grads,
        grad_branch,
        out_matrix,
        qkv,
        mixed,
        log_sum,
        output_away,
    )
    quarter = block // 4
    scatter_out = []
    if paired:
        scatter_out = [
            Scatter(
                (grad_out, quarter, 2 * quarter, 0, False), (grad_out, quarter, 2 * quarter, quarter, True)
            )
        ]

    def in_grads(normed_one, grad_qkv, in_matrix):
        right = tn(normed_one, grad_qkv[:, width:]).astype(BF16)
        return (
            matmul_rows(grad_qkv, in_matrix, nt, "norm_one_away"),
            tn(normed_one, grad_qkv[:, :width]).astype(BF16),
            pair(right) if paired else right,
        )

    one_away, left, right = phase(
        bits, [scatter_up, *scatter_out, scatter_down], in_grads, normed_one, grad_qkv, in_matrix
    )
    if paired:
        scatter_in = Scatter(
            (left, 3 * quarter, block, 0, False),
            (left, quarter, block, 3 * quarter, True),
            (right, 2 * quarter, 2 * quarter, 0, True),
        )
    else:
        scatter_in = Scatter((left, block, block, 0, False), (join(right, grad_out, 1), block, block, 0, True))

    def widen(row):
        zero = jnp.zeros_like(row)
        return jnp.concatenate([pick(own_c, row, zero), pick(own_c, zero, row)], axis=1)

    narrow_rows = vector_count + table_size
    narrow_rows += -narrow_rows % 16

    def norm_one_back(grad_qkv, one_away, in_matrix, hat_one, inverse_one, grad_two, grad_pre, grad_branch, grad_last):
        grad_stream, grad_low, grad_gain_one, grad_shift_one = norm_back(
            grad_qkv, one_away, in_matrix, hat_one, inverse_one, grad_two, gain_one, "norm_one_back"
        )
        wide_place = jnp.pad(place, ((0, 0), (vector_count, narrow_rows - vector_count - table_size)))
        table_part = lax.dot_general(
            wide_place, grad_stream, (((0,), (0,)), ((), ())), precision=PRECISE, preferred_element_type=F32
        )
        bias_part = roll_bias(token_sums(grad_pre), own_c, width, narrow_rows, ff_rows)
        sums = token_sums(grad_qkv)
        rows_of_sums = [
            grad_gain_one,
            grad_shift_one,
            widen(sums[:, :half]),
            widen(sums[:, 2 * half :]),
            token_sums(grad_branch[:own]),
            grad_gain_two,
            grad_shift_two,
            token_sums(grad_last[:own]),
        ]

        def stack(*refs):
            refs[-1][...] = refs[0][...] + refs[1][...]
            for i in range(len(rows_of_sums)):
                refs[-1][i : i + 1] = refs[2 + i][...]

        narrow = pl.pallas_call(
            stack,
            name="narrow",
            out_shape=jax.ShapeDtypeStruct((narrow_rows, width), F32),
            compiler_params=pltpu.CompilerParams(vmem_limit_bytes=4 << 20),
            cost_estimate=pl.CostEstimate(flops=0, bytes_accessed=0, transcendentals=0),
        )(table_part, bias_part, *rows_of_sums)
        return grad_low, add_came(narrow, swap_core(narrow.astype(BF16)))

    def finish_output(hidden, came, stream_two, down_matrix):
        def body(hidden, came, stream_two, usable, matrix, bias):
            return ((stream_two + nn(hidden, matrix) + came.astype(F32) + bias) * usable[:, :1],)

        return by_rows(
            body,
            [(hidden, 0, own), came, stream_two, wide_usable],
            [down_matrix, bias_down],
            [(width, BF16)],
            name="output",
            tile=own // 2,
        )

    (grad_low, narrow), (output,) = phase(
        bits,
        [scatter_in, *scatter_out, scatter_up, (scatter_down, len(far) - 1)],
        lambda values, others: (norm_one_back(*values), finish_output(*others)),
        (grad_qkv, one_away, in_matrix, hat_one, inverse_one, grad_two, grad_pre, grad_branch, grad_last),
        (hidden, came_output, stream_two, down_matrix),
    )

    def rows_of(array, core):
        return lax.dynamic_slice_in_dim(array, core * rows, rows, 0)

    def trade(array, blocks):
        away, keep = rows_of(array, 1 - own_c), rows_of(array, own_c)
        came = swap_core(away).reshape(rows, blocks, -1)
        keep = keep.reshape(rows, blocks, -1)
        both = jnp.stack([pick(own_c, keep, came), pick(own_c, came, keep)], axis=2)
        return both.reshape(rows, -1)

    factor = 1.0 / slot_total

    def adam(weight, gradient, first_moment, second_moment):
        return by_rows(
            lambda w, g, m, v: adam_update(w, g, m, v, factor, 0.05),
            [weight, gradient, first_moment, second_moment],
            [],
            [(weight.shape[1], F32)] * 3,
            name="adam",
            tile=weight.shape[0],
        )

    scatters = [scatter_in, *scatter_out, scatter_up]
    total = Total(narrow, [0, *ahead, 1])
    phase(bits, [*scatters, total], None)
    core = own_c.astype(jnp.int32).reshape(1)

    def split_rows(pieces, columns, rule):
        arrays = []
        for p in pieces:
            arrays += [p.held[0], p.came[0]]

        def kernel(own, *refs):
            away, keep = refs[-2:]
            for here in (0, 1):

                @pl.when(own[0] == here)
                def _(here=here):
                    for out, which in ((keep, here), (away, 1 - here)):
                        for i, (low, high), (left, right), row, column in rule(which):
                            p = pieces[i]
                            at, came = p.held[1] + low, p.came[1] + low
                            out[row : row + high - low, column : column + right - left] = refs[2 * i][
                                at : at + high - low, left:right
                            ].astype(F32) + refs[2 * i + 1][came : came + high - low, left:right].astype(F32)

        size = sum(a.size * jnp.dtype(a.dtype).itemsize for a in arrays) + 8 * rows * columns
        return pl.pallas_call(
            kernel,
            name="split_rows",
            out_shape=[jax.ShapeDtypeStruct((rows, columns), F32)] * 2,
            in_specs=[pl.BlockSpec(memory_space=pltpu.SMEM)]
            + [pl.BlockSpec(memory_space=pltpu.VMEM)] * len(arrays),
            compiler_params=pltpu.CompilerParams(vmem_limit_bytes=size + (2 << 20)),
            cost_estimate=pl.CostEstimate(flops=0, bytes_accessed=0, transcendentals=0),
        )(core, *arrays)

    def adam_joined(keep, came, blocks, weight, first_moment, second_moment):
        span = keep.shape[1] // blocks

        def kernel(own, keep, came, weight, first, second, *outs):
            low_is_own = own[0] == 0
            for i in range(blocks):
                mine, other = keep[:, i * span : (i + 1) * span], came[:, i * span : (i + 1) * span]
                for j, values in enumerate(
                    (jnp.where(low_is_own, mine, other), jnp.where(low_is_own, other, mine))
                ):
                    at = slice((2 * i + j) * span, (2 * i + j + 1) * span)
                    made = adam_update(weight[:, at], values, first[:, at], second[:, at], factor, 0.05)
                    for out, value in zip(outs, (values, *made)):
                        out[:, at] = value

        size = 4 * (2 * keep.size + 7 * weight.size)
        gradient, *updated = pl.pallas_call(
            kernel,
            name="adam_joined",
            out_shape=[jax.ShapeDtypeStruct(weight.shape, F32)] * 4,
            in_specs=[pl.BlockSpec(memory_space=pltpu.SMEM)] + [pl.BlockSpec(memory_space=pltpu.VMEM)] * 5,
            compiler_params=pltpu.CompilerParams(vmem_limit_bytes=size + (2 << 20)),
            cost_estimate=pl.CostEstimate(flops=0, bytes_accessed=0, transcendentals=0),
        )(core, keep, came, weight, first_moment, second_moment)
        return gradient, updated

    def finish_up():
        away, keep = split_rows(
            scatter_up.pieces,
            ff_half,
            lambda c: [(i, (c * rows, (c + 1) * rows), (0, width), 0, i * width) for i in (0, 1)],
        )
        return adam_joined(keep, swap_core(away), chips, mlp_in, first_mlp_in, second_mlp_in)

    def finish_mlp():
        shard_down = jnp.concatenate(scatter_down.result(bits), axis=0)
        if paired:
            shard_up, adam_up = finish_up()
        else:
            shard_up = trade(jnp.concatenate(scatter_up.result(bits), axis=1), chips)
            adam_up = adam(mlp_in, shard_up, first_mlp_in, second_mlp_in)
        return shard_up, shard_down, adam_up, adam(mlp_out, shard_down, first_mlp_out, second_mlp_out)

    send_output = Rider(output, 0, local_len, local_len)
    send_grad = Rider(grad_low, 0, local_len, local_len)
    rest = [scatter_in, *scatter_out, total]
    if scatter_up.left():
        phase(bits, [*rest, (scatter_up, 9)], None)
    grad_up_shard, shard_down, adam_up, adam_down = phase(
        bits, [*rest, send_output], finish_mlp, also=[scatter_up, scatter_down]
    )

    def back_to_rows(array, other):
        mine = array[:local_len]
        return jnp.stack([pick(own_y, mine, other), pick(own_y, other, mine)], axis=0)

    output = phase(bits, [*rest, send_grad], back_to_rows, output, send_output.result())
    while scatter_in.left():
        phase(bits, rest, None)
    while total.left() > 1:
        phase(bits, [total], None)
    if total.left():
        phase(bits, [total], None)
    input_grad = back_to_rows(grad_low, send_grad.result())
    narrow = total.result()
    if paired:

        def in_rule(c):
            left = [(0, (0, rows), (0, width), 0, 0)]
            if c == 1:
                left = [
                    (0, (rows, 3 * quarter), (0, width), 0, 0),
                    (1, (0, quarter), (0, width), 3 * quarter - rows, 0),
                ]
            return [*left, (2, (0, rows), (c * half, (c + 1) * half), 0, width)]

        away, keep = split_rows(scatter_in.pieces, in_width, in_rule)
        grad_in_shard, adam_in = adam_joined(keep, swap_core(away), 3, attn_in, first_attn_in, second_attn_in)
        away, keep = split_rows(
            scatter_out[0].pieces,
            half,
            lambda c: [(i, (0, quarter), (c * half, (c + 1) * half), i * quarter, 0) for i in (0, 1)],
        )
        grad_out_shard, adam_out = adam_joined(
            keep, swap_core(away), 1, attn_out, first_attn_out, second_attn_out
        )
    else:
        shard_in = jnp.concatenate(scatter_in.result(bits), axis=1)
        grad_out_shard, grad_in_shard = trade(shard_in[:, in_width:], 1), trade(shard_in[:, :in_width], 3)
        adam_in = adam(attn_in, grad_in_shard, first_attn_in, second_attn_in)
        adam_out = adam(attn_out, grad_out_shard, first_attn_out, second_attn_out)
    updated = [adam_in, adam_out, adam_up, adam_down]
    device = (lax.axis_index("img") * halves + own_y) * 2 + own_c
    grad_vectors_shard = lax.dynamic_slice_in_dim(narrow[:vector_count], device * rows, rows, 1).T
    table_grad = narrow[vector_count : vector_count + table_size]

    shards = (grad_in_shard, grad_out_shard, grad_up_shard, shard_down, grad_vectors_shard)
    updated.append(adam_update(vectors, grad_vectors_shard, first_vectors, second_vectors, factor, 0.0))
    return (
        output,
        input_grad,
        table_grad,
        *shards,
        *(updated[i][0] for i in range(5)),
        *(updated[i][1] for i in range(5)),
        *(updated[i][2] for i in range(5)),
    )


def solution(mesh):
    img, seq = mesh.shape["img"], mesh.shape["seq"]
    inner = Mesh(mesh.devices.reshape(img, seq // 2, 2), ("img", "sy", "sc"))
    tokens = P("img", ("sy", "sc"), None)
    shard = P(("img", "sy", "sc"), None)
    return jax.shard_map(
        per_device,
        mesh=inner,
        in_specs=(tokens, tokens, P("img", None), P()) + (shard,) * 15,
        out_specs=(tokens, tokens, P()) + (shard,) * 20,
        check_vma=False,
    )
```

```python
import functools
import math

import jax
import jax.numpy as jnp
from jax import lax
from jax.experimental import pallas as pl
from jax.experimental.pallas import tpu as pltpu
from jax.sharding import Mesh
from jax.sharding import PartitionSpec as P

HEADS = 16
GRID = 7
GRID_HI = 12
TILE = 128

PRECISE = lax.Precision.HIGHEST
FIRST_CORRECTION = 0.9999734386011124
SECOND_CORRECTION = 0.0952078528862911
EPS = 1e-06

F32 = jnp.float32
BF16 = jnp.bfloat16


def image_spans(res_row):
    side = jnp.where(res_row == 384, GRID_HI, jnp.where(res_row == 224, GRID, 0)).astype(jnp.int32)
    lengths = side * side
    slots = res_row.shape[0]
    order = jnp.arange(slots, dtype=jnp.int32)
    earlier = order[None, :] < order[:, None]
    starts = jnp.sum(jnp.where(earlier, lengths[None, :], 0), axis=1)
    return side, lengths, starts


def layout(res_row, positions):
    side, lengths, starts = image_spans(res_row)
    slots = res_row.shape[0]
    places = positions[:, None]
    inside = ((places >= starts[None, :]) & (places < (starts + lengths)[None, :])).astype(jnp.int32)
    usable = jnp.sum(inside, axis=1)
    image_number = jnp.arange(slots, dtype=jnp.int32)
    segment = jnp.sum(inside * image_number, axis=1) + (1 - usable) * slots
    start_of = jnp.sum(inside * starts[None, :], axis=1)
    side_of = jnp.sum(inside * side[None, :], axis=1)
    patch_index = (positions - start_of) * usable
    return segment, side_of, patch_index, usable


def key_bounds(res_row, row_len):
    _, lengths, starts = image_spans(res_row)
    total = jnp.sum(lengths)
    firsts = jnp.arange(row_len // TILE, dtype=jnp.int32) * TILE

    def span(positions):
        places = positions[:, None]
        inside = (places >= starts[None, :]) & (places < (starts + lengths)[None, :])
        found = positions < total
        begin = jnp.sum(jnp.where(inside, starts[None, :], 0), axis=1)
        end = jnp.sum(jnp.where(inside, (starts + lengths)[None, :], 0), axis=1)
        return jnp.where(found, begin, total), jnp.where(found, end, row_len)

    begin, _ = span(firsts)
    _, end = span(firsts + (TILE - 1))
    return begin // TILE, (end + TILE - 1) // TILE


def axis_weights(coord, side_of):
    scaled = jnp.maximum((2 * coord + 1) * GRID - GRID_HI, 0)
    lower_fine = scaled // (2 * GRID_HI)
    fraction_fine = (scaled - lower_fine * 2 * GRID_HI).astype(F32) / (2.0 * GRID_HI)
    resized = side_of == GRID_HI
    lower_cell = jnp.where(resized, lower_fine, coord)
    fraction = jnp.where(resized, fraction_fine, jnp.zeros_like(fraction_fine))
    upper_cell = jnp.minimum(lower_cell + 1, GRID - 1)
    cell_index = jnp.arange(GRID, dtype=jnp.int32)
    below = (cell_index == lower_cell[..., None]).astype(F32)
    above = (cell_index == upper_cell[..., None]).astype(F32)
    return (1.0 - fraction)[..., None] * below + fraction[..., None] * above


def table_weights(side_of, patch_index, usable):
    safe_side = jnp.maximum(side_of, 1)
    row_coord = patch_index // safe_side
    column_coord = patch_index % safe_side
    outer = axis_weights(row_coord, side_of)[:, :, None] * axis_weights(column_coord, side_of)[:, None, :]
    outer = outer * usable.astype(F32)[:, None, None]
    return outer.reshape(side_of.shape[0], GRID * GRID)


def place_of(block, own_y, own_c, per):
    quarter = block // per
    core = (quarter % 2 + own_c) % 2
    half = (quarter // 2 + own_y) % 2
    return (core * 2 + half) * per + block % per


def split_heads(pair):
    lane = lax.broadcasted_iota(jnp.int32, pair.shape, 1)
    zero = jnp.zeros_like(pair)
    low = lane < pair.shape[1] // 2
    return jnp.concatenate([jnp.where(low, pair, zero), jnp.where(low, zero, pair)], axis=0)


def join_heads(stacked):
    half = stacked.shape[0] // 2
    lane = lax.broadcasted_iota(jnp.int32, (half, stacked.shape[1]), 1)
    return jnp.where(lane < stacked.shape[1] // 2, stacked[:half], stacked[half:])


def down_lanes(row):
    return jnp.transpose(jnp.broadcast_to(row, (TILE, TILE)))


def nt(left, right):
    return lax.dot_general(left, right, (((1,), (1,)), ((), ())), preferred_element_type=F32)


def tn(left, right):
    return lax.dot_general(left, right, (((0,), (0,)), ((), ())), preferred_element_type=F32)


def nn(left, right):
    return jnp.dot(left, right, preferred_element_type=F32)


def fold(array, over):
    parts = array.reshape(array.shape[0] // 8, 8, array.shape[1])
    return jnp.max(parts, axis=0) if over == "max" else jnp.sum(parts, axis=0)


def same_segment(seg_down, chunk, seg_q):
    same = seg_down[chunk] == seg_q
    return jnp.concatenate([same, same], axis=1)


def fill_segments(seg, seg_down):
    chunks, span, _ = seg_down.shape
    for chunk in range(chunks):
        row = seg[0:1, chunk * span : (chunk + 1) * span]
        seg_down[chunk] = jnp.transpose(jnp.broadcast_to(row, (TILE, span)))


def join_turned(turned):
    half = turned.shape[1] // 2
    row = lax.broadcasted_iota(jnp.int32, (turned.shape[0], half), 0)
    return jnp.transpose(jnp.where(row < turned.shape[0] // 2, turned[:, :half], turned[:, half:]))


def columns_of(base, j):
    return slice(base + j * TILE, base + (j + 1) * TILE)


def attend_kernel(pairs, width, per, scale, info, qkv, seg, out, log_sum, scores, turned, seg_down):
    tile = pl.program_id(0)
    chunks, span, _ = seg_down.shape
    own_y, own_c = info[0], info[1]
    ratio = span // TILE
    first = info[2 + tile] // ratio
    last = (info[2 + pl.num_programs(0) + tile] + ratio - 1) // ratio

    def at(chunk):
        return pl.multiple_of(place_of(chunk * ratio, own_y, own_c, per) * TILE, TILE)

    @pl.when(tile == 0)
    def _():
        fill_segments(seg, seg_down)
        for chunk in range(chunks):
            for j in range(pairs):
                turned[chunk, j] = jnp.transpose(qkv[pl.ds(at(chunk), span), columns_of(2 * width, j)])

    q_at = pl.multiple_of(place_of(tile, own_y, own_c, per) * TILE, TILE)
    seg_q = seg[0:1, pl.ds(pl.multiple_of(tile * TILE, TILE), TILE)]
    queries = [
        split_heads(qkv[pl.ds(q_at, TILE), columns_of(0, j)] * jnp.asarray(scale, BF16)) for j in range(pairs)
    ]

    def score(chunk, high):
        same = same_segment(seg_down, chunk, seg_q)
        products = [nt(qkv[pl.ds(at(chunk), span), columns_of(width, j)], queries[j]) for j in range(pairs)]
        made = []
        for j in range(pairs):
            s = jnp.where(same, products[j], -1e30)
            scores[j, chunk] = s
            made.append(jnp.maximum(high[j], fold(s, "max")))
        return tuple(made)

    high = lax.fori_loop(first, last, score, (jnp.full((8, 2 * TILE), -1e30, F32),) * pairs)
    tops = [jnp.max(high[j], axis=0, keepdims=True) for j in range(pairs)]

    def mix(chunk, carry):
        total, mixed = carry
        powers = [jnp.exp(scores[j, chunk] - tops[j]) for j in range(pairs)]
        return (
            tuple(total[j] + fold(powers[j], "sum") for j in range(pairs)),
            tuple(mixed[j] + nn(turned[chunk, j], powers[j].astype(BF16)) for j in range(pairs)),
        )

    total, mixed = lax.fori_loop(
        first,
        last,
        mix,
        ((jnp.zeros((8, 2 * TILE), F32),) * pairs, (jnp.zeros((TILE, 2 * TILE), F32),) * pairs),
    )
    for j in range(pairs):
        sums = jnp.sum(total[j], axis=0, keepdims=True)
        out[:, columns_of(0, j)] = join_turned(mixed[j] / sums).astype(BF16)
        log_total = tops[j] + jnp.log(sums)
        log_sum[2 * j : 2 * j + 1] = log_total[:, :TILE]
        log_sum[2 * j + 1 : 2 * j + 2] = log_total[:, TILE:]


def attend_back_kernel(
    start, pairs, width, per, scale, info, qkv, mixed, grad, seg, log_sum, out, grad_keys, grad_values, turned, seg_down
):
    tile = pl.program_id(0)
    chunks, span, _ = seg_down.shape
    own_y, own_c = info[0], info[1]
    ratio = span // TILE
    first = info[2 + tile] // ratio
    last = (info[2 + pl.num_programs(0) + tile] + ratio - 1) // ratio
    heads = range(start, start + pairs)

    def at(chunk):
        return pl.multiple_of(place_of(chunk * ratio, own_y, own_c, per) * TILE, TILE)

    @pl.when(tile == 0)
    def _():
        fill_segments(seg, seg_down)
        grad_keys[...] = jnp.zeros_like(grad_keys)
        grad_values[...] = jnp.zeros_like(grad_values)
        for chunk in range(chunks):
            for i, j in enumerate(heads):
                turned[chunk, i] = jnp.transpose(qkv[pl.ds(at(chunk), span), columns_of(width, j)])

    q_at = pl.multiple_of(place_of(tile, own_y, own_c, per) * TILE, TILE)
    q_from = pl.multiple_of(tile * TILE, TILE)
    seg_q = seg[0:1, pl.ds(q_from, TILE)]
    queries, grads, logs, inner = [], [], [], []
    for j in heads:
        queries.append(split_heads(qkv[pl.ds(q_at, TILE), columns_of(0, j)] * jnp.asarray(scale, BF16)))
        g = grad[pl.ds(q_at, TILE), columns_of(0, j)]
        grads.append(split_heads(g))
        both = jnp.transpose(g.astype(F32) * mixed[pl.ds(q_at, TILE), columns_of(0, j)].astype(F32))
        low = jnp.sum(both[: TILE // 2], axis=0, keepdims=True)
        high = jnp.sum(both[TILE // 2 :], axis=0, keepdims=True)
        inner.append(jnp.concatenate([low, high], axis=1))
        here = log_sum[2 * j : 2 * j + 2, pl.ds(q_from, TILE)]
        logs.append(jnp.concatenate([here[0:1], here[1:2]], axis=1))

    def step(chunk, carry):
        k_at = at(chunk)
        same = same_segment(seg_down, chunk, seg_q)
        scores = [nt(qkv[pl.ds(k_at, span), columns_of(width, j)], queries[i]) for i, j in enumerate(heads)]
        slopes = [nt(qkv[pl.ds(k_at, span), columns_of(2 * width, j)], grads[i]) for i, j in enumerate(heads)]
        powers = [jnp.exp(jnp.where(same, scores[i], -1e30) - logs[i]) for i in range(pairs)]
        changes = [(powers[i] * (slopes[i] - inner[i])).astype(BF16) for i in range(pairs)]
        to_values = [nn(powers[i].astype(BF16), grads[i]) for i in range(pairs)]
        to_keys = [nn(changes[i], queries[i]) for i in range(pairs)]
        to_query = tuple(carry[i] + nn(turned[chunk, i], changes[i]) for i in range(pairs))
        for i in range(pairs):
            grad_values[chunk, :, columns_of(0, i)] += to_values[i]
            grad_keys[chunk, :, columns_of(0, i)] += to_keys[i]
        return to_query

    grad_query = lax.fori_loop(first, last, step, (jnp.zeros((TILE, 2 * TILE), F32),) * pairs)
    for i in range(pairs):
        out[pl.ds(q_at, TILE), columns_of(0, i)] = (join_turned(grad_query[i]) * scale).astype(BF16)

    @pl.when(tile == pl.num_programs(0) - 1)
    def _():
        all_heads = pairs * TILE
        for chunk in range(chunks):
            out[pl.ds(at(chunk), span), all_heads : 2 * all_heads] = grad_keys[chunk].astype(BF16)
            out[pl.ds(at(chunk), span), 2 * all_heads :] = grad_values[chunk].astype(BF16)


def attention(qkv, seg, info, per, head_size):
    length, width = qkv.shape[0], qkv.shape[1] // 3
    pairs, tiles = width // TILE, length // TILE
    span = per * TILE
    chunks = length // span
    scale = head_size ** (-0.5)

    def place(i, info):
        return place_of(i, info[0], info[1], per)

    return pl.pallas_call(
        functools.partial(attend_kernel, pairs, width, per, scale),
        name="attend",
        out_shape=(
            jax.ShapeDtypeStruct((length, width), BF16),
            jax.ShapeDtypeStruct((2 * pairs, length), F32),
        ),
        grid_spec=pltpu.PrefetchScalarGridSpec(
            num_scalar_prefetch=1,
            grid=(tiles,),
            in_specs=[
                pl.BlockSpec(qkv.shape, lambda i, info: (0, 0), pipeline_mode=pl.Buffered(1)),
                pl.BlockSpec(seg.shape, lambda i, info: (0, 0), pipeline_mode=pl.Buffered(1)),
            ],
            out_specs=[
                pl.BlockSpec((TILE, width), lambda i, info: (place(i, info), 0)),
                pl.BlockSpec((2 * pairs, TILE), lambda i, info: (0, i)),
            ],
            scratch_shapes=[
                pltpu.VMEM((pairs, chunks, span, 2 * TILE), F32),
                pltpu.VMEM((chunks, pairs, TILE, span), BF16),
                pltpu.VMEM((chunks, span, TILE), F32),
            ],
        ),
        compiler_params=pltpu.CompilerParams(
            dimension_semantics=("arbitrary",), vmem_limit_bytes=20 << 20
        ),
        cost_estimate=pl.CostEstimate(flops=0, bytes_accessed=0, transcendentals=0),
    )(info, qkv, seg)


def attention_back(part, parts, qkv, mixed, grad, seg, log_sum, info, per, head_size):
    length, width = qkv.shape[0], qkv.shape[1] // 3
    pairs, tiles = width // TILE // parts, length // TILE
    span = per * TILE
    chunks = length // span
    out = jax.ShapeDtypeStruct((length, 3 * pairs * TILE), BF16)
    scale = head_size ** (-0.5)

    def whole(array):
        return pl.BlockSpec(array.shape, lambda i, info: (0, 0), pipeline_mode=pl.Buffered(1))

    return pl.pallas_call(
        functools.partial(attend_back_kernel, part * pairs, pairs, width, per, scale),
        name="attend_back",
        out_shape=out,
        grid_spec=pltpu.PrefetchScalarGridSpec(
            num_scalar_prefetch=1,
            grid=(tiles,),
            in_specs=[whole(qkv), whole(mixed), whole(grad), whole(seg), whole(log_sum)],
            out_specs=pl.BlockSpec(out.shape, lambda i, info: (0, 0)),
            scratch_shapes=[
                pltpu.VMEM((chunks, span, pairs * TILE), F32),
                pltpu.VMEM((chunks, span, pairs * TILE), F32),
                pltpu.VMEM((chunks, pairs, TILE, span), BF16),
                pltpu.VMEM((chunks, span, TILE), F32),
            ],
        ),
        compiler_params=pltpu.CompilerParams(
            dimension_semantics=("arbitrary",), vmem_limit_bytes=28 << 20
        ),
        cost_estimate=pl.CostEstimate(
            flops=32 * length * length * width, bytes_accessed=8 * length * width * 2, transcendentals=0
        ),
    )(info, qkv, mixed, grad, seg, log_sum)


SWAP = [(0, 1), (1, 0)]


def swap_core(array):
    return lax.ppermute(array, "sc", SWAP)


def swap_chip(array):
    return lax.ppermute(array, "sy", SWAP)


def swap_bit(array, bit):
    if bit == 0:
        return swap_chip(array)
    count = lax.axis_size("img")
    return lax.ppermute(array, "img", [(i, i ^ (1 << (bit - 1))) for i in range(count)])


def own_bit(bit):
    if bit == 0:
        return lax.axis_index("sy")
    return (lax.axis_index("img") >> (bit - 1)) & 1


def fence(*values):
    return lax.optimization_barrier(values)


def axis_of(bit, done):
    return sum(1 for other in done if other > bit)


def pick(index, low, high):
    return jnp.where(index == 0, low, high)


def far_bits():
    return list(range(2, int(math.log2(lax.axis_size("img"))) + 1))


def join(first, second, axis):
    shape = list(first.shape)
    shape[axis] += second.shape[axis]
    held = lax.dynamic_update_slice_in_dim(jnp.zeros(shape, first.dtype), first, 0, axis)
    return lax.dynamic_update_slice_in_dim(held, second, first.shape[axis], axis)


class Turn:
    def __init__(self):
        self.arrays, self.shapes, self.jobs = [], [], []
        self.kept = None

    def keep(self, rows, columns):
        if self.kept is None:
            self.kept = self.write((0, columns), BF16)
        before = self.shapes[self.kept].shape[0]
        self.shapes[self.kept] = jax.ShapeDtypeStruct((before + rows, columns), BF16)
        return self.kept, before

    def read(self, array):
        for i, other in enumerate(self.arrays):
            if other is array:
                return i
        self.arrays.append(array)
        return len(self.arrays) - 1

    def write(self, shape, dtype):
        self.shapes.append(jax.ShapeDtypeStruct(shape, dtype))
        return len(self.shapes) - 1

    def run(self, bits):
        count = len(self.arrays)

        def kernel(own, *refs):
            mine = [own[i] for i in range(bits.shape[0])]
            for job in self.jobs:
                job(mine, refs[:count], refs[count:])

        spent = sum(a.size * jnp.dtype(a.dtype).itemsize for a in [*self.arrays, *self.shapes])
        return pl.pallas_call(
            kernel,
            name="turn",
            out_shape=tuple(self.shapes),
            in_specs=[pl.BlockSpec(memory_space=pltpu.SMEM)] + [pl.BlockSpec(memory_space=pltpu.VMEM)] * count,
            out_specs=tuple(pl.BlockSpec(memory_space=pltpu.VMEM) for _ in self.shapes),
            compiler_params=pltpu.CompilerParams(vmem_limit_bytes=spent + (2 << 20)),
            cost_estimate=pl.CostEstimate(flops=0, bytes_accessed=0, transcendentals=0),
        )(bits, *self.arrays)


def combinations(bits):
    made = [{}]
    for bit in bits:
        made = [{**choice, bit: value} for choice in made for value in (0, 1)]
    return made


def flat_index(choice, bits):
    at = 0
    for bit in sorted(bits, reverse=True):
        at = at * 2 + choice[bit]
    return at


def block_of(at, rows, base=0):
    start = at * rows + base
    if isinstance(start, int):
        return pl.ds(start, rows)
    return pl.ds(pl.multiple_of(start, math.gcd(rows, base) if base else rows), rows)


class Piece:
    def __init__(self, array, rows, bits, order, stride=None, base=0):
        self.held, self.rows, self.bits = (array, base), rows, list(bits)
        self.fixed, self.order, self.came = [], list(order), None
        self.stride, self.source = stride or rows, bool(bits)


class Gather:
    def __init__(self, *parts):
        self.pieces = []
        for array, first, rows, order in parts:
            piece = Piece(array, rows, [], order)
            piece.held = (array, first)
            self.pieces.append(piece)

    def wants(self):
        return [(p.order[0], p.rows << (len(p.bits) + (p.came is not None))) for p in self.pieces]

    def turn(self, turn, places):
        for p, (out, base) in zip(self.pieces, places):
            if p.came is None:
                turn.jobs.append(copy_rows(turn.read(p.held[0]), p.held[1], out, base, p.rows << len(p.bits)))
            else:
                bit = p.sent
                absorb_gather(turn, p, bit, lambda choice, p=p, out=out, base=base: [(out, choice, base)])
            p.sent = p.order.pop(0)
            p.next_held = (out, base)

    def settle(self, outs, came):
        for p, where in zip(self.pieces, came):
            if p.came is not None:
                p.bits.append(p.last)
            p.held, p.came, p.last = (outs[p.next_held[0]], p.next_held[1]), where, p.sent

    def arrays(self):
        return [a for p in self.pieces for a in ([p.held[0]] + ([p.came[0]] if p.came else []))]

    def relabel(self, swap):
        for p in self.pieces:
            p.held = (swap(p.held[0]), p.held[1])
            if p.came:
                p.came = (swap(p.came[0]), p.came[1])

    def left(self):
        return len(self.pieces[0].order)


def gathered(pieces, bits, outs):
    turn = Turn()
    made = [turn.write(shape, BF16) for shape, _ in outs]
    for i, p in enumerate(pieces):
        held, came = turn.read(p.held[0]), turn.read(p.came[0])
        moves = [(out, move) for out, (_, moves) in zip(made, outs) for move in moves[i]]

        def job(mine, ins, refs, p=p, held=held, came=came, moves=moves):
            everyone = [*p.bits, p.last]
            for choice in combinations(p.bits):
                at = flat_index(choice, p.bits)
                for source, base, value in (
                    (ins[held], p.held[1], mine[p.last]),
                    (ins[came], p.came[1], 1 - mine[p.last]),
                ):
                    chip = flat_index({**choice, p.last: value}, everyone)
                    for out, ((low, high), (left, right), stride, row, column) in moves:
                        start = pl.multiple_of(chip * stride + row, math.gcd(stride, row) if row else stride)
                        refs[out][pl.ds(start, high - low), column : column + right - left] = source[
                            pl.ds(base + at * p.rows + low, high - low), left:right
                        ]

        turn.jobs.append(job)
    return turn.run(bits)


class Spread:
    def __init__(self, array):
        self.pieces = [Piece(array, array.shape[0], [], [*reversed(far_bits()), 0, 1])]

    def wants(self):
        return [(self.pieces[0].order[0], self.pieces[0].rows)]

    def turn(self, turn, places):
        [p], [(out, base)] = self.pieces, places
        p.order.pop(0)
        p.next_held = (out, base)
        if p.came is None:
            turn.jobs.append(copy_rows(turn.read(p.held[0]), p.held[1], out, base, p.rows))
            return
        held, came, held_base, came_base, rows = turn.read(p.held[0]), turn.read(p.came[0]), p.held[1], p.came[1], p.rows

        def job(mine, ins, refs):
            refs[out][base : base + rows] = (
                ins[held][held_base : held_base + rows] + ins[came][came_base : came_base + rows]
            )

        turn.jobs.append(job)

    def settle(self, outs, came):
        [p] = self.pieces
        p.held, p.came = (outs[p.next_held[0]], p.next_held[1]), came[0]

    arrays, relabel, left = Gather.arrays, Gather.relabel, Gather.left

    def result(self):
        [p] = self.pieces
        return sum(array[base : base + p.rows] for array, base in (p.held, p.came))


class Rider:
    def __init__(self, array, bit, first, rows):
        self.pieces = [Piece(array, rows, [], [bit])]
        self.pieces[0].held = (array, first)

    wants, turn, settle = Spread.wants, Spread.turn, Spread.settle
    arrays, relabel, left = Gather.arrays, Gather.relabel, Gather.left

    def result(self):
        [p] = self.pieces
        return p.came[0][p.came[1] : p.came[1] + p.rows]


class Total:
    def __init__(self, array, order):
        self.pieces = [Piece(array, array.shape[0], [], order)]

    wants, arrays, relabel, left = Spread.wants, Gather.arrays, Gather.relabel, Gather.left

    def turn(self, turn, places):
        [p], [(out, base)] = self.pieces, places
        p.order.pop(0)
        held, rows = turn.read(p.held[0]), p.rows
        came, came_base = (None, 0) if p.came is None else (turn.read(p.came[0]), p.came[1])
        p.next = None if came is None else turn.write(p.held[0].shape, F32)

        def job(mine, ins, refs, keep=p.next):
            own = ins[held][...].astype(BF16)
            if came is not None:
                total = own.astype(F32) + ins[came][came_base : came_base + rows].astype(F32)
                refs[keep][...] = total
                own = total.astype(BF16)
            refs[out][base : base + rows] = own

        turn.jobs.append(job)

    def settle(self, outs, came):
        [p] = self.pieces
        if p.next is not None:
            p.held = (outs[p.next], 0)
        p.came = came[0]

    def result(self):
        [p] = self.pieces
        return add_came(p.held[0], p.came[0][p.came[1] : p.came[1] + p.rows])


def copy_rows(source, source_base, out, base, rows):
    def job(mine, ins, refs):
        refs[out][base : base + rows] = ins[source][source_base : source_base + rows]

    return job


def absorb_gather(turn, p, bit, targets):
    held, came = turn.read(p.held[0]), turn.read(p.came[0])
    last = p.last
    known = list(p.bits)
    held_base, came_base, rows = p.held[1], p.came[1], p.rows
    [(out, _, base)] = targets(None)

    def job(mine, ins, refs):
        for choice in combinations(known):
            at = flat_index(choice, known)
            for source, start, value in ((held, held_base, mine[last]), (came, came_base, 1 - mine[last])):
                to = flat_index({**choice, last: value}, [*known, last])
                refs[out][block_of(to, rows, base)] = ins[source][block_of(at, rows, start)]

    turn.jobs.append(job)


class Scatter:
    def __init__(self, *parts):
        far = far_bits()
        bits = sorted([0, 1, *far], reverse=True)
        self.pieces = [
            Piece(array, rows, bits, [*((1, 0) if turned else (0, 1)), *far], stride, first)
            for array, rows, stride, first, turned in parts
        ]

    def wants(self):
        return [(p.order[0], p.rows << (len(p.bits) - len(p.fixed) - 1)) for p in self.pieces]

    def turn(self, turn, places):
        for p, (out, base) in zip(self.pieces, places):
            bit = p.order.pop(0)
            free = [b for b in p.bits if b not in p.fixed and b != bit]
            rows, bits, fixed = p.rows, list(p.bits), list(p.fixed)
            held = turn.read(p.held[0])
            stride, first = p.stride, p.held[1]

            def block(choice, bits=bits, stride=stride, first=first, rows=rows):
                start = flat_index(choice, bits) * stride + first
                return pl.ds(pl.multiple_of(start, math.gcd(stride, first) if first else stride), rows)

            if p.came is None:
                p.next = None

                def job(mine, ins, refs, held=held, rows=rows, free=free, bit=bit, out=out, base=base, block=block):
                    for choice in combinations(free):
                        refs[out][block_of(flat_index(choice, free), rows, base)] = ins[held][
                            block({**choice, bit: 1 - mine[bit]})
                        ]

            else:
                came, came_base = turn.read(p.came[0]), p.came[1]
                keep, keep_base = turn.keep(rows << len(free), p.held[0].shape[1])
                p.next = (keep, keep_base)

                def job(
                    mine, ins, refs, held=held, rows=rows, fixed=fixed, free=free, bit=bit, out=out, base=base,
                    came=came, came_base=came_base, keep=keep, keep_base=keep_base, block=block,
                ):
                    settled = {b: mine[b] for b in fixed}
                    for choice in combinations(free):
                        for value, target, start in ((1 - mine[bit], out, base), (mine[bit], keep, keep_base)):
                            now = {**choice, bit: value}
                            total = ins[held][block({**now, **settled})].astype(F32) + ins[came][
                                block_of(flat_index(now, [*free, bit]), rows, came_base)
                            ].astype(F32)
                            refs[target][block_of(flat_index(choice, free), rows, start)] = total.astype(BF16)

            turn.jobs.append(job)
            p.sent, p.free = bit, free

    def settle(self, outs, came):
        for p, where in zip(self.pieces, came):
            if p.next is None:
                p.fixed = [p.sent]
            else:
                p.held, p.bits, p.fixed = (outs[p.next[0]], p.next[1]), list(p.free), []
                p.stride, p.source = p.rows, False
            p.came = where

    arrays, relabel, left = Gather.arrays, Gather.relabel, Gather.left

    def result(self, bits):
        turn = Turn()
        for p in self.pieces:
            held, came, base, rows, first = turn.read(p.held[0]), turn.read(p.came[0]), p.came[1], p.rows, p.held[1]
            out = turn.write((rows, p.held[0].shape[1]), F32)

            def job(mine, ins, refs, held=held, came=came, base=base, rows=rows, out=out, first=first):
                refs[out][...] = ins[held][first : first + rows].astype(F32) + ins[came][base : base + rows].astype(F32)

            turn.jobs.append(job)
        return turn.run(bits)


def swap_rows(moves, bits):
    wants = [move.wants() for move in moves]
    sizes, places = {}, []
    for bit, rows in (want for group in wants for want in group):
        places.append((bit, sizes.get(bit, 0)))
        sizes[bit] = sizes.get(bit, 0) + rows
    turn = Turn()
    width = moves[0].pieces[0].held[0].shape[1]
    outs = {bit: turn.write((rows, width), BF16) for bit, rows in sizes.items()}
    located = [(outs[bit], base) for bit, base in places]
    starts = [0]
    for move in moves:
        starts.append(starts[-1] + len(move.pieces))
    for i, move in enumerate(moves):
        move.turn(turn, located[starts[i] : starts[i + 1]])
    made = turn.run(bits)
    got = {bit: swap_bit(made[out], bit) for bit, out in outs.items()}
    came = [(got[bit], base) for bit, base in places]
    for i, move in enumerate(moves):
        move.settle(made, came[starts[i] : starts[i + 1]])


def add_came(own, came):
    return own.astype(BF16).astype(F32) + came.astype(F32)


def add_hop(array, bit):
    return add_came(array, swap_bit(array.astype(BF16), bit))


def phase(bits, moves, work, *values, also=()):
    chains = [move if isinstance(move, tuple) else (move, 1) for move in moves]
    chains = [
        ([move for move in chain[:-1] if move.left()], min(chain[-1], chain[0].left())) for chain in chains
    ]
    moves = [move for chain, _ in chains for move in chain]

    def tie(extra):
        arrays = []
        for array in (a for move in [*moves, *also] for a in move.arrays()):
            if not any(array is other for other in arrays):
                arrays.append(array)
        held, extra = fence(arrays, extra)
        table = list(zip(arrays, held))
        for move in [*moves, *also]:
            move.relabel(lambda array: next(new for old, new in table if old is array))
        return extra

    values = tie(values)
    if moves:
        swap_rows(moves, bits)
    for chain, count in chains:
        for _ in range(count - 1):
            swap_rows(chain, bits)
    made = work(*values) if work else ()
    return tie(made)


def by_rows(body, rows, whole, outs, sums=0, tile=TILE, name="rows"):
    rows = [array if isinstance(array, tuple) else (array, 0, array.shape[0]) for array in rows]
    length = rows[0][2]
    width = outs[0][0]

    def kernel(*refs):
        ins, results = refs[: len(rows) + len(whole)], refs[len(rows) + len(whole) :]
        made = body(*(ref[...] for ref in ins))
        for ref, value in zip(results, made):
            if ref.shape[0] == 1:

                @pl.when(pl.program_id(0) == 0)
                def _(ref=ref):
                    ref[...] = jnp.zeros_like(ref)

                ref[...] += value
            else:
                ref[...] = value.astype(ref.dtype)

    spent = sum(array.size * array.dtype.itemsize for array in whole)
    for columns, kind in [*outs, *((array.shape[1], array.dtype) for array, _, _ in rows)]:
        spent += 2 * tile * columns * jnp.dtype(kind).itemsize

    def steps(columns, first=0):
        return pl.BlockSpec((tile, columns), lambda i: (i + first // tile, 0))

    def fixed(shape, **how):
        return pl.BlockSpec(shape, lambda i: (0,) * len(shape), **how)

    return pl.pallas_call(
        kernel,
        name=name,
        grid=(length // tile,),
        out_shape=[jax.ShapeDtypeStruct((length, columns), dtype) for columns, dtype in outs]
        + [jax.ShapeDtypeStruct((1, width), F32)] * sums,
        in_specs=[steps(array.shape[1], first) for array, first, _ in rows]
        + [fixed(array.shape, pipeline_mode=pl.Buffered(1)) for array in whole],
        out_specs=[steps(columns) for columns, _ in outs] + [fixed((1, width))] * sums,
        compiler_params=pltpu.CompilerParams(
            dimension_semantics=("arbitrary",), vmem_limit_bytes=spent + (12 << 20)
        ),
        cost_estimate=pl.CostEstimate(flops=0, bytes_accessed=0, transcendentals=0),
    )(*(array for array, _, _ in rows), *whole)


def normalize(stream):
    center = jnp.mean(stream, axis=-1, keepdims=True)
    centered = stream - center
    spread = jnp.mean(centered * centered, axis=-1, keepdims=True)
    inverse = lax.rsqrt(spread + EPS)
    return centered * inverse, inverse


def normalize_back(normed, inverse, gain, grad):
    scaled = grad * gain
    middle = jnp.mean(scaled, axis=-1, keepdims=True)
    along = jnp.mean(scaled * normed, axis=-1, keepdims=True)
    return (
        inverse[:, :1] * (scaled - middle - normed * along),
        jnp.sum(grad * normed, axis=0, keepdims=True),
        jnp.sum(grad, axis=0, keepdims=True),
    )


def rows_from(columns, count):
    one_hot = (jnp.arange(16)[:, None] == jnp.arange(TILE)[None, :]).astype(BF16)
    rows = nt(one_hot, columns)
    return [rows[i : i + 1] for i in range(count)]


def column_choice(rows, columns):
    row, lane = jnp.arange(rows)[:, None], jnp.arange(TILE)[None, :]
    return (row == 8 + lane % columns).astype(F32)


def own_place(width, columns):
    per_run = TILE // columns
    row, lane = jnp.arange(width)[:, None], jnp.arange(TILE)[None, :]
    return row % per_run == lane // columns


def unroll_bias(columns, own_c, ff_rows):
    width, extra = columns.shape[0], 4
    spread = nn(columns, column_choice(TILE, extra).astype(BF16))
    runs = jnp.where(own_place(width, extra), spread, 0.0).reshape(-1, TILE // extra, TILE).sum(axis=1)
    runs = runs.reshape(-1, 2, ff_rows)
    return pick(own_c, runs[:, 0], runs[:, 1]).reshape(1, -1)


def roll_bias(sums, own_c, width, rows, ff_rows):
    extra = 4
    runs = sums.reshape(-1, ff_rows)
    zero = jnp.zeros_like(runs)
    runs = jnp.stack([pick(own_c, runs, zero), pick(own_c, zero, runs)], axis=1).reshape(-1, 1, TILE)
    spread = jnp.broadcast_to(runs, (runs.shape[0], TILE // extra, TILE)).reshape(width, TILE)
    spread = jnp.where(own_place(width, extra), spread, 0.0)
    return lax.dot_general(
        column_choice(rows, extra), spread, (((1,), (1,)), ((), ())), precision=PRECISE, preferred_element_type=F32
    )


def token_sums(array):
    return nn(jnp.ones((8, array.shape[0]), BF16), array)[:1]


def gelu_and_slope(values):
    cdf = 0.5 * (1.0 + lax.erf(values * (0.5**0.5)))
    density = jnp.exp(-0.5 * values * values) * (1.0 / math.sqrt(2.0 * math.pi))
    return values * cdf, cdf + values * density


def adam_update(weight, gradient, first_moment, second_moment, factor, decay):
    scaled = gradient * factor
    first_new = 0.9 * first_moment + 0.1 * scaled
    second_new = 0.999 * second_moment + 0.001 * scaled * scaled
    first_hat = first_new / FIRST_CORRECTION
    second_hat = second_new / SECOND_CORRECTION
    direction = first_hat / (jnp.sqrt(second_hat) + 1e-08) + decay * weight
    return (direction, first_new, second_new)


def per_device(
    patches,
    cotangent,
    res_ids,
    pos_table,
    attn_in,
    attn_out,
    mlp_in,
    mlp_out,
    vectors,
    first_attn_in,
    first_attn_out,
    first_mlp_in,
    first_mlp_out,
    first_vectors,
    second_attn_in,
    second_attn_out,
    second_mlp_in,
    second_mlp_out,
    second_vectors,
):
    row_count, local_len, width = patches.shape
    img_count, halves = lax.axis_size("img"), lax.axis_size("sy")
    chips = img_count * halves
    row_len = local_len * halves * 2
    slot_total = row_count * img_count * row_len
    head_size = width // HEADS
    own_y, own_c = lax.axis_index("sy"), lax.axis_index("sc")
    rows = attn_in.shape[0]
    half = width // 2
    ff_rows = mlp_out.shape[0]
    ff_half = chips * ff_rows
    table_size = GRID * GRID
    vector_count = vectors.shape[1]

    bits = jnp.stack([own_bit(bit) for bit in [0, 1, *far_bits()]]).astype(jnp.int32)

    def to_rows(array):
        mine = lax.dynamic_index_in_dim(array, own_y, 0, keepdims=False)
        other = lax.dynamic_index_in_dim(array, 1 - own_y, 0, keepdims=False)
        return join(mine, swap_chip(other), 0)

    res_row = pick(own_y, res_ids[0], res_ids[1])
    all_positions = jnp.arange(row_len, dtype=jnp.int32)
    segment_all, _, _, _ = layout(res_row, all_positions)
    seg = jnp.broadcast_to(segment_all.astype(F32)[None, :], (8, row_len))
    begin, end = key_bounds(res_row, row_len)
    info = jnp.concatenate([jnp.stack([own_y, own_c]).astype(jnp.int32), begin, end])
    near = jnp.arange(local_len, dtype=jnp.int32)
    positions = jnp.concatenate(
        [(2 * own_y + own_c) * local_len + near, (2 * (1 - own_y) + own_c) * local_len + near]
    )
    _, side_of, patch_index, usable = layout(res_row, positions)
    place = table_weights(side_of, patch_index, usable)
    usable = usable.astype(F32)[:, None]

    def by_core(array, blocks):
        split = array.reshape(rows, blocks, 2, -1)
        low, high = split[:, :, 0].reshape(rows, -1), split[:, :, 1].reshape(rows, -1)
        return pick(own_c, low, high), pick(own_c, high, low)

    vector_pad = jnp.pad(vectors, ((0, 0), (0, TILE - vector_count))).astype(BF16)
    mine_in, away_in = by_core(attn_in.astype(BF16), 3)
    mine_out, away_out = by_core(attn_out.astype(BF16), 1)
    mine_up, away_up = by_core(mlp_in.astype(BF16), chips)
    mine = jnp.concatenate([mine_in, mine_out, mine_up], axis=1)
    away = jnp.concatenate([away_in, away_out, away_up], axis=1)
    came, came_vector = swap_core(away), swap_core(vector_pad)
    shard = jnp.concatenate([pick(own_c, mine, came), pick(own_c, came, mine)], axis=0)
    vector_shard = jnp.concatenate(
        [pick(own_c, vector_pad, came_vector), pick(own_c, came_vector, vector_pad)], axis=0
    )[:, :16].reshape(1, -1)
    vector_row = jnp.pad(vector_shard, ((0, 0), (0, width - vector_shard.shape[1])))
    chip = lax.axis_index("img") * halves + own_y
    vector_rows = jnp.where(jnp.arange(chips)[:, None] == chip, vector_row, jnp.zeros_like(vector_row))
    in_width = 3 * half
    own = local_len * row_count
    per = local_len // TILE

    def with_core(array):
        return join(array, swap_core(array), 0)

    def sum_core(left, weights, product):
        away = product(left[own:], weights).astype(BF16)
        came = swap_core(away)
        return product(left[:own], weights) + came.astype(F32)

    low_down, high_down = jnp.split(mlp_out.astype(BF16), 2)
    ahead = list(reversed(far_bits()))
    one_way, other_way = [*ahead, 1, 0], [*ahead, 0, 1]
    block = 2 * rows
    gather_in = Gather(
        (shard[:, :width], 0, block, one_way), (shard[:, width : 2 * width], 0, block, other_way)
    )
    gather_vectors = Spread(vector_rows)
    gather_up = Gather(
        (shard[:, 2 * width : 2 * width + half * 2], 0, block, one_way),
        (shard[:, 2 * width + half * 2 :], 0, block, other_way),
    )
    low_down = mlp_out.astype(BF16)
    side = 3 * ff_rows // 8 if ff_rows % 128 == 0 else ff_rows // 2
    rest_rows = ff_rows - 2 * side
    gather_down = Gather((low_down, 0, side, one_way), (low_down, side, side, other_way))
    gather_rest = [Gather((low_down, 2 * side, rest_rows, [1, 0, *ahead]))] if rest_rows else []

    patches, cotangent = phase(
        bits,
        [(gather_in, gather_vectors, len(far_bits())), *gather_rest],
        lambda *arrays: [to_rows(array) for array in arrays],
        patches,
        cotangent,
    )

    wide_place = jnp.pad(place, ((0, 0), (0, TILE - table_size)))
    wide_table = jnp.pad(pos_table, ((0, TILE - table_size), (0, 0)))
    wide_usable = jnp.broadcast_to(usable, (own, TILE))
    small = TILE

    def first(patches, cotangent):
        def body(patches, place, cotangent, usable, table):
            stream = patches.astype(F32) + jnp.dot(place, table, precision=PRECISE, preferred_element_type=F32)
            normed, inverse = normalize(stream)
            grad = cotangent.astype(F32) * usable[:, :1]
            return stream, normed, jnp.broadcast_to(inverse, (stream.shape[0], TILE)), grad

        stream, hat_one, inverse_one, grad_own = by_rows(
            body,
            [patches, wide_place, cotangent, wide_usable],
            [wide_table],
            [(width, F32), (width, F32), (TILE, F32), (width, BF16)],
            name="first",
        )
        return stream, hat_one, inverse_one, grad_own

    far = far_bits()
    stream, hat_one, inverse_one, grad_own = phase(
        bits, [gather_in, gather_vectors, gather_up, *gather_rest], first, patches, cotangent
    )
    phase(bits, [gather_in, gather_vectors, (gather_up, len(far) - 1), gather_down], None)
    spare = in_width - width
    in_matrix, out_columns = gathered(
        gather_in.pieces,
        bits,
        [
            (
                (width, in_width),
                ([((0, block), (0, width), block, 0, 0)], [((0, block), (0, spare), block, 0, width)]),
            ),
            ((width, width - spare), ([], [((0, block), (spare, width), block, 0, 0)])),
        ],
    )
    vector_part = jnp.pad(
        gather_vectors.result()[:, : block * 16].reshape(-1, 16), ((0, 0), (0, TILE - 16))
    )
    gain_one, shift_one, bias_query, bias_value, bias_out, gain_two, shift_two, bias_down = (
        rows_from(vector_part, 8)
    )
    bias_query = pick(own_c, bias_query[:, :half], bias_query[:, half:])
    bias_value = pick(own_c, bias_value[:, :half], bias_value[:, half:])
    bias_up = unroll_bias(vector_part, own_c, ff_rows)
    bias_qkv = jnp.concatenate([bias_query, jnp.zeros_like(bias_query), bias_value], axis=1)

    def project(hat_one, out_columns):
        low, high = out_columns[:half], out_columns[half:]
        keep_out, came_out = pick(own_c, low, high), swap_core(pick(own_c, high, low))
        out_matrix = join(pick(own_c, keep_out, came_out), pick(own_c, came_out, keep_out), 1)
        return out_matrix, (hat_one * gain_one + shift_one).astype(BF16)

    out_matrix, normed_one = phase(
        bits, [gather_up, (gather_down, len(far) - 1)], project, hat_one, out_columns
    )

    def matmul_rows(left, right, product, name):
        return product(left[own:], right).astype(BF16)

    def attend(normed_one, in_matrix, out_matrix, grad_own):
        normed_one = with_core(normed_one)
        qkv = (nn(normed_one, in_matrix) + bias_qkv).astype(BF16)
        mixed, log_sum = attention(qkv, seg, info, per, head_size)
        away = matmul_rows(mixed, out_matrix, nn, "out_away")
        return normed_one, qkv, mixed, log_sum, away, with_core(grad_own)

    normed_one, qkv, mixed, log_sum, out_away, grad_last = phase(
        bits, [gather_up, *gather_rest], attend, normed_one, in_matrix, out_matrix, grad_own
    )

    def project_out(stream, mixed, out_away, out_matrix):
        def body(stream, mixed, came, matrix, bias, gain, shift):
            stream_two = stream + nn(mixed, matrix) + came.astype(F32) + bias
            normed, inverse = normalize(stream_two)
            return stream_two, normed, jnp.broadcast_to(inverse, (stream.shape[0], TILE)), normed * gain + shift

        return by_rows(
            body,
            [(stream, 0, own), mixed, swap_core(out_away)],
            [out_matrix, bias_out, gain_two, shift_two],
            [(width, F32), (width, F32), (TILE, F32), (width, BF16)],
            name="out_norm",
            tile=own // 2,
        )

    stream_two, hat_two, inverse_two, normed_two = phase(
        bits, [gather_down], project_out, stream, mixed, out_away, out_matrix
    )
    (up_matrix,) = gathered(
        gather_up.pieces,
        bits,
        [
            (
                (width, ff_half),
                ([((0, block), (0, width), block, 0, 0)], [((0, block), (0, width), block, 0, width)]),
            )
        ],
    )

    def expand(normed_two, up_matrix, grad_last):
        normed_two = with_core(normed_two)
        hidden_pre = nn(normed_two, up_matrix) + bias_up
        hidden, slope = gelu_and_slope(hidden_pre)
        hidden = hidden.astype(BF16)
        return normed_two, hidden, slope, tn(hidden, grad_last).astype(BF16)

    normed_two, hidden, slope, grad_down = phase(
        bits, [gather_down, *((move, 9) for move in gather_rest)], expand, normed_two, up_matrix, grad_last
    )
    part_rows = ff_rows // 2
    down_pieces = [piece for move in [gather_down, *gather_rest] for piece in move.pieces]
    (down_matrix,) = gathered(
        down_pieces,
        bits,
        [
            (
                (ff_half, width),
                [[((0, piece.rows), (0, width), ff_rows, i * side, 0)] for i, piece in enumerate(down_pieces)],
            )
        ],
    )

    scatter_down = Scatter(
        (grad_down, part_rows, ff_rows, 0, False), (grad_down, part_rows, ff_rows, part_rows, True)
    )

    def hidden_back(grad_last, down_matrix, slope, normed_two, up_matrix):
        grad_pre = (nt(grad_last, down_matrix) * slope).astype(BF16)
        return (
            grad_pre,
            matmul_rows(grad_pre, up_matrix, nt, "norm_two_away"),
            tn(normed_two, grad_pre[:, :width]).astype(BF16),
            tn(normed_two, grad_pre[:, width:]).astype(BF16),
        )

    grad_pre, two_away, *grad_up = phase(
        bits, [scatter_down], hidden_back, grad_last, down_matrix, slope, normed_two, up_matrix
    )
    scatter_up = Scatter((grad_up[0], block, block, 0, False), (grad_up[1], block, block, 0, True))

    def norm_back(grad, away, matrix, hat, inverse, added, gain, name):
        def body(grad, came, hat, inverse, added, matrix, gain):
            back, gain_sum, shift_sum = normalize_back(hat, inverse, gain, nt(grad, matrix) + came.astype(F32))
            total = added.astype(F32) + back
            return total, total, gain_sum, shift_sum

        return by_rows(
            body,
            [(grad, 0, own), swap_core(away), hat, inverse, added],
            [matrix, gain],
            [(width, F32), (width, BF16)],
            sums=2,
            name=name,
            tile=own // 2,
        )

    def middle(values, hidden, down_matrix):
        return norm_back(*values, "norm_two_back"), matmul_rows(hidden, down_matrix, nn, "output_away")

    (grad_two, grad_branch, grad_gain_two, grad_shift_two), output_away = phase(
        bits,
        [scatter_down],
        middle,
        (grad_pre, two_away, up_matrix, hat_two, inverse_two, grad_own, gain_two),
        hidden,
        down_matrix,
    )

    paired = block % 64 == 0

    def pair(array):
        blocks = array.reshape(chips, 2, -1, array.shape[1])
        return jnp.concatenate([blocks[:, 0], blocks[:, 1]], axis=2).reshape(-1, 2 * array.shape[1])

    def part(array):
        columns = array.shape[1] // 2
        return jnp.concatenate([array[:, :columns], array[:, columns:]], axis=0)

    def attention_grads(grad_branch, out_matrix, qkv, mixed, log_sum, output_away):
        grad_branch = with_core(grad_branch)
        grad_mixed = nt(grad_branch, out_matrix).astype(BF16)
        grad_qkv = attention_back(0, 1, qkv, mixed, grad_mixed, seg, log_sum, info, per, head_size)
        grad_rows = tn(mixed, grad_branch).astype(BF16)
        low, high = grad_rows[:, :half], grad_rows[:, half:]
        keep_rows, came_rows = pick(own_c, low, high), swap_core(pick(own_c, high, low))
        grad_out = join(pick(own_c, keep_rows, came_rows), pick(own_c, came_rows, keep_rows), 0)
        return grad_branch, swap_core(output_away), grad_qkv, pair(grad_out) if paired else grad_out

    grad_branch, came_output, grad_qkv, grad_out = phase(
        bits,
        [scatter_up, scatter_down],
        attention_grads,
        grad_branch,
        out_matrix,
        qkv,
        mixed,
        log_sum,
        output_away,
    )
    quarter = block // 4
    scatter_out = []
    if paired:
        scatter_out = [
            Scatter(
                (grad_out, quarter, 2 * quarter, 0, False), (grad_out, quarter, 2 * quarter, quarter, True)
            )
        ]

    def in_grads(normed_one, grad_qkv, in_matrix):
        right = tn(normed_one, grad_qkv[:, width:]).astype(BF16)
        return (
            matmul_rows(grad_qkv, in_matrix, nt, "norm_one_away"),
            tn(normed_one, grad_qkv[:, :width]).astype(BF16),
            pair(right) if paired else right,
        )

    one_away, left, right = phase(
        bits, [scatter_up, *scatter_out, scatter_down], in_grads, normed_one, grad_qkv, in_matrix
    )
    if paired:
        scatter_in = Scatter(
            (left, 3 * quarter, block, 0, False),
            (left, quarter, block, 3 * quarter, True),
            (right, 2 * quarter, 2 * quarter, 0, True),
        )
    else:
        scatter_in = Scatter((left, block, block, 0, False), (join(right, grad_out, 1), block, block, 0, True))

    def widen(row):
        zero = jnp.zeros_like(row)
        return jnp.concatenate([pick(own_c, row, zero), pick(own_c, zero, row)], axis=1)

    narrow_rows = vector_count + table_size
    narrow_rows += -narrow_rows % 16

    def norm_one_back(grad_qkv, one_away, in_matrix, hat_one, inverse_one, grad_two, grad_pre, grad_branch, grad_last):
        grad_stream, grad_low, grad_gain_one, grad_shift_one = norm_back(
            grad_qkv, one_away, in_matrix, hat_one, inverse_one, grad_two, gain_one, "norm_one_back"
        )
        wide_place = jnp.pad(place, ((0, 0), (vector_count, narrow_rows - vector_count - table_size)))
        table_part = lax.dot_general(
            wide_place, grad_stream, (((0,), (0,)), ((), ())), precision=PRECISE, preferred_element_type=F32
        )
        bias_part = roll_bias(token_sums(grad_pre), own_c, width, narrow_rows, ff_rows)
        sums = token_sums(grad_qkv)
        rows_of_sums = [
            grad_gain_one,
            grad_shift_one,
            widen(sums[:, :half]),
            widen(sums[:, 2 * half :]),
            token_sums(grad_branch[:own]),
            grad_gain_two,
            grad_shift_two,
            token_sums(grad_last[:own]),
        ]

        def stack(*refs):
            refs[-1][...] = refs[0][...] + refs[1][...]
            for i in range(len(rows_of_sums)):
                refs[-1][i : i + 1] = refs[2 + i][...]

        narrow = pl.pallas_call(
            stack,
            name="narrow",
            out_shape=jax.ShapeDtypeStruct((narrow_rows, width), F32),
            compiler_params=pltpu.CompilerParams(vmem_limit_bytes=4 << 20),
            cost_estimate=pl.CostEstimate(flops=0, bytes_accessed=0, transcendentals=0),
        )(table_part, bias_part, *rows_of_sums)
        return grad_low, add_came(narrow, swap_core(narrow.astype(BF16)))

    def finish_output(hidden, came, stream_two, down_matrix):
        def body(hidden, came, stream_two, usable, matrix, bias):
            return ((stream_two + nn(hidden, matrix) + came.astype(F32) + bias) * usable[:, :1],)

        return by_rows(
            body,
            [(hidden, 0, own), came, stream_two, wide_usable],
            [down_matrix, bias_down],
            [(width, BF16)],
            name="output",
            tile=own // 2,
        )

    (grad_low, narrow), (output,) = phase(
        bits,
        [scatter_in, *scatter_out, scatter_up, (scatter_down, len(far) - 1)],
        lambda values, others: (norm_one_back(*values), finish_output(*others)),
        (grad_qkv, one_away, in_matrix, hat_one, inverse_one, grad_two, grad_pre, grad_branch, grad_last),
        (hidden, came_output, stream_two, down_matrix),
    )

    def rows_of(array, core):
        return lax.dynamic_slice_in_dim(array, core * rows, rows, 0)

    def trade(array, blocks):
        away, keep = rows_of(array, 1 - own_c), rows_of(array, own_c)
        came = swap_core(away).reshape(rows, blocks, -1)
        keep = keep.reshape(rows, blocks, -1)
        both = jnp.stack([pick(own_c, keep, came), pick(own_c, came, keep)], axis=2)
        return both.reshape(rows, -1)

    factor = 1.0 / slot_total

    def adam(weight, gradient, first_moment, second_moment):
        return by_rows(
            lambda w, g, m, v: adam_update(w, g, m, v, factor, 0.05),
            [weight, gradient, first_moment, second_moment],
            [],
            [(weight.shape[1], F32)] * 3,
            name="adam",
            tile=weight.shape[0],
        )

    scatters = [scatter_in, *scatter_out, scatter_up]
    total = Total(narrow, [0, far[-1], 1, *far[:-1]])
    phase(bits, [*scatters, total], None)
    core = own_c.astype(jnp.int32).reshape(1)

    def split_rows(pieces, columns, rule):
        arrays = []
        for p in pieces:
            arrays += [p.held[0], p.came[0]]

        def kernel(own, *refs):
            away, keep = refs[-2:]
            for here in (0, 1):

                @pl.when(own[0] == here)
                def _(here=here):
                    for out, which in ((keep, here), (away, 1 - here)):
                        for i, (low, high), (left, right), row, column in rule(which):
                            p = pieces[i]
                            at, came = p.held[1] + low, p.came[1] + low
                            out[row : row + high - low, column : column + right - left] = refs[2 * i][
                                at : at + high - low, left:right
                            ].astype(F32) + refs[2 * i + 1][came : came + high - low, left:right].astype(F32)

        size = sum(a.size * jnp.dtype(a.dtype).itemsize for a in arrays) + 8 * rows * columns
        return pl.pallas_call(
            kernel,
            name="split_rows",
            out_shape=[jax.ShapeDtypeStruct((rows, columns), F32)] * 2,
            in_specs=[pl.BlockSpec(memory_space=pltpu.SMEM)]
            + [pl.BlockSpec(memory_space=pltpu.VMEM)] * len(arrays),
            compiler_params=pltpu.CompilerParams(vmem_limit_bytes=size + (2 << 20)),
            cost_estimate=pl.CostEstimate(flops=0, bytes_accessed=0, transcendentals=0),
        )(core, *arrays)

    def adam_joined(keep, came, blocks, weight, first_moment, second_moment):
        span = keep.shape[1] // blocks

        def kernel(own, keep, came, weight, first, second, *outs):
            low_is_own = own[0] == 0
            for i in range(blocks):
                mine, other = keep[:, i * span : (i + 1) * span], came[:, i * span : (i + 1) * span]
                for j, values in enumerate(
                    (jnp.where(low_is_own, mine, other), jnp.where(low_is_own, other, mine))
                ):
                    at = slice((2 * i + j) * span, (2 * i + j + 1) * span)
                    made = adam_update(weight[:, at], values, first[:, at], second[:, at], factor, 0.05)
                    for out, value in zip(outs, (values, *made)):
                        out[:, at] = value

        size = 4 * (2 * keep.size + 7 * weight.size)
        gradient, *updated = pl.pallas_call(
            kernel,
            name="adam_joined",
            out_shape=[jax.ShapeDtypeStruct(weight.shape, F32)] * 4,
            in_specs=[pl.BlockSpec(memory_space=pltpu.SMEM)] + [pl.BlockSpec(memory_space=pltpu.VMEM)] * 5,
            compiler_params=pltpu.CompilerParams(vmem_limit_bytes=size + (2 << 20)),
            cost_estimate=pl.CostEstimate(flops=0, bytes_accessed=0, transcendentals=0),
        )(core, keep, came, weight, first_moment, second_moment)
        return gradient, updated

    def finish_up():
        away, keep = split_rows(
            scatter_up.pieces,
            ff_half,
            lambda c: [(i, (c * rows, (c + 1) * rows), (0, width), 0, i * width) for i in (0, 1)],
        )
        return adam_joined(keep, swap_core(away), chips, mlp_in, first_mlp_in, second_mlp_in)

    def finish_mlp():
        shard_down = jnp.concatenate(scatter_down.result(bits), axis=0)
        if paired:
            shard_up, adam_up = finish_up()
        else:
            shard_up = trade(jnp.concatenate(scatter_up.result(bits), axis=1), chips)
            adam_up = adam(mlp_in, shard_up, first_mlp_in, second_mlp_in)
        return shard_up, shard_down, adam_up, adam(mlp_out, shard_down, first_mlp_out, second_mlp_out)

    send_output = Rider(output, 0, local_len, local_len)
    send_grad = Rider(grad_low, 0, local_len, local_len)
    rest = [scatter_in, *scatter_out, total]
    if scatter_up.left():
        phase(bits, [*rest, (scatter_up, 9)], None)
    grad_up_shard, shard_down, adam_up, adam_down = phase(
        bits, [*rest, send_output], finish_mlp, also=[scatter_up, scatter_down]
    )

    def back_to_rows(array, other):
        mine = array[:local_len]
        return jnp.stack([pick(own_y, mine, other), pick(own_y, other, mine)], axis=0)

    output = phase(bits, [*rest, send_grad], back_to_rows, output, send_output.result())
    while scatter_in.left():
        phase(bits, rest, None)
    while total.left() > 1:
        phase(bits, [total], None)
    if total.left():
        phase(bits, [total], None)
    input_grad = back_to_rows(grad_low, send_grad.result())
    narrow = total.result()
    if paired:

        def in_rule(c):
            left = [(0, (0, rows), (0, width), 0, 0)]
            if c == 1:
                left = [
                    (0, (rows, 3 * quarter), (0, width), 0, 0),
                    (1, (0, quarter), (0, width), 3 * quarter - rows, 0),
                ]
            return [*left, (2, (0, rows), (c * half, (c + 1) * half), 0, width)]

        away, keep = split_rows(scatter_in.pieces, in_width, in_rule)
        grad_in_shard, adam_in = adam_joined(keep, swap_core(away), 3, attn_in, first_attn_in, second_attn_in)
        away, keep = split_rows(
            scatter_out[0].pieces,
            half,
            lambda c: [(i, (0, quarter), (c * half, (c + 1) * half), i * quarter, 0) for i in (0, 1)],
        )
        grad_out_shard, adam_out = adam_joined(
            keep, swap_core(away), 1, attn_out, first_attn_out, second_attn_out
        )
    else:
        shard_in = jnp.concatenate(scatter_in.result(bits), axis=1)
        grad_out_shard, grad_in_shard = trade(shard_in[:, in_width:], 1), trade(shard_in[:, :in_width], 3)
        adam_in = adam(attn_in, grad_in_shard, first_attn_in, second_attn_in)
        adam_out = adam(attn_out, grad_out_shard, first_attn_out, second_attn_out)
    updated = [adam_in, adam_out, adam_up, adam_down]
    device = (lax.axis_index("img") * halves + own_y) * 2 + own_c
    grad_vectors_shard = lax.dynamic_slice_in_dim(narrow[:vector_count], device * rows, rows, 1).T
    table_grad = narrow[vector_count : vector_count + table_size]

    shards = (grad_in_shard, grad_out_shard, grad_up_shard, shard_down, grad_vectors_shard)
    updated.append(adam_update(vectors, grad_vectors_shard, first_vectors, second_vectors, factor, 0.0))
    return (
        output,
        input_grad,
        table_grad,
        *shards,
        *(updated[i][0] for i in range(5)),
        *(updated[i][1] for i in range(5)),
        *(updated[i][2] for i in range(5)),
    )


def solution(mesh):
    img, seq = mesh.shape["img"], mesh.shape["seq"]
    inner = Mesh(mesh.devices.reshape(img, seq // 2, 2), ("img", "sy", "sc"))
    tokens = P("img", ("sy", "sc"), None)
    shard = P(("img", "sy", "sc"), None)
    return jax.shard_map(
        per_device,
        mesh=inner,
        in_specs=(tokens, tokens, P("img", None), P()) + (shard,) * 15,
        out_specs=(tokens, tokens, P()) + (shard,) * 20,
        check_vma=False,
    )
```

```python
import functools
import math

import jax
import jax.numpy as jnp
from jax import lax
from jax.experimental import pallas as pl
from jax.experimental.pallas import tpu as pltpu
from jax.sharding import Mesh
from jax.sharding import PartitionSpec as P

HEADS = 16
GRID = 7
GRID_HI = 12
TILE = 128

PRECISE = lax.Precision.HIGHEST
FIRST_CORRECTION = 0.9999734386011124
SECOND_CORRECTION = 0.0952078528862911
EPS = 1e-06

F32 = jnp.float32
BF16 = jnp.bfloat16


def image_spans(res_row):
    side = jnp.where(res_row == 384, GRID_HI, jnp.where(res_row == 224, GRID, 0)).astype(jnp.int32)
    lengths = side * side
    slots = res_row.shape[0]
    order = jnp.arange(slots, dtype=jnp.int32)
    earlier = order[None, :] < order[:, None]
    starts = jnp.sum(jnp.where(earlier, lengths[None, :], 0), axis=1)
    return side, lengths, starts


def layout(res_row, positions):
    side, lengths, starts = image_spans(res_row)
    slots = res_row.shape[0]
    places = positions[:, None]
    inside = ((places >= starts[None, :]) & (places < (starts + lengths)[None, :])).astype(jnp.int32)
    usable = jnp.sum(inside, axis=1)
    image_number = jnp.arange(slots, dtype=jnp.int32)
    segment = jnp.sum(inside * image_number, axis=1) + (1 - usable) * slots
    start_of = jnp.sum(inside * starts[None, :], axis=1)
    side_of = jnp.sum(inside * side[None, :], axis=1)
    patch_index = (positions - start_of) * usable
    return segment, side_of, patch_index, usable


def key_bounds(res_row, row_len):
    _, lengths, starts = image_spans(res_row)
    total = jnp.sum(lengths)
    firsts = jnp.arange(row_len // TILE, dtype=jnp.int32) * TILE

    def span(positions):
        places = positions[:, None]
        inside = (places >= starts[None, :]) & (places < (starts + lengths)[None, :])
        found = positions < total
        begin = jnp.sum(jnp.where(inside, starts[None, :], 0), axis=1)
        end = jnp.sum(jnp.where(inside, (starts + lengths)[None, :], 0), axis=1)
        return jnp.where(found, begin, total), jnp.where(found, end, row_len)

    begin, _ = span(firsts)
    _, end = span(firsts + (TILE - 1))
    return begin // TILE, (end + TILE - 1) // TILE


def axis_weights(coord, side_of):
    scaled = jnp.maximum((2 * coord + 1) * GRID - GRID_HI, 0)
    lower_fine = scaled // (2 * GRID_HI)
    fraction_fine = (scaled - lower_fine * 2 * GRID_HI).astype(F32) / (2.0 * GRID_HI)
    resized = side_of == GRID_HI
    lower_cell = jnp.where(resized, lower_fine, coord)
    fraction = jnp.where(resized, fraction_fine, jnp.zeros_like(fraction_fine))
    upper_cell = jnp.minimum(lower_cell + 1, GRID - 1)
    cell_index = jnp.arange(GRID, dtype=jnp.int32)
    below = (cell_index == lower_cell[..., None]).astype(F32)
    above = (cell_index == upper_cell[..., None]).astype(F32)
    return (1.0 - fraction)[..., None] * below + fraction[..., None] * above


def table_weights(side_of, patch_index, usable):
    safe_side = jnp.maximum(side_of, 1)
    row_coord = patch_index // safe_side
    column_coord = patch_index % safe_side
    outer = axis_weights(row_coord, side_of)[:, :, None] * axis_weights(column_coord, side_of)[:, None, :]
    outer = outer * usable.astype(F32)[:, None, None]
    return outer.reshape(side_of.shape[0], GRID * GRID)


def place_of(block, own_y, own_c, per):
    quarter = block // per
    core = (quarter % 2 + own_c) % 2
    half = (quarter // 2 + own_y) % 2
    return (core * 2 + half) * per + block % per


def split_heads(pair):
    lane = lax.broadcasted_iota(jnp.int32, pair.shape, 1)
    zero = jnp.zeros_like(pair)
    low = lane < pair.shape[1] // 2
    return jnp.concatenate([jnp.where(low, pair, zero), jnp.where(low, zero, pair)], axis=0)


def join_heads(stacked):
    half = stacked.shape[0] // 2
    lane = lax.broadcasted_iota(jnp.int32, (half, stacked.shape[1]), 1)
    return jnp.where(lane < stacked.shape[1] // 2, stacked[:half], stacked[half:])


def down_lanes(row):
    return jnp.transpose(jnp.broadcast_to(row, (TILE, TILE)))


def nt(left, right):
    return lax.dot_general(left, right, (((1,), (1,)), ((), ())), preferred_element_type=F32)


def tn(left, right):
    return lax.dot_general(left, right, (((0,), (0,)), ((), ())), preferred_element_type=F32)


def nn(left, right):
    return jnp.dot(left, right, preferred_element_type=F32)


def fold(array, over):
    parts = array.reshape(array.shape[0] // 8, 8, array.shape[1])
    return jnp.max(parts, axis=0) if over == "max" else jnp.sum(parts, axis=0)


def same_segment(seg_down, chunk, seg_q):
    same = seg_down[chunk] == seg_q
    return jnp.concatenate([same, same], axis=1)


def fill_segments(seg, seg_down):
    chunks, span, _ = seg_down.shape
    for chunk in range(chunks):
        row = seg[0:1, chunk * span : (chunk + 1) * span]
        seg_down[chunk] = jnp.transpose(jnp.broadcast_to(row, (TILE, span)))


def join_turned(turned):
    half = turned.shape[1] // 2
    row = lax.broadcasted_iota(jnp.int32, (turned.shape[0], half), 0)
    return jnp.transpose(jnp.where(row < turned.shape[0] // 2, turned[:, :half], turned[:, half:]))


def columns_of(base, j):
    return slice(base + j * TILE, base + (j + 1) * TILE)


def attend_kernel(pairs, width, per, scale, info, qkv, seg, out, log_sum, scores, turned, seg_down):
    tile = pl.program_id(0)
    chunks, span, _ = seg_down.shape
    own_y, own_c = info[0], info[1]
    ratio = span // TILE
    first = info[2 + tile] // ratio
    last = (info[2 + pl.num_programs(0) + tile] + ratio - 1) // ratio

    def at(chunk):
        return pl.multiple_of(place_of(chunk * ratio, own_y, own_c, per) * TILE, TILE)

    @pl.when(tile == 0)
    def _():
        fill_segments(seg, seg_down)
        for chunk in range(chunks):
            for j in range(pairs):
                turned[chunk, j] = jnp.transpose(qkv[pl.ds(at(chunk), span), columns_of(2 * width, j)])

    q_at = pl.multiple_of(place_of(tile, own_y, own_c, per) * TILE, TILE)
    seg_q = seg[0:1, pl.ds(pl.multiple_of(tile * TILE, TILE), TILE)]
    queries = [
        split_heads(qkv[pl.ds(q_at, TILE), columns_of(0, j)] * jnp.asarray(scale, BF16)) for j in range(pairs)
    ]

    def score(chunk, high):
        same = same_segment(seg_down, chunk, seg_q)
        products = [nt(qkv[pl.ds(at(chunk), span), columns_of(width, j)], queries[j]) for j in range(pairs)]
        made = []
        for j in range(pairs):
            s = jnp.where(same, products[j], -1e30)
            scores[j, chunk] = s
            made.append(jnp.maximum(high[j], fold(s, "max")))
        return tuple(made)

    high = lax.fori_loop(first, last, score, (jnp.full((8, 2 * TILE), -1e30, F32),) * pairs)
    tops = [jnp.max(high[j], axis=0, keepdims=True) for j in range(pairs)]

    def mix(chunk, carry):
        total, mixed = carry
        powers = [jnp.exp(scores[j, chunk] - tops[j]) for j in range(pairs)]
        return (
            tuple(total[j] + fold(powers[j], "sum") for j in range(pairs)),
            tuple(mixed[j] + nn(turned[chunk, j], powers[j].astype(BF16)) for j in range(pairs)),
        )

    total, mixed = lax.fori_loop(
        first,
        last,
        mix,
        ((jnp.zeros((8, 2 * TILE), F32),) * pairs, (jnp.zeros((TILE, 2 * TILE), F32),) * pairs),
    )
    for j in range(pairs):
        sums = jnp.sum(total[j], axis=0, keepdims=True)
        out[:, columns_of(0, j)] = join_turned(mixed[j] / sums).astype(BF16)
        log_total = tops[j] + jnp.log(sums)
        log_sum[2 * j : 2 * j + 1] = log_total[:, :TILE]
        log_sum[2 * j + 1 : 2 * j + 2] = log_total[:, TILE:]


def attend_back_kernel(
    start, pairs, width, per, scale, info, qkv, mixed, grad, seg, log_sum, out, grad_keys, grad_values, turned, seg_down
):
    tile = pl.program_id(0)
    chunks, span, _ = seg_down.shape
    own_y, own_c = info[0], info[1]
    ratio = span // TILE
    first = info[2 + tile] // ratio
    last = (info[2 + pl.num_programs(0) + tile] + ratio - 1) // ratio
    heads = range(start, start + pairs)

    def at(chunk):
        return pl.multiple_of(place_of(chunk * ratio, own_y, own_c, per) * TILE, TILE)

    @pl.when(tile == 0)
    def _():
        fill_segments(seg, seg_down)
        grad_keys[...] = jnp.zeros_like(grad_keys)
        grad_values[...] = jnp.zeros_like(grad_values)
        for chunk in range(chunks):
            for i, j in enumerate(heads):
                turned[chunk, i] = jnp.transpose(qkv[pl.ds(at(chunk), span), columns_of(width, j)])

    q_at = pl.multiple_of(place_of(tile, own_y, own_c, per) * TILE, TILE)
    q_from = pl.multiple_of(tile * TILE, TILE)
    seg_q = seg[0:1, pl.ds(q_from, TILE)]
    queries, grads, logs, inner = [], [], [], []
    for j in heads:
        queries.append(split_heads(qkv[pl.ds(q_at, TILE), columns_of(0, j)] * jnp.asarray(scale, BF16)))
        g = grad[pl.ds(q_at, TILE), columns_of(0, j)]
        grads.append(split_heads(g))
        both = jnp.transpose(g.astype(F32) * mixed[pl.ds(q_at, TILE), columns_of(0, j)].astype(F32))
        low = jnp.sum(both[: TILE // 2], axis=0, keepdims=True)
        high = jnp.sum(both[TILE // 2 :], axis=0, keepdims=True)
        inner.append(jnp.concatenate([low, high], axis=1))
        here = log_sum[2 * j : 2 * j + 2, pl.ds(q_from, TILE)]
        logs.append(jnp.concatenate([here[0:1], here[1:2]], axis=1))

    def step(chunk, carry):
        k_at = at(chunk)
        same = same_segment(seg_down, chunk, seg_q)
        scores = [nt(qkv[pl.ds(k_at, span), columns_of(width, j)], queries[i]) for i, j in enumerate(heads)]
        slopes = [nt(qkv[pl.ds(k_at, span), columns_of(2 * width, j)], grads[i]) for i, j in enumerate(heads)]
        powers = [jnp.exp(jnp.where(same, scores[i], -1e30) - logs[i]) for i in range(pairs)]
        changes = [(powers[i] * (slopes[i] - inner[i])).astype(BF16) for i in range(pairs)]
        to_values = [nn(powers[i].astype(BF16), grads[i]) for i in range(pairs)]
        to_keys = [nn(changes[i], queries[i]) for i in range(pairs)]
        to_query = tuple(carry[i] + nn(turned[chunk, i], changes[i]) for i in range(pairs))
        for i in range(pairs):
            grad_values[chunk, :, columns_of(0, i)] += to_values[i]
            grad_keys[chunk, :, columns_of(0, i)] += to_keys[i]
        return to_query

    grad_query = lax.fori_loop(first, last, step, (jnp.zeros((TILE, 2 * TILE), F32),) * pairs)
    for i in range(pairs):
        out[pl.ds(q_at, TILE), columns_of(0, i)] = (join_turned(grad_query[i]) * scale).astype(BF16)

    @pl.when(tile == pl.num_programs(0) - 1)
    def _():
        all_heads = pairs * TILE
        for chunk in range(chunks):
            out[pl.ds(at(chunk), span), all_heads : 2 * all_heads] = grad_keys[chunk].astype(BF16)
            out[pl.ds(at(chunk), span), 2 * all_heads :] = grad_values[chunk].astype(BF16)


def attention(qkv, seg, info, per, head_size):
    length, width = qkv.shape[0], qkv.shape[1] // 3
    pairs, tiles = width // TILE, length // TILE
    span = per * TILE
    chunks = length // span
    scale = head_size ** (-0.5)

    def place(i, info):
        return place_of(i, info[0], info[1], per)

    return pl.pallas_call(
        functools.partial(attend_kernel, pairs, width, per, scale),
        name="attend",
        out_shape=(
            jax.ShapeDtypeStruct((length, width), BF16),
            jax.ShapeDtypeStruct((2 * pairs, length), F32),
        ),
        grid_spec=pltpu.PrefetchScalarGridSpec(
            num_scalar_prefetch=1,
            grid=(tiles,),
            in_specs=[
                pl.BlockSpec(qkv.shape, lambda i, info: (0, 0), pipeline_mode=pl.Buffered(1)),
                pl.BlockSpec(seg.shape, lambda i, info: (0, 0), pipeline_mode=pl.Buffered(1)),
            ],
            out_specs=[
                pl.BlockSpec((TILE, width), lambda i, info: (place(i, info), 0)),
                pl.BlockSpec((2 * pairs, TILE), lambda i, info: (0, i)),
            ],
            scratch_shapes=[
                pltpu.VMEM((pairs, chunks, span, 2 * TILE), F32),
                pltpu.VMEM((chunks, pairs, TILE, span), BF16),
                pltpu.VMEM((chunks, span, TILE), F32),
            ],
        ),
        compiler_params=pltpu.CompilerParams(
            dimension_semantics=("arbitrary",), vmem_limit_bytes=20 << 20
        ),
        cost_estimate=pl.CostEstimate(flops=0, bytes_accessed=0, transcendentals=0),
    )(info, qkv, seg)


def attention_back(part, parts, qkv, mixed, grad, seg, log_sum, info, per, head_size):
    length, width = qkv.shape[0], qkv.shape[1] // 3
    pairs, tiles = width // TILE // parts, length // TILE
    span = per * TILE
    chunks = length // span
    out = jax.ShapeDtypeStruct((length, 3 * pairs * TILE), BF16)
    scale = head_size ** (-0.5)

    def whole(array):
        return pl.BlockSpec(array.shape, lambda i, info: (0, 0), pipeline_mode=pl.Buffered(1))

    return pl.pallas_call(
        functools.partial(attend_back_kernel, part * pairs, pairs, width, per, scale),
        name="attend_back",
        out_shape=out,
        grid_spec=pltpu.PrefetchScalarGridSpec(
            num_scalar_prefetch=1,
            grid=(tiles,),
            in_specs=[whole(qkv), whole(mixed), whole(grad), whole(seg), whole(log_sum)],
            out_specs=pl.BlockSpec(out.shape, lambda i, info: (0, 0)),
            scratch_shapes=[
                pltpu.VMEM((chunks, span, pairs * TILE), F32),
                pltpu.VMEM((chunks, span, pairs * TILE), F32),
                pltpu.VMEM((chunks, pairs, TILE, span), BF16),
                pltpu.VMEM((chunks, span, TILE), F32),
            ],
        ),
        compiler_params=pltpu.CompilerParams(
            dimension_semantics=("arbitrary",), vmem_limit_bytes=28 << 20
        ),
        cost_estimate=pl.CostEstimate(
            flops=32 * length * length * width, bytes_accessed=8 * length * width * 2, transcendentals=0
        ),
    )(info, qkv, mixed, grad, seg, log_sum)


SWAP = [(0, 1), (1, 0)]


def swap_core(array):
    return lax.ppermute(array, "sc", SWAP)


def swap_chip(array):
    return lax.ppermute(array, "sy", SWAP)


def swap_bit(array, bit):
    if bit == 0:
        return swap_chip(array)
    count = lax.axis_size("img")
    return lax.ppermute(array, "img", [(i, i ^ (1 << (bit - 1))) for i in range(count)])


def own_bit(bit):
    if bit == 0:
        return lax.axis_index("sy")
    return (lax.axis_index("img") >> (bit - 1)) & 1


def fence(*values):
    return lax.optimization_barrier(values)


def axis_of(bit, done):
    return sum(1 for other in done if other > bit)


def pick(index, low, high):
    return jnp.where(index == 0, low, high)


def far_bits():
    return list(range(2, int(math.log2(lax.axis_size("img"))) + 1))


def join(first, second, axis):
    shape = list(first.shape)
    shape[axis] += second.shape[axis]
    held = lax.dynamic_update_slice_in_dim(jnp.zeros(shape, first.dtype), first, 0, axis)
    return lax.dynamic_update_slice_in_dim(held, second, first.shape[axis], axis)


class Turn:
    def __init__(self):
        self.arrays, self.shapes, self.jobs = [], [], []
        self.kept = None

    def keep(self, rows, columns):
        if self.kept is None:
            self.kept = self.write((0, columns), BF16)
        before = self.shapes[self.kept].shape[0]
        self.shapes[self.kept] = jax.ShapeDtypeStruct((before + rows, columns), BF16)
        return self.kept, before

    def read(self, array):
        for i, other in enumerate(self.arrays):
            if other is array:
                return i
        self.arrays.append(array)
        return len(self.arrays) - 1

    def write(self, shape, dtype):
        self.shapes.append(jax.ShapeDtypeStruct(shape, dtype))
        return len(self.shapes) - 1

    def run(self, bits):
        count = len(self.arrays)

        def kernel(own, *refs):
            mine = [own[i] for i in range(bits.shape[0])]
            for job in self.jobs:
                job(mine, refs[:count], refs[count:])

        spent = sum(a.size * jnp.dtype(a.dtype).itemsize for a in [*self.arrays, *self.shapes])
        return pl.pallas_call(
            kernel,
            name="turn",
            out_shape=tuple(self.shapes),
            in_specs=[pl.BlockSpec(memory_space=pltpu.SMEM)] + [pl.BlockSpec(memory_space=pltpu.VMEM)] * count,
            out_specs=tuple(pl.BlockSpec(memory_space=pltpu.VMEM) for _ in self.shapes),
            compiler_params=pltpu.CompilerParams(vmem_limit_bytes=spent + (2 << 20)),
            cost_estimate=pl.CostEstimate(flops=0, bytes_accessed=0, transcendentals=0),
        )(bits, *self.arrays)


def combinations(bits):
    made = [{}]
    for bit in bits:
        made = [{**choice, bit: value} for choice in made for value in (0, 1)]
    return made


def flat_index(choice, bits):
    at = 0
    for bit in sorted(bits, reverse=True):
        at = at * 2 + choice[bit]
    return at


def block_of(at, rows, base=0):
    start = at * rows + base
    if isinstance(start, int):
        return pl.ds(start, rows)
    return pl.ds(pl.multiple_of(start, math.gcd(rows, base) if base else rows), rows)


class Piece:
    def __init__(self, array, rows, bits, order, stride=None, base=0):
        self.held, self.rows, self.bits = (array, base), rows, list(bits)
        self.fixed, self.order, self.came = [], list(order), None
        self.stride, self.source = stride or rows, bool(bits)


class Gather:
    def __init__(self, *parts):
        self.pieces = []
        for array, first, rows, order in parts:
            piece = Piece(array, rows, [], order)
            piece.held = (array, first)
            self.pieces.append(piece)

    def wants(self):
        return [(p.order[0], p.rows << (len(p.bits) + (p.came is not None))) for p in self.pieces]

    def turn(self, turn, places):
        for p, (out, base) in zip(self.pieces, places):
            if p.came is None:
                turn.jobs.append(copy_rows(turn.read(p.held[0]), p.held[1], out, base, p.rows << len(p.bits)))
            else:
                bit = p.sent
                absorb_gather(turn, p, bit, lambda choice, p=p, out=out, base=base: [(out, choice, base)])
            p.sent = p.order.pop(0)
            p.next_held = (out, base)

    def settle(self, outs, came):
        for p, where in zip(self.pieces, came):
            if p.came is not None:
                p.bits.append(p.last)
            p.held, p.came, p.last = (outs[p.next_held[0]], p.next_held[1]), where, p.sent

    def arrays(self):
        return [a for p in self.pieces for a in ([p.held[0]] + ([p.came[0]] if p.came else []))]

    def relabel(self, swap):
        for p in self.pieces:
            p.held = (swap(p.held[0]), p.held[1])
            if p.came:
                p.came = (swap(p.came[0]), p.came[1])

    def left(self):
        return len(self.pieces[0].order)


def gathered(pieces, bits, outs):
    turn = Turn()
    made = [turn.write(shape, BF16) for shape, _ in outs]
    for i, p in enumerate(pieces):
        held, came = turn.read(p.held[0]), turn.read(p.came[0])
        moves = [(out, move) for out, (_, moves) in zip(made, outs) for move in moves[i]]

        def job(mine, ins, refs, p=p, held=held, came=came, moves=moves):
            everyone = [*p.bits, p.last]
            for choice in combinations(p.bits):
                at = flat_index(choice, p.bits)
                for source, base, value in (
                    (ins[held], p.held[1], mine[p.last]),
                    (ins[came], p.came[1], 1 - mine[p.last]),
                ):
                    chip = flat_index({**choice, p.last: value}, everyone)
                    for out, ((low, high), (left, right), stride, row, column) in moves:
                        start = pl.multiple_of(chip * stride + row, math.gcd(stride, row) if row else stride)
                        refs[out][pl.ds(start, high - low), column : column + right - left] = source[
                            pl.ds(base + at * p.rows + low, high - low), left:right
                        ]

        turn.jobs.append(job)
    return turn.run(bits)


class Spread:
    def __init__(self, array):
        self.pieces = [Piece(array, array.shape[0], [], [*reversed(far_bits()), 0, 1])]

    def wants(self):
        return [(self.pieces[0].order[0], self.pieces[0].rows)]

    def turn(self, turn, places):
        [p], [(out, base)] = self.pieces, places
        p.order.pop(0)
        p.next_held = (out, base)
        if p.came is None:
            turn.jobs.append(copy_rows(turn.read(p.held[0]), p.held[1], out, base, p.rows))
            return
        held, came, held_base, came_base, rows = turn.read(p.held[0]), turn.read(p.came[0]), p.held[1], p.came[1], p.rows

        def job(mine, ins, refs):
            refs[out][base : base + rows] = (
                ins[held][held_base : held_base + rows] + ins[came][came_base : came_base + rows]
            )

        turn.jobs.append(job)

    def settle(self, outs, came):
        [p] = self.pieces
        p.held, p.came = (outs[p.next_held[0]], p.next_held[1]), came[0]

    arrays, relabel, left = Gather.arrays, Gather.relabel, Gather.left

    def result(self):
        [p] = self.pieces
        return sum(array[base : base + p.rows] for array, base in (p.held, p.came))


class Rider:
    def __init__(self, array, bit, first, rows):
        self.pieces = [Piece(array, rows, [], [bit])]
        self.pieces[0].held = (array, first)

    wants, turn, settle = Spread.wants, Spread.turn, Spread.settle
    arrays, relabel, left = Gather.arrays, Gather.relabel, Gather.left

    def result(self):
        [p] = self.pieces
        return p.came[0][p.came[1] : p.came[1] + p.rows]


class Total:
    def __init__(self, array, order):
        self.pieces = [Piece(array, array.shape[0], [], order)]

    wants, arrays, relabel, left = Spread.wants, Gather.arrays, Gather.relabel, Gather.left

    def turn(self, turn, places):
        [p], [(out, base)] = self.pieces, places
        p.order.pop(0)
        held, rows = turn.read(p.held[0]), p.rows
        came, came_base = (None, 0) if p.came is None else (turn.read(p.came[0]), p.came[1])
        p.next = None if came is None else turn.write(p.held[0].shape, F32)

        def job(mine, ins, refs, keep=p.next):
            own = ins[held][...].astype(BF16)
            if came is not None:
                total = own.astype(F32) + ins[came][came_base : came_base + rows].astype(F32)
                refs[keep][...] = total
                own = total.astype(BF16)
            refs[out][base : base + rows] = own

        turn.jobs.append(job)

    def settle(self, outs, came):
        [p] = self.pieces
        if p.next is not None:
            p.held = (outs[p.next], 0)
        p.came = came[0]

    def result(self):
        [p] = self.pieces
        return add_came(p.held[0], p.came[0][p.came[1] : p.came[1] + p.rows])


def copy_rows(source, source_base, out, base, rows):
    def job(mine, ins, refs):
        refs[out][base : base + rows] = ins[source][source_base : source_base + rows]

    return job


def absorb_gather(turn, p, bit, targets):
    held, came = turn.read(p.held[0]), turn.read(p.came[0])
    last = p.last
    known = list(p.bits)
    held_base, came_base, rows = p.held[1], p.came[1], p.rows
    [(out, _, base)] = targets(None)

    def job(mine, ins, refs):
        for choice in combinations(known):
            at = flat_index(choice, known)
            for source, start, value in ((held, held_base, mine[last]), (came, came_base, 1 - mine[last])):
                to = flat_index({**choice, last: value}, [*known, last])
                refs[out][block_of(to, rows, base)] = ins[source][block_of(at, rows, start)]

    turn.jobs.append(job)


class Scatter:
    def __init__(self, *parts):
        far = far_bits()
        bits = sorted([0, 1, *far], reverse=True)
        self.pieces = [
            Piece(array, rows, bits, [*((1, 0) if turned else (0, 1)), *far], stride, first)
            for array, rows, stride, first, turned in parts
        ]

    def wants(self):
        return [(p.order[0], p.rows << (len(p.bits) - len(p.fixed) - 1)) for p in self.pieces]

    def turn(self, turn, places):
        for p, (out, base) in zip(self.pieces, places):
            bit = p.order.pop(0)
            free = [b for b in p.bits if b not in p.fixed and b != bit]
            rows, bits, fixed = p.rows, list(p.bits), list(p.fixed)
            held = turn.read(p.held[0])
            stride, first = p.stride, p.held[1]

            def block(choice, bits=bits, stride=stride, first=first, rows=rows):
                start = flat_index(choice, bits) * stride + first
                return pl.ds(pl.multiple_of(start, math.gcd(stride, first) if first else stride), rows)

            if p.came is None:
                p.next = None

                def job(mine, ins, refs, held=held, rows=rows, free=free, bit=bit, out=out, base=base, block=block):
                    for choice in combinations(free):
                        refs[out][block_of(flat_index(choice, free), rows, base)] = ins[held][
                            block({**choice, bit: 1 - mine[bit]})
                        ]

            else:
                came, came_base = turn.read(p.came[0]), p.came[1]
                keep, keep_base = turn.keep(rows << len(free), p.held[0].shape[1])
                p.next = (keep, keep_base)

                def job(
                    mine, ins, refs, held=held, rows=rows, fixed=fixed, free=free, bit=bit, out=out, base=base,
                    came=came, came_base=came_base, keep=keep, keep_base=keep_base, block=block,
                ):
                    settled = {b: mine[b] for b in fixed}
                    for choice in combinations(free):
                        for value, target, start in ((1 - mine[bit], out, base), (mine[bit], keep, keep_base)):
                            now = {**choice, bit: value}
                            total = ins[held][block({**now, **settled})].astype(F32) + ins[came][
                                block_of(flat_index(now, [*free, bit]), rows, came_base)
                            ].astype(F32)
                            refs[target][block_of(flat_index(choice, free), rows, start)] = total.astype(BF16)

            turn.jobs.append(job)
            p.sent, p.free = bit, free

    def settle(self, outs, came):
        for p, where in zip(self.pieces, came):
            if p.next is None:
                p.fixed = [p.sent]
            else:
                p.held, p.bits, p.fixed = (outs[p.next[0]], p.next[1]), list(p.free), []
                p.stride, p.source = p.rows, False
            p.came = where

    arrays, relabel, left = Gather.arrays, Gather.relabel, Gather.left

    def result(self, bits):
        turn = Turn()
        for p in self.pieces:
            held, came, base, rows, first = turn.read(p.held[0]), turn.read(p.came[0]), p.came[1], p.rows, p.held[1]
            out = turn.write((rows, p.held[0].shape[1]), F32)

            def job(mine, ins, refs, held=held, came=came, base=base, rows=rows, out=out, first=first):
                refs[out][...] = ins[held][first : first + rows].astype(F32) + ins[came][base : base + rows].astype(F32)

            turn.jobs.append(job)
        return turn.run(bits)


def swap_rows(moves, bits):
    wants = [move.wants() for move in moves]
    sizes, places = {}, []
    for bit, rows in (want for group in wants for want in group):
        places.append((bit, sizes.get(bit, 0)))
        sizes[bit] = sizes.get(bit, 0) + rows
    turn = Turn()
    width = moves[0].pieces[0].held[0].shape[1]
    outs = {bit: turn.write((rows, width), BF16) for bit, rows in sizes.items()}
    located = [(outs[bit], base) for bit, base in places]
    starts = [0]
    for move in moves:
        starts.append(starts[-1] + len(move.pieces))
    for i, move in enumerate(moves):
        move.turn(turn, located[starts[i] : starts[i + 1]])
    made = turn.run(bits)
    got = {bit: swap_bit(made[out], bit) for bit, out in outs.items()}
    came = [(got[bit], base) for bit, base in places]
    for i, move in enumerate(moves):
        move.settle(made, came[starts[i] : starts[i + 1]])


def add_came(own, came):
    return own.astype(BF16).astype(F32) + came.astype(F32)


def add_hop(array, bit):
    return add_came(array, swap_bit(array.astype(BF16), bit))


def phase(bits, moves, work, *values, also=()):
    chains = [move if isinstance(move, tuple) else (move, 1) for move in moves]
    chains = [
        ([move for move in chain[:-1] if move.left()], min(chain[-1], chain[0].left())) for chain in chains
    ]
    moves = [move for chain, _ in chains for move in chain]

    def tie(extra):
        arrays = []
        for array in (a for move in [*moves, *also] for a in move.arrays()):
            if not any(array is other for other in arrays):
                arrays.append(array)
        held, extra = fence(arrays, extra)
        table = list(zip(arrays, held))
        for move in [*moves, *also]:
            move.relabel(lambda array: next(new for old, new in table if old is array))
        return extra

    values = tie(values)
    if moves:
        swap_rows(moves, bits)
    for chain, count in chains:
        for _ in range(count - 1):
            swap_rows(chain, bits)
    made = work(*values) if work else ()
    return tie(made)


def by_rows(body, rows, whole, outs, sums=0, tile=TILE, name="rows"):
    rows = [array if isinstance(array, tuple) else (array, 0, array.shape[0]) for array in rows]
    length = rows[0][2]
    width = outs[0][0]

    def kernel(*refs):
        ins, results = refs[: len(rows) + len(whole)], refs[len(rows) + len(whole) :]
        made = body(*(ref[...] for ref in ins))
        for ref, value in zip(results, made):
            if ref.shape[0] == 1:

                @pl.when(pl.program_id(0) == 0)
                def _(ref=ref):
                    ref[...] = jnp.zeros_like(ref)

                ref[...] += value
            else:
                ref[...] = value.astype(ref.dtype)

    spent = sum(array.size * array.dtype.itemsize for array in whole)
    for columns, kind in [*outs, *((array.shape[1], array.dtype) for array, _, _ in rows)]:
        spent += 2 * tile * columns * jnp.dtype(kind).itemsize

    def steps(columns, first=0):
        return pl.BlockSpec((tile, columns), lambda i: (i + first // tile, 0))

    def fixed(shape, **how):
        return pl.BlockSpec(shape, lambda i: (0,) * len(shape), **how)

    return pl.pallas_call(
        kernel,
        name=name,
        grid=(length // tile,),
        out_shape=[jax.ShapeDtypeStruct((length, columns), dtype) for columns, dtype in outs]
        + [jax.ShapeDtypeStruct((1, width), F32)] * sums,
        in_specs=[steps(array.shape[1], first) for array, first, _ in rows]
        + [fixed(array.shape, pipeline_mode=pl.Buffered(1)) for array in whole],
        out_specs=[steps(columns) for columns, _ in outs] + [fixed((1, width))] * sums,
        compiler_params=pltpu.CompilerParams(
            dimension_semantics=("arbitrary",), vmem_limit_bytes=spent + (12 << 20)
        ),
        cost_estimate=pl.CostEstimate(flops=0, bytes_accessed=0, transcendentals=0),
    )(*(array for array, _, _ in rows), *whole)


def normalize(stream):
    center = jnp.mean(stream, axis=-1, keepdims=True)
    centered = stream - center
    spread = jnp.mean(centered * centered, axis=-1, keepdims=True)
    inverse = lax.rsqrt(spread + EPS)
    return centered * inverse, inverse


def normalize_back(normed, inverse, gain, grad):
    scaled = grad * gain
    middle = jnp.mean(scaled, axis=-1, keepdims=True)
    along = jnp.mean(scaled * normed, axis=-1, keepdims=True)
    return (
        inverse[:, :1] * (scaled - middle - normed * along),
        jnp.sum(grad * normed, axis=0, keepdims=True),
        jnp.sum(grad, axis=0, keepdims=True),
    )


def rows_from(columns, count):
    one_hot = (jnp.arange(16)[:, None] == jnp.arange(TILE)[None, :]).astype(BF16)
    rows = nt(one_hot, columns)
    return [rows[i : i + 1] for i in range(count)]


def column_choice(rows, columns):
    row, lane = jnp.arange(rows)[:, None], jnp.arange(TILE)[None, :]
    return (row == 8 + lane % columns).astype(F32)


def own_place(width, columns):
    per_run = TILE // columns
    row, lane = jnp.arange(width)[:, None], jnp.arange(TILE)[None, :]
    return row % per_run == lane // columns


def unroll_bias(columns, own_c, ff_rows):
    width, extra = columns.shape[0], 4
    spread = nn(columns, column_choice(TILE, extra).astype(BF16))
    runs = jnp.where(own_place(width, extra), spread, 0.0).reshape(-1, TILE // extra, TILE).sum(axis=1)
    runs = runs.reshape(-1, 2, ff_rows)
    return pick(own_c, runs[:, 0], runs[:, 1]).reshape(1, -1)


def roll_bias(sums, own_c, width, rows, ff_rows):
    extra = 4
    runs = sums.reshape(-1, ff_rows)
    zero = jnp.zeros_like(runs)
    runs = jnp.stack([pick(own_c, runs, zero), pick(own_c, zero, runs)], axis=1).reshape(-1, 1, TILE)
    spread = jnp.broadcast_to(runs, (runs.shape[0], TILE // extra, TILE)).reshape(width, TILE)
    spread = jnp.where(own_place(width, extra), spread, 0.0)
    return lax.dot_general(
        column_choice(rows, extra), spread, (((1,), (1,)), ((), ())), precision=PRECISE, preferred_element_type=F32
    )


def token_sums(array):
    return nn(jnp.ones((8, array.shape[0]), BF16), array)[:1]


def gelu_and_slope(values):
    cdf = 0.5 * (1.0 + lax.erf(values * (0.5**0.5)))
    density = jnp.exp(-0.5 * values * values) * (1.0 / math.sqrt(2.0 * math.pi))
    return values * cdf, cdf + values * density


def adam_update(weight, gradient, first_moment, second_moment, factor, decay):
    scaled = gradient * factor
    first_new = 0.9 * first_moment + 0.1 * scaled
    second_new = 0.999 * second_moment + 0.001 * scaled * scaled
    first_hat = first_new / FIRST_CORRECTION
    second_hat = second_new / SECOND_CORRECTION
    direction = first_hat / (jnp.sqrt(second_hat) + 1e-08) + decay * weight
    return (direction, first_new, second_new)


def per_device(
    patches,
    cotangent,
    res_ids,
    pos_table,
    attn_in,
    attn_out,
    mlp_in,
    mlp_out,
    vectors,
    first_attn_in,
    first_attn_out,
    first_mlp_in,
    first_mlp_out,
    first_vectors,
    second_attn_in,
    second_attn_out,
    second_mlp_in,
    second_mlp_out,
    second_vectors,
):
    row_count, local_len, width = patches.shape
    img_count, halves = lax.axis_size("img"), lax.axis_size("sy")
    chips = img_count * halves
    row_len = local_len * halves * 2
    slot_total = row_count * img_count * row_len
    head_size = width // HEADS
    own_y, own_c = lax.axis_index("sy"), lax.axis_index("sc")
    rows = attn_in.shape[0]
    half = width // 2
    ff_rows = mlp_out.shape[0]
    ff_half = chips * ff_rows
    table_size = GRID * GRID
    vector_count = vectors.shape[1]

    bits = jnp.stack([own_bit(bit) for bit in [0, 1, *far_bits()]]).astype(jnp.int32)

    def to_rows(array):
        mine = lax.dynamic_index_in_dim(array, own_y, 0, keepdims=False)
        other = lax.dynamic_index_in_dim(array, 1 - own_y, 0, keepdims=False)
        return join(mine, swap_chip(other), 0)

    res_row = pick(own_y, res_ids[0], res_ids[1])
    all_positions = jnp.arange(row_len, dtype=jnp.int32)
    segment_all, _, _, _ = layout(res_row, all_positions)
    seg = jnp.broadcast_to(segment_all.astype(F32)[None, :], (8, row_len))
    begin, end = key_bounds(res_row, row_len)
    info = jnp.concatenate([jnp.stack([own_y, own_c]).astype(jnp.int32), begin, end])
    near = jnp.arange(local_len, dtype=jnp.int32)
    positions = jnp.concatenate(
        [(2 * own_y + own_c) * local_len + near, (2 * (1 - own_y) + own_c) * local_len + near]
    )
    _, side_of, patch_index, usable = layout(res_row, positions)
    place = table_weights(side_of, patch_index, usable)
    usable = usable.astype(F32)[:, None]

    def by_core(array, blocks):
        split = array.reshape(rows, blocks, 2, -1)
        low, high = split[:, :, 0].reshape(rows, -1), split[:, :, 1].reshape(rows, -1)
        return pick(own_c, low, high), pick(own_c, high, low)

    vector_pad = jnp.pad(vectors, ((0, 0), (0, TILE - vector_count))).astype(BF16)
    mine_in, away_in = by_core(attn_in.astype(BF16), 3)
    mine_out, away_out = by_core(attn_out.astype(BF16), 1)
    mine_up, away_up = by_core(mlp_in.astype(BF16), chips)
    mine = jnp.concatenate([mine_in, mine_out, mine_up], axis=1)
    away = jnp.concatenate([away_in, away_out, away_up], axis=1)
    came, came_vector = swap_core(away), swap_core(vector_pad)
    shard = jnp.concatenate([pick(own_c, mine, came), pick(own_c, came, mine)], axis=0)
    vector_shard = jnp.concatenate(
        [pick(own_c, vector_pad, came_vector), pick(own_c, came_vector, vector_pad)], axis=0
    )[:, :16].reshape(1, -1)
    vector_row = jnp.pad(vector_shard, ((0, 0), (0, width - vector_shard.shape[1])))
    chip = lax.axis_index("img") * halves + own_y
    vector_rows = jnp.where(jnp.arange(chips)[:, None] == chip, vector_row, jnp.zeros_like(vector_row))
    in_width = 3 * half
    own = local_len * row_count
    per = local_len // TILE

    def with_core(array):
        return join(array, swap_core(array), 0)

    def sum_core(left, weights, product):
        away = product(left[own:], weights).astype(BF16)
        came = swap_core(away)
        return product(left[:own], weights) + came.astype(F32)

    low_down, high_down = jnp.split(mlp_out.astype(BF16), 2)
    ahead = list(reversed(far_bits()))
    one_way, other_way = [*ahead, 1, 0], [*ahead, 0, 1]
    block = 2 * rows
    gather_in = Gather(
        (shard[:, :width], 0, block, one_way), (shard[:, width : 2 * width], 0, block, other_way)
    )
    gather_vectors = Spread(vector_rows)
    gather_up = Gather(
        (shard[:, 2 * width : 2 * width + half * 2], 0, block, one_way),
        (shard[:, 2 * width + half * 2 :], 0, block, other_way),
    )
    low_down = mlp_out.astype(BF16)
    side = 3 * ff_rows // 8 if ff_rows % 128 == 0 else ff_rows // 2
    rest_rows = ff_rows - 2 * side
    gather_down = Gather((low_down, 0, side, one_way), (low_down, side, side, other_way))
    gather_rest = [Gather((low_down, 2 * side, rest_rows, [1, 0, *ahead]))] if rest_rows else []

    patches, cotangent = phase(
        bits,
        [(gather_in, gather_vectors, len(far_bits())), *gather_rest],
        lambda *arrays: [to_rows(array) for array in arrays],
        patches,
        cotangent,
    )

    wide_place = jnp.pad(place, ((0, 0), (0, TILE - table_size)))
    wide_table = jnp.pad(pos_table, ((0, TILE - table_size), (0, 0)))
    wide_usable = jnp.broadcast_to(usable, (own, TILE))
    small = TILE

    def first(patches, cotangent):
        def body(patches, place, cotangent, usable, table):
            stream = patches.astype(F32) + jnp.dot(place, table, precision=PRECISE, preferred_element_type=F32)
            normed, inverse = normalize(stream)
            grad = cotangent.astype(F32) * usable[:, :1]
            return stream, normed, jnp.broadcast_to(inverse, (stream.shape[0], TILE)), grad

        stream, hat_one, inverse_one, grad_own = by_rows(
            body,
            [patches, wide_place, cotangent, wide_usable],
            [wide_table],
            [(width, F32), (width, F32), (TILE, F32), (width, BF16)],
            name="first",
        )
        return stream, hat_one, inverse_one, grad_own

    far = far_bits()
    stream, hat_one, inverse_one, grad_own = phase(
        bits, [gather_in, gather_vectors, gather_up, *gather_rest], first, patches, cotangent
    )
    phase(bits, [gather_in, gather_vectors, (gather_up, len(far) - 1), gather_down], None)
    spare = in_width - width
    in_matrix, out_columns = gathered(
        gather_in.pieces,
        bits,
        [
            (
                (width, in_width),
                ([((0, block), (0, width), block, 0, 0)], [((0, block), (0, spare), block, 0, width)]),
            ),
            ((width, width - spare), ([], [((0, block), (spare, width), block, 0, 0)])),
        ],
    )
    vector_part = jnp.pad(
        gather_vectors.result()[:, : block * 16].reshape(-1, 16), ((0, 0), (0, TILE - 16))
    )
    gain_one, shift_one, bias_query, bias_value, bias_out, gain_two, shift_two, bias_down = (
        rows_from(vector_part, 8)
    )
    bias_query = pick(own_c, bias_query[:, :half], bias_query[:, half:])
    bias_value = pick(own_c, bias_value[:, :half], bias_value[:, half:])
    bias_up = unroll_bias(vector_part, own_c, ff_rows)
    bias_qkv = jnp.concatenate([bias_query, jnp.zeros_like(bias_query), bias_value], axis=1)

    def project(hat_one, out_columns):
        low, high = out_columns[:half], out_columns[half:]
        keep_out, came_out = pick(own_c, low, high), swap_core(pick(own_c, high, low))
        out_matrix = join(pick(own_c, keep_out, came_out), pick(own_c, came_out, keep_out), 1)
        return out_matrix, (hat_one * gain_one + shift_one).astype(BF16)

    out_matrix, normed_one = phase(
        bits, [gather_up, (gather_down, len(far) - 1)], project, hat_one, out_columns
    )

    def matmul_rows(left, right, product, name):
        return product(left[own:], right).astype(BF16)

    def attend(normed_one, in_matrix, out_matrix, grad_own):
        normed_one = with_core(normed_one)
        qkv = (nn(normed_one, in_matrix) + bias_qkv).astype(BF16)
        mixed, log_sum = attention(qkv, seg, info, per, head_size)
        away = matmul_rows(mixed, out_matrix, nn, "out_away")
        return normed_one, qkv, mixed, log_sum, away, with_core(grad_own)

    normed_one, qkv, mixed, log_sum, out_away, grad_last = phase(
        bits, [gather_up, *gather_rest], attend, normed_one, in_matrix, out_matrix, grad_own
    )

    def project_out(stream, mixed, out_away, out_matrix):
        def body(stream, mixed, came, matrix, bias, gain, shift):
            stream_two = stream + nn(mixed, matrix) + came.astype(F32) + bias
            normed, inverse = normalize(stream_two)
            return stream_two, normed, jnp.broadcast_to(inverse, (stream.shape[0], TILE)), normed * gain + shift

        return by_rows(
            body,
            [(stream, 0, own), mixed, swap_core(out_away)],
            [out_matrix, bias_out, gain_two, shift_two],
            [(width, F32), (width, F32), (TILE, F32), (width, BF16)],
            name="out_norm",
            tile=own // 2,
        )

    stream_two, hat_two, inverse_two, normed_two = phase(
        bits, [gather_down], project_out, stream, mixed, out_away, out_matrix
    )
    (up_matrix,) = gathered(
        gather_up.pieces,
        bits,
        [
            (
                (width, ff_half),
                ([((0, block), (0, width), block, 0, 0)], [((0, block), (0, width), block, 0, width)]),
            )
        ],
    )

    def expand(normed_two, up_matrix, grad_last):
        normed_two = with_core(normed_two)
        hidden_pre = nn(normed_two, up_matrix) + bias_up
        hidden, slope = gelu_and_slope(hidden_pre)
        hidden = hidden.astype(BF16)
        return normed_two, hidden, slope, tn(hidden, grad_last).astype(BF16)

    normed_two, hidden, slope, grad_down = phase(
        bits, [gather_down, *((move, 9) for move in gather_rest)], expand, normed_two, up_matrix, grad_last
    )
    part_rows = ff_rows // 2
    down_pieces = [piece for move in [gather_down, *gather_rest] for piece in move.pieces]
    (down_matrix,) = gathered(
        down_pieces,
        bits,
        [
            (
                (ff_half, width),
                [[((0, piece.rows), (0, width), ff_rows, i * side, 0)] for i, piece in enumerate(down_pieces)],
            )
        ],
    )

    scatter_down = Scatter(
        (grad_down, part_rows, ff_rows, 0, False), (grad_down, part_rows, ff_rows, part_rows, True)
    )

    def hidden_back(grad_last, down_matrix, slope, normed_two, up_matrix):
        grad_pre = (nt(grad_last, down_matrix) * slope).astype(BF16)
        return (
            grad_pre,
            matmul_rows(grad_pre, up_matrix, nt, "norm_two_away"),
            tn(normed_two, grad_pre[:, :width]).astype(BF16),
            tn(normed_two, grad_pre[:, width:]).astype(BF16),
        )

    grad_pre, two_away, *grad_up = phase(
        bits, [scatter_down], hidden_back, grad_last, down_matrix, slope, normed_two, up_matrix
    )
    scatter_up = Scatter((grad_up[0], block, block, 0, False), (grad_up[1], block, block, 0, True))

    def norm_back(grad, away, matrix, hat, inverse, added, gain, name):
        def body(grad, came, hat, inverse, added, matrix, gain):
            back, gain_sum, shift_sum = normalize_back(hat, inverse, gain, nt(grad, matrix) + came.astype(F32))
            total = added.astype(F32) + back
            return total, total, gain_sum, shift_sum

        return by_rows(
            body,
            [(grad, 0, own), swap_core(away), hat, inverse, added],
            [matrix, gain],
            [(width, F32), (width, BF16)],
            sums=2,
            name=name,
            tile=own // 2,
        )

    def middle(values, hidden, down_matrix):
        return norm_back(*values, "norm_two_back"), matmul_rows(hidden, down_matrix, nn, "output_away")

    (grad_two, grad_branch, grad_gain_two, grad_shift_two), output_away = phase(
        bits,
        [scatter_down],
        middle,
        (grad_pre, two_away, up_matrix, hat_two, inverse_two, grad_own, gain_two),
        hidden,
        down_matrix,
    )

    paired = block % 64 == 0

    def pair(array):
        blocks = array.reshape(chips, 2, -1, array.shape[1])
        return jnp.concatenate([blocks[:, 0], blocks[:, 1]], axis=2).reshape(-1, 2 * array.shape[1])

    def part(array):
        columns = array.shape[1] // 2
        return jnp.concatenate([array[:, :columns], array[:, columns:]], axis=0)

    def attention_grads(grad_branch, out_matrix, qkv, mixed, log_sum, output_away):
        grad_branch = with_core(grad_branch)
        grad_mixed = nt(grad_branch, out_matrix).astype(BF16)
        grad_qkv = attention_back(0, 1, qkv, mixed, grad_mixed, seg, log_sum, info, per, head_size)
        grad_rows = tn(mixed, grad_branch).astype(BF16)
        low, high = grad_rows[:, :half], grad_rows[:, half:]
        keep_rows, came_rows = pick(own_c, low, high), swap_core(pick(own_c, high, low))
        grad_out = join(pick(own_c, keep_rows, came_rows), pick(own_c, came_rows, keep_rows), 0)
        return grad_branch, swap_core(output_away), grad_qkv, pair(grad_out) if paired else grad_out

    grad_branch, came_output, grad_qkv, grad_out = phase(
        bits,
        [scatter_up, scatter_down],
        attention_grads,
        grad_branch,
        out_matrix,
        qkv,
        mixed,
        log_sum,
        output_away,
    )
    quarter = block // 4
    scatter_out = []
    if paired:
        scatter_out = [
            Scatter(
                (grad_out, quarter, 2 * quarter, 0, False), (grad_out, quarter, 2 * quarter, quarter, True)
            )
        ]

    def in_grads(normed_one, grad_qkv, in_matrix):
        right = tn(normed_one, grad_qkv[:, width:]).astype(BF16)
        return (
            matmul_rows(grad_qkv, in_matrix, nt, "norm_one_away"),
            tn(normed_one, grad_qkv[:, :width]).astype(BF16),
            pair(right) if paired else right,
        )

    one_away, left, right = phase(
        bits, [scatter_up, *scatter_out, scatter_down], in_grads, normed_one, grad_qkv, in_matrix
    )
    if paired:
        scatter_in = Scatter(
            (left, 3 * quarter, block, 0, False),
            (left, quarter, block, 3 * quarter, True),
            (right, 2 * quarter, 2 * quarter, 0, True),
        )
    else:
        scatter_in = Scatter((left, block, block, 0, False), (join(right, grad_out, 1), block, block, 0, True))

    def widen(row):
        zero = jnp.zeros_like(row)
        return jnp.concatenate([pick(own_c, row, zero), pick(own_c, zero, row)], axis=1)

    narrow_rows = vector_count + table_size
    narrow_rows += -narrow_rows % 16

    def norm_one_back(grad_qkv, one_away, in_matrix, hat_one, inverse_one, grad_two, grad_pre, grad_branch, grad_last):
        grad_stream, grad_low, grad_gain_one, grad_shift_one = norm_back(
            grad_qkv, one_away, in_matrix, hat_one, inverse_one, grad_two, gain_one, "norm_one_back"
        )
        wide_place = jnp.pad(place, ((0, 0), (vector_count, narrow_rows - vector_count - table_size)))
        table_part = lax.dot_general(
            wide_place, grad_stream, (((0,), (0,)), ((), ())), precision=PRECISE, preferred_element_type=F32
        )
        bias_part = roll_bias(token_sums(grad_pre), own_c, width, narrow_rows, ff_rows)
        sums = token_sums(grad_qkv)
        rows_of_sums = [
            grad_gain_one,
            grad_shift_one,
            widen(sums[:, :half]),
            widen(sums[:, 2 * half :]),
            token_sums(grad_branch[:own]),
            grad_gain_two,
            grad_shift_two,
            token_sums(grad_last[:own]),
        ]

        def stack(*refs):
            refs[-1][...] = refs[0][...] + refs[1][...]
            for i in range(len(rows_of_sums)):
                refs[-1][i : i + 1] = refs[2 + i][...]

        narrow = pl.pallas_call(
            stack,
            name="narrow",
            out_shape=jax.ShapeDtypeStruct((narrow_rows, width), F32),
            compiler_params=pltpu.CompilerParams(vmem_limit_bytes=4 << 20),
            cost_estimate=pl.CostEstimate(flops=0, bytes_accessed=0, transcendentals=0),
        )(table_part, bias_part, *rows_of_sums)
        return grad_low, add_came(narrow, swap_core(narrow.astype(BF16)))

    def finish_output(hidden, came, stream_two, down_matrix):
        def body(hidden, came, stream_two, usable, matrix, bias):
            return ((stream_two + nn(hidden, matrix) + came.astype(F32) + bias) * usable[:, :1],)

        return by_rows(
            body,
            [(hidden, 0, own), came, stream_two, wide_usable],
            [down_matrix, bias_down],
            [(width, BF16)],
            name="output",
            tile=own // 2,
        )

    (grad_low, narrow), (output,) = phase(
        bits,
        [scatter_in, *scatter_out, scatter_up, (scatter_down, len(far) - 1)],
        lambda values, others: (norm_one_back(*values), finish_output(*others)),
        (grad_qkv, one_away, in_matrix, hat_one, inverse_one, grad_two, grad_pre, grad_branch, grad_last),
        (hidden, came_output, stream_two, down_matrix),
    )

    def rows_of(array, core):
        return lax.dynamic_slice_in_dim(array, core * rows, rows, 0)

    def trade(array, blocks):
        away, keep = rows_of(array, 1 - own_c), rows_of(array, own_c)
        came = swap_core(away).reshape(rows, blocks, -1)
        keep = keep.reshape(rows, blocks, -1)
        both = jnp.stack([pick(own_c, keep, came), pick(own_c, came, keep)], axis=2)
        return both.reshape(rows, -1)

    factor = 1.0 / slot_total

    def adam(weight, gradient, first_moment, second_moment):
        return by_rows(
            lambda w, g, m, v: adam_update(w, g, m, v, factor, 0.05),
            [weight, gradient, first_moment, second_moment],
            [],
            [(weight.shape[1], F32)] * 3,
            name="adam",
            tile=weight.shape[0],
        )

    scatters = [scatter_in, *scatter_out, scatter_up]
    square = len(far) == 2
    total = Total(narrow, [0, far[-1], *([] if square else [1, *far[:-1]])])
    phase(bits, [*scatters, total], None)
    core = own_c.astype(jnp.int32).reshape(1)

    def split_rows(pieces, columns, rule):
        arrays = []
        for p in pieces:
            arrays += [p.held[0], p.came[0]]

        def kernel(own, *refs):
            away, keep = refs[-2:]
            for here in (0, 1):

                @pl.when(own[0] == here)
                def _(here=here):
                    for out, which in ((keep, here), (away, 1 - here)):
                        for i, (low, high), (left, right), row, column in rule(which):
                            p = pieces[i]
                            at, came = p.held[1] + low, p.came[1] + low
                            out[row : row + high - low, column : column + right - left] = refs[2 * i][
                                at : at + high - low, left:right
                            ].astype(F32) + refs[2 * i + 1][came : came + high - low, left:right].astype(F32)

        size = sum(a.size * jnp.dtype(a.dtype).itemsize for a in arrays) + 8 * rows * columns
        return pl.pallas_call(
            kernel,
            name="split_rows",
            out_shape=[jax.ShapeDtypeStruct((rows, columns), F32)] * 2,
            in_specs=[pl.BlockSpec(memory_space=pltpu.SMEM)]
            + [pl.BlockSpec(memory_space=pltpu.VMEM)] * len(arrays),
            compiler_params=pltpu.CompilerParams(vmem_limit_bytes=size + (2 << 20)),
            cost_estimate=pl.CostEstimate(flops=0, bytes_accessed=0, transcendentals=0),
        )(core, *arrays)

    def adam_joined(keep, came, blocks, weight, first_moment, second_moment):
        span = keep.shape[1] // blocks

        def kernel(own, keep, came, weight, first, second, *outs):
            low_is_own = own[0] == 0
            for i in range(blocks):
                mine, other = keep[:, i * span : (i + 1) * span], came[:, i * span : (i + 1) * span]
                for j, values in enumerate(
                    (jnp.where(low_is_own, mine, other), jnp.where(low_is_own, other, mine))
                ):
                    at = slice((2 * i + j) * span, (2 * i + j + 1) * span)
                    made = adam_update(weight[:, at], values, first[:, at], second[:, at], factor, 0.05)
                    for out, value in zip(outs, (values, *made)):
                        out[:, at] = value

        size = 4 * (2 * keep.size + 7 * weight.size)
        gradient, *updated = pl.pallas_call(
            kernel,
            name="adam_joined",
            out_shape=[jax.ShapeDtypeStruct(weight.shape, F32)] * 4,
            in_specs=[pl.BlockSpec(memory_space=pltpu.SMEM)] + [pl.BlockSpec(memory_space=pltpu.VMEM)] * 5,
            compiler_params=pltpu.CompilerParams(vmem_limit_bytes=size + (2 << 20)),
            cost_estimate=pl.CostEstimate(flops=0, bytes_accessed=0, transcendentals=0),
        )(core, keep, came, weight, first_moment, second_moment)
        return gradient, updated

    def finish_up():
        away, keep = split_rows(
            scatter_up.pieces,
            ff_half,
            lambda c: [(i, (c * rows, (c + 1) * rows), (0, width), 0, i * width) for i in (0, 1)],
        )
        return adam_joined(keep, swap_core(away), chips, mlp_in, first_mlp_in, second_mlp_in)

    def finish_mlp():
        shard_down = jnp.concatenate(scatter_down.result(bits), axis=0)
        if paired:
            shard_up, adam_up = finish_up()
        else:
            shard_up = trade(jnp.concatenate(scatter_up.result(bits), axis=1), chips)
            adam_up = adam(mlp_in, shard_up, first_mlp_in, second_mlp_in)
        return shard_up, shard_down, adam_up, adam(mlp_out, shard_down, first_mlp_out, second_mlp_out)

    send_output = Rider(output, 0, local_len, local_len)
    send_grad = Rider(grad_low, 0, local_len, local_len)
    rest = [scatter_in, *scatter_out, total]
    if scatter_up.left():
        phase(bits, [*rest, (scatter_up, 9)], None)
    grad_up_shard, shard_down, adam_up, adam_down = phase(
        bits, [*rest, send_output], finish_mlp, also=[scatter_up, scatter_down]
    )

    def back_to_rows(array, other):
        mine = array[:local_len]
        return jnp.stack([pick(own_y, mine, other), pick(own_y, other, mine)], axis=0)

    if square:
        low = total.result().astype(BF16)
        sides = [Rider(low, bit, 0, narrow_rows) for bit in (1, far[0])]
        corner = 1 | (1 << (far[0] - 1))

        def last_work(output, came, low):
            across = lax.ppermute(low, "img", [(i, i ^ corner) for i in range(img_count)])
            return back_to_rows(output, came), across

        output, across = phase(
            bits, [scatter_in, *scatter_out, *sides, send_grad], last_work, output, send_output.result(), low
        )
        near, far_side = (side.result().astype(F32) for side in sides)
        narrow = (low.astype(F32) + near) + (far_side + across.astype(F32))
    else:
        output = phase(bits, [*rest, send_grad], back_to_rows, output, send_output.result())
    while scatter_in.left():
        phase(bits, rest, None)
    while total.left():
        phase(bits, [total], None)
    input_grad = back_to_rows(grad_low, send_grad.result())
    if not square:
        narrow = total.result()
    if paired:

        def in_rule(c):
            left = [(0, (0, rows), (0, width), 0, 0)]
            if c == 1:
                left = [
                    (0, (rows, 3 * quarter), (0, width), 0, 0),
                    (1, (0, quarter), (0, width), 3 * quarter - rows, 0),
                ]
            return [*left, (2, (0, rows), (c * half, (c + 1) * half), 0, width)]

        away, keep = split_rows(scatter_in.pieces, in_width, in_rule)
        grad_in_shard, adam_in = adam_joined(keep, swap_core(away), 3, attn_in, first_attn_in, second_attn_in)
        away, keep = split_rows(
            scatter_out[0].pieces,
            half,
            lambda c: [(i, (0, quarter), (c * half, (c + 1) * half), i * quarter, 0) for i in (0, 1)],
        )
        grad_out_shard, adam_out = adam_joined(
            keep, swap_core(away), 1, attn_out, first_attn_out, second_attn_out
        )
    else:
        shard_in = jnp.concatenate(scatter_in.result(bits), axis=1)
        grad_out_shard, grad_in_shard = trade(shard_in[:, in_width:], 1), trade(shard_in[:, :in_width], 3)
        adam_in = adam(attn_in, grad_in_shard, first_attn_in, second_attn_in)
        adam_out = adam(attn_out, grad_out_shard, first_attn_out, second_attn_out)
    updated = [adam_in, adam_out, adam_up, adam_down]
    device = (lax.axis_index("img") * halves + own_y) * 2 + own_c
    grad_vectors_shard = lax.dynamic_slice_in_dim(narrow[:vector_count], device * rows, rows, 1).T
    table_grad = narrow[vector_count : vector_count + table_size]

    shards = (grad_in_shard, grad_out_shard, grad_up_shard, shard_down, grad_vectors_shard)
    updated.append(adam_update(vectors, grad_vectors_shard, first_vectors, second_vectors, factor, 0.0))
    return (
        output,
        input_grad,
        table_grad,
        *shards,
        *(updated[i][0] for i in range(5)),
        *(updated[i][1] for i in range(5)),
        *(updated[i][2] for i in range(5)),
    )


def solution(mesh):
    img, seq = mesh.shape["img"], mesh.shape["seq"]
    inner = Mesh(mesh.devices.reshape(img, seq // 2, 2), ("img", "sy", "sc"))
    tokens = P("img", ("sy", "sc"), None)
    shard = P(("img", "sy", "sc"), None)
    return jax.shard_map(
        per_device,
        mesh=inner,
        in_specs=(tokens, tokens, P("img", None), P()) + (shard,) * 15,
        out_specs=(tokens, tokens, P()) + (shard,) * 20,
        check_vma=False,
    )
```

```python
import functools
import math

import jax
import jax.numpy as jnp
from jax import lax
from jax.experimental import pallas as pl
from jax.experimental.pallas import tpu as pltpu
from jax.sharding import Mesh
from jax.sharding import PartitionSpec as P

HEADS = 16
GRID = 7
GRID_HI = 12
TILE = 128

PRECISE = lax.Precision.HIGHEST
FIRST_CORRECTION = 0.9999734386011124
SECOND_CORRECTION = 0.0952078528862911
EPS = 1e-06

F32 = jnp.float32
BF16 = jnp.bfloat16


def image_spans(res_row):
    side = jnp.where(res_row == 384, GRID_HI, jnp.where(res_row == 224, GRID, 0)).astype(jnp.int32)
    lengths = side * side
    slots = res_row.shape[0]
    order = jnp.arange(slots, dtype=jnp.int32)
    earlier = order[None, :] < order[:, None]
    starts = jnp.sum(jnp.where(earlier, lengths[None, :], 0), axis=1)
    return side, lengths, starts


def layout(res_row, positions):
    side, lengths, starts = image_spans(res_row)
    slots = res_row.shape[0]
    places = positions[:, None]
    inside = ((places >= starts[None, :]) & (places < (starts + lengths)[None, :])).astype(jnp.int32)
    usable = jnp.sum(inside, axis=1)
    image_number = jnp.arange(slots, dtype=jnp.int32)
    segment = jnp.sum(inside * image_number, axis=1) + (1 - usable) * slots
    start_of = jnp.sum(inside * starts[None, :], axis=1)
    side_of = jnp.sum(inside * side[None, :], axis=1)
    patch_index = (positions - start_of) * usable
    return segment, side_of, patch_index, usable


def key_bounds(res_row, row_len):
    _, lengths, starts = image_spans(res_row)
    total = jnp.sum(lengths)
    firsts = jnp.arange(row_len // TILE, dtype=jnp.int32) * TILE

    def span(positions):
        places = positions[:, None]
        inside = (places >= starts[None, :]) & (places < (starts + lengths)[None, :])
        found = positions < total
        begin = jnp.sum(jnp.where(inside, starts[None, :], 0), axis=1)
        end = jnp.sum(jnp.where(inside, (starts + lengths)[None, :], 0), axis=1)
        return jnp.where(found, begin, total), jnp.where(found, end, row_len)

    begin, _ = span(firsts)
    _, end = span(firsts + (TILE - 1))
    return begin // TILE, (end + TILE - 1) // TILE


def axis_weights(coord, side_of):
    scaled = jnp.maximum((2 * coord + 1) * GRID - GRID_HI, 0)
    lower_fine = scaled // (2 * GRID_HI)
    fraction_fine = (scaled - lower_fine * 2 * GRID_HI).astype(F32) / (2.0 * GRID_HI)
    resized = side_of == GRID_HI
    lower_cell = jnp.where(resized, lower_fine, coord)
    fraction = jnp.where(resized, fraction_fine, jnp.zeros_like(fraction_fine))
    upper_cell = jnp.minimum(lower_cell + 1, GRID - 1)
    cell_index = jnp.arange(GRID, dtype=jnp.int32)
    below = (cell_index == lower_cell[..., None]).astype(F32)
    above = (cell_index == upper_cell[..., None]).astype(F32)
    return (1.0 - fraction)[..., None] * below + fraction[..., None] * above


def table_weights(side_of, patch_index, usable):
    safe_side = jnp.maximum(side_of, 1)
    row_coord = patch_index // safe_side
    column_coord = patch_index % safe_side
    outer = axis_weights(row_coord, side_of)[:, :, None] * axis_weights(column_coord, side_of)[:, None, :]
    outer = outer * usable.astype(F32)[:, None, None]
    return outer.reshape(side_of.shape[0], GRID * GRID)


def place_of(block, own_y, own_c, per):
    quarter = block // per
    core = (quarter % 2 + own_c) % 2
    half = (quarter // 2 + own_y) % 2
    return (core * 2 + half) * per + block % per


def split_heads(pair):
    lane = lax.broadcasted_iota(jnp.int32, pair.shape, 1)
    zero = jnp.zeros_like(pair)
    low = lane < pair.shape[1] // 2
    return jnp.concatenate([jnp.where(low, pair, zero), jnp.where(low, zero, pair)], axis=0)


def join_heads(stacked):
    half = stacked.shape[0] // 2
    lane = lax.broadcasted_iota(jnp.int32, (half, stacked.shape[1]), 1)
    return jnp.where(lane < stacked.shape[1] // 2, stacked[:half], stacked[half:])


def down_lanes(row):
    return jnp.transpose(jnp.broadcast_to(row, (TILE, TILE)))


def nt(left, right):
    return lax.dot_general(left, right, (((1,), (1,)), ((), ())), preferred_element_type=F32)


def tn(left, right):
    return lax.dot_general(left, right, (((0,), (0,)), ((), ())), preferred_element_type=F32)


def nn(left, right):
    return jnp.dot(left, right, preferred_element_type=F32)


def fold(array, over):
    parts = array.reshape(array.shape[0] // 8, 8, array.shape[1])
    return jnp.max(parts, axis=0) if over == "max" else jnp.sum(parts, axis=0)


def same_segment(seg_down, chunk, seg_q):
    same = seg_down[chunk] == seg_q
    return jnp.concatenate([same, same], axis=1)


def fill_segments(seg, seg_down):
    chunks, span, _ = seg_down.shape
    for chunk in range(chunks):
        row = seg[0:1, chunk * span : (chunk + 1) * span]
        seg_down[chunk] = jnp.transpose(jnp.broadcast_to(row, (TILE, span)))


def join_turned(turned):
    half = turned.shape[1] // 2
    row = lax.broadcasted_iota(jnp.int32, (turned.shape[0], half), 0)
    return jnp.transpose(jnp.where(row < turned.shape[0] // 2, turned[:, :half], turned[:, half:]))


def columns_of(base, j):
    return slice(base + j * TILE, base + (j + 1) * TILE)


def attend_kernel(pairs, width, per, scale, info, qkv, seg, out, log_sum, scores, turned, seg_down):
    tile = pl.program_id(0)
    chunks, span, _ = seg_down.shape
    own_y, own_c = info[0], info[1]
    ratio = span // TILE
    first = info[2 + tile] // ratio
    last = (info[2 + pl.num_programs(0) + tile] + ratio - 1) // ratio

    def at(chunk):
        return pl.multiple_of(place_of(chunk * ratio, own_y, own_c, per) * TILE, TILE)

    @pl.when(tile == 0)
    def _():
        fill_segments(seg, seg_down)
        for chunk in range(chunks):
            for j in range(pairs):
                turned[chunk, j] = jnp.transpose(qkv[pl.ds(at(chunk), span), columns_of(2 * width, j)])

    q_at = pl.multiple_of(place_of(tile, own_y, own_c, per) * TILE, TILE)
    seg_q = seg[0:1, pl.ds(pl.multiple_of(tile * TILE, TILE), TILE)]
    queries = [
        split_heads(qkv[pl.ds(q_at, TILE), columns_of(0, j)] * jnp.asarray(scale, BF16)) for j in range(pairs)
    ]

    def score(chunk, high):
        same = same_segment(seg_down, chunk, seg_q)
        products = [nt(qkv[pl.ds(at(chunk), span), columns_of(width, j)], queries[j]) for j in range(pairs)]
        made = []
        for j in range(pairs):
            s = jnp.where(same, products[j], -1e30)
            scores[j, chunk] = s
            made.append(jnp.maximum(high[j], fold(s, "max")))
        return tuple(made)

    high = lax.fori_loop(first, last, score, (jnp.full((8, 2 * TILE), -1e30, F32),) * pairs)
    tops = [jnp.max(high[j], axis=0, keepdims=True) for j in range(pairs)]

    def mix(chunk, carry):
        total, mixed = carry
        powers = [jnp.exp(scores[j, chunk] - tops[j]) for j in range(pairs)]
        return (
            tuple(total[j] + fold(powers[j], "sum") for j in range(pairs)),
            tuple(mixed[j] + nn(turned[chunk, j], powers[j].astype(BF16)) for j in range(pairs)),
        )

    total, mixed = lax.fori_loop(
        first,
        last,
        mix,
        ((jnp.zeros((8, 2 * TILE), F32),) * pairs, (jnp.zeros((TILE, 2 * TILE), F32),) * pairs),
    )
    for j in range(pairs):
        sums = jnp.sum(total[j], axis=0, keepdims=True)
        out[:, columns_of(0, j)] = join_turned(mixed[j] / sums).astype(BF16)
        log_total = tops[j] + jnp.log(sums)
        log_sum[2 * j : 2 * j + 1] = log_total[:, :TILE]
        log_sum[2 * j + 1 : 2 * j + 2] = log_total[:, TILE:]


def attend_back_kernel(
    start, pairs, width, per, scale, info, qkv, mixed, grad, seg, log_sum, out, grad_keys, grad_values, turned, seg_down
):
    tile = pl.program_id(0)
    chunks, span, _ = seg_down.shape
    own_y, own_c = info[0], info[1]
    ratio = span // TILE
    first = info[2 + tile] // ratio
    last = (info[2 + pl.num_programs(0) + tile] + ratio - 1) // ratio
    heads = range(start, start + pairs)

    def at(chunk):
        return pl.multiple_of(place_of(chunk * ratio, own_y, own_c, per) * TILE, TILE)

    @pl.when(tile == 0)
    def _():
        fill_segments(seg, seg_down)
        grad_keys[...] = jnp.zeros_like(grad_keys)
        grad_values[...] = jnp.zeros_like(grad_values)
        for chunk in range(chunks):
            for i, j in enumerate(heads):
                turned[chunk, i] = jnp.transpose(qkv[pl.ds(at(chunk), span), columns_of(width, j)])

    q_at = pl.multiple_of(place_of(tile, own_y, own_c, per) * TILE, TILE)
    q_from = pl.multiple_of(tile * TILE, TILE)
    seg_q = seg[0:1, pl.ds(q_from, TILE)]
    queries, grads, logs, inner = [], [], [], []
    for j in heads:
        queries.append(split_heads(qkv[pl.ds(q_at, TILE), columns_of(0, j)] * jnp.asarray(scale, BF16)))
        g = grad[pl.ds(q_at, TILE), columns_of(0, j)]
        grads.append(split_heads(g))
        both = jnp.transpose(g.astype(F32) * mixed[pl.ds(q_at, TILE), columns_of(0, j)].astype(F32))
        low = jnp.sum(both[: TILE // 2], axis=0, keepdims=True)
        high = jnp.sum(both[TILE // 2 :], axis=0, keepdims=True)
        inner.append(jnp.concatenate([low, high], axis=1))
        here = log_sum[2 * j : 2 * j + 2, pl.ds(q_from, TILE)]
        logs.append(jnp.concatenate([here[0:1], here[1:2]], axis=1))

    def step(chunk, carry):
        k_at = at(chunk)
        same = same_segment(seg_down, chunk, seg_q)
        scores = [nt(qkv[pl.ds(k_at, span), columns_of(width, j)], queries[i]) for i, j in enumerate(heads)]
        slopes = [nt(qkv[pl.ds(k_at, span), columns_of(2 * width, j)], grads[i]) for i, j in enumerate(heads)]
        powers = [jnp.exp(jnp.where(same, scores[i], -1e30) - logs[i]) for i in range(pairs)]
        changes = [(powers[i] * (slopes[i] - inner[i])).astype(BF16) for i in range(pairs)]
        to_values = [nn(powers[i].astype(BF16), grads[i]) for i in range(pairs)]
        to_keys = [nn(changes[i], queries[i]) for i in range(pairs)]
        to_query = tuple(carry[i] + nn(turned[chunk, i], changes[i]) for i in range(pairs))
        for i in range(pairs):
            grad_values[chunk, :, columns_of(0, i)] += to_values[i]
            grad_keys[chunk, :, columns_of(0, i)] += to_keys[i]
        return to_query

    grad_query = lax.fori_loop(first, last, step, (jnp.zeros((TILE, 2 * TILE), F32),) * pairs)
    for i in range(pairs):
        out[pl.ds(q_at, TILE), columns_of(0, i)] = (join_turned(grad_query[i]) * scale).astype(BF16)

    @pl.when(tile == pl.num_programs(0) - 1)
    def _():
        all_heads = pairs * TILE
        for chunk in range(chunks):
            out[pl.ds(at(chunk), span), all_heads : 2 * all_heads] = grad_keys[chunk].astype(BF16)
            out[pl.ds(at(chunk), span), 2 * all_heads :] = grad_values[chunk].astype(BF16)


def attention(qkv, seg, info, per, head_size):
    length, width = qkv.shape[0], qkv.shape[1] // 3
    pairs, tiles = width // TILE, length // TILE
    span = per * TILE
    chunks = length // span
    scale = head_size ** (-0.5)

    def place(i, info):
        return place_of(i, info[0], info[1], per)

    return pl.pallas_call(
        functools.partial(attend_kernel, pairs, width, per, scale),
        name="attend",
        out_shape=(
            jax.ShapeDtypeStruct((length, width), BF16),
            jax.ShapeDtypeStruct((2 * pairs, length), F32),
        ),
        grid_spec=pltpu.PrefetchScalarGridSpec(
            num_scalar_prefetch=1,
            grid=(tiles,),
            in_specs=[
                pl.BlockSpec(qkv.shape, lambda i, info: (0, 0), pipeline_mode=pl.Buffered(1)),
                pl.BlockSpec(seg.shape, lambda i, info: (0, 0), pipeline_mode=pl.Buffered(1)),
            ],
            out_specs=[
                pl.BlockSpec((TILE, width), lambda i, info: (place(i, info), 0)),
                pl.BlockSpec((2 * pairs, TILE), lambda i, info: (0, i)),
            ],
            scratch_shapes=[
                pltpu.VMEM((pairs, chunks, span, 2 * TILE), F32),
                pltpu.VMEM((chunks, pairs, TILE, span), BF16),
                pltpu.VMEM((chunks, span, TILE), F32),
            ],
        ),
        compiler_params=pltpu.CompilerParams(
            dimension_semantics=("arbitrary",), vmem_limit_bytes=20 << 20
        ),
        cost_estimate=pl.CostEstimate(flops=0, bytes_accessed=0, transcendentals=0),
    )(info, qkv, seg)


def attention_back(part, parts, qkv, mixed, grad, seg, log_sum, info, per, head_size):
    length, width = qkv.shape[0], qkv.shape[1] // 3
    pairs, tiles = width // TILE // parts, length // TILE
    span = per * TILE
    chunks = length // span
    out = jax.ShapeDtypeStruct((length, 3 * pairs * TILE), BF16)
    scale = head_size ** (-0.5)

    def whole(array):
        return pl.BlockSpec(array.shape, lambda i, info: (0, 0), pipeline_mode=pl.Buffered(1))

    return pl.pallas_call(
        functools.partial(attend_back_kernel, part * pairs, pairs, width, per, scale),
        name="attend_back",
        out_shape=out,
        grid_spec=pltpu.PrefetchScalarGridSpec(
            num_scalar_prefetch=1,
            grid=(tiles,),
            in_specs=[whole(qkv), whole(mixed), whole(grad), whole(seg), whole(log_sum)],
            out_specs=pl.BlockSpec(out.shape, lambda i, info: (0, 0)),
            scratch_shapes=[
                pltpu.VMEM((chunks, span, pairs * TILE), F32),
                pltpu.VMEM((chunks, span, pairs * TILE), F32),
                pltpu.VMEM((chunks, pairs, TILE, span), BF16),
                pltpu.VMEM((chunks, span, TILE), F32),
            ],
        ),
        compiler_params=pltpu.CompilerParams(
            dimension_semantics=("arbitrary",), vmem_limit_bytes=28 << 20
        ),
        cost_estimate=pl.CostEstimate(
            flops=32 * length * length * width, bytes_accessed=8 * length * width * 2, transcendentals=0
        ),
    )(info, qkv, mixed, grad, seg, log_sum)


SWAP = [(0, 1), (1, 0)]


def swap_core(array):
    return lax.ppermute(array, "sc", SWAP)


def swap_chip(array):
    return lax.ppermute(array, "sy", SWAP)


def swap_bit(array, bit):
    if bit == 0:
        return swap_chip(array)
    count = lax.axis_size("img")
    return lax.ppermute(array, "img", [(i, i ^ (1 << (bit - 1))) for i in range(count)])


def own_bit(bit):
    if bit == 0:
        return lax.axis_index("sy")
    return (lax.axis_index("img") >> (bit - 1)) & 1


def fence(*values):
    return lax.optimization_barrier(values)


def axis_of(bit, done):
    return sum(1 for other in done if other > bit)


def pick(index, low, high):
    return jnp.where(index == 0, low, high)


def far_bits():
    return list(range(2, int(math.log2(lax.axis_size("img"))) + 1))


def join(first, second, axis):
    shape = list(first.shape)
    shape[axis] += second.shape[axis]
    held = lax.dynamic_update_slice_in_dim(jnp.zeros(shape, first.dtype), first, 0, axis)
    return lax.dynamic_update_slice_in_dim(held, second, first.shape[axis], axis)


class Turn:
    def __init__(self):
        self.arrays, self.shapes, self.jobs = [], [], []
        self.kept = None

    def keep(self, rows, columns):
        if self.kept is None:
            self.kept = self.write((0, columns), BF16)
        before = self.shapes[self.kept].shape[0]
        self.shapes[self.kept] = jax.ShapeDtypeStruct((before + rows, columns), BF16)
        return self.kept, before

    def read(self, array):
        for i, other in enumerate(self.arrays):
            if other is array:
                return i
        self.arrays.append(array)
        return len(self.arrays) - 1

    def write(self, shape, dtype):
        self.shapes.append(jax.ShapeDtypeStruct(shape, dtype))
        return len(self.shapes) - 1

    def run(self, bits):
        count = len(self.arrays)

        def kernel(own, *refs):
            mine = [own[i] for i in range(bits.shape[0])]
            for job in self.jobs:
                job(mine, refs[:count], refs[count:])

        spent = sum(a.size * jnp.dtype(a.dtype).itemsize for a in [*self.arrays, *self.shapes])
        return pl.pallas_call(
            kernel,
            name="turn",
            out_shape=tuple(self.shapes),
            in_specs=[pl.BlockSpec(memory_space=pltpu.SMEM)] + [pl.BlockSpec(memory_space=pltpu.VMEM)] * count,
            out_specs=tuple(pl.BlockSpec(memory_space=pltpu.VMEM) for _ in self.shapes),
            compiler_params=pltpu.CompilerParams(vmem_limit_bytes=spent + (2 << 20)),
            cost_estimate=pl.CostEstimate(flops=0, bytes_accessed=0, transcendentals=0),
        )(bits, *self.arrays)


def combinations(bits):
    made = [{}]
    for bit in bits:
        made = [{**choice, bit: value} for choice in made for value in (0, 1)]
    return made


def flat_index(choice, bits):
    at = 0
    for bit in sorted(bits, reverse=True):
        at = at * 2 + choice[bit]
    return at


def block_of(at, rows, base=0):
    start = at * rows + base
    if isinstance(start, int):
        return pl.ds(start, rows)
    return pl.ds(pl.multiple_of(start, math.gcd(rows, base) if base else rows), rows)


class Piece:
    def __init__(self, array, rows, bits, order, stride=None, base=0):
        self.held, self.rows, self.bits = (array, base), rows, list(bits)
        self.fixed, self.order, self.came = [], list(order), None
        self.stride, self.source = stride or rows, bool(bits)


class Gather:
    def __init__(self, *parts):
        self.pieces = []
        for array, first, rows, order in parts:
            piece = Piece(array, rows, [], order)
            piece.held = (array, first)
            self.pieces.append(piece)

    def wants(self):
        return [(p.order[0], p.rows << (len(p.bits) + (p.came is not None))) for p in self.pieces]

    def turn(self, turn, places):
        for p, (out, base) in zip(self.pieces, places):
            if p.came is None:
                turn.jobs.append(copy_rows(turn.read(p.held[0]), p.held[1], out, base, p.rows << len(p.bits)))
            else:
                bit = p.sent
                absorb_gather(turn, p, bit, lambda choice, p=p, out=out, base=base: [(out, choice, base)])
            p.sent = p.order.pop(0)
            p.next_held = (out, base)

    def settle(self, outs, came):
        for p, where in zip(self.pieces, came):
            if p.came is not None:
                p.bits.append(p.last)
            p.held, p.came, p.last = (outs[p.next_held[0]], p.next_held[1]), where, p.sent

    def arrays(self):
        return [a for p in self.pieces for a in ([p.held[0]] + ([p.came[0]] if p.came else []))]

    def relabel(self, swap):
        for p in self.pieces:
            p.held = (swap(p.held[0]), p.held[1])
            if p.came:
                p.came = (swap(p.came[0]), p.came[1])

    def left(self):
        return len(self.pieces[0].order)


def gathered(pieces, bits, outs):
    turn = Turn()
    made = [turn.write(shape, BF16) for shape, _ in outs]
    for i, p in enumerate(pieces):
        held, came = turn.read(p.held[0]), turn.read(p.came[0])
        moves = [(out, move) for out, (_, moves) in zip(made, outs) for move in moves[i]]

        def job(mine, ins, refs, p=p, held=held, came=came, moves=moves):
            everyone = [*p.bits, p.last]
            for choice in combinations(p.bits):
                at = flat_index(choice, p.bits)
                for source, base, value in (
                    (ins[held], p.held[1], mine[p.last]),
                    (ins[came], p.came[1], 1 - mine[p.last]),
                ):
                    chip = flat_index({**choice, p.last: value}, everyone)
                    for out, ((low, high), (left, right), stride, row, column) in moves:
                        start = pl.multiple_of(chip * stride + row, math.gcd(stride, row) if row else stride)
                        refs[out][pl.ds(start, high - low), column : column + right - left] = source[
                            pl.ds(base + at * p.rows + low, high - low), left:right
                        ]

        turn.jobs.append(job)
    return turn.run(bits)


class Spread:
    def __init__(self, array):
        self.pieces = [Piece(array, array.shape[0], [], [*reversed(far_bits()), 0, 1])]

    def wants(self):
        return [(self.pieces[0].order[0], self.pieces[0].rows)]

    def turn(self, turn, places):
        [p], [(out, base)] = self.pieces, places
        p.order.pop(0)
        p.next_held = (out, base)
        if p.came is None:
            turn.jobs.append(copy_rows(turn.read(p.held[0]), p.held[1], out, base, p.rows))
            return
        held, came, held_base, came_base, rows = turn.read(p.held[0]), turn.read(p.came[0]), p.held[1], p.came[1], p.rows

        def job(mine, ins, refs):
            refs[out][base : base + rows] = (
                ins[held][held_base : held_base + rows] + ins[came][came_base : came_base + rows]
            )

        turn.jobs.append(job)

    def settle(self, outs, came):
        [p] = self.pieces
        p.held, p.came = (outs[p.next_held[0]], p.next_held[1]), came[0]

    arrays, relabel, left = Gather.arrays, Gather.relabel, Gather.left

    def result(self):
        [p] = self.pieces
        return sum(array[base : base + p.rows] for array, base in (p.held, p.came))


class Rider:
    def __init__(self, array, bit, first, rows):
        self.pieces = [Piece(array, rows, [], [bit])]
        self.pieces[0].held = (array, first)

    wants, turn, settle = Spread.wants, Spread.turn, Spread.settle
    arrays, relabel, left = Gather.arrays, Gather.relabel, Gather.left

    def result(self):
        [p] = self.pieces
        return p.came[0][p.came[1] : p.came[1] + p.rows]


class Total:
    def __init__(self, array, order):
        self.pieces = [Piece(array, array.shape[0], [], order)]

    wants, arrays, relabel, left = Spread.wants, Gather.arrays, Gather.relabel, Gather.left

    def turn(self, turn, places):
        [p], [(out, base)] = self.pieces, places
        p.order.pop(0)
        held, rows = turn.read(p.held[0]), p.rows
        came, came_base = (None, 0) if p.came is None else (turn.read(p.came[0]), p.came[1])
        p.next = None if came is None else turn.write(p.held[0].shape, F32)

        def job(mine, ins, refs, keep=p.next):
            own = ins[held][...].astype(BF16)
            if came is not None:
                total = own.astype(F32) + ins[came][came_base : came_base + rows].astype(F32)
                refs[keep][...] = total
                own = total.astype(BF16)
            refs[out][base : base + rows] = own

        turn.jobs.append(job)

    def settle(self, outs, came):
        [p] = self.pieces
        if p.next is not None:
            p.held = (outs[p.next], 0)
        p.came = came[0]

    def result(self):
        [p] = self.pieces
        return add_came(p.held[0], p.came[0][p.came[1] : p.came[1] + p.rows])


def copy_rows(source, source_base, out, base, rows):
    def job(mine, ins, refs):
        refs[out][base : base + rows] = ins[source][source_base : source_base + rows]

    return job


def absorb_gather(turn, p, bit, targets):
    held, came = turn.read(p.held[0]), turn.read(p.came[0])
    last = p.last
    known = list(p.bits)
    held_base, came_base, rows = p.held[1], p.came[1], p.rows
    [(out, _, base)] = targets(None)

    def job(mine, ins, refs):
        for choice in combinations(known):
            at = flat_index(choice, known)
            for source, start, value in ((held, held_base, mine[last]), (came, came_base, 1 - mine[last])):
                to = flat_index({**choice, last: value}, [*known, last])
                refs[out][block_of(to, rows, base)] = ins[source][block_of(at, rows, start)]

    turn.jobs.append(job)


class Scatter:
    def __init__(self, *parts):
        far = far_bits()
        bits = sorted([0, 1, *far], reverse=True)
        self.pieces = [
            Piece(array, rows, bits, [*((1, 0) if turned else (0, 1)), *far], stride, first)
            for array, rows, stride, first, turned in parts
        ]

    def wants(self):
        return [(p.order[0], p.rows << (len(p.bits) - len(p.fixed) - 1)) for p in self.pieces]

    def turn(self, turn, places):
        for p, (out, base) in zip(self.pieces, places):
            bit = p.order.pop(0)
            free = [b for b in p.bits if b not in p.fixed and b != bit]
            rows, bits, fixed = p.rows, list(p.bits), list(p.fixed)
            held = turn.read(p.held[0])
            stride, first = p.stride, p.held[1]

            def block(choice, bits=bits, stride=stride, first=first, rows=rows):
                start = flat_index(choice, bits) * stride + first
                return pl.ds(pl.multiple_of(start, math.gcd(stride, first) if first else stride), rows)

            if p.came is None:
                p.next = None

                def job(mine, ins, refs, held=held, rows=rows, free=free, bit=bit, out=out, base=base, block=block):
                    for choice in combinations(free):
                        refs[out][block_of(flat_index(choice, free), rows, base)] = ins[held][
                            block({**choice, bit: 1 - mine[bit]})
                        ]

            else:
                came, came_base = turn.read(p.came[0]), p.came[1]
                keep, keep_base = turn.keep(rows << len(free), p.held[0].shape[1])
                p.next = (keep, keep_base)

                def job(
                    mine, ins, refs, held=held, rows=rows, fixed=fixed, free=free, bit=bit, out=out, base=base,
                    came=came, came_base=came_base, keep=keep, keep_base=keep_base, block=block,
                ):
                    settled = {b: mine[b] for b in fixed}
                    for choice in combinations(free):
                        for value, target, start in ((1 - mine[bit], out, base), (mine[bit], keep, keep_base)):
                            now = {**choice, bit: value}
                            total = ins[held][block({**now, **settled})].astype(F32) + ins[came][
                                block_of(flat_index(now, [*free, bit]), rows, came_base)
                            ].astype(F32)
                            refs[target][block_of(flat_index(choice, free), rows, start)] = total.astype(BF16)

            turn.jobs.append(job)
            p.sent, p.free = bit, free

    def settle(self, outs, came):
        for p, where in zip(self.pieces, came):
            if p.next is None:
                p.fixed = [p.sent]
            else:
                p.held, p.bits, p.fixed = (outs[p.next[0]], p.next[1]), list(p.free), []
                p.stride, p.source = p.rows, False
            p.came = where

    arrays, relabel, left = Gather.arrays, Gather.relabel, Gather.left

    def result(self, bits):
        turn = Turn()
        for p in self.pieces:
            held, came, base, rows, first = turn.read(p.held[0]), turn.read(p.came[0]), p.came[1], p.rows, p.held[1]
            out = turn.write((rows, p.held[0].shape[1]), F32)

            def job(mine, ins, refs, held=held, came=came, base=base, rows=rows, out=out, first=first):
                refs[out][...] = ins[held][first : first + rows].astype(F32) + ins[came][base : base + rows].astype(F32)

            turn.jobs.append(job)
        return turn.run(bits)


def swap_rows(moves, bits):
    wants = [move.wants() for move in moves]
    sizes, places = {}, []
    for bit, rows in (want for group in wants for want in group):
        places.append((bit, sizes.get(bit, 0)))
        sizes[bit] = sizes.get(bit, 0) + rows
    turn = Turn()
    width = moves[0].pieces[0].held[0].shape[1]
    outs = {bit: turn.write((rows, width), BF16) for bit, rows in sizes.items()}
    located = [(outs[bit], base) for bit, base in places]
    starts = [0]
    for move in moves:
        starts.append(starts[-1] + len(move.pieces))
    for i, move in enumerate(moves):
        move.turn(turn, located[starts[i] : starts[i + 1]])
    made = turn.run(bits)
    got = {bit: swap_bit(made[out], bit) for bit, out in outs.items()}
    came = [(got[bit], base) for bit, base in places]
    for i, move in enumerate(moves):
        move.settle(made, came[starts[i] : starts[i + 1]])


def add_came(own, came):
    return own.astype(BF16).astype(F32) + came.astype(F32)


def add_hop(array, bit):
    return add_came(array, swap_bit(array.astype(BF16), bit))


def phase(bits, moves, work, *values, also=()):
    chains = [move if isinstance(move, tuple) else (move, 1) for move in moves]
    chains = [
        ([move for move in chain[:-1] if move.left()], min(chain[-1], chain[0].left())) for chain in chains
    ]
    moves = [move for chain, _ in chains for move in chain]

    def tie(extra):
        arrays = []
        for array in (a for move in [*moves, *also] for a in move.arrays()):
            if not any(array is other for other in arrays):
                arrays.append(array)
        held, extra = fence(arrays, extra)
        table = list(zip(arrays, held))
        for move in [*moves, *also]:
            move.relabel(lambda array: next(new for old, new in table if old is array))
        return extra

    values = tie(values)
    if moves:
        swap_rows(moves, bits)
    for chain, count in chains:
        for _ in range(count - 1):
            swap_rows(chain, bits)
    made = work(*values) if work else ()
    return tie(made)


def by_rows(body, rows, whole, outs, sums=0, tile=TILE, name="rows"):
    rows = [array if isinstance(array, tuple) else (array, 0, array.shape[0]) for array in rows]
    length = rows[0][2]
    width = outs[0][0]

    def kernel(*refs):
        ins, results = refs[: len(rows) + len(whole)], refs[len(rows) + len(whole) :]
        made = body(*(ref[...] for ref in ins))
        for ref, value in zip(results, made):
            if ref.shape[0] == 1:

                @pl.when(pl.program_id(0) == 0)
                def _(ref=ref):
                    ref[...] = jnp.zeros_like(ref)

                ref[...] += value
            else:
                ref[...] = value.astype(ref.dtype)

    spent = sum(array.size * array.dtype.itemsize for array in whole)
    for columns, kind in [*outs, *((array.shape[1], array.dtype) for array, _, _ in rows)]:
        spent += 2 * tile * columns * jnp.dtype(kind).itemsize

    def steps(columns, first=0):
        return pl.BlockSpec((tile, columns), lambda i: (i + first // tile, 0))

    def fixed(shape, **how):
        return pl.BlockSpec(shape, lambda i: (0,) * len(shape), **how)

    return pl.pallas_call(
        kernel,
        name=name,
        grid=(length // tile,),
        out_shape=[jax.ShapeDtypeStruct((length, columns), dtype) for columns, dtype in outs]
        + [jax.ShapeDtypeStruct((1, width), F32)] * sums,
        in_specs=[steps(array.shape[1], first) for array, first, _ in rows]
        + [fixed(array.shape, pipeline_mode=pl.Buffered(1)) for array in whole],
        out_specs=[steps(columns) for columns, _ in outs] + [fixed((1, width))] * sums,
        compiler_params=pltpu.CompilerParams(
            dimension_semantics=("arbitrary",), vmem_limit_bytes=spent + (12 << 20)
        ),
        cost_estimate=pl.CostEstimate(flops=0, bytes_accessed=0, transcendentals=0),
    )(*(array for array, _, _ in rows), *whole)


def normalize(stream):
    center = jnp.mean(stream, axis=-1, keepdims=True)
    centered = stream - center
    spread = jnp.mean(centered * centered, axis=-1, keepdims=True)
    inverse = lax.rsqrt(spread + EPS)
    return centered * inverse, inverse


def normalize_back(normed, inverse, gain, grad):
    scaled = grad * gain
    middle = jnp.mean(scaled, axis=-1, keepdims=True)
    along = jnp.mean(scaled * normed, axis=-1, keepdims=True)
    return (
        inverse[:, :1] * (scaled - middle - normed * along),
        jnp.sum(grad * normed, axis=0, keepdims=True),
        jnp.sum(grad, axis=0, keepdims=True),
    )


def rows_from(columns, count):
    one_hot = (jnp.arange(16)[:, None] == jnp.arange(TILE)[None, :]).astype(BF16)
    rows = nt(one_hot, columns)
    return [rows[i : i + 1] for i in range(count)]


def column_choice(rows, columns):
    row, lane = jnp.arange(rows)[:, None], jnp.arange(TILE)[None, :]
    return (row == 8 + lane % columns).astype(F32)


def own_place(width, columns):
    per_run = TILE // columns
    row, lane = jnp.arange(width)[:, None], jnp.arange(TILE)[None, :]
    return row % per_run == lane // columns


def unroll_bias(columns, own_c, ff_rows):
    width, extra = columns.shape[0], 4
    spread = nn(columns, column_choice(TILE, extra).astype(BF16))
    runs = jnp.where(own_place(width, extra), spread, 0.0).reshape(-1, TILE // extra, TILE).sum(axis=1)
    runs = runs.reshape(-1, 2, ff_rows)
    return pick(own_c, runs[:, 0], runs[:, 1]).reshape(1, -1)


def roll_bias(sums, own_c, width, rows, ff_rows):
    extra = 4
    runs = sums.reshape(-1, ff_rows)
    zero = jnp.zeros_like(runs)
    runs = jnp.stack([pick(own_c, runs, zero), pick(own_c, zero, runs)], axis=1).reshape(-1, 1, TILE)
    spread = jnp.broadcast_to(runs, (runs.shape[0], TILE // extra, TILE)).reshape(width, TILE)
    spread = jnp.where(own_place(width, extra), spread, 0.0)
    return lax.dot_general(
        column_choice(rows, extra), spread, (((1,), (1,)), ((), ())), precision=PRECISE, preferred_element_type=F32
    )


def token_sums(array):
    return nn(jnp.ones((8, array.shape[0]), BF16), array)[:1]


def gelu_and_slope(values):
    cdf = 0.5 * (1.0 + lax.erf(values * (0.5**0.5)))
    density = jnp.exp(-0.5 * values * values) * (1.0 / math.sqrt(2.0 * math.pi))
    return values * cdf, cdf + values * density


def adam_update(weight, gradient, first_moment, second_moment, factor, decay):
    scaled = gradient * factor
    first_new = 0.9 * first_moment + 0.1 * scaled
    second_new = 0.999 * second_moment + 0.001 * scaled * scaled
    first_hat = first_new / FIRST_CORRECTION
    second_hat = second_new / SECOND_CORRECTION
    direction = first_hat / (jnp.sqrt(second_hat) + 1e-08) + decay * weight
    return (direction, first_new, second_new)


def per_device(
    patches,
    cotangent,
    res_ids,
    pos_table,
    attn_in,
    attn_out,
    mlp_in,
    mlp_out,
    vectors,
    first_attn_in,
    first_attn_out,
    first_mlp_in,
    first_mlp_out,
    first_vectors,
    second_attn_in,
    second_attn_out,
    second_mlp_in,
    second_mlp_out,
    second_vectors,
):
    row_count, local_len, width = patches.shape
    img_count, halves = lax.axis_size("img"), lax.axis_size("sy")
    chips = img_count * halves
    row_len = local_len * halves * 2
    slot_total = row_count * img_count * row_len
    head_size = width // HEADS
    own_y, own_c = lax.axis_index("sy"), lax.axis_index("sc")
    rows = attn_in.shape[0]
    half = width // 2
    ff_rows = mlp_out.shape[0]
    ff_half = chips * ff_rows
    table_size = GRID * GRID
    vector_count = vectors.shape[1]

    bits = jnp.stack([own_bit(bit) for bit in [0, 1, *far_bits()]]).astype(jnp.int32)

    def to_rows(array):
        mine = lax.dynamic_index_in_dim(array, own_y, 0, keepdims=False)
        other = lax.dynamic_index_in_dim(array, 1 - own_y, 0, keepdims=False)
        return join(mine, swap_chip(other), 0)

    res_row = pick(own_y, res_ids[0], res_ids[1])
    all_positions = jnp.arange(row_len, dtype=jnp.int32)
    segment_all, _, _, _ = layout(res_row, all_positions)
    seg = jnp.broadcast_to(segment_all.astype(F32)[None, :], (8, row_len))
    begin, end = key_bounds(res_row, row_len)
    info = jnp.concatenate([jnp.stack([own_y, own_c]).astype(jnp.int32), begin, end])
    near = jnp.arange(local_len, dtype=jnp.int32)
    positions = jnp.concatenate(
        [(2 * own_y + own_c) * local_len + near, (2 * (1 - own_y) + own_c) * local_len + near]
    )
    _, side_of, patch_index, usable = layout(res_row, positions)
    place = table_weights(side_of, patch_index, usable)
    usable = usable.astype(F32)[:, None]

    def by_core(array, blocks):
        split = array.reshape(rows, blocks, 2, -1)
        low, high = split[:, :, 0].reshape(rows, -1), split[:, :, 1].reshape(rows, -1)
        return pick(own_c, low, high), pick(own_c, high, low)

    vector_pad = jnp.pad(vectors, ((0, 0), (0, TILE - vector_count))).astype(BF16)
    mine_in, away_in = by_core(attn_in.astype(BF16), 3)
    mine_out, away_out = by_core(attn_out.astype(BF16), 1)
    mine_up, away_up = by_core(mlp_in.astype(BF16), chips)
    mine = jnp.concatenate([mine_in, mine_out, mine_up], axis=1)
    away = jnp.concatenate([away_in, away_out, away_up], axis=1)
    came, came_vector = swap_core(away), swap_core(vector_pad)
    shard = jnp.concatenate([pick(own_c, mine, came), pick(own_c, came, mine)], axis=0)
    vector_shard = jnp.concatenate(
        [pick(own_c, vector_pad, came_vector), pick(own_c, came_vector, vector_pad)], axis=0
    )[:, :16].reshape(1, -1)
    vector_row = jnp.pad(vector_shard, ((0, 0), (0, width - vector_shard.shape[1])))
    chip = lax.axis_index("img") * halves + own_y
    vector_rows = jnp.where(jnp.arange(chips)[:, None] == chip, vector_row, jnp.zeros_like(vector_row))
    in_width = 3 * half
    own = local_len * row_count
    per = local_len // TILE

    def with_core(array):
        return join(array, swap_core(array), 0)

    def sum_core(left, weights, product):
        away = product(left[own:], weights).astype(BF16)
        came = swap_core(away)
        return product(left[:own], weights) + came.astype(F32)

    low_down, high_down = jnp.split(mlp_out.astype(BF16), 2)
    ahead = list(reversed(far_bits()))
    one_way, other_way = [*ahead, 1, 0], [*ahead, 0, 1]
    block = 2 * rows
    gather_in = Gather(
        (shard[:, :width], 0, block, one_way), (shard[:, width : 2 * width], 0, block, other_way)
    )
    gather_vectors = Spread(vector_rows)
    gather_up = Gather(
        (shard[:, 2 * width : 2 * width + half * 2], 0, block, one_way),
        (shard[:, 2 * width + half * 2 :], 0, block, other_way),
    )
    low_down = mlp_out.astype(BF16)
    side = 3 * ff_rows // 8 if ff_rows % 128 == 0 else ff_rows // 2
    rest_rows = ff_rows - 2 * side
    gather_down = Gather((low_down, 0, side, one_way), (low_down, side, side, other_way))
    gather_rest = [Gather((low_down, 2 * side, rest_rows, [1, 0, *ahead]))] if rest_rows else []

    patches, cotangent = phase(
        bits,
        [(gather_in, gather_vectors, len(far_bits())), *gather_rest],
        lambda *arrays: [to_rows(array) for array in arrays],
        patches,
        cotangent,
    )

    wide_place = jnp.pad(place, ((0, 0), (0, TILE - table_size)))
    wide_table = jnp.pad(pos_table, ((0, TILE - table_size), (0, 0)))
    wide_usable = jnp.broadcast_to(usable, (own, TILE))
    small = TILE

    def first(patches, cotangent):
        def body(patches, place, cotangent, usable, table):
            stream = patches.astype(F32) + jnp.dot(place, table, precision=PRECISE, preferred_element_type=F32)
            normed, inverse = normalize(stream)
            grad = cotangent.astype(F32) * usable[:, :1]
            return stream, normed, jnp.broadcast_to(inverse, (stream.shape[0], TILE)), grad

        stream, hat_one, inverse_one, grad_own = by_rows(
            body,
            [patches, wide_place, cotangent, wide_usable],
            [wide_table],
            [(width, F32), (width, F32), (TILE, F32), (width, BF16)],
            name="first",
        )
        return stream, hat_one, inverse_one, grad_own

    far = far_bits()
    stream, hat_one, inverse_one, grad_own = phase(
        bits, [gather_in, gather_vectors, gather_up, *gather_rest], first, patches, cotangent
    )
    phase(bits, [gather_in, gather_vectors, (gather_up, len(far) - 1), gather_down], None)
    spare = in_width - width
    in_matrix, out_columns = gathered(
        gather_in.pieces,
        bits,
        [
            (
                (width, in_width),
                ([((0, block), (0, width), block, 0, 0)], [((0, block), (0, spare), block, 0, width)]),
            ),
            ((width, width - spare), ([], [((0, block), (spare, width), block, 0, 0)])),
        ],
    )
    vector_part = jnp.pad(
        gather_vectors.result()[:, : block * 16].reshape(-1, 16), ((0, 0), (0, TILE - 16))
    )
    gain_one, shift_one, bias_query, bias_value, bias_out, gain_two, shift_two, bias_down = (
        rows_from(vector_part, 8)
    )
    bias_query = pick(own_c, bias_query[:, :half], bias_query[:, half:])
    bias_value = pick(own_c, bias_value[:, :half], bias_value[:, half:])
    bias_up = unroll_bias(vector_part, own_c, ff_rows)
    bias_qkv = jnp.concatenate([bias_query, jnp.zeros_like(bias_query), bias_value], axis=1)

    def project(hat_one, out_columns):
        low, high = out_columns[:half], out_columns[half:]
        keep_out, came_out = pick(own_c, low, high), swap_core(pick(own_c, high, low))
        out_matrix = join(pick(own_c, keep_out, came_out), pick(own_c, came_out, keep_out), 1)
        return out_matrix, (hat_one * gain_one + shift_one).astype(BF16)

    out_matrix, normed_one = phase(
        bits, [gather_up, (gather_down, len(far) - 1)], project, hat_one, out_columns
    )

    def matmul_rows(left, right, product, name):
        return product(left[own:], right).astype(BF16)

    def attend(normed_one, in_matrix, out_matrix, grad_own):
        normed_one = with_core(normed_one)
        qkv = (nn(normed_one, in_matrix) + bias_qkv).astype(BF16)
        for move in gather_rest:
            old = move.arrays()
            new, qkv = fence(old, qkv)
            move.relabel(lambda array, table=list(zip(old, new)): next(b for a, b in table if a is array))
            swap_rows([move], bits)
        mixed, log_sum = attention(qkv, seg, info, per, head_size)
        away = matmul_rows(mixed, out_matrix, nn, "out_away")
        return normed_one, qkv, mixed, log_sum, away, with_core(grad_own)

    normed_one, qkv, mixed, log_sum, out_away, grad_last = phase(
        bits, [gather_up], attend, normed_one, in_matrix, out_matrix, grad_own, also=gather_rest
    )

    def project_out(stream, mixed, out_away, out_matrix):
        def body(stream, mixed, came, matrix, bias, gain, shift):
            stream_two = stream + nn(mixed, matrix) + came.astype(F32) + bias
            normed, inverse = normalize(stream_two)
            return stream_two, normed, jnp.broadcast_to(inverse, (stream.shape[0], TILE)), normed * gain + shift

        return by_rows(
            body,
            [(stream, 0, own), mixed, swap_core(out_away)],
            [out_matrix, bias_out, gain_two, shift_two],
            [(width, F32), (width, F32), (TILE, F32), (width, BF16)],
            name="out_norm",
            tile=own // 2,
        )

    stream_two, hat_two, inverse_two, normed_two = phase(
        bits, [gather_down], project_out, stream, mixed, out_away, out_matrix
    )
    (up_matrix,) = gathered(
        gather_up.pieces,
        bits,
        [
            (
                (width, ff_half),
                ([((0, block), (0, width), block, 0, 0)], [((0, block), (0, width), block, 0, width)]),
            )
        ],
    )

    def expand(normed_two, up_matrix, grad_last):
        normed_two = with_core(normed_two)
        hidden_pre = nn(normed_two, up_matrix) + bias_up
        hidden, slope = gelu_and_slope(hidden_pre)
        hidden = hidden.astype(BF16)
        return normed_two, hidden, slope, tn(hidden, grad_last).astype(BF16)

    normed_two, hidden, slope, grad_down = phase(
        bits, [gather_down, *((move, 9) for move in gather_rest)], expand, normed_two, up_matrix, grad_last
    )
    part_rows = ff_rows // 2
    down_pieces = [piece for move in [gather_down, *gather_rest] for piece in move.pieces]
    (down_matrix,) = gathered(
        down_pieces,
        bits,
        [
            (
                (ff_half, width),
                [[((0, piece.rows), (0, width), ff_rows, i * side, 0)] for i, piece in enumerate(down_pieces)],
            )
        ],
    )

    scatter_down = Scatter(
        (grad_down, part_rows, ff_rows, 0, False), (grad_down, part_rows, ff_rows, part_rows, True)
    )

    def hidden_back(grad_last, down_matrix, slope, normed_two, up_matrix):
        grad_pre = (nt(grad_last, down_matrix) * slope).astype(BF16)
        return (
            grad_pre,
            matmul_rows(grad_pre, up_matrix, nt, "norm_two_away"),
            tn(normed_two, grad_pre[:, :width]).astype(BF16),
            tn(normed_two, grad_pre[:, width:]).astype(BF16),
        )

    grad_pre, two_away, *grad_up = phase(
        bits, [scatter_down], hidden_back, grad_last, down_matrix, slope, normed_two, up_matrix
    )
    scatter_up = Scatter((grad_up[0], block, block, 0, False), (grad_up[1], block, block, 0, True))

    def norm_back(grad, away, matrix, hat, inverse, added, gain, name):
        def body(grad, came, hat, inverse, added, matrix, gain):
            back, gain_sum, shift_sum = normalize_back(hat, inverse, gain, nt(grad, matrix) + came.astype(F32))
            total = added.astype(F32) + back
            return total, total, gain_sum, shift_sum

        return by_rows(
            body,
            [(grad, 0, own), swap_core(away), hat, inverse, added],
            [matrix, gain],
            [(width, F32), (width, BF16)],
            sums=2,
            name=name,
            tile=own // 2,
        )

    def middle(values, hidden, down_matrix):
        return norm_back(*values, "norm_two_back"), matmul_rows(hidden, down_matrix, nn, "output_away")

    (grad_two, grad_branch, grad_gain_two, grad_shift_two), output_away = phase(
        bits,
        [scatter_down],
        middle,
        (grad_pre, two_away, up_matrix, hat_two, inverse_two, grad_own, gain_two),
        hidden,
        down_matrix,
    )

    paired = block % 64 == 0

    def pair(array):
        blocks = array.reshape(chips, 2, -1, array.shape[1])
        return jnp.concatenate([blocks[:, 0], blocks[:, 1]], axis=2).reshape(-1, 2 * array.shape[1])

    def part(array):
        columns = array.shape[1] // 2
        return jnp.concatenate([array[:, :columns], array[:, columns:]], axis=0)

    def attention_grads(grad_branch, out_matrix, qkv, mixed, log_sum, output_away):
        grad_branch = with_core(grad_branch)
        grad_mixed = nt(grad_branch, out_matrix).astype(BF16)
        grad_qkv = attention_back(0, 1, qkv, mixed, grad_mixed, seg, log_sum, info, per, head_size)
        grad_rows = tn(mixed, grad_branch).astype(BF16)
        low, high = grad_rows[:, :half], grad_rows[:, half:]
        keep_rows, came_rows = pick(own_c, low, high), swap_core(pick(own_c, high, low))
        grad_out = join(pick(own_c, keep_rows, came_rows), pick(own_c, came_rows, keep_rows), 0)
        return grad_branch, swap_core(output_away), grad_qkv, pair(grad_out) if paired else grad_out

    grad_branch, came_output, grad_qkv, grad_out = phase(
        bits,
        [scatter_up, scatter_down],
        attention_grads,
        grad_branch,
        out_matrix,
        qkv,
        mixed,
        log_sum,
        output_away,
    )
    quarter = block // 4
    scatter_out = []
    if paired:
        scatter_out = [
            Scatter(
                (grad_out, quarter, 2 * quarter, 0, False), (grad_out, quarter, 2 * quarter, quarter, True)
            )
        ]

    def in_grads(normed_one, grad_qkv, in_matrix):
        right = tn(normed_one, grad_qkv[:, width:]).astype(BF16)
        return (
            matmul_rows(grad_qkv, in_matrix, nt, "norm_one_away"),
            tn(normed_one, grad_qkv[:, :width]).astype(BF16),
            pair(right) if paired else right,
        )

    one_away, left, right = phase(
        bits, [scatter_up, *scatter_out, scatter_down], in_grads, normed_one, grad_qkv, in_matrix
    )
    if paired:
        scatter_in = Scatter(
            (left, 3 * quarter, block, 0, False),
            (left, quarter, block, 3 * quarter, True),
            (right, 2 * quarter, 2 * quarter, 0, True),
        )
    else:
        scatter_in = Scatter((left, block, block, 0, False), (join(right, grad_out, 1), block, block, 0, True))

    def widen(row):
        zero = jnp.zeros_like(row)
        return jnp.concatenate([pick(own_c, row, zero), pick(own_c, zero, row)], axis=1)

    narrow_rows = vector_count + table_size
    narrow_rows += -narrow_rows % 16

    def norm_one_back(grad_qkv, one_away, in_matrix, hat_one, inverse_one, grad_two, grad_pre, grad_branch, grad_last):
        grad_stream, grad_low, grad_gain_one, grad_shift_one = norm_back(
            grad_qkv, one_away, in_matrix, hat_one, inverse_one, grad_two, gain_one, "norm_one_back"
        )
        wide_place = jnp.pad(place, ((0, 0), (vector_count, narrow_rows - vector_count - table_size)))
        table_part = lax.dot_general(
            wide_place, grad_stream, (((0,), (0,)), ((), ())), precision=PRECISE, preferred_element_type=F32
        )
        bias_part = roll_bias(token_sums(grad_pre), own_c, width, narrow_rows, ff_rows)
        sums = token_sums(grad_qkv)
        rows_of_sums = [
            grad_gain_one,
            grad_shift_one,
            widen(sums[:, :half]),
            widen(sums[:, 2 * half :]),
            token_sums(grad_branch[:own]),
            grad_gain_two,
            grad_shift_two,
            token_sums(grad_last[:own]),
        ]

        def stack(*refs):
            refs[-1][...] = refs[0][...] + refs[1][...]
            for i in range(len(rows_of_sums)):
                refs[-1][i : i + 1] = refs[2 + i][...]

        narrow = pl.pallas_call(
            stack,
            name="narrow",
            out_shape=jax.ShapeDtypeStruct((narrow_rows, width), F32),
            compiler_params=pltpu.CompilerParams(vmem_limit_bytes=4 << 20),
            cost_estimate=pl.CostEstimate(flops=0, bytes_accessed=0, transcendentals=0),
        )(table_part, bias_part, *rows_of_sums)
        return grad_low, add_came(narrow, swap_core(narrow.astype(BF16)))

    def finish_output(hidden, came, stream_two, down_matrix):
        def body(hidden, came, stream_two, usable, matrix, bias):
            return ((stream_two + nn(hidden, matrix) + came.astype(F32) + bias) * usable[:, :1],)

        return by_rows(
            body,
            [(hidden, 0, own), came, stream_two, wide_usable],
            [down_matrix, bias_down],
            [(width, BF16)],
            name="output",
            tile=own // 2,
        )

    (grad_low, narrow), (output,) = phase(
        bits,
        [scatter_in, *scatter_out, scatter_up, (scatter_down, len(far) - 1)],
        lambda values, others: (norm_one_back(*values), finish_output(*others)),
        (grad_qkv, one_away, in_matrix, hat_one, inverse_one, grad_two, grad_pre, grad_branch, grad_last),
        (hidden, came_output, stream_two, down_matrix),
    )

    def rows_of(array, core):
        return lax.dynamic_slice_in_dim(array, core * rows, rows, 0)

    def trade(array, blocks):
        away, keep = rows_of(array, 1 - own_c), rows_of(array, own_c)
        came = swap_core(away).reshape(rows, blocks, -1)
        keep = keep.reshape(rows, blocks, -1)
        both = jnp.stack([pick(own_c, keep, came), pick(own_c, came, keep)], axis=2)
        return both.reshape(rows, -1)

    factor = 1.0 / slot_total

    def adam(weight, gradient, first_moment, second_moment):
        return by_rows(
            lambda w, g, m, v: adam_update(w, g, m, v, factor, 0.05),
            [weight, gradient, first_moment, second_moment],
            [],
            [(weight.shape[1], F32)] * 3,
            name="adam",
            tile=weight.shape[0],
        )

    scatters = [scatter_in, *scatter_out, scatter_up]
    square = len(far) == 2
    total = Total(narrow, [0, far[-1], *([] if square else [1, *far[:-1]])])
    phase(bits, [*scatters, total], None)
    core = own_c.astype(jnp.int32).reshape(1)

    def split_rows(pieces, columns, rule):
        arrays = []
        for p in pieces:
            arrays += [p.held[0], p.came[0]]

        def kernel(own, *refs):
            away, keep = refs[-2:]
            for here in (0, 1):

                @pl.when(own[0] == here)
                def _(here=here):
                    for out, which in ((keep, here), (away, 1 - here)):
                        for i, (low, high), (left, right), row, column in rule(which):
                            p = pieces[i]
                            at, came = p.held[1] + low, p.came[1] + low
                            out[row : row + high - low, column : column + right - left] = refs[2 * i][
                                at : at + high - low, left:right
                            ].astype(F32) + refs[2 * i + 1][came : came + high - low, left:right].astype(F32)

        size = sum(a.size * jnp.dtype(a.dtype).itemsize for a in arrays) + 8 * rows * columns
        return pl.pallas_call(
            kernel,
            name="split_rows",
            out_shape=[jax.ShapeDtypeStruct((rows, columns), F32)] * 2,
            in_specs=[pl.BlockSpec(memory_space=pltpu.SMEM)]
            + [pl.BlockSpec(memory_space=pltpu.VMEM)] * len(arrays),
            compiler_params=pltpu.CompilerParams(vmem_limit_bytes=size + (2 << 20)),
            cost_estimate=pl.CostEstimate(flops=0, bytes_accessed=0, transcendentals=0),
        )(core, *arrays)

    def adam_joined(keep, came, blocks, weight, first_moment, second_moment):
        span = keep.shape[1] // blocks

        def kernel(own, keep, came, weight, first, second, *outs):
            low_is_own = own[0] == 0
            for i in range(blocks):
                mine, other = keep[:, i * span : (i + 1) * span], came[:, i * span : (i + 1) * span]
                for j, values in enumerate(
                    (jnp.where(low_is_own, mine, other), jnp.where(low_is_own, other, mine))
                ):
                    at = slice((2 * i + j) * span, (2 * i + j + 1) * span)
                    made = adam_update(weight[:, at], values, first[:, at], second[:, at], factor, 0.05)
                    for out, value in zip(outs, (values, *made)):
                        out[:, at] = value

        size = 4 * (2 * keep.size + 7 * weight.size)
        gradient, *updated = pl.pallas_call(
            kernel,
            name="adam_joined",
            out_shape=[jax.ShapeDtypeStruct(weight.shape, F32)] * 4,
            in_specs=[pl.BlockSpec(memory_space=pltpu.SMEM)] + [pl.BlockSpec(memory_space=pltpu.VMEM)] * 5,
            compiler_params=pltpu.CompilerParams(vmem_limit_bytes=size + (2 << 20)),
            cost_estimate=pl.CostEstimate(flops=0, bytes_accessed=0, transcendentals=0),
        )(core, keep, came, weight, first_moment, second_moment)
        return gradient, updated

    def finish_up():
        away, keep = split_rows(
            scatter_up.pieces,
            ff_half,
            lambda c: [(i, (c * rows, (c + 1) * rows), (0, width), 0, i * width) for i in (0, 1)],
        )
        return adam_joined(keep, swap_core(away), chips, mlp_in, first_mlp_in, second_mlp_in)

    def finish_mlp():
        shard_down = jnp.concatenate(scatter_down.result(bits), axis=0)
        if paired:
            shard_up, adam_up = finish_up()
        else:
            shard_up = trade(jnp.concatenate(scatter_up.result(bits), axis=1), chips)
            adam_up = adam(mlp_in, shard_up, first_mlp_in, second_mlp_in)
        return shard_up, shard_down, adam_up, adam(mlp_out, shard_down, first_mlp_out, second_mlp_out)

    send_output = Rider(output, 0, local_len, local_len)
    send_grad = Rider(grad_low, 0, local_len, local_len)
    rest = [scatter_in, *scatter_out, total]
    if scatter_up.left():
        phase(bits, [*rest, (scatter_up, 9)], None)
    grad_up_shard, shard_down, adam_up, adam_down = phase(
        bits, [*rest, send_output], finish_mlp, also=[scatter_up, scatter_down]
    )

    def back_to_rows(array, other):
        mine = array[:local_len]
        return jnp.stack([pick(own_y, mine, other), pick(own_y, other, mine)], axis=0)

    if square:
        low = total.result().astype(BF16)
        sides = [Rider(low, bit, 0, narrow_rows) for bit in (1, far[0])]
        corner = 1 | (1 << (far[0] - 1))

        def last_work(output, came, low):
            across = lax.ppermute(low, "img", [(i, i ^ corner) for i in range(img_count)])
            return back_to_rows(output, came), across

        output, across = phase(
            bits, [scatter_in, *scatter_out, *sides, send_grad], last_work, output, send_output.result(), low
        )
        near, far_side = (side.result().astype(F32) for side in sides)
        narrow = (low.astype(F32) + near) + (far_side + across.astype(F32))
    else:
        output = phase(bits, [*rest, send_grad], back_to_rows, output, send_output.result())
    while scatter_in.left():
        phase(bits, rest, None)
    while total.left():
        phase(bits, [total], None)
    input_grad = back_to_rows(grad_low, send_grad.result())
    if not square:
        narrow = total.result()
    if paired:

        def in_rule(c):
            left = [(0, (0, rows), (0, width), 0, 0)]
            if c == 1:
                left = [
                    (0, (rows, 3 * quarter), (0, width), 0, 0),
                    (1, (0, quarter), (0, width), 3 * quarter - rows, 0),
                ]
            return [*left, (2, (0, rows), (c * half, (c + 1) * half), 0, width)]

        away, keep = split_rows(scatter_in.pieces, in_width, in_rule)
        grad_in_shard, adam_in = adam_joined(keep, swap_core(away), 3, attn_in, first_attn_in, second_attn_in)
        away, keep = split_rows(
            scatter_out[0].pieces,
            half,
            lambda c: [(i, (0, quarter), (c * half, (c + 1) * half), i * quarter, 0) for i in (0, 1)],
        )
        grad_out_shard, adam_out = adam_joined(
            keep, swap_core(away), 1, attn_out, first_attn_out, second_attn_out
        )
    else:
        shard_in = jnp.concatenate(scatter_in.result(bits), axis=1)
        grad_out_shard, grad_in_shard = trade(shard_in[:, in_width:], 1), trade(shard_in[:, :in_width], 3)
        adam_in = adam(attn_in, grad_in_shard, first_attn_in, second_attn_in)
        adam_out = adam(attn_out, grad_out_shard, first_attn_out, second_attn_out)
    updated = [adam_in, adam_out, adam_up, adam_down]
    device = (lax.axis_index("img") * halves + own_y) * 2 + own_c
    grad_vectors_shard = lax.dynamic_slice_in_dim(narrow[:vector_count], device * rows, rows, 1).T
    table_grad = narrow[vector_count : vector_count + table_size]

    shards = (grad_in_shard, grad_out_shard, grad_up_shard, shard_down, grad_vectors_shard)
    updated.append(adam_update(vectors, grad_vectors_shard, first_vectors, second_vectors, factor, 0.0))
    return (
        output,
        input_grad,
        table_grad,
        *shards,
        *(updated[i][0] for i in range(5)),
        *(updated[i][1] for i in range(5)),
        *(updated[i][2] for i in range(5)),
    )


def solution(mesh):
    img, seq = mesh.shape["img"], mesh.shape["seq"]
    inner = Mesh(mesh.devices.reshape(img, seq // 2, 2), ("img", "sy", "sc"))
    tokens = P("img", ("sy", "sc"), None)
    shard = P(("img", "sy", "sc"), None)
    return jax.shard_map(
        per_device,
        mesh=inner,
        in_specs=(tokens, tokens, P("img", None), P()) + (shard,) * 15,
        out_specs=(tokens, tokens, P()) + (shard,) * 20,
        check_vma=False,
    )
```

```python
import functools
import math

import jax
import jax.numpy as jnp
from jax import lax
from jax.experimental import pallas as pl
from jax.experimental.pallas import tpu as pltpu
from jax.sharding import Mesh
from jax.sharding import PartitionSpec as P

HEADS = 16
GRID = 7
GRID_HI = 12
TILE = 128

PRECISE = lax.Precision.HIGHEST
FIRST_CORRECTION = 0.9999734386011124
SECOND_CORRECTION = 0.0952078528862911
EPS = 1e-06

F32 = jnp.float32
BF16 = jnp.bfloat16


def image_spans(res_row):
    side = jnp.where(res_row == 384, GRID_HI, jnp.where(res_row == 224, GRID, 0)).astype(jnp.int32)
    lengths = side * side
    slots = res_row.shape[0]
    order = jnp.arange(slots, dtype=jnp.int32)
    earlier = order[None, :] < order[:, None]
    starts = jnp.sum(jnp.where(earlier, lengths[None, :], 0), axis=1)
    return side, lengths, starts


def layout(res_row, positions):
    side, lengths, starts = image_spans(res_row)
    slots = res_row.shape[0]
    places = positions[:, None]
    inside = ((places >= starts[None, :]) & (places < (starts + lengths)[None, :])).astype(jnp.int32)
    usable = jnp.sum(inside, axis=1)
    image_number = jnp.arange(slots, dtype=jnp.int32)
    segment = jnp.sum(inside * image_number, axis=1) + (1 - usable) * slots
    start_of = jnp.sum(inside * starts[None, :], axis=1)
    side_of = jnp.sum(inside * side[None, :], axis=1)
    patch_index = (positions - start_of) * usable
    return segment, side_of, patch_index, usable


def key_bounds(res_row, row_len):
    _, lengths, starts = image_spans(res_row)
    total = jnp.sum(lengths)
    firsts = jnp.arange(row_len // TILE, dtype=jnp.int32) * TILE

    def span(positions):
        places = positions[:, None]
        inside = (places >= starts[None, :]) & (places < (starts + lengths)[None, :])
        found = positions < total
        begin = jnp.sum(jnp.where(inside, starts[None, :], 0), axis=1)
        end = jnp.sum(jnp.where(inside, (starts + lengths)[None, :], 0), axis=1)
        return jnp.where(found, begin, total), jnp.where(found, end, row_len)

    begin, _ = span(firsts)
    _, end = span(firsts + (TILE - 1))
    return begin // TILE, (end + TILE - 1) // TILE


def axis_weights(coord, side_of):
    scaled = jnp.maximum((2 * coord + 1) * GRID - GRID_HI, 0)
    lower_fine = scaled // (2 * GRID_HI)
    fraction_fine = (scaled - lower_fine * 2 * GRID_HI).astype(F32) / (2.0 * GRID_HI)
    resized = side_of == GRID_HI
    lower_cell = jnp.where(resized, lower_fine, coord)
    fraction = jnp.where(resized, fraction_fine, jnp.zeros_like(fraction_fine))
    upper_cell = jnp.minimum(lower_cell + 1, GRID - 1)
    cell_index = jnp.arange(GRID, dtype=jnp.int32)
    below = (cell_index == lower_cell[..., None]).astype(F32)
    above = (cell_index == upper_cell[..., None]).astype(F32)
    return (1.0 - fraction)[..., None] * below + fraction[..., None] * above


def table_weights(side_of, patch_index, usable):
    safe_side = jnp.maximum(side_of, 1)
    row_coord = patch_index // safe_side
    column_coord = patch_index % safe_side
    outer = axis_weights(row_coord, side_of)[:, :, None] * axis_weights(column_coord, side_of)[:, None, :]
    outer = outer * usable.astype(F32)[:, None, None]
    return outer.reshape(side_of.shape[0], GRID * GRID)


def place_of(block, own_y, own_c, per):
    quarter = block // per
    core = (quarter % 2 + own_c) % 2
    half = (quarter // 2 + own_y) % 2
    return (core * 2 + half) * per + block % per


def split_heads(pair):
    lane = lax.broadcasted_iota(jnp.int32, pair.shape, 1)
    zero = jnp.zeros_like(pair)
    low = lane < pair.shape[1] // 2
    return jnp.concatenate([jnp.where(low, pair, zero), jnp.where(low, zero, pair)], axis=0)


def join_heads(stacked):
    half = stacked.shape[0] // 2
    lane = lax.broadcasted_iota(jnp.int32, (half, stacked.shape[1]), 1)
    return jnp.where(lane < stacked.shape[1] // 2, stacked[:half], stacked[half:])


def down_lanes(row):
    return jnp.transpose(jnp.broadcast_to(row, (TILE, TILE)))


def nt(left, right):
    return lax.dot_general(left, right, (((1,), (1,)), ((), ())), preferred_element_type=F32)


def tn(left, right):
    return lax.dot_general(left, right, (((0,), (0,)), ((), ())), preferred_element_type=F32)


def nn(left, right):
    return jnp.dot(left, right, preferred_element_type=F32)


def fold(array, over):
    parts = array.reshape(array.shape[0] // 8, 8, array.shape[1])
    return jnp.max(parts, axis=0) if over == "max" else jnp.sum(parts, axis=0)


def same_segment(seg_down, chunk, seg_q):
    same = seg_down[chunk] == seg_q
    return jnp.concatenate([same, same], axis=1)


def fill_segments(seg, seg_down):
    chunks, span, _ = seg_down.shape
    for chunk in range(chunks):
        row = seg[0:1, chunk * span : (chunk + 1) * span]
        seg_down[chunk] = jnp.transpose(jnp.broadcast_to(row, (TILE, span)))


def join_turned(turned):
    half = turned.shape[1] // 2
    row = lax.broadcasted_iota(jnp.int32, (turned.shape[0], half), 0)
    return jnp.transpose(jnp.where(row < turned.shape[0] // 2, turned[:, :half], turned[:, half:]))


def columns_of(base, j):
    return slice(base + j * TILE, base + (j + 1) * TILE)


def attend_kernel(pairs, width, per, scale, info, qkv, seg, out, log_sum, scores, turned, seg_down):
    tile = pl.program_id(0)
    chunks, span, _ = seg_down.shape
    own_y, own_c = info[0], info[1]
    ratio = span // TILE
    first = info[2 + tile] // ratio
    last = (info[2 + pl.num_programs(0) + tile] + ratio - 1) // ratio

    def at(chunk):
        return pl.multiple_of(place_of(chunk * ratio, own_y, own_c, per) * TILE, TILE)

    @pl.when(tile == 0)
    def _():
        fill_segments(seg, seg_down)
        for chunk in range(chunks):
            for j in range(pairs):
                turned[chunk, j] = jnp.transpose(qkv[pl.ds(at(chunk), span), columns_of(2 * width, j)])

    q_at = pl.multiple_of(place_of(tile, own_y, own_c, per) * TILE, TILE)
    seg_q = seg[0:1, pl.ds(pl.multiple_of(tile * TILE, TILE), TILE)]
    queries = [
        split_heads(qkv[pl.ds(q_at, TILE), columns_of(0, j)] * jnp.asarray(scale, BF16)) for j in range(pairs)
    ]

    def score(chunk, high):
        same = same_segment(seg_down, chunk, seg_q)
        products = [nt(qkv[pl.ds(at(chunk), span), columns_of(width, j)], queries[j]) for j in range(pairs)]
        made = []
        for j in range(pairs):
            s = jnp.where(same, products[j], -1e30)
            scores[j, chunk] = s
            made.append(jnp.maximum(high[j], fold(s, "max")))
        return tuple(made)

    high = lax.fori_loop(first, last, score, (jnp.full((8, 2 * TILE), -1e30, F32),) * pairs)
    tops = [jnp.max(high[j], axis=0, keepdims=True) for j in range(pairs)]

    def mix(chunk, carry):
        total, mixed = carry
        powers = [jnp.exp(scores[j, chunk] - tops[j]) for j in range(pairs)]
        return (
            tuple(total[j] + fold(powers[j], "sum") for j in range(pairs)),
            tuple(mixed[j] + nn(turned[chunk, j], powers[j].astype(BF16)) for j in range(pairs)),
        )

    total, mixed = lax.fori_loop(
        first,
        last,
        mix,
        ((jnp.zeros((8, 2 * TILE), F32),) * pairs, (jnp.zeros((TILE, 2 * TILE), F32),) * pairs),
    )
    for j in range(pairs):
        sums = jnp.sum(total[j], axis=0, keepdims=True)
        out[:, columns_of(0, j)] = join_turned(mixed[j] / sums).astype(BF16)
        log_total = tops[j] + jnp.log(sums)
        log_sum[2 * j : 2 * j + 1] = log_total[:, :TILE]
        log_sum[2 * j + 1 : 2 * j + 2] = log_total[:, TILE:]


def attend_back_kernel(
    start, pairs, width, per, scale, info, qkv, mixed, grad, seg, log_sum, out, grad_keys, grad_values, turned, seg_down
):
    tile = pl.program_id(0)
    chunks, span, _ = seg_down.shape
    own_y, own_c = info[0], info[1]
    ratio = span // TILE
    first = info[2 + tile] // ratio
    last = (info[2 + pl.num_programs(0) + tile] + ratio - 1) // ratio
    heads = range(start, start + pairs)

    def at(chunk):
        return pl.multiple_of(place_of(chunk * ratio, own_y, own_c, per) * TILE, TILE)

    @pl.when(tile == 0)
    def _():
        fill_segments(seg, seg_down)
        grad_keys[...] = jnp.zeros_like(grad_keys)
        grad_values[...] = jnp.zeros_like(grad_values)
        for chunk in range(chunks):
            for i, j in enumerate(heads):
                turned[chunk, i] = jnp.transpose(qkv[pl.ds(at(chunk), span), columns_of(width, j)])

    q_at = pl.multiple_of(place_of(tile, own_y, own_c, per) * TILE, TILE)
    q_from = pl.multiple_of(tile * TILE, TILE)
    seg_q = seg[0:1, pl.ds(q_from, TILE)]
    queries, grads, logs, inner = [], [], [], []
    for j in heads:
        queries.append(split_heads(qkv[pl.ds(q_at, TILE), columns_of(0, j)] * jnp.asarray(scale, BF16)))
        g = grad[pl.ds(q_at, TILE), columns_of(0, j)]
        grads.append(split_heads(g))
        both = jnp.transpose(g.astype(F32) * mixed[pl.ds(q_at, TILE), columns_of(0, j)].astype(F32))
        low = jnp.sum(both[: TILE // 2], axis=0, keepdims=True)
        high = jnp.sum(both[TILE // 2 :], axis=0, keepdims=True)
        inner.append(jnp.concatenate([low, high], axis=1))
        here = log_sum[2 * j : 2 * j + 2, pl.ds(q_from, TILE)]
        logs.append(jnp.concatenate([here[0:1], here[1:2]], axis=1))

    def step(chunk, carry):
        k_at = at(chunk)
        same = same_segment(seg_down, chunk, seg_q)
        scores = [nt(qkv[pl.ds(k_at, span), columns_of(width, j)], queries[i]) for i, j in enumerate(heads)]
        slopes = [nt(qkv[pl.ds(k_at, span), columns_of(2 * width, j)], grads[i]) for i, j in enumerate(heads)]
        powers = [jnp.exp(jnp.where(same, scores[i], -1e30) - logs[i]) for i in range(pairs)]
        changes = [(powers[i] * (slopes[i] - inner[i])).astype(BF16) for i in range(pairs)]
        to_values = [nn(powers[i].astype(BF16), grads[i]) for i in range(pairs)]
        to_keys = [nn(changes[i], queries[i]) for i in range(pairs)]
        to_query = tuple(carry[i] + nn(turned[chunk, i], changes[i]) for i in range(pairs))
        for i in range(pairs):
            grad_values[chunk, :, columns_of(0, i)] += to_values[i]
            grad_keys[chunk, :, columns_of(0, i)] += to_keys[i]
        return to_query

    grad_query = lax.fori_loop(first, last, step, (jnp.zeros((TILE, 2 * TILE), F32),) * pairs)
    for i in range(pairs):
        out[pl.ds(q_at, TILE), columns_of(0, i)] = (join_turned(grad_query[i]) * scale).astype(BF16)

    @pl.when(tile == pl.num_programs(0) - 1)
    def _():
        all_heads = pairs * TILE
        for chunk in range(chunks):
            out[pl.ds(at(chunk), span), all_heads : 2 * all_heads] = grad_keys[chunk].astype(BF16)
            out[pl.ds(at(chunk), span), 2 * all_heads :] = grad_values[chunk].astype(BF16)


def attention(qkv, seg, info, per, head_size):
    length, width = qkv.shape[0], qkv.shape[1] // 3
    pairs, tiles = width // TILE, length // TILE
    span = per * TILE
    chunks = length // span
    scale = head_size ** (-0.5)

    def place(i, info):
        return place_of(i, info[0], info[1], per)

    return pl.pallas_call(
        functools.partial(attend_kernel, pairs, width, per, scale),
        name="attend",
        out_shape=(
            jax.ShapeDtypeStruct((length, width), BF16),
            jax.ShapeDtypeStruct((2 * pairs, length), F32),
        ),
        grid_spec=pltpu.PrefetchScalarGridSpec(
            num_scalar_prefetch=1,
            grid=(tiles,),
            in_specs=[
                pl.BlockSpec(qkv.shape, lambda i, info: (0, 0), pipeline_mode=pl.Buffered(1)),
                pl.BlockSpec(seg.shape, lambda i, info: (0, 0), pipeline_mode=pl.Buffered(1)),
            ],
            out_specs=[
                pl.BlockSpec((TILE, width), lambda i, info: (place(i, info), 0)),
                pl.BlockSpec((2 * pairs, TILE), lambda i, info: (0, i)),
            ],
            scratch_shapes=[
                pltpu.VMEM((pairs, chunks, span, 2 * TILE), F32),
                pltpu.VMEM((chunks, pairs, TILE, span), BF16),
                pltpu.VMEM((chunks, span, TILE), F32),
            ],
        ),
        compiler_params=pltpu.CompilerParams(
            dimension_semantics=("arbitrary",), vmem_limit_bytes=20 << 20
        ),
        cost_estimate=pl.CostEstimate(flops=0, bytes_accessed=0, transcendentals=0),
    )(info, qkv, seg)


def attention_back(part, parts, qkv, mixed, grad, seg, log_sum, info, per, head_size):
    length, width = qkv.shape[0], qkv.shape[1] // 3
    pairs, tiles = width // TILE // parts, length // TILE
    span = per * TILE
    chunks = length // span
    out = jax.ShapeDtypeStruct((length, 3 * pairs * TILE), BF16)
    scale = head_size ** (-0.5)

    def whole(array):
        return pl.BlockSpec(array.shape, lambda i, info: (0, 0), pipeline_mode=pl.Buffered(1))

    return pl.pallas_call(
        functools.partial(attend_back_kernel, part * pairs, pairs, width, per, scale),
        name="attend_back",
        out_shape=out,
        grid_spec=pltpu.PrefetchScalarGridSpec(
            num_scalar_prefetch=1,
            grid=(tiles,),
            in_specs=[whole(qkv), whole(mixed), whole(grad), whole(seg), whole(log_sum)],
            out_specs=pl.BlockSpec(out.shape, lambda i, info: (0, 0)),
            scratch_shapes=[
                pltpu.VMEM((chunks, span, pairs * TILE), F32),
                pltpu.VMEM((chunks, span, pairs * TILE), F32),
                pltpu.VMEM((chunks, pairs, TILE, span), BF16),
                pltpu.VMEM((chunks, span, TILE), F32),
            ],
        ),
        compiler_params=pltpu.CompilerParams(
            dimension_semantics=("arbitrary",), vmem_limit_bytes=28 << 20
        ),
        cost_estimate=pl.CostEstimate(
            flops=32 * length * length * width, bytes_accessed=8 * length * width * 2, transcendentals=0
        ),
    )(info, qkv, mixed, grad, seg, log_sum)


SWAP = [(0, 1), (1, 0)]


def swap_core(array):
    return lax.ppermute(array, "sc", SWAP)


def swap_chip(array):
    return lax.ppermute(array, "sy", SWAP)


def swap_bit(array, bit):
    if bit == 0:
        return swap_chip(array)
    count = lax.axis_size("img")
    return lax.ppermute(array, "img", [(i, i ^ (1 << (bit - 1))) for i in range(count)])


def own_bit(bit):
    if bit == 0:
        return lax.axis_index("sy")
    return (lax.axis_index("img") >> (bit - 1)) & 1


def fence(*values):
    return lax.optimization_barrier(values)


def axis_of(bit, done):
    return sum(1 for other in done if other > bit)


def pick(index, low, high):
    return jnp.where(index == 0, low, high)


def far_bits():
    return list(range(2, int(math.log2(lax.axis_size("img"))) + 1))


def join(first, second, axis):
    shape = list(first.shape)
    shape[axis] += second.shape[axis]
    held = lax.dynamic_update_slice_in_dim(jnp.zeros(shape, first.dtype), first, 0, axis)
    return lax.dynamic_update_slice_in_dim(held, second, first.shape[axis], axis)


class Turn:
    def __init__(self):
        self.arrays, self.shapes, self.jobs = [], [], []
        self.kept = None

    def keep(self, rows, columns):
        if self.kept is None:
            self.kept = self.write((0, columns), BF16)
        before = self.shapes[self.kept].shape[0]
        self.shapes[self.kept] = jax.ShapeDtypeStruct((before + rows, columns), BF16)
        return self.kept, before

    def read(self, array):
        for i, other in enumerate(self.arrays):
            if other is array:
                return i
        self.arrays.append(array)
        return len(self.arrays) - 1

    def write(self, shape, dtype):
        self.shapes.append(jax.ShapeDtypeStruct(shape, dtype))
        return len(self.shapes) - 1

    def run(self, bits):
        count = len(self.arrays)

        def kernel(own, *refs):
            mine = [own[i] for i in range(bits.shape[0])]
            for job in self.jobs:
                job(mine, refs[:count], refs[count:])

        spent = sum(a.size * jnp.dtype(a.dtype).itemsize for a in [*self.arrays, *self.shapes])
        return pl.pallas_call(
            kernel,
            name="turn",
            out_shape=tuple(self.shapes),
            in_specs=[pl.BlockSpec(memory_space=pltpu.SMEM)] + [pl.BlockSpec(memory_space=pltpu.VMEM)] * count,
            out_specs=tuple(pl.BlockSpec(memory_space=pltpu.VMEM) for _ in self.shapes),
            compiler_params=pltpu.CompilerParams(vmem_limit_bytes=spent + (2 << 20)),
            cost_estimate=pl.CostEstimate(flops=0, bytes_accessed=0, transcendentals=0),
        )(bits, *self.arrays)


def combinations(bits):
    made = [{}]
    for bit in bits:
        made = [{**choice, bit: value} for choice in made for value in (0, 1)]
    return made


def flat_index(choice, bits):
    at = 0
    for bit in sorted(bits, reverse=True):
        at = at * 2 + choice[bit]
    return at


def block_of(at, rows, base=0):
    start = at * rows + base
    if isinstance(start, int):
        return pl.ds(start, rows)
    return pl.ds(pl.multiple_of(start, math.gcd(rows, base) if base else rows), rows)


class Piece:
    def __init__(self, array, rows, bits, order, stride=None, base=0):
        self.held, self.rows, self.bits = (array, base), rows, list(bits)
        self.fixed, self.order, self.came = [], list(order), None
        self.stride, self.source = stride or rows, bool(bits)


class Gather:
    def __init__(self, *parts):
        self.pieces = []
        for array, first, rows, order in parts:
            piece = Piece(array, rows, [], order)
            piece.held = (array, first)
            self.pieces.append(piece)

    def wants(self):
        return [(p.order[0], p.rows << (len(p.bits) + (p.came is not None))) for p in self.pieces]

    def turn(self, turn, places):
        for p, (out, base) in zip(self.pieces, places):
            if p.came is None:
                turn.jobs.append(copy_rows(turn.read(p.held[0]), p.held[1], out, base, p.rows << len(p.bits)))
            else:
                bit = p.sent
                absorb_gather(turn, p, bit, lambda choice, p=p, out=out, base=base: [(out, choice, base)])
            p.sent = p.order.pop(0)
            p.next_held = (out, base)

    def settle(self, outs, came):
        for p, where in zip(self.pieces, came):
            if p.came is not None:
                p.bits.append(p.last)
            p.held, p.came, p.last = (outs[p.next_held[0]], p.next_held[1]), where, p.sent

    def arrays(self):
        return [a for p in self.pieces for a in ([p.held[0]] + ([p.came[0]] if p.came else []))]

    def relabel(self, swap):
        for p in self.pieces:
            p.held = (swap(p.held[0]), p.held[1])
            if p.came:
                p.came = (swap(p.came[0]), p.came[1])

    def left(self):
        return len(self.pieces[0].order)


def gathered(pieces, bits, outs):
    turn = Turn()
    made = [turn.write(shape, BF16) for shape, _ in outs]
    for i, p in enumerate(pieces):
        held, came = turn.read(p.held[0]), turn.read(p.came[0])
        moves = [(out, move) for out, (_, moves) in zip(made, outs) for move in moves[i]]

        def job(mine, ins, refs, p=p, held=held, came=came, moves=moves):
            everyone = [*p.bits, p.last]
            for choice in combinations(p.bits):
                at = flat_index(choice, p.bits)
                for source, base, value in (
                    (ins[held], p.held[1], mine[p.last]),
                    (ins[came], p.came[1], 1 - mine[p.last]),
                ):
                    chip = flat_index({**choice, p.last: value}, everyone)
                    for out, ((low, high), (left, right), stride, row, column) in moves:
                        start = pl.multiple_of(chip * stride + row, math.gcd(stride, row) if row else stride)
                        refs[out][pl.ds(start, high - low), column : column + right - left] = source[
                            pl.ds(base + at * p.rows + low, high - low), left:right
                        ]

        turn.jobs.append(job)
    return turn.run(bits)


class Spread:
    def __init__(self, array):
        self.pieces = [Piece(array, array.shape[0], [], [*reversed(far_bits()), 0, 1])]

    def wants(self):
        return [(self.pieces[0].order[0], self.pieces[0].rows)]

    def turn(self, turn, places):
        [p], [(out, base)] = self.pieces, places
        p.order.pop(0)
        p.next_held = (out, base)
        if p.came is None:
            turn.jobs.append(copy_rows(turn.read(p.held[0]), p.held[1], out, base, p.rows))
            return
        held, came, held_base, came_base, rows = turn.read(p.held[0]), turn.read(p.came[0]), p.held[1], p.came[1], p.rows

        def job(mine, ins, refs):
            refs[out][base : base + rows] = (
                ins[held][held_base : held_base + rows] + ins[came][came_base : came_base + rows]
            )

        turn.jobs.append(job)

    def settle(self, outs, came):
        [p] = self.pieces
        p.held, p.came = (outs[p.next_held[0]], p.next_held[1]), came[0]

    arrays, relabel, left = Gather.arrays, Gather.relabel, Gather.left

    def result(self):
        [p] = self.pieces
        return sum(array[base : base + p.rows] for array, base in (p.held, p.came))


class Rider:
    def __init__(self, array, bit, first, rows):
        self.pieces = [Piece(array, rows, [], [bit])]
        self.pieces[0].held = (array, first)

    wants, turn, settle = Spread.wants, Spread.turn, Spread.settle
    arrays, relabel, left = Gather.arrays, Gather.relabel, Gather.left

    def result(self):
        [p] = self.pieces
        return p.came[0][p.came[1] : p.came[1] + p.rows]


class Total:
    def __init__(self, array, order):
        self.pieces = [Piece(array, array.shape[0], [], order)]

    wants, arrays, relabel, left = Spread.wants, Gather.arrays, Gather.relabel, Gather.left

    def turn(self, turn, places):
        [p], [(out, base)] = self.pieces, places
        p.order.pop(0)
        held, rows = turn.read(p.held[0]), p.rows
        came, came_base = (None, 0) if p.came is None else (turn.read(p.came[0]), p.came[1])
        p.next = None if came is None else turn.write(p.held[0].shape, F32)

        def job(mine, ins, refs, keep=p.next):
            own = ins[held][...].astype(BF16)
            if came is not None:
                total = own.astype(F32) + ins[came][came_base : came_base + rows].astype(F32)
                refs[keep][...] = total
                own = total.astype(BF16)
            refs[out][base : base + rows] = own

        turn.jobs.append(job)

    def settle(self, outs, came):
        [p] = self.pieces
        if p.next is not None:
            p.held = (outs[p.next], 0)
        p.came = came[0]

    def result(self):
        [p] = self.pieces
        return add_came(p.held[0], p.came[0][p.came[1] : p.came[1] + p.rows])


def copy_rows(source, source_base, out, base, rows):
    def job(mine, ins, refs):
        refs[out][base : base + rows] = ins[source][source_base : source_base + rows]

    return job


def absorb_gather(turn, p, bit, targets):
    held, came = turn.read(p.held[0]), turn.read(p.came[0])
    last = p.last
    known = list(p.bits)
    held_base, came_base, rows = p.held[1], p.came[1], p.rows
    [(out, _, base)] = targets(None)

    def job(mine, ins, refs):
        for choice in combinations(known):
            at = flat_index(choice, known)
            for source, start, value in ((held, held_base, mine[last]), (came, came_base, 1 - mine[last])):
                to = flat_index({**choice, last: value}, [*known, last])
                refs[out][block_of(to, rows, base)] = ins[source][block_of(at, rows, start)]

    turn.jobs.append(job)


class Scatter:
    def __init__(self, *parts):
        far = far_bits()
        bits = sorted([0, 1, *far], reverse=True)
        self.pieces = [
            Piece(array, rows, bits, [*((1, 0) if turned else (0, 1)), *far], stride, first)
            for array, rows, stride, first, turned in parts
        ]

    def wants(self):
        return [(p.order[0], p.rows << (len(p.bits) - len(p.fixed) - 1)) for p in self.pieces]

    def turn(self, turn, places):
        for p, (out, base) in zip(self.pieces, places):
            bit = p.order.pop(0)
            free = [b for b in p.bits if b not in p.fixed and b != bit]
            rows, bits, fixed = p.rows, list(p.bits), list(p.fixed)
            held = turn.read(p.held[0])
            stride, first = p.stride, p.held[1]

            def block(choice, bits=bits, stride=stride, first=first, rows=rows):
                start = flat_index(choice, bits) * stride + first
                return pl.ds(pl.multiple_of(start, math.gcd(stride, first) if first else stride), rows)

            if p.came is None:
                p.next = None

                def job(mine, ins, refs, held=held, rows=rows, free=free, bit=bit, out=out, base=base, block=block):
                    for choice in combinations(free):
                        refs[out][block_of(flat_index(choice, free), rows, base)] = ins[held][
                            block({**choice, bit: 1 - mine[bit]})
                        ]

            else:
                came, came_base = turn.read(p.came[0]), p.came[1]
                keep, keep_base = turn.keep(rows << len(free), p.held[0].shape[1])
                p.next = (keep, keep_base)

                def job(
                    mine, ins, refs, held=held, rows=rows, fixed=fixed, free=free, bit=bit, out=out, base=base,
                    came=came, came_base=came_base, keep=keep, keep_base=keep_base, block=block,
                ):
                    settled = {b: mine[b] for b in fixed}
                    for choice in combinations(free):
                        for value, target, start in ((1 - mine[bit], out, base), (mine[bit], keep, keep_base)):
                            now = {**choice, bit: value}
                            total = ins[held][block({**now, **settled})].astype(F32) + ins[came][
                                block_of(flat_index(now, [*free, bit]), rows, came_base)
                            ].astype(F32)
                            refs[target][block_of(flat_index(choice, free), rows, start)] = total.astype(BF16)

            turn.jobs.append(job)
            p.sent, p.free = bit, free

    def settle(self, outs, came):
        for p, where in zip(self.pieces, came):
            if p.next is None:
                p.fixed = [p.sent]
            else:
                p.held, p.bits, p.fixed = (outs[p.next[0]], p.next[1]), list(p.free), []
                p.stride, p.source = p.rows, False
            p.came = where

    arrays, relabel, left = Gather.arrays, Gather.relabel, Gather.left

    def result(self, bits):
        turn = Turn()
        for p in self.pieces:
            held, came, base, rows, first = turn.read(p.held[0]), turn.read(p.came[0]), p.came[1], p.rows, p.held[1]
            out = turn.write((rows, p.held[0].shape[1]), F32)

            def job(mine, ins, refs, held=held, came=came, base=base, rows=rows, out=out, first=first):
                refs[out][...] = ins[held][first : first + rows].astype(F32) + ins[came][base : base + rows].astype(F32)

            turn.jobs.append(job)
        return turn.run(bits)


def swap_rows(moves, bits):
    wants = [move.wants() for move in moves]
    sizes, places = {}, []
    for bit, rows in (want for group in wants for want in group):
        places.append((bit, sizes.get(bit, 0)))
        sizes[bit] = sizes.get(bit, 0) + rows
    turn = Turn()
    width = moves[0].pieces[0].held[0].shape[1]
    outs = {bit: turn.write((rows, width), BF16) for bit, rows in sizes.items()}
    located = [(outs[bit], base) for bit, base in places]
    starts = [0]
    for move in moves:
        starts.append(starts[-1] + len(move.pieces))
    for i, move in enumerate(moves):
        move.turn(turn, located[starts[i] : starts[i + 1]])
    made = turn.run(bits)
    got = {bit: swap_bit(made[out], bit) for bit, out in outs.items()}
    came = [(got[bit], base) for bit, base in places]
    for i, move in enumerate(moves):
        move.settle(made, came[starts[i] : starts[i + 1]])


def add_came(own, came):
    return own.astype(BF16).astype(F32) + came.astype(F32)


def add_hop(array, bit):
    return add_came(array, swap_bit(array.astype(BF16), bit))


def phase(bits, moves, work, *values, also=()):
    chains = [move if isinstance(move, tuple) else (move, 1) for move in moves]
    chains = [
        ([move for move in chain[:-1] if move.left()], min(chain[-1], chain[0].left())) for chain in chains
    ]
    moves = [move for chain, _ in chains for move in chain]

    def tie(extra):
        arrays = []
        for array in (a for move in [*moves, *also] for a in move.arrays()):
            if not any(array is other for other in arrays):
                arrays.append(array)
        held, extra = fence(arrays, extra)
        table = list(zip(arrays, held))
        for move in [*moves, *also]:
            move.relabel(lambda array: next(new for old, new in table if old is array))
        return extra

    values = tie(values)
    if moves:
        swap_rows(moves, bits)
    for chain, count in chains:
        for _ in range(count - 1):
            swap_rows(chain, bits)
    made = work(*values) if work else ()
    return tie(made)


def by_rows(body, rows, whole, outs, sums=0, tile=TILE, name="rows"):
    rows = [array if isinstance(array, tuple) else (array, 0, array.shape[0]) for array in rows]
    length = rows[0][2]
    width = outs[0][0]

    def kernel(*refs):
        ins, results = refs[: len(rows) + len(whole)], refs[len(rows) + len(whole) :]
        made = body(*(ref[...] for ref in ins))
        for ref, value in zip(results, made):
            if ref.shape[0] == 1:

                @pl.when(pl.program_id(0) == 0)
                def _(ref=ref):
                    ref[...] = jnp.zeros_like(ref)

                ref[...] += value
            else:
                ref[...] = value.astype(ref.dtype)

    spent = sum(array.size * array.dtype.itemsize for array in whole)
    for columns, kind in [*outs, *((array.shape[1], array.dtype) for array, _, _ in rows)]:
        spent += 2 * tile * columns * jnp.dtype(kind).itemsize

    def steps(columns, first=0):
        return pl.BlockSpec((tile, columns), lambda i: (i + first // tile, 0))

    def fixed(shape, **how):
        return pl.BlockSpec(shape, lambda i: (0,) * len(shape), **how)

    return pl.pallas_call(
        kernel,
        name=name,
        grid=(length // tile,),
        out_shape=[jax.ShapeDtypeStruct((length, columns), dtype) for columns, dtype in outs]
        + [jax.ShapeDtypeStruct((1, width), F32)] * sums,
        in_specs=[steps(array.shape[1], first) for array, first, _ in rows]
        + [fixed(array.shape, pipeline_mode=pl.Buffered(1)) for array in whole],
        out_specs=[steps(columns) for columns, _ in outs] + [fixed((1, width))] * sums,
        compiler_params=pltpu.CompilerParams(
            dimension_semantics=("arbitrary",), vmem_limit_bytes=spent + (12 << 20)
        ),
        cost_estimate=pl.CostEstimate(flops=0, bytes_accessed=0, transcendentals=0),
    )(*(array for array, _, _ in rows), *whole)


def normalize(stream):
    center = jnp.mean(stream, axis=-1, keepdims=True)
    centered = stream - center
    spread = jnp.mean(centered * centered, axis=-1, keepdims=True)
    inverse = lax.rsqrt(spread + EPS)
    return centered * inverse, inverse


def normalize_back(normed, inverse, gain, grad):
    scaled = grad * gain
    middle = jnp.mean(scaled, axis=-1, keepdims=True)
    along = jnp.mean(scaled * normed, axis=-1, keepdims=True)
    return (
        inverse[:, :1] * (scaled - middle - normed * along),
        jnp.sum(grad * normed, axis=0, keepdims=True),
        jnp.sum(grad, axis=0, keepdims=True),
    )


def rows_from(columns, count):
    one_hot = (jnp.arange(16)[:, None] == jnp.arange(TILE)[None, :]).astype(BF16)
    rows = nt(one_hot, columns)
    return [rows[i : i + 1] for i in range(count)]


def column_choice(rows, columns):
    row, lane = jnp.arange(rows)[:, None], jnp.arange(TILE)[None, :]
    return (row == 8 + lane % columns).astype(F32)


def own_place(width, columns):
    per_run = TILE // columns
    row, lane = jnp.arange(width)[:, None], jnp.arange(TILE)[None, :]
    return row % per_run == lane // columns


def unroll_bias(columns, own_c, ff_rows):
    width, extra = columns.shape[0], 4
    spread = nn(columns, column_choice(TILE, extra).astype(BF16))
    runs = jnp.where(own_place(width, extra), spread, 0.0).reshape(-1, TILE // extra, TILE).sum(axis=1)
    runs = runs.reshape(-1, 2, ff_rows)
    return pick(own_c, runs[:, 0], runs[:, 1]).reshape(1, -1)


def roll_bias(sums, own_c, width, rows, ff_rows):
    extra = 4
    runs = sums.reshape(-1, ff_rows)
    zero = jnp.zeros_like(runs)
    runs = jnp.stack([pick(own_c, runs, zero), pick(own_c, zero, runs)], axis=1).reshape(-1, 1, TILE)
    spread = jnp.broadcast_to(runs, (runs.shape[0], TILE // extra, TILE)).reshape(width, TILE)
    spread = jnp.where(own_place(width, extra), spread, 0.0)
    return lax.dot_general(
        column_choice(rows, extra), spread, (((1,), (1,)), ((), ())), precision=PRECISE, preferred_element_type=F32
    )


def token_sums(array):
    return nn(jnp.ones((8, array.shape[0]), BF16), array)[:1]


def gelu_and_slope(values):
    cdf = 0.5 * (1.0 + lax.erf(values * (0.5**0.5)))
    density = jnp.exp(-0.5 * values * values) * (1.0 / math.sqrt(2.0 * math.pi))
    return values * cdf, cdf + values * density


def adam_update(weight, gradient, first_moment, second_moment, factor, decay):
    scaled = gradient * factor
    first_new = 0.9 * first_moment + 0.1 * scaled
    second_new = 0.999 * second_moment + 0.001 * scaled * scaled
    first_hat = first_new / FIRST_CORRECTION
    second_hat = second_new / SECOND_CORRECTION
    direction = first_hat / (jnp.sqrt(second_hat) + 1e-08) + decay * weight
    return (direction, first_new, second_new)


def per_device(
    patches,
    cotangent,
    res_ids,
    pos_table,
    attn_in,
    attn_out,
    mlp_in,
    mlp_out,
    vectors,
    first_attn_in,
    first_attn_out,
    first_mlp_in,
    first_mlp_out,
    first_vectors,
    second_attn_in,
    second_attn_out,
    second_mlp_in,
    second_mlp_out,
    second_vectors,
):
    row_count, local_len, width = patches.shape
    img_count, halves = lax.axis_size("img"), lax.axis_size("sy")
    chips = img_count * halves
    row_len = local_len * halves * 2
    slot_total = row_count * img_count * row_len
    head_size = width // HEADS
    own_y, own_c = lax.axis_index("sy"), lax.axis_index("sc")
    rows = attn_in.shape[0]
    half = width // 2
    ff_rows = mlp_out.shape[0]
    ff_half = chips * ff_rows
    table_size = GRID * GRID
    vector_count = vectors.shape[1]

    bits = jnp.stack([own_bit(bit) for bit in [0, 1, *far_bits()]]).astype(jnp.int32)

    def to_rows(array):
        mine = lax.dynamic_index_in_dim(array, own_y, 0, keepdims=False)
        other = lax.dynamic_index_in_dim(array, 1 - own_y, 0, keepdims=False)
        return join(mine, swap_chip(other), 0)

    res_row = pick(own_y, res_ids[0], res_ids[1])
    all_positions = jnp.arange(row_len, dtype=jnp.int32)
    segment_all, _, _, _ = layout(res_row, all_positions)
    seg = jnp.broadcast_to(segment_all.astype(F32)[None, :], (8, row_len))
    begin, end = key_bounds(res_row, row_len)
    info = jnp.concatenate([jnp.stack([own_y, own_c]).astype(jnp.int32), begin, end])
    near = jnp.arange(local_len, dtype=jnp.int32)
    positions = jnp.concatenate(
        [(2 * own_y + own_c) * local_len + near, (2 * (1 - own_y) + own_c) * local_len + near]
    )
    _, side_of, patch_index, usable = layout(res_row, positions)
    place = table_weights(side_of, patch_index, usable)
    usable = usable.astype(F32)[:, None]

    def by_core(array, blocks):
        split = array.reshape(rows, blocks, 2, -1)
        low, high = split[:, :, 0].reshape(rows, -1), split[:, :, 1].reshape(rows, -1)
        return pick(own_c, low, high), pick(own_c, high, low)

    vector_pad = jnp.pad(vectors, ((0, 0), (0, TILE - vector_count))).astype(BF16)
    mine_in, away_in = by_core(attn_in.astype(BF16), 3)
    mine_out, away_out = by_core(attn_out.astype(BF16), 1)
    mine_up, away_up = by_core(mlp_in.astype(BF16), chips)
    mine = jnp.concatenate([mine_in, mine_out, mine_up], axis=1)
    away = jnp.concatenate([away_in, away_out, away_up], axis=1)
    came, came_vector = swap_core(away), swap_core(vector_pad)
    shard = jnp.concatenate([pick(own_c, mine, came), pick(own_c, came, mine)], axis=0)
    vector_shard = jnp.concatenate(
        [pick(own_c, vector_pad, came_vector), pick(own_c, came_vector, vector_pad)], axis=0
    )[:, :16].reshape(1, -1)
    vector_row = jnp.pad(vector_shard, ((0, 0), (0, width - vector_shard.shape[1])))
    chip = lax.axis_index("img") * halves + own_y
    vector_rows = jnp.where(jnp.arange(chips)[:, None] == chip, vector_row, jnp.zeros_like(vector_row))
    in_width = 3 * half
    own = local_len * row_count
    per = local_len // TILE

    def with_core(array):
        return join(array, swap_core(array), 0)

    def sum_core(left, weights, product):
        away = product(left[own:], weights).astype(BF16)
        came = swap_core(away)
        return product(left[:own], weights) + came.astype(F32)

    low_down, high_down = jnp.split(mlp_out.astype(BF16), 2)
    ahead = list(reversed(far_bits()))
    one_way, other_way = [*ahead, 1, 0], [*ahead, 0, 1]
    block = 2 * rows
    gather_in = Gather(
        (shard[:, :width], 0, block, one_way), (shard[:, width : 2 * width], 0, block, other_way)
    )
    gather_vectors = Spread(vector_rows)
    gather_up = Gather(
        (shard[:, 2 * width : 2 * width + half * 2], 0, block, one_way),
        (shard[:, 2 * width + half * 2 :], 0, block, other_way),
    )
    low_down = mlp_out.astype(BF16)
    side = 3 * ff_rows // 8 if ff_rows % 128 == 0 else ff_rows // 2
    rest_rows = ff_rows - 2 * side
    gather_down = Gather((low_down, 0, side, one_way), (low_down, side, side, other_way))
    gather_rest = [Gather((low_down, 2 * side, rest_rows, [1, 0, *ahead]))] if rest_rows else []

    patches, cotangent = phase(
        bits,
        [(gather_in, gather_vectors, len(far_bits())), *gather_rest],
        lambda *arrays: [to_rows(array) for array in arrays],
        patches,
        cotangent,
    )

    wide_place = jnp.pad(place, ((0, 0), (0, TILE - table_size)))
    wide_table = jnp.pad(pos_table, ((0, TILE - table_size), (0, 0)))
    wide_usable = jnp.broadcast_to(usable, (own, TILE))
    small = TILE

    def first(patches, cotangent):
        def body(patches, place, cotangent, usable, table):
            stream = patches.astype(F32) + jnp.dot(place, table, precision=PRECISE, preferred_element_type=F32)
            normed, inverse = normalize(stream)
            grad = cotangent.astype(F32) * usable[:, :1]
            return stream, normed, jnp.broadcast_to(inverse, (stream.shape[0], TILE)), grad

        stream, hat_one, inverse_one, grad_own = by_rows(
            body,
            [patches, wide_place, cotangent, wide_usable],
            [wide_table],
            [(width, F32), (width, F32), (TILE, F32), (width, BF16)],
            name="first",
        )
        return stream, hat_one, inverse_one, grad_own

    far = far_bits()
    stream, hat_one, inverse_one, grad_own = phase(
        bits, [gather_in, gather_vectors, gather_up, *gather_rest], first, patches, cotangent
    )
    phase(bits, [gather_in, gather_vectors, (gather_up, len(far) - 1), gather_down], None)
    spare = in_width - width
    in_matrix, out_columns = gathered(
        gather_in.pieces,
        bits,
        [
            (
                (width, in_width),
                ([((0, block), (0, width), block, 0, 0)], [((0, block), (0, spare), block, 0, width)]),
            ),
            ((width, width - spare), ([], [((0, block), (spare, width), block, 0, 0)])),
        ],
    )
    vector_part = jnp.pad(
        gather_vectors.result()[:, : block * 16].reshape(-1, 16), ((0, 0), (0, TILE - 16))
    )
    gain_one, shift_one, bias_query, bias_value, bias_out, gain_two, shift_two, bias_down = (
        rows_from(vector_part, 8)
    )
    bias_query = pick(own_c, bias_query[:, :half], bias_query[:, half:])
    bias_value = pick(own_c, bias_value[:, :half], bias_value[:, half:])
    bias_up = unroll_bias(vector_part, own_c, ff_rows)
    bias_qkv = jnp.concatenate([bias_query, jnp.zeros_like(bias_query), bias_value], axis=1)

    def project(hat_one, out_columns):
        low, high = out_columns[:half], out_columns[half:]
        keep_out, came_out = pick(own_c, low, high), swap_core(pick(own_c, high, low))
        out_matrix = join(pick(own_c, keep_out, came_out), pick(own_c, came_out, keep_out), 1)
        return out_matrix, (hat_one * gain_one + shift_one).astype(BF16)

    out_matrix, normed_one = phase(
        bits, [gather_up, (gather_down, len(far) - 1)], project, hat_one, out_columns
    )

    def matmul_rows(left, right, product, name):
        return product(left[own:], right).astype(BF16)

    def attend(normed_one, in_matrix, out_matrix, grad_own):
        normed_one = with_core(normed_one)
        qkv = (nn(normed_one, in_matrix) + bias_qkv).astype(BF16)
        for move in gather_rest:
            old = move.arrays()
            new, qkv = fence(old, qkv)
            move.relabel(lambda array, table=list(zip(old, new)): next(b for a, b in table if a is array))
            swap_rows([move], bits)
        mixed, log_sum = attention(qkv, seg, info, per, head_size)
        away = matmul_rows(mixed, out_matrix, nn, "out_away")
        return normed_one, qkv, mixed, log_sum, away, with_core(grad_own)

    normed_one, qkv, mixed, log_sum, out_away, grad_last = phase(
        bits, [gather_up], attend, normed_one, in_matrix, out_matrix, grad_own, also=gather_rest
    )

    def project_out(stream, mixed, out_away, out_matrix):
        def body(stream, mixed, came, matrix, bias, gain, shift):
            stream_two = stream + nn(mixed, matrix) + came.astype(F32) + bias
            normed, inverse = normalize(stream_two)
            return stream_two, normed, jnp.broadcast_to(inverse, (stream.shape[0], TILE)), normed * gain + shift

        return by_rows(
            body,
            [(stream, 0, own), mixed, swap_core(out_away)],
            [out_matrix, bias_out, gain_two, shift_two],
            [(width, F32), (width, F32), (TILE, F32), (width, BF16)],
            name="out_norm",
            tile=own // 2,
        )

    stream_two, hat_two, inverse_two, normed_two = phase(
        bits, [gather_down], project_out, stream, mixed, out_away, out_matrix
    )
    (up_matrix,) = gathered(
        gather_up.pieces,
        bits,
        [
            (
                (width, ff_half),
                ([((0, block), (0, width), block, 0, 0)], [((0, block), (0, width), block, 0, width)]),
            )
        ],
    )

    def expand(normed_two, up_matrix, grad_last):
        normed_two = with_core(normed_two)
        hidden_pre = nn(normed_two, up_matrix) + bias_up
        hidden, slope = gelu_and_slope(hidden_pre)
        hidden = hidden.astype(BF16)
        return normed_two, hidden, slope, tn(hidden, grad_last).astype(BF16)

    normed_two, hidden, slope, grad_down = phase(
        bits, [gather_down, *((move, 9) for move in gather_rest)], expand, normed_two, up_matrix, grad_last
    )
    part_rows = ff_rows // 2
    down_pieces = [piece for move in [gather_down, *gather_rest] for piece in move.pieces]
    (down_matrix,) = gathered(
        down_pieces,
        bits,
        [
            (
                (ff_half, width),
                [[((0, piece.rows), (0, width), ff_rows, i * side, 0)] for i, piece in enumerate(down_pieces)],
            )
        ],
    )

    scatter_down = Scatter(
        (grad_down, part_rows, ff_rows, 0, False), (grad_down, part_rows, ff_rows, part_rows, True)
    )

    def hidden_back(grad_last, down_matrix, slope, normed_two, up_matrix):
        grad_pre = (nt(grad_last, down_matrix) * slope).astype(BF16)
        return (
            grad_pre,
            matmul_rows(grad_pre, up_matrix, nt, "norm_two_away"),
            tn(normed_two, grad_pre[:, :width]).astype(BF16),
            tn(normed_two, grad_pre[:, width:]).astype(BF16),
        )

    grad_pre, two_away, *grad_up = phase(
        bits, [scatter_down], hidden_back, grad_last, down_matrix, slope, normed_two, up_matrix
    )
    scatter_up = Scatter((grad_up[0], block, block, 0, False), (grad_up[1], block, block, 0, True))

    def norm_back(grad, away, matrix, hat, inverse, added, gain, name):
        def body(grad, came, hat, inverse, added, matrix, gain):
            back, gain_sum, shift_sum = normalize_back(hat, inverse, gain, nt(grad, matrix) + came.astype(F32))
            total = added.astype(F32) + back
            return total, total, gain_sum, shift_sum

        return by_rows(
            body,
            [(grad, 0, own), swap_core(away), hat, inverse, added],
            [matrix, gain],
            [(width, F32), (width, BF16)],
            sums=2,
            name=name,
            tile=own // 2,
        )

    def middle(values, hidden, down_matrix):
        return norm_back(*values, "norm_two_back"), matmul_rows(hidden, down_matrix, nn, "output_away")

    (grad_two, grad_branch, grad_gain_two, grad_shift_two), output_away = phase(
        bits,
        [scatter_down],
        middle,
        (grad_pre, two_away, up_matrix, hat_two, inverse_two, grad_own, gain_two),
        hidden,
        down_matrix,
    )

    paired = block % 64 == 0

    def pair(array):
        blocks = array.reshape(chips, 2, -1, array.shape[1])
        return jnp.concatenate([blocks[:, 0], blocks[:, 1]], axis=2).reshape(-1, 2 * array.shape[1])

    def part(array):
        columns = array.shape[1] // 2
        return jnp.concatenate([array[:, :columns], array[:, columns:]], axis=0)

    def attention_grads(grad_branch, out_matrix, qkv, mixed, log_sum, output_away):
        grad_branch = with_core(grad_branch)
        grad_mixed = nt(grad_branch, out_matrix).astype(BF16)
        grad_qkv = attention_back(0, 1, qkv, mixed, grad_mixed, seg, log_sum, info, per, head_size)
        grad_rows = tn(mixed, grad_branch).astype(BF16)
        low, high = grad_rows[:, :half], grad_rows[:, half:]
        keep_rows, came_rows = pick(own_c, low, high), swap_core(pick(own_c, high, low))
        grad_out = join(pick(own_c, keep_rows, came_rows), pick(own_c, came_rows, keep_rows), 0)
        return grad_branch, swap_core(output_away), grad_qkv, pair(grad_out) if paired else grad_out

    grad_branch, came_output, grad_qkv, grad_out = phase(
        bits,
        [scatter_up, scatter_down],
        attention_grads,
        grad_branch,
        out_matrix,
        qkv,
        mixed,
        log_sum,
        output_away,
    )
    quarter = block // 4
    scatter_out = []
    if paired:
        scatter_out = [
            Scatter(
                (grad_out, quarter, 2 * quarter, 0, False), (grad_out, quarter, 2 * quarter, quarter, True)
            )
        ]

    def in_grads(normed_one, grad_qkv, in_matrix):
        right = tn(normed_one, grad_qkv[:, width:]).astype(BF16)
        return (
            matmul_rows(grad_qkv, in_matrix, nt, "norm_one_away"),
            tn(normed_one, grad_qkv[:, :width]).astype(BF16),
            pair(right) if paired else right,
        )

    one_away, left, right = phase(
        bits, [scatter_up, *scatter_out, scatter_down], in_grads, normed_one, grad_qkv, in_matrix
    )
    if paired:
        scatter_in = Scatter(
            (left, 3 * quarter, block, 0, False),
            (left, quarter, block, 3 * quarter, True),
            (right, 2 * quarter, 2 * quarter, 0, True),
        )
    else:
        scatter_in = Scatter((left, block, block, 0, False), (join(right, grad_out, 1), block, block, 0, True))

    def widen(row):
        zero = jnp.zeros_like(row)
        return jnp.concatenate([pick(own_c, row, zero), pick(own_c, zero, row)], axis=1)

    narrow_rows = vector_count + table_size
    narrow_rows += -narrow_rows % 16

    def norm_one_back(grad_qkv, one_away, in_matrix, hat_one, inverse_one, grad_two, grad_pre, grad_branch, grad_last):
        grad_stream, grad_low, grad_gain_one, grad_shift_one = norm_back(
            grad_qkv, one_away, in_matrix, hat_one, inverse_one, grad_two, gain_one, "norm_one_back"
        )
        wide_place = jnp.pad(place, ((0, 0), (vector_count, narrow_rows - vector_count - table_size)))
        table_part = lax.dot_general(
            wide_place, grad_stream, (((0,), (0,)), ((), ())), precision=PRECISE, preferred_element_type=F32
        )
        bias_part = roll_bias(token_sums(grad_pre), own_c, width, narrow_rows, ff_rows)
        sums = token_sums(grad_qkv)
        rows_of_sums = [
            grad_gain_one,
            grad_shift_one,
            widen(sums[:, :half]),
            widen(sums[:, 2 * half :]),
            token_sums(grad_branch[:own]),
            grad_gain_two,
            grad_shift_two,
            token_sums(grad_last[:own]),
        ]

        def stack(*refs):
            refs[-1][...] = refs[0][...] + refs[1][...]
            for i in range(len(rows_of_sums)):
                refs[-1][i : i + 1] = refs[2 + i][...]

        narrow = pl.pallas_call(
            stack,
            name="narrow",
            out_shape=jax.ShapeDtypeStruct((narrow_rows, width), F32),
            compiler_params=pltpu.CompilerParams(vmem_limit_bytes=4 << 20),
            cost_estimate=pl.CostEstimate(flops=0, bytes_accessed=0, transcendentals=0),
        )(table_part, bias_part, *rows_of_sums)
        return grad_low, add_came(narrow, swap_core(narrow.astype(BF16)))

    def finish_output(hidden, came, stream_two, down_matrix):
        def body(hidden, came, stream_two, usable, matrix, bias):
            return ((stream_two + nn(hidden, matrix) + came.astype(F32) + bias) * usable[:, :1],)

        return by_rows(
            body,
            [(hidden, 0, own), came, stream_two, wide_usable],
            [down_matrix, bias_down],
            [(width, BF16)],
            name="output",
            tile=own // 2,
        )

    (grad_low, narrow), (output,) = phase(
        bits,
        [scatter_in, *scatter_out, scatter_up, (scatter_down, len(far) - 1)],
        lambda values, others: (norm_one_back(*values), finish_output(*others)),
        (grad_qkv, one_away, in_matrix, hat_one, inverse_one, grad_two, grad_pre, grad_branch, grad_last),
        (hidden, came_output, stream_two, down_matrix),
    )

    def rows_of(array, core):
        return lax.dynamic_slice_in_dim(array, core * rows, rows, 0)

    def trade(array, blocks):
        away, keep = rows_of(array, 1 - own_c), rows_of(array, own_c)
        came = swap_core(away).reshape(rows, blocks, -1)
        keep = keep.reshape(rows, blocks, -1)
        both = jnp.stack([pick(own_c, keep, came), pick(own_c, came, keep)], axis=2)
        return both.reshape(rows, -1)

    factor = 1.0 / slot_total

    def adam(weight, gradient, first_moment, second_moment):
        return by_rows(
            lambda w, g, m, v: adam_update(w, g, m, v, factor, 0.05),
            [weight, gradient, first_moment, second_moment],
            [],
            [(weight.shape[1], F32)] * 3,
            name="adam",
            tile=weight.shape[0],
        )

    scatters = [scatter_in, *scatter_out, scatter_up]
    square = len(far) == 2
    total = Total(narrow, [0, far[-1], *([] if square else [1, *far[:-1]])])
    phase(bits, [*scatters, total], None)
    core = own_c.astype(jnp.int32).reshape(1)

    def split_rows(pieces, columns, rule):
        arrays = []
        for p in pieces:
            arrays += [p.held[0], p.came[0]]

        def kernel(own, *refs):
            away, keep = refs[-2:]
            for here in (0, 1):

                @pl.when(own[0] == here)
                def _(here=here):
                    for out, which in ((keep, here), (away, 1 - here)):
                        for i, (low, high), (left, right), row, column in rule(which):
                            p = pieces[i]
                            at, came = p.held[1] + low, p.came[1] + low
                            out[row : row + high - low, column : column + right - left] = refs[2 * i][
                                at : at + high - low, left:right
                            ].astype(F32) + refs[2 * i + 1][came : came + high - low, left:right].astype(F32)

        size = sum(a.size * jnp.dtype(a.dtype).itemsize for a in arrays) + 8 * rows * columns
        return pl.pallas_call(
            kernel,
            name="split_rows",
            out_shape=[jax.ShapeDtypeStruct((rows, columns), F32)] * 2,
            in_specs=[pl.BlockSpec(memory_space=pltpu.SMEM)]
            + [pl.BlockSpec(memory_space=pltpu.VMEM)] * len(arrays),
            compiler_params=pltpu.CompilerParams(vmem_limit_bytes=size + (2 << 20)),
            cost_estimate=pl.CostEstimate(flops=0, bytes_accessed=0, transcendentals=0),
        )(core, *arrays)

    def adam_joined(keep, came, blocks, weight, first_moment, second_moment):
        span = keep.shape[1] // blocks

        def kernel(own, keep, came, weight, first, second, *outs):
            low_is_own = own[0] == 0
            for i in range(blocks):
                mine, other = keep[:, i * span : (i + 1) * span], came[:, i * span : (i + 1) * span]
                for j, values in enumerate(
                    (jnp.where(low_is_own, mine, other), jnp.where(low_is_own, other, mine))
                ):
                    at = slice((2 * i + j) * span, (2 * i + j + 1) * span)
                    made = adam_update(weight[:, at], values, first[:, at], second[:, at], factor, 0.05)
                    for out, value in zip(outs, (values, *made)):
                        out[:, at] = value

        size = 4 * (2 * keep.size + 7 * weight.size)
        gradient, *updated = pl.pallas_call(
            kernel,
            name="adam_joined",
            out_shape=[jax.ShapeDtypeStruct(weight.shape, F32)] * 4,
            in_specs=[pl.BlockSpec(memory_space=pltpu.SMEM)] + [pl.BlockSpec(memory_space=pltpu.VMEM)] * 5,
            compiler_params=pltpu.CompilerParams(vmem_limit_bytes=size + (2 << 20)),
            cost_estimate=pl.CostEstimate(flops=0, bytes_accessed=0, transcendentals=0),
        )(core, keep, came, weight, first_moment, second_moment)
        return gradient, updated

    def finish_up():
        away, keep = split_rows(
            scatter_up.pieces,
            ff_half,
            lambda c: [(i, (c * rows, (c + 1) * rows), (0, width), 0, i * width) for i in (0, 1)],
        )
        return adam_joined(keep, swap_core(away), chips, mlp_in, first_mlp_in, second_mlp_in)

    def finish_mlp():
        shard_down = jnp.concatenate(scatter_down.result(bits), axis=0)
        if paired:
            shard_up, adam_up = finish_up()
        else:
            shard_up = trade(jnp.concatenate(scatter_up.result(bits), axis=1), chips)
            adam_up = adam(mlp_in, shard_up, first_mlp_in, second_mlp_in)
        return shard_up, shard_down, adam_up, adam(mlp_out, shard_down, first_mlp_out, second_mlp_out)

    send_output = Rider(output, 0, local_len, local_len)
    send_grad = Rider(grad_low, 0, local_len, local_len)
    rest = [scatter_in, *scatter_out, total]
    if scatter_up.left():
        phase(bits, [*rest, (scatter_up, 9)], None)
    grad_up_shard, shard_down, adam_up, adam_down = phase(
        bits, [*rest, send_output], finish_mlp, also=[scatter_up, scatter_down]
    )

    def back_to_rows(array, other):
        mine = array[:local_len]
        return jnp.stack([pick(own_y, mine, other), pick(own_y, other, mine)], axis=0)

    if square:
        low = total.result().astype(BF16)
        sides = [Rider(low, bit, 0, narrow_rows) for bit in (1, far[0])]
        corner = 1 | (1 << (far[0] - 1))

        def last_work(output, came, low):
            across = lax.ppermute(low, "img", [(i, i ^ corner) for i in range(img_count)])
            return back_to_rows(output, came), across

        output, across = phase(
            bits, [send_grad, scatter_in, *scatter_out, *sides], last_work, output, send_output.result(), low
        )
        near, far_side = (side.result().astype(F32) for side in sides)
        narrow = (low.astype(F32) + near) + (far_side + across.astype(F32))
    else:
        output = phase(bits, [*rest, send_grad], back_to_rows, output, send_output.result())
    while scatter_in.left():
        phase(bits, rest, None)
    while total.left():
        phase(bits, [total], None)
    input_grad = back_to_rows(grad_low, send_grad.result())
    if not square:
        narrow = total.result()
    if paired:

        def in_rule(c):
            left = [(0, (0, rows), (0, width), 0, 0)]
            if c == 1:
                left = [
                    (0, (rows, 3 * quarter), (0, width), 0, 0),
                    (1, (0, quarter), (0, width), 3 * quarter - rows, 0),
                ]
            return [*left, (2, (0, rows), (c * half, (c + 1) * half), 0, width)]

        away, keep = split_rows(scatter_in.pieces, in_width, in_rule)
        grad_in_shard, adam_in = adam_joined(keep, swap_core(away), 3, attn_in, first_attn_in, second_attn_in)
        away, keep = split_rows(
            scatter_out[0].pieces,
            half,
            lambda c: [(i, (0, quarter), (c * half, (c + 1) * half), i * quarter, 0) for i in (0, 1)],
        )
        grad_out_shard, adam_out = adam_joined(
            keep, swap_core(away), 1, attn_out, first_attn_out, second_attn_out
        )
    else:
        shard_in = jnp.concatenate(scatter_in.result(bits), axis=1)
        grad_out_shard, grad_in_shard = trade(shard_in[:, in_width:], 1), trade(shard_in[:, :in_width], 3)
        adam_in = adam(attn_in, grad_in_shard, first_attn_in, second_attn_in)
        adam_out = adam(attn_out, grad_out_shard, first_attn_out, second_attn_out)
    updated = [adam_in, adam_out, adam_up, adam_down]
    device = (lax.axis_index("img") * halves + own_y) * 2 + own_c
    grad_vectors_shard = lax.dynamic_slice_in_dim(narrow[:vector_count], device * rows, rows, 1).T
    table_grad = narrow[vector_count : vector_count + table_size]

    shards = (grad_in_shard, grad_out_shard, grad_up_shard, shard_down, grad_vectors_shard)
    updated.append(adam_update(vectors, grad_vectors_shard, first_vectors, second_vectors, factor, 0.0))
    return (
        output,
        input_grad,
        table_grad,
        *shards,
        *(updated[i][0] for i in range(5)),
        *(updated[i][1] for i in range(5)),
        *(updated[i][2] for i in range(5)),
    )


def solution(mesh):
    img, seq = mesh.shape["img"], mesh.shape["seq"]
    inner = Mesh(mesh.devices.reshape(img, seq // 2, 2), ("img", "sy", "sc"))
    tokens = P("img", ("sy", "sc"), None)
    shard = P(("img", "sy", "sc"), None)
    return jax.shard_map(
        per_device,
        mesh=inner,
        in_specs=(tokens, tokens, P("img", None), P()) + (shard,) * 15,
        out_specs=(tokens, tokens, P()) + (shard,) * 20,
        check_vma=False,
    )
```
